32 devices in a mesh: seq: 16 (over z, x, core), head: 2 (over y).
Axes of the slice: x: 2, y: 2, z: 4, core: 2. Of those that a mesh axis runs over, the one named last changes fastest.
Arguments:
- tokens: bfloat16 [2048, 768], P('seq'), may hold values from -6 to 6
- cotangent: bfloat16 [2048, 768], P('seq'), may hold values from -6 to 6
- doc_lengths: int32 [2], replicated, may hold values from 1 to 1600, 2048 in all
- plane_bits: int32 [64, 7, 12, 64], P(None, None, 'head'), may hold values from 0 to 1
- qkv_weight: float32 [3, 768, 768], P(None, 'seq', 'head'), may hold values from -0.21875 to 0.21875
- qkv_first: float32 [3, 768, 768], P(None, 'seq', 'head'), may hold values from -16 to 16
- qkv_second: float32 [3, 768, 768], P(None, 'seq', 'head'), may hold values from 0.256 to 4.096
- out_weight: float32 [768, 768], P('head', 'seq'), may hold values from -0.21875 to 0.21875
- out_first: float32 [768, 768], P('head', 'seq'), may hold values from -16 to 16
- out_second: float32 [768, 768], P('head', 'seq'), may hold values from 0.256 to 4.096
- up_weight: float32 [768, 3072], P('seq', 'head'), may hold values from -0.21875 to 0.21875
- up_first: float32 [768, 3072], P('seq', 'head'), may hold values from -16 to 16
- up_second: float32 [768, 3072], P('seq', 'head'), may hold values from 0.256 to 4.096
- down_weight: float32 [3072, 768], P('head', 'seq'), may hold values from -0.109375 to 0.109375
- down_first: float32 [3072, 768], P('head', 'seq'), may hold values from -16 to 16
- down_second: float32 [3072, 768], P('head', 'seq'), may hold values from 0.256 to 4.096
- norm_params: float32 [4, 768], replicated, may hold values from -1 to 1.65, as said below
- norm_first: float32 [4, 768], replicated, may hold values from -24 to 24
- norm_second: float32 [4, 768], replicated, may hold values from 0.6144 to 10.24
- conv_taps: float32 [12, 33], P('head'), may hold values from -1 to 1
- conv_first: float32 [12, 33], P('head'), may hold values from -160 to 160
- conv_second: float32 [12, 33], P('head'), may hold values from 32.768 to 524.288
Outputs:
- block_out: float32 [2048, 768], P('seq')
- tokens_grad: float32 [2048, 768], P('seq')
- occupancy: float32 [2, 64, 12, 128], P(None, None, 'head', 'seq')
- qkv_new: float32 [3, 768, 768], P(None, 'seq', 'head')
- qkv_first_new: float32 [3, 768, 768], P(None, 'seq', 'head')
- qkv_second_new: float32 [3, 768, 768], P(None, 'seq', 'head')
- qkv_copy: bfloat16 [3, 768, 768], P(None, 'seq', 'head')
- out_new: float32 [768, 768], P('head', 'seq')
- out_first_new: float32 [768, 768], P('head', 'seq')
- out_second_new: float32 [768, 768], P('head', 'seq')
- out_copy: bfloat16 [768, 768], P('head', 'seq')
- up_new: float32 [768, 3072], P('seq', 'head')
- up_first_new: float32 [768, 3072], P('seq', 'head')
- up_second_new: float32 [768, 3072], P('seq', 'head')
- up_copy: bfloat16 [768, 3072], P('seq', 'head')
- down_new: float32 [3072, 768], P('head', 'seq')
- down_first_new: float32 [3072, 768], P('head', 'seq')
- down_second_new: float32 [3072, 768], P('head', 'seq')
- down_copy: bfloat16 [3072, 768], P('head', 'seq')
- norm_new: float32 [4, 768], replicated
- norm_first_new: float32 [4, 768], replicated
- norm_second_new: float32 [4, 768], replicated
- conv_new: float32 [12, 33], P('head')
- conv_first_new: float32 [12, 33], P('head')
- conv_second_new: float32 [12, 33], P('head')
The draws below stay inside these ranges and needn't reach their ends.
Inputs may be any that keep to these rules, and one draw needn't show every extreme that they name: `doc_lengths`: the documents lie end to end in the stream; the longest has at most 1600 tokens. `norm_params`: rows 0 and 2 are gains, rows 1 and 3 offsets.
All inputs are finite; a program needn't handle non-finite values.
Results may differ from the reference program's by a relative error of at most 0.015.
Values may be sent and summed in bfloat16 or wider, within the bound.
No kernel may reach another device: no remote copies, remote signals or barrier semaphores. Data moves between devices by JAX's collectives and lax.ppermute only.
A program may use at most 128 MiB of HBM per device.

```python
import math
import jax
import jax.numpy as jnp
import numpy as np
from jax import lax

D = 768
H = 12
HD = 64
FF = 3072
NH = 64
BITS = 7
CONV = 33
SEGS = 2
STEP = 7
TOK_DEV = 128
TOKENS = 2048


def draw_norm_params(key, part):
    gain_key, offset_key = jax.random.split(jax.random.fold_in(key, 11))
    gains = jnp.exp(jax.random.uniform(gain_key, (2, D), jnp.float32, -0.5, 0.5))
    offsets = jnp.clip(0.3 * jax.random.normal(offset_key, (2, D), jnp.float32), -1.0, 1.0)
    return jnp.stack([gains[0], offsets[0], gains[1], offsets[1]]).astype(jnp.float32)


def set_ends(drawn, stream_key, least, largest):
    spot = [jax.random.randint(jax.random.fold_in(stream_key, axis), (), 0, length) for axis, length in enumerate(drawn.shape)]
    main_axis = drawn.shape.index(max(drawn.shape))
    next_to = spot[:main_axis] + [(spot[main_axis] + 1) % drawn.shape[main_axis]] + spot[main_axis + 1:]
    return drawn.at[tuple(spot)].set(least).at[tuple(next_to)].set(largest)


def shard_levels(key, extent, pieces, low, top_value):
    def one(position, blocks):
        steps = jax.random.uniform(jax.random.fold_in(jax.random.fold_in(key, 6), position), (blocks,), jnp.float32, low / len(pieces), top_value / len(pieces))
        return jnp.repeat(jnp.exp(steps), extent[position] // blocks).reshape((-1,) + (1,) * (len(extent) - position - 1))

    factor_of = one(*pieces[0])
    for cut in pieces[1:]:
        factor_of = factor_of * one(*cut)
    return factor_of


def split_up(amount, total, reach, slope):
    weights = [(1 << 20) // math.isqrt(rank ** slope) + 1 for rank in range(2, amount + 1)]
    surplus, given = total - reach - (amount - 1), [1] * (amount - 1)
    while surplus > 0:
        candidates = [i for i in range(amount - 1) if given[i] < reach]
        whole, remaining = sum([weights[i] for i in candidates]), surplus
        for i in candidates:
            more = min(reach - given[i], max(1, remaining * weights[i] // whole), surplus)
            given[i] = given[i] + more
            surplus = surplus - more
    return np.array([reach] + given)


def ragged_sizes(rng, number_of, total, limit, skew):
    if number_of == 2:
        one = jax.random.randint(rng, (), max(1, total - limit), min(limit, total - 1) + 1)
        return jnp.stack([one, total - one])
    sizes = jnp.asarray(split_up(number_of, total, limit, skew), jnp.int32)
    couples = (number_of - 1) // 2
    source_of, receiver = sizes[1:1 + 2 * couples:2], sizes[2:2 + 2 * couples:2]
    margin = jnp.minimum(source_of - 1, limit - receiver)
    moved = jax.random.randint(jax.random.fold_in(rng, 1), (couples,), 0, 1 << 20) % (margin + 1)
    sizes = sizes.at[1:1 + 2 * couples:2].set(source_of - moved).at[2:2 + 2 * couples:2].set(receiver + moved)
    return sizes[jax.random.permutation(jax.random.fold_in(rng, 2), number_of)]


def centred(key, dims, scale, bound, cuts=(), kind=jnp.bfloat16):
    result = scale * jax.random.normal(key, dims, jnp.float32)
    if cuts:
        result = result * shard_levels(key, dims, cuts, -0.22, 0.18)
    return jnp.clip(result, -bound, bound).astype(kind)


def setup_inputs(seed: int = 0) -> dict:
    streams_of = jax.random.split(jax.random.key(seed), 23)
    tokens = centred(streams_of[0], (TOKENS, D), 1.0, 6.0, ((0, 16),))
    cotangent = centred(streams_of[1], (TOKENS, D), 1.0, 6.0, ((0, 16),))
    doc_lengths = ragged_sizes(streams_of[2], SEGS, TOKENS, TOKENS * 3 // 4 + TOK_DEV // 2, 0).astype(jnp.int32)
    plane_bits = set_ends(jax.random.randint(streams_of[3], (NH, BITS, H, HD), 0, 2), jax.random.fold_in(streams_of[3], 1), 0, 1).astype(jnp.int32)
    qkv_weight = centred(streams_of[4], (3, D, D), D ** -0.5, 0.21875, ((1, 16), (2, 2)), jnp.float32)
    qkv_first = centred(streams_of[5], (3, D, D), (0.055 * TOKENS ** 0.5), 16.0, ((1, 16), (2, 2)), jnp.float32)
    qkv_second = jnp.clip(jnp.exp(math.log(4.096) - 2.7725887 * jax.random.uniform(streams_of[6], (3, D, D), jnp.float32) ** shard_levels(streams_of[6], (3, D, D), ((1, 16), (2, 2)), -0.2, 0.2)), 0.256, 4.096)
    out_weight = centred(streams_of[7], (D, D), D ** -0.5, 0.21875, ((0, 2), (1, 16)), jnp.float32)
    out_first = centred(streams_of[8], (D, D), (0.055 * TOKENS ** 0.5), 16.0, ((0, 2), (1, 16)), jnp.float32)
    out_second = jnp.clip(jnp.exp(math.log(4.096) - 2.7725887 * jax.random.uniform(streams_of[9], (D, D), jnp.float32) ** shard_levels(streams_of[9], (D, D), ((0, 2), (1, 16)), -0.2, 0.2)), 0.256, 4.096)
    up_weight = centred(streams_of[10], (D, FF), D ** -0.5, 0.21875, ((0, 16), (1, 2)), jnp.float32)
    up_first = centred(streams_of[11], (D, FF), (0.055 * TOKENS ** 0.5), 16.0, ((0, 16), (1, 2)), jnp.float32)
    up_second = jnp.clip(jnp.exp(math.log(4.096) - 2.7725887 * jax.random.uniform(streams_of[12], (D, FF), jnp.float32) ** shard_levels(streams_of[12], (D, FF), ((0, 16), (1, 2)), -0.2, 0.2)), 0.256, 4.096)
    down_weight = centred(streams_of[13], (FF, D), FF ** -0.5, 0.109375, ((0, 2), (1, 16)), jnp.float32)
    down_first = centred(streams_of[14], (FF, D), (0.055 * TOKENS ** 0.5), 16.0, ((0, 2), (1, 16)), jnp.float32)
    down_second = jnp.clip(jnp.exp(math.log(4.096) - 2.7725887 * jax.random.uniform(streams_of[15], (FF, D), jnp.float32) ** shard_levels(streams_of[15], (FF, D), ((0, 2), (1, 16)), -0.2, 0.2)), 0.256, 4.096)
    norm_params = draw_norm_params(jax.random.fold_in(streams_of[22], 71), 0)
    norm_first = centred(streams_of[17], (4, D), (0.09 * TOKENS ** 0.5), 24.0, (), jnp.float32)
    norm_second = jnp.clip(jnp.exp(jax.random.uniform(streams_of[18], (4, D), jnp.float32, math.log(0.6144), math.log(10.24))), 0.6144, 10.24)
    conv_taps = centred(streams_of[19], (H, CONV), CONV ** -0.5, 1.0, ((0, 2),), jnp.float32)
    conv_first = centred(streams_of[20], (H, CONV), (0.08 * (TOKENS * HD) ** 0.5), 160.0, ((0, 2),), jnp.float32)
    conv_second = jnp.clip(jnp.exp(math.log(524.288) - 2.7725887 * jax.random.uniform(streams_of[21], (H, CONV), jnp.float32) ** shard_levels(streams_of[21], (H, CONV), ((0, 2),), -0.2, 0.2)), 32.768, 524.288)
    return dict(tokens=tokens, cotangent=cotangent, doc_lengths=doc_lengths, plane_bits=plane_bits, qkv_weight=qkv_weight, qkv_first=qkv_first, qkv_second=qkv_second, out_weight=out_weight, out_first=out_first, out_second=out_second, up_weight=up_weight, up_first=up_first, up_second=up_second, down_weight=down_weight, down_first=down_first, down_second=down_second, norm_params=norm_params, norm_first=norm_first, norm_second=norm_second, conv_taps=conv_taps, conv_first=conv_first, conv_second=conv_second)


@jax.custom_vjp
def low(v):
    return lax.optimization_barrier(v.astype(jnp.bfloat16)).astype(jnp.float32)

@jax.custom_vjp
def low_back(v):
    return v

def low_keep(v):
    return (low(v), None)

def low_pass(kept, grad):
    return (grad,)

def back_keep(v):
    return (v, None)

def back_low(kept, grad):
    return (low(grad),)
low.defvjp(low_keep, low_pass)
low_back.defvjp(back_keep, back_low)
sharpness = 4.0
norm_eps = 1e-06
layer_eps = 1e-05
beta_one = 0.9
beta_two = 0.999
adam_eps = 1e-08
decay_rate = 0.01
highest = lax.Precision.HIGHEST

def bit_table(bit_count):
    all_codes = jnp.arange(2 ** bit_count, dtype=jnp.int32)
    places = 2 ** jnp.arange(bit_count, dtype=jnp.int32)
    return (all_codes[None, :] // places[:, None] % 2).astype(jnp.float32)

def soft_codes(unit_vals, planes):
    scaled = jnp.einsum('thd,rjhd->rhjt', unit_vals, planes, precision=highest) * (sharpness / math.sqrt(unit_vals.shape[2]))
    selector = bit_table(planes.shape[1])
    logits = jnp.einsum('rhjt,jb->rhtb', jax.nn.log_sigmoid(scaled), selector, precision=highest)
    logits = logits + jnp.einsum('rhjt,jb->rhtb', jax.nn.log_sigmoid(-scaled), 1.0 - selector, precision=highest)
    return jnp.exp(logits)

def unit_rows(source):
    return source * lax.rsqrt(lax.optimization_barrier(jnp.mean(source * source, axis=-1, keepdims=True)) + norm_eps)

def layer_norm(source, gain, offset):
    centered = source - lax.optimization_barrier(jnp.mean(source, axis=-1, keepdims=True))
    spread = lax.optimization_barrier(jnp.mean(centered * centered, axis=-1, keepdims=True))
    return centered * lax.rsqrt(spread + layer_eps) * gain + offset

def segment_masks(positions, doc_lengths):
    bounds = jnp.cumsum(doc_lengths).astype(jnp.int32)[:-1]
    seg_ids = lax.optimization_barrier(jnp.sum((positions[:, None] >= bounds[None, :]).astype(jnp.int32), axis=1)).astype(jnp.int32)
    seg_mask = (seg_ids[:, None] == jnp.arange(doc_lengths.shape[0], dtype=jnp.int32)[None, :]).astype(jnp.float32)
    return (seg_ids, seg_mask)

def conv_values(ext_rows, seg_ext, seg_own, tap_weights):
    tok_rows = seg_own.shape[0]
    running = jnp.zeros((tok_rows, tap_weights.shape[0], ext_rows.shape[2]), jnp.float32)
    for offset in range(tap_weights.shape[1]):
        same_doc = (seg_ext[offset:offset + tok_rows] == seg_own).astype(jnp.float32)
        running = running + tap_weights[:, offset][None, :, None] * ext_rows[offset:offset + tok_rows].astype(jnp.float32) * same_doc[:, None, None]
    return running

def fill_part(key_unit, masked, seg_mask, plane):
    hash_codes = soft_codes(key_unit, plane[None])[0]
    table_set = jnp.einsum('htb,thf->hbf', low(hash_codes), masked, precision=highest)
    count_set = jnp.einsum('htb,ts->shb', hash_codes, seg_mask, precision=highest)
    return (table_set, count_set)

def read_part(query_unit, plane, table_set):
    hash_codes = low(soft_codes(query_unit, plane[None])[0])
    return jnp.einsum('htb,hbf->thf', hash_codes, table_set, precision=highest)

def forward(inputs, qkv_w, out_w, up_w, down_w, norm_w, conv_w, planes, seg_mask, seg_ids):
    tok_rows, feat_width = inputs.shape
    head_count, head_dim = (planes.shape[2], planes.shape[3])
    seg_count = seg_mask.shape[1]
    proj = low_back(jnp.einsum('tc,pcf->ptf', inputs, low(qkv_w), precision=highest))
    queries = proj[0].reshape(tok_rows, head_count, head_dim)
    key_proj = proj[1].reshape(tok_rows, head_count, head_dim)
    values = low(proj[2]).reshape(tok_rows, head_count, head_dim)
    query_unit = low(unit_rows(queries))
    key_unit = low(unit_rows(key_proj))
    masked = (values[:, :, None, :] * seg_mask[:, None, :, None]).reshape(tok_rows, head_count, seg_count * head_dim)
    fill_saved = jax.checkpoint(fill_part)
    tables, counts = lax.map(lambda plane: fill_saved(key_unit, masked, seg_mask, plane), planes)
    table_low = low(low_back(tables))
    read_saved = jax.checkpoint(read_part)

    def read_step(running, step_items):
        return (running + read_saved(query_unit, step_items[0], step_items[1]), None)
    gathered, unused = lax.scan(read_step, jnp.zeros((tok_rows, head_count, seg_count * head_dim), jnp.float32), (planes, table_low))
    numerator = low_back(lax.optimization_barrier(jnp.sum(gathered.reshape(tok_rows, head_count, seg_count, head_dim) * seg_mask[:, None, :, None], axis=2)))
    attention = unit_rows(numerator)
    rim_width = conv_w.shape[1] // 2
    ext_rows = jnp.pad(values, ((rim_width, rim_width), (0, 0), (0, 0)))
    seg_ext = jnp.pad(seg_ids, (rim_width, rim_width), constant_values=-1)
    mixed_rows = attention + conv_values(ext_rows, seg_ext, seg_ids, conv_w)
    context = low(mixed_rows.reshape(tok_rows, feat_width))
    mixer_out = low_back(jnp.dot(context, low(out_w), precision=highest))
    first_out = layer_norm(inputs + mixer_out, norm_w[0], norm_w[1])
    hidden = low_back(jnp.dot(low(first_out), low(up_w), precision=highest))
    active = low(jax.nn.gelu(hidden, approximate=False))
    feed_out = low_back(jnp.dot(active, low(down_w), precision=highest))
    block_out = layer_norm(first_out + feed_out, norm_w[2], norm_w[3])
    return (block_out, jnp.transpose(counts, (1, 0, 2, 3)))

def adam_step(weight, first, second, grad, rate):
    first_new = beta_one * first + (1.0 - beta_one) * grad
    second_new = beta_two * second + (1.0 - beta_two) * grad * grad
    fix_one = 1.0 - beta_one ** STEP
    fix_two = 1.0 - beta_two ** STEP
    update = first_new / fix_one / (jnp.sqrt(second_new / fix_two) + adam_eps) + decay_rate * weight
    return (weight - rate * update, first_new, second_new)

def reference(tokens, cotangent, doc_lengths, plane_bits, qkv_weight, qkv_first, qkv_second, out_weight, out_first, out_second, up_weight, up_first, up_second, down_weight, down_first, down_second, norm_params, norm_first, norm_second, conv_taps, conv_first, conv_second):
    tok_rows = tokens.shape[0]
    positions = jnp.arange(tok_rows, dtype=jnp.int32)
    seg_ids, seg_mask = segment_masks(positions, doc_lengths)
    planes = (2 * plane_bits - 1).astype(jnp.float32)
    inputs = tokens.astype(jnp.float32)

    def run_layer(inputs, qkv_w, out_w, up_w, down_w, norm_w, conv_w):
        return forward(inputs, qkv_w, out_w, up_w, down_w, norm_w, conv_w, planes, seg_mask, seg_ids)
    block_out, pullback, counts = jax.vjp(run_layer, inputs, qkv_weight, out_weight, up_weight, down_weight, norm_params, conv_taps, has_aux=True)
    gradients = pullback(cotangent.astype(jnp.float32))
    bucket_count = 2 ** plane_bits.shape[1]
    occupancy = counts * (bucket_count / tok_rows)
    qkv_new, qkv_first_new, qkv_second_new = adam_step(qkv_weight, qkv_first, qkv_second, gradients[1], D ** (-0.5))
    out_new, out_first_new, out_second_new = adam_step(out_weight, out_first, out_second, gradients[2], D ** (-0.5))
    up_new, up_first_new, up_second_new = adam_step(up_weight, up_first, up_second, gradients[3], D ** (-0.5))
    down_new, down_first_new, down_second_new = adam_step(down_weight, down_first, down_second, gradients[4], FF ** (-0.5))
    norm_new, norm_first_new, norm_second_new = adam_step(norm_params, norm_first, norm_second, gradients[5], 0.3)
    conv_new, conv_first_new, conv_second_new = adam_step(conv_taps, conv_first, conv_second, gradients[6], CONV ** (-0.5))
    return (block_out, gradients[0], occupancy, qkv_new, qkv_first_new, qkv_second_new, qkv_new.astype(jnp.bfloat16), out_new, out_first_new, out_second_new, out_new.astype(jnp.bfloat16), up_new, up_first_new, up_second_new, up_new.astype(jnp.bfloat16), down_new, down_first_new, down_second_new, down_new.astype(jnp.bfloat16), norm_new, norm_first_new, norm_second_new, conv_new, conv_first_new, conv_second_new)
```

```python
from functools import partial
import math

import jax
import jax.numpy as jnp
from jax import lax
from jax.experimental import pallas as pl
from jax.experimental.pallas import tpu as pltpu
from jax.sharding import PartitionSpec as P

D = 768
FF = 3072
CONV = 33
STEP = 7
CORES = 2

sharpness = 4.0
norm_eps = 1e-06
layer_eps = 1e-05
beta_one = 0.9
beta_two = 0.999
adam_eps = 1e-08
decay_rate = 0.01
highest = lax.Precision.HIGHEST
f32 = jnp.float32
bf16 = jnp.bfloat16
VMEM_LIMIT = 56 * 1024 * 1024


def nn(a, b):
    return lax.dot_general(a, b, (((1,), (0,)), ((), ())), preferred_element_type=f32)


def nt(a, b):
    return lax.dot_general(a, b, (((1,), (1,)), ((), ())), preferred_element_type=f32)


def swap_sum(value):
    own = lax.optimization_barrier(value.astype(bf16))
    other = lax.ppermute(own, "head", [(0, 1), (1, 0)])
    return own.astype(f32) + other.astype(f32)


def normalize(source):
    centered = source - jnp.mean(source, axis=-1, keepdims=True)
    inverse = lax.rsqrt(jnp.mean(centered * centered, axis=-1, keepdims=True) + layer_eps)
    return (centered * inverse, inverse)


def norm_back(grad, normed, inverse, gain):
    scaled = grad * gain
    inner = (
        scaled
        - jnp.mean(scaled, axis=-1, keepdims=True)
        - normed * jnp.mean(scaled * normed, axis=-1, keepdims=True)
    )
    return (inverse * inner, jnp.sum(grad * normed, axis=0), jnp.sum(grad, axis=0))


def adam_step(weight, first, second, grad, rate):
    first_new = beta_one * first + (1.0 - beta_one) * grad
    second_new = beta_two * second + (1.0 - beta_two) * grad * grad
    fix_one = 1.0 - beta_one**STEP
    fix_two = 1.0 - beta_two**STEP
    update = first_new / fix_one / (jnp.sqrt(second_new / fix_two) + adam_eps) + decay_rate * weight
    return (weight - rate * update, first_new, second_new)


def head_units(source):
    inverse = lax.rsqrt(jnp.mean(source * source, axis=0, keepdims=True) + norm_eps)
    return source * inverse, inverse


def log_norms(unit, bit_planes, bits, rows):
    z = jnp.abs(nn(bit_planes, unit))
    parts = 0.5 * z + jnp.log1p(jnp.exp(-z))
    total = parts[0:rows]
    for j in range(1, bits):
        total = total + parts[j * rows : (j + 1) * rows]
    return total


def seg_rows(limit, start, width):
    pos = start + lax.broadcasted_iota(jnp.int32, (1, width), 1)
    late = (pos >= limit).astype(f32)
    return 1.0 - late, late


def masked_pair(rows, early, late):
    return jnp.concatenate([rows * early, rows * late], axis=0).astype(bf16)


def forward_kernel(
    hashes, bits, rows, tile, tiles,
    limit_ref, tok_ref, w_ref, code_ref, bit_ref,
    num_ref, qu_ref, ku_ref, v_ref, inv_ref, table_ref, count_ref,
    acc_ref, codes_ref,
):
    buckets = 2**bits
    limit = limit_ref[0]
    acc_ref[...] = jnp.zeros_like(acc_ref)

    def fill(i, carry):
        start = pl.multiple_of(i * tile, tile)
        span = pl.ds(start, tile)
        proj = nt(w_ref[0], tok_ref[span, :])
        q_unit, q_inv = head_units(proj[0:64])
        k_unit, k_inv = head_units(proj[64:128])
        q_low = q_unit.astype(bf16)
        k_low = k_unit.astype(bf16)
        values = proj[128:192].astype(bf16)
        qu_ref[:, span] = q_low
        ku_ref[:, span] = k_low
        v_ref[:, span] = values
        inv_ref[0, 0:1, span] = q_inv
        inv_ref[0, 1:2, span] = k_inv
        norms = log_norms(k_low, bit_ref[0], bits, rows)
        logits = nn(code_ref[0], k_low)
        for r in range(hashes):
            part = slice(r * buckets, (r + 1) * buckets)
            codes_ref[part, :] = jnp.exp(logits[part] - norms[r : r + 1]).astype(bf16)
        early, late = seg_rows(limit, start, tile)
        marks = jnp.concatenate([early, late, jnp.zeros((14, tile), f32)], axis=0).astype(bf16)
        pair = jnp.concatenate([masked_pair(values.astype(f32), early, late), marks], axis=0)
        acc_ref[...] += nt(codes_ref[...], pair)
        return carry

    lax.fori_loop(0, tiles, fill, 0)
    table = acc_ref[:, 0:128].astype(bf16)
    table_ref[0] = table
    table_t = jnp.transpose(table.astype(f32)).astype(bf16)
    counts = jnp.concatenate(
        [acc_ref[:, 128:144], jnp.zeros((hashes * buckets, 112), f32)], axis=1
    )
    count_ref[0] = jnp.transpose(counts)[0:8]

    def read(i, carry):
        start = pl.multiple_of(i * tile, tile)
        span = pl.ds(start, tile)
        q_low = qu_ref[:, span]
        norms = log_norms(q_low, bit_ref[0], bits, rows)
        logits = nn(code_ref[0], q_low)
        for r in range(hashes):
            part = slice(r * buckets, (r + 1) * buckets)
            codes_ref[part, :] = jnp.exp(logits[part] - norms[r : r + 1]).astype(bf16)
        both = nn(table_t, codes_ref[...])
        early, late = seg_rows(limit, start, tile)
        num_ref[i] = (both[0:64] * early + both[64:128] * late).astype(bf16)
        return carry

    lax.fori_loop(0, tiles, read, 0)


def backward_kernel(
    hashes, bits, rows, tile, tiles, heads,
    limit_ref, spot_ref, tok_ref, w_ref, code_ref, code_t_ref, bit_ref,
    qu_ref, ku_ref, v_ref, inv_ref, table_ref, gnum_ref, conv_ref,
    grad_ref, back_ref,
    acc_ref, codes_ref, slopes_ref, proj_ref,
):
    buckets = 2**bits
    limit = limit_ref[0]
    spot = spot_ref[0]
    head = pl.program_id(0)
    acc_ref[...] = jnp.zeros_like(acc_ref)

    def soften(unit, slopes, span):
        norms = log_norms(unit, bit_ref[0], bits, rows)
        logits = nn(code_ref[0], unit)
        for r in range(hashes):
            part = slice(r * buckets, (r + 1) * buckets)
            codes = jnp.exp(logits[part] - norms[r : r + 1])
            weighted = codes * slopes[part]
            total = jnp.sum(weighted, axis=0, keepdims=True)
            codes_ref[part, :] = codes.astype(bf16)
            slopes_ref[part, :] = (weighted - codes * total).astype(bf16)
        return nn(code_t_ref[0], slopes_ref[...])

    def unit_back(grad, unit, inverse):
        unit = unit.astype(f32)
        inner = jnp.mean(grad * unit, axis=0, keepdims=True)
        return inverse * (grad - unit * inner)

    def queries(i, carry):
        start = pl.multiple_of(i * tile, tile)
        span = pl.ds(start, tile)
        early, late = seg_rows(limit, start, tile)
        pair = masked_pair(gnum_ref[i].astype(f32), early, late)
        unit = qu_ref[:, span]
        grad = soften(unit, nn(table_ref[0], pair), span)
        acc_ref[...] += nt(codes_ref[...], pair)
        proj_ref[head, 0:64, span] = unit_back(grad, unit, inv_ref[0, 0:1, span]).astype(bf16)
        return carry

    lax.fori_loop(0, tiles, queries, 0)
    table_grad = acc_ref[...].astype(bf16)
    table_grad_t = jnp.transpose(table_grad.astype(f32)).astype(bf16)

    def keys(i, carry):
        start = pl.multiple_of(i * tile, tile)
        span = pl.ds(start, tile)
        early, late = seg_rows(limit, start, tile)
        pair = masked_pair(v_ref[:, span].astype(f32), early, late)
        unit = ku_ref[:, span]
        grad = soften(unit, nn(table_grad, pair), span)
        both = nn(table_grad_t, codes_ref[...])
        here = (spot == i).astype(f32)
        value_grad = both[0:64] * early + both[64:128] * late + conv_ref[...] * here
        proj_ref[head, 64:128, span] = unit_back(grad, unit, inv_ref[0, 1:2, span]).astype(bf16)
        proj_ref[head, 128:192, span] = value_grad.astype(bf16)
        return carry

    lax.fori_loop(0, tiles, keys, 0)
    grad_ref[...] = nn(proj_ref[head], tok_ref[...])

    @pl.when(head == heads - 1)
    def _():
        def inputs(i, carry):
            span = pl.ds(pl.multiple_of(i * tile, tile), tile)
            part = nn(w_ref[0], proj_ref[0, :, span])
            for h in range(1, heads):
                part = part + nn(w_ref[h], proj_ref[h, :, span])
            half = tile // CORES
            for k in range(CORES):
                back_ref[k, i] = part[:, k * half : (k + 1) * half].astype(bf16)
            return carry

        lax.fori_loop(0, tiles, inputs, 0)


def on_device(
    tokens,
    cotangent,
    doc_lengths,
    plane_bits,
    qkv_weight,
    qkv_first,
    qkv_second,
    out_weight,
    out_first,
    out_second,
    up_weight,
    up_first,
    up_second,
    down_weight,
    down_first,
    down_second,
    norm_params,
    norm_first,
    norm_second,
    conv_taps,
    conv_first,
    conv_second,
):
    tok_rows, width = tokens.shape
    hash_count, bits, group_heads, head_dim = plane_bits.shape
    buckets = 2**bits
    taps = conv_taps.shape[1]
    rim = taps // 2
    seq_count = lax.axis_size("seq")
    chips = seq_count // CORES
    place = lax.axis_index("seq")
    spot, core = place // CORES, place % CORES
    heads = group_heads // CORES
    feats = heads * head_dim
    group_feats = group_heads * head_dim
    hashes = hash_count // chips
    rows = -(-hashes // 8) * 8
    tile = CORES * tok_rows
    total = chips * tile
    own_rows = width // seq_count
    ff = up_weight.shape[1]
    pairs = [[CORES * c + k for k in range(CORES)] for c in range(chips)]
    planes_of = [[CORES * c + k for c in range(chips)] for k in range(CORES)]
    across = partial(
        lax.all_to_all, axis_name="seq", split_axis=0, concat_axis=0, tiled=True,
        axis_index_groups=planes_of,
    )
    within = partial(
        lax.all_to_all, axis_name="seq", split_axis=0, concat_axis=0, tiled=True,
        axis_index_groups=pairs,
    )
    limit = doc_lengths[0:1]

    qkv_rows = jnp.transpose(qkv_weight, (1, 0, 2)).astype(bf16)
    qkv_extra = qkv_rows.size // width
    first_send = jnp.concatenate([tokens, qkv_rows.reshape(qkv_extra, width)], axis=0)
    first_got = lax.all_gather(first_send, "seq", axis=0, tiled=False)
    all_tokens = first_got[:, :tok_rows].reshape(total, width)
    qkv_all = first_got[:, tok_rows:].reshape(width, 3, group_feats)
    second_send = jnp.concatenate(
        [out_weight.T.astype(bf16), up_weight.astype(bf16), down_weight.T.astype(bf16)], axis=1
    )
    second_send, first_got_tie = lax.optimization_barrier((second_send, first_got[0, 0, 0:1]))
    weights = lax.all_gather(second_send, "seq", axis=0, tiled=True)
    out_wt = weights[:, :group_feats]
    up_w = weights[:, group_feats : group_feats + ff]
    down_wt = weights[:, group_feats + ff :]

    own_planes = lax.dynamic_slice(
        plane_bits, (spot * hashes, 0, core * heads, 0), (hashes, bits, heads, head_dim)
    )
    signs = (2 * own_planes - 1).astype(f32)
    scale = sharpness / math.sqrt(head_dim)
    table_bits = (
        jnp.arange(buckets, dtype=jnp.int32)[None, :] // (2 ** jnp.arange(bits, dtype=jnp.int32))[:, None] % 2
    ).astype(f32) - 0.5
    code_w = scale * sum(
        table_bits[j][None, None, :, None] * jnp.transpose(signs[:, j], (1, 0, 2))[:, :, None, :]
        for j in range(bits)
    )
    code_w = code_w.reshape(heads, hashes * buckets, head_dim).astype(bf16)
    code_wt = jnp.transpose(code_w, (0, 2, 1))
    bit_w = scale * jnp.pad(
        jnp.transpose(signs, (2, 1, 0, 3)), ((0, 0), (0, 0), (0, rows - hashes), (0, 0))
    )
    bit_w = bit_w.reshape(heads, bits * rows, head_dim).astype(bf16)

    own_w = lax.dynamic_slice(qkv_all, (0, 0, core * feats), (width, 3, feats))
    own_w = own_w.reshape(width, 3, heads, head_dim)
    w_rows = jnp.transpose(own_w, (2, 1, 3, 0)).reshape(heads, 3 * head_dim, width)
    w_cols = jnp.transpose(own_w, (2, 0, 1, 3)).reshape(heads, width, 3 * head_dim)

    smem = pl.BlockSpec(memory_space=pltpu.SMEM)
    whole = lambda shape: pl.BlockSpec(
        shape, lambda h: (0,) * len(shape), pipeline_mode=pl.Buffered(1)
    )
    by_head = lambda *shape: pl.BlockSpec((1,) + shape, lambda h: (h,) + (0,) * len(shape))
    head_rows = pl.BlockSpec((head_dim, total), lambda h: (h, 0))
    code_rows = hashes * buckets
    params = pltpu.CompilerParams(
        dimension_semantics=("arbitrary",), vmem_limit_bytes=VMEM_LIMIT
    )
    num_parts, q_unit, k_unit, values, inverses, tables, counts = pl.pallas_call(
        partial(forward_kernel, hashes, bits, rows, tile, chips),
        grid=(heads,),
        in_specs=[
            smem,
            whole((total, width)),
            by_head(3 * head_dim, width),
            by_head(code_rows, head_dim),
            by_head(bits * rows, head_dim),
        ],
        out_specs=[
            pl.BlockSpec((chips, head_dim, tile), lambda h: (0, h, 0)),
            head_rows,
            head_rows,
            head_rows,
            by_head(8, total),
            by_head(code_rows, 2 * head_dim),
            by_head(8, code_rows),
        ],
        out_shape=[
            jax.ShapeDtypeStruct((chips, feats, tile), bf16),
            jax.ShapeDtypeStruct((feats, total), bf16),
            jax.ShapeDtypeStruct((feats, total), bf16),
            jax.ShapeDtypeStruct((feats, total), bf16),
            jax.ShapeDtypeStruct((heads, 8, total), f32),
            jax.ShapeDtypeStruct((heads, code_rows, 2 * head_dim), bf16),
            jax.ShapeDtypeStruct((heads, 8, code_rows), f32),
        ],
        scratch_shapes=[
            pltpu.VMEM((code_rows, 2 * head_dim + 16), f32),
            pltpu.VMEM((code_rows, tile), bf16),
        ],
        compiler_params=params,
        name="hash_forward",
    )(limit, all_tokens, w_rows, code_w, bit_w)

    slice_width = buckets // seq_count
    count_send = counts[:, 0:2].reshape(heads, 2, hashes, seq_count, slice_width)
    count_got = lax.all_to_all(
        jnp.transpose(count_send, (3, 1, 2, 0, 4)), "seq", 0, 0, tiled=True
    ).reshape(chips, CORES, 2, hashes, heads, slice_width)
    occupancy = jnp.transpose(count_got, (2, 0, 3, 1, 4, 5)).reshape(
        2, hash_count, group_heads, slice_width
    ) * (buckets / (tok_rows * seq_count))

    ext = tile + 2 * rim
    chip_start = spot * tile
    tok_pos = chip_start + jnp.arange(tile, dtype=jnp.int32)
    ext_pos = chip_start - rim + jnp.arange(ext, dtype=jnp.int32)
    same = ((tok_pos >= limit[0])[None, :] == (ext_pos >= limit[0])[:, None]).astype(f32)
    apart = jnp.arange(ext, dtype=jnp.int32)[:, None] - jnp.arange(tile, dtype=jnp.int32)[None, :]
    own_taps = lax.dynamic_slice(conv_taps, (core * heads, 0), (heads, taps))
    spread = jnp.zeros((heads, ext, tile), f32)
    gather_back = jnp.zeros((heads, ext, tile), f32)
    for o in range(taps):
        spread = spread + own_taps[:, o][:, None, None] * (apart == o)
        gather_back = gather_back + own_taps[:, o][:, None, None] * (apart == 2 * rim - o)
    spread = spread * same
    gather_back = gather_back * same

    num_got = across(num_parts)
    numerator = jnp.sum(num_got.astype(f32), axis=0).reshape(heads, head_dim, tile)
    mean_sq = jnp.mean(numerator * numerator, axis=1, keepdims=True)
    att_inv = lax.rsqrt(mean_sq + norm_eps)
    attention = numerator * att_inv
    value_ext = lax.dynamic_slice(
        jnp.pad(values, ((0, 0), (rim, rim))), (0, chip_start), (feats, ext)
    ).reshape(heads, head_dim, ext)
    conv = jnp.einsum("hfe,het->hft", value_ext.astype(f32), spread, precision=highest)
    context = (attention + conv).astype(bf16).reshape(feats, CORES, tok_rows)
    context = within(jnp.transpose(context, (1, 0, 2))).reshape(group_feats, tok_rows)

    mixer_out = swap_sum(jnp.einsum("ft,cf->tc", context, out_wt, preferred_element_type=f32))
    first_hat, first_inverse = normalize(tokens.astype(f32) + mixer_out)
    first_out = first_hat * norm_params[0] + norm_params[1]
    first_low = first_out.astype(bf16)
    hidden = jnp.dot(first_low, up_w, preferred_element_type=f32)
    gelu_out, gelu_pull = jax.vjp(partial(jax.nn.gelu, approximate=False), hidden)
    active = gelu_out.astype(bf16)
    feed_out = swap_sum(jnp.einsum("tf,cf->tc", active, down_wt, preferred_element_type=f32))
    second_hat, second_inverse = normalize(first_out + feed_out)
    block_out = second_hat * norm_params[2] + norm_params[3]
    grad_out = cotangent.astype(f32)
    grad_second, gain_two, offset_two = norm_back(
        grad_out, second_hat, second_inverse, norm_params[2]
    )
    grad_feed_low = grad_second.astype(bf16)
    grad_active = jnp.dot(grad_feed_low, down_wt, preferred_element_type=f32)
    grad_hidden_low = gelu_pull(grad_active)[0].astype(bf16)
    grad_first = grad_second + swap_sum(
        jnp.einsum("tf,cf->tc", grad_hidden_low, up_w, preferred_element_type=f32)
    )
    grad_mixer, gain_one, offset_one = norm_back(
        grad_first, first_hat, first_inverse, norm_params[0]
    )
    grad_mixer_low = grad_mixer.astype(bf16)
    grad_context = jnp.einsum("tc,cf->ft", grad_mixer_low, out_wt, preferred_element_type=f32)
    grad_context = within(grad_context.reshape(CORES, feats, tok_rows))
    grad_context = jnp.transpose(grad_context, (1, 0, 2)).reshape(heads, head_dim, tile)
    att_grad = att_inv * (
        grad_context - attention * jnp.mean(grad_context * attention, axis=1, keepdims=True)
    )
    gnum = att_grad.astype(bf16).reshape(feats, tile)
    gnum_all = across(jnp.broadcast_to(gnum[None], (chips, feats, tile)))

    big_grad = jnp.concatenate(
        [
            jnp.einsum("tc,ft->cf", grad_mixer_low, context, preferred_element_type=f32).astype(bf16),
            jnp.einsum("tc,tf->cf", first_low, grad_hidden_low, preferred_element_type=f32).astype(bf16),
            jnp.einsum("tc,tf->cf", grad_feed_low, active, preferred_element_type=f32).astype(bf16),
        ],
        axis=1,
    )
    big_owned = lax.psum_scatter(big_grad, "seq", scatter_dimension=0, tiled=True).astype(f32)

    low_context = grad_context.astype(bf16).reshape(feats, tile)
    up_moves = [(i, i + CORES) for i in range(seq_count - CORES)]
    down_moves = [(j, i) for i, j in up_moves]
    before = lax.ppermute(low_context[:, tile - rim :], "seq", up_moves)
    after = lax.ppermute(low_context[:, :rim], "seq", down_moves)
    context_ext = jnp.concatenate([before, low_context, after], axis=1).reshape(
        heads, head_dim, ext
    )
    conv_grad = jnp.einsum(
        "hfe,het->hft", context_ext.astype(f32), gather_back, precision=highest
    ).reshape(feats, tile)
    crossed = jnp.einsum(
        "hfe,hft->het", value_ext.astype(f32), grad_context, precision=highest
    ) * same
    tap_grad = jnp.stack(
        [jnp.sum(crossed * (apart == o), axis=(1, 2)) for o in range(taps)], axis=1
    )
    tap_rows = lax.dynamic_update_slice(
        jnp.zeros((group_heads, taps), f32), tap_grad, (core * heads, 0)
    )
    small = jnp.concatenate(
        [
            jnp.stack([gain_one, offset_one, gain_two, offset_two]),
            jnp.pad(tap_rows, ((0, 8 - group_heads), (0, width - taps))),
        ],
        axis=0,
    )
    small_got = lax.all_to_all(
        jnp.broadcast_to(small[None], (seq_count,) + small.shape), "seq", 0, 0, tiled=True
    )
    small_sum = jnp.sum(small_got, axis=0)
    norm_grad = small_sum[:4]
    conv_tap_grad = small_sum[4 : 4 + group_heads, :taps]

    grad_parts, back_parts = pl.pallas_call(
        partial(backward_kernel, hashes, bits, rows, tile, chips, heads),
        grid=(heads,),
        in_specs=[
            smem,
            smem,
            whole((total, width)),
            whole((heads, width, 3 * head_dim)),
            by_head(code_rows, head_dim),
            by_head(head_dim, code_rows),
            by_head(bits * rows, head_dim),
            head_rows,
            head_rows,
            head_rows,
            by_head(8, total),
            by_head(code_rows, 2 * head_dim),
            pl.BlockSpec((chips, head_dim, tile), lambda h: (0, h, 0)),
            pl.BlockSpec((head_dim, tile), lambda h: (h, 0)),
        ],
        out_specs=[
            pl.BlockSpec((3 * head_dim, width), lambda h: (h, 0)),
            pl.BlockSpec(
                (CORES, chips, width, tok_rows), lambda h: (0, 0, 0, 0),
                pipeline_mode=pl.Buffered(1),
            ),
        ],
        out_shape=[
            jax.ShapeDtypeStruct((3 * feats, width), f32),
            jax.ShapeDtypeStruct((CORES, chips, width, tok_rows), bf16),
        ],
        scratch_shapes=[
            pltpu.VMEM((code_rows, 2 * head_dim), f32),
            pltpu.VMEM((code_rows, tile), bf16),
            pltpu.VMEM((code_rows, tile), bf16),
            pltpu.VMEM((heads, 3 * head_dim, total), bf16),
        ],
        compiler_params=params,
        name="hash_backward",
    )(
        limit, spot[None], all_tokens, w_cols, code_w, code_wt, bit_w,
        q_unit, k_unit, values, inverses, tables, gnum_all, conv_grad,
    )

    qkv_send = grad_parts.T.astype(bf16).reshape(chips, CORES * own_rows, 3 * feats)
    qkv_half = jnp.sum(across(qkv_send).astype(f32), axis=0)
    qkv_half = within(qkv_half.reshape(CORES, own_rows, 3 * feats))
    qkv_owned = jnp.transpose(
        qkv_half.reshape(CORES, own_rows, heads, 3, head_dim), (3, 1, 0, 2, 4)
    ).reshape(3, own_rows, group_feats)

    mine = lax.dynamic_index_in_dim(back_parts, core, 0, keepdims=False)
    theirs = lax.dynamic_index_in_dim(back_parts, 1 - core, 0, keepdims=False)
    swap = [(i, i ^ 1) for i in range(seq_count)]
    chip_sum = mine.astype(f32) + lax.ppermute(theirs, "seq", swap).astype(f32)
    side = lax.axis_index("head")
    half = width // 2
    chip_sum = chip_sum.astype(bf16).reshape(chips, 2, half, tok_rows)
    keep = lax.dynamic_index_in_dim(chip_sum, side, 1, keepdims=False)
    give = lax.dynamic_index_in_dim(chip_sum, 1 - side, 1, keepdims=False)
    pair_sum = keep.astype(f32) + lax.ppermute(give, "head", [(0, 1), (1, 0)]).astype(f32)
    back_half = jnp.sum(across(pair_sum.astype(bf16)).astype(f32), axis=0)
    back_other = lax.ppermute(back_half, "head", [(0, 1), (1, 0)])
    upper = jnp.where(side == 0, back_half, back_other)
    lower = jnp.where(side == 0, back_other, back_half)
    tokens_grad = grad_mixer + jnp.concatenate([upper, lower], axis=0).T

    out_owned = big_owned[:, :group_feats].T
    up_owned = big_owned[:, group_feats : group_feats + ff]
    down_owned = big_owned[:, group_feats + ff :].T
    qkv_new, qkv_first_new, qkv_second_new = adam_step(
        qkv_weight, qkv_first, qkv_second, qkv_owned, D ** (-0.5)
    )
    out_new, out_first_new, out_second_new = adam_step(
        out_weight, out_first, out_second, out_owned, D ** (-0.5)
    )
    up_new, up_first_new, up_second_new = adam_step(
        up_weight, up_first, up_second, up_owned, D ** (-0.5)
    )
    down_new, down_first_new, down_second_new = adam_step(
        down_weight, down_first, down_second, down_owned, FF ** (-0.5)
    )
    norm_new, norm_first_new, norm_second_new = adam_step(
        norm_params, norm_first, norm_second, norm_grad, 0.3
    )
    conv_new, conv_first_new, conv_second_new = adam_step(
        conv_taps, conv_first, conv_second, conv_tap_grad, CONV ** (-0.5)
    )
    return (
        block_out,
        tokens_grad,
        occupancy,
        qkv_new,
        qkv_first_new,
        qkv_second_new,
        qkv_new.astype(jnp.bfloat16),
        out_new,
        out_first_new,
        out_second_new,
        out_new.astype(jnp.bfloat16),
        up_new,
        up_first_new,
        up_second_new,
        up_new.astype(jnp.bfloat16),
        down_new,
        down_first_new,
        down_second_new,
        down_new.astype(jnp.bfloat16),
        norm_new,
        norm_first_new,
        norm_second_new,
        conv_new,
        conv_first_new,
        conv_second_new,
    )


def solution(mesh):
    in_specs = (
        P("seq", None),
        P("seq", None),
        P(),
        P(None, None, "head", None),
        P(None, "seq", "head"),
        P(None, "seq", "head"),
        P(None, "seq", "head"),
        P("head", "seq"),
        P("head", "seq"),
        P("head", "seq"),
        P("seq", "head"),
        P("seq", "head"),
        P("seq", "head"),
        P("head", "seq"),
        P("head", "seq"),
        P("head", "seq"),
        P(),
        P(),
        P(),
        P("head", None),
        P("head", None),
        P("head", None),
    )
    out_specs = (
        P("seq", None),
        P("seq", None),
        P(None, None, "head", "seq"),
        P(None, "seq", "head"),
        P(None, "seq", "head"),
        P(None, "seq", "head"),
        P(None, "seq", "head"),
        P("head", "seq"),
        P("head", "seq"),
        P("head", "seq"),
        P("head", "seq"),
        P("seq", "head"),
        P("seq", "head"),
        P("seq", "head"),
        P("seq", "head"),
        P("head", "seq"),
        P("head", "seq"),
        P("head", "seq"),
        P("head", "seq"),
        P(),
        P(),
        P(),
        P("head", None),
        P("head", None),
        P("head", None),
    )
    return jax.shard_map(
        on_device, mesh=mesh, in_specs=in_specs, out_specs=out_specs, check_vma=False
    )
```

```python
from functools import partial
import math

import jax
import jax.numpy as jnp
from jax import lax
from jax.experimental import pallas as pl
from jax.experimental.pallas import tpu as pltpu
from jax.sharding import PartitionSpec as P

D = 768
FF = 3072
CONV = 33
STEP = 7
CORES = 2

sharpness = 4.0
norm_eps = 1e-06
layer_eps = 1e-05
beta_one = 0.9
beta_two = 0.999
adam_eps = 1e-08
decay_rate = 0.01
highest = lax.Precision.HIGHEST
f32 = jnp.float32
bf16 = jnp.bfloat16
VMEM_LIMIT = 56 * 1024 * 1024


def nn(a, b):
    return lax.dot_general(a, b, (((1,), (0,)), ((), ())), preferred_element_type=f32)


def nt(a, b):
    return lax.dot_general(a, b, (((1,), (1,)), ((), ())), preferred_element_type=f32)


def normalize(source):
    centered = source - jnp.mean(source, axis=-1, keepdims=True)
    inverse = lax.rsqrt(jnp.mean(centered * centered, axis=-1, keepdims=True) + layer_eps)
    return (centered * inverse, inverse)


def norm_back(grad, normed, inverse, gain):
    scaled = grad * gain
    inner = (
        scaled
        - jnp.mean(scaled, axis=-1, keepdims=True)
        - normed * jnp.mean(scaled * normed, axis=-1, keepdims=True)
    )
    gains = jnp.sum(grad * normed, axis=0, keepdims=True)
    return (inverse * inner, gains, jnp.sum(grad, axis=0, keepdims=True))


def adam_step(weight, first, second, grad, rate):
    first_new = beta_one * first + (1.0 - beta_one) * grad
    second_new = beta_two * second + (1.0 - beta_two) * grad * grad
    fix_one = 1.0 - beta_one**STEP
    fix_two = 1.0 - beta_two**STEP
    update = first_new / fix_one / (jnp.sqrt(second_new / fix_two) + adam_eps) + decay_rate * weight
    return (weight - rate * update, first_new, second_new)


def head_units(source):
    inverse = lax.rsqrt(jnp.mean(source * source, axis=0, keepdims=True) + norm_eps)
    return source * inverse, inverse


def log_norms(unit, bit_planes, bits, rows):
    z = jnp.abs(nn(bit_planes, unit))
    parts = 0.5 * z + jnp.log(1.0 + jnp.exp(-z))
    total = parts[0:rows]
    for j in range(1, bits):
        total = total + parts[j * rows : (j + 1) * rows]
    return total


def seg_rows(limit, start, width):
    pos = start + lax.broadcasted_iota(jnp.int32, (1, width), 1)
    late = (pos >= limit).astype(f32)
    return 1.0 - late, late


def masked_pair(rows, early, late):
    return jnp.concatenate([rows * early, rows * late], axis=0).astype(bf16)


def flip(value):
    return jnp.transpose(value.astype(f32)).astype(bf16)


def bit_halves(buckets, bits):
    place = lax.broadcasted_iota(jnp.int32, (buckets, 8), 1)
    bucket = lax.broadcasted_iota(jnp.int32, (buckets, 8), 0)
    value = ((bucket >> place) & 1).astype(f32) - 0.5
    return jnp.where(place < bits, value, 0.0).astype(bf16)


def code_matrix(sign_ref, code_ref, hashes, bits):
    buckets = 2**bits
    halves = bit_halves(buckets, bits)
    for r in range(hashes):
        code_ref[r * buckets : (r + 1) * buckets, :] = nn(halves, sign_ref[0, r]).astype(bf16)


def forward_kernel(
    hashes, bits, rows, tile, tiles, heads, group_feats,
    spots_ref, got_ref, qk_ref, vo_ref, sign_ref, bit_ref,
    num_ref, qu_ref, ku_ref, v_ref, inv_ref, table_ref, count_ref, w_ref,
    acc_ref, codes_ref, code_ref, wt_ref,
):
    buckets = 2**bits
    limit = spots_ref[0]
    core = spots_ref[2]
    head = pl.program_id(0)
    feats = heads * 64
    tok_rows = tile // CORES

    for k in range(CORES):
        @pl.when((head == 0) & (core == k))
        def _():
            for h in range(heads):
                for p, (ref, base) in enumerate(((qk_ref, 0), (qk_ref, group_feats), (vo_ref, 0))):
                    start = base + k * feats + h * 64
                    part = ref[:, start : start + 64]
                    spot = (3 * h + p) * 64
                    w_ref[:, spot : spot + 64] = part
                    wt_ref[h, p * 64 : (p + 1) * 64, :] = flip(part)

    code_matrix(sign_ref, code_ref, hashes, bits)
    acc_ref[...] = jnp.zeros_like(acc_ref)
    v_ref[:, 0:128] = jnp.zeros((64, 128), bf16)
    v_ref[:, 128 + tiles * tile :] = jnp.zeros((64, 128), bf16)

    def fill(i, carry):
        start = pl.multiple_of(i * tile, tile)
        span = pl.ds(start, tile)
        toks = got_ref[pl.ds(i * CORES, CORES), 0:tok_rows, :].reshape(tile, got_ref.shape[2])
        proj = nt(wt_ref[head], toks)
        q_unit, q_inv = head_units(proj[0:64])
        k_unit, k_inv = head_units(proj[64:128])
        q_low = q_unit.astype(bf16)
        k_low = k_unit.astype(bf16)
        values = proj[128:192].astype(bf16)
        qu_ref[:, span] = q_low
        ku_ref[:, span] = k_low
        v_ref[:, pl.ds(pl.multiple_of(start + 128, 128), tile)] = values
        inv_ref[0, 0:1, span] = q_inv
        inv_ref[0, 1:2, span] = k_inv
        norms = log_norms(k_low, bit_ref[0], bits, rows)
        logits = nn(code_ref[...], k_low)
        for r in range(hashes):
            part = slice(r * buckets, (r + 1) * buckets)
            codes_ref[part, :] = jnp.exp(logits[part] - norms[r : r + 1]).astype(bf16)
        early, late = seg_rows(limit, start, tile)
        marks = jnp.concatenate([early, late, jnp.zeros((14, tile), f32)], axis=0).astype(bf16)
        pair = jnp.concatenate([masked_pair(values.astype(f32), early, late), marks], axis=0)
        acc_ref[...] += nt(codes_ref[...], pair)
        return carry

    lax.fori_loop(0, tiles, fill, 0)
    table = acc_ref[:, 0:128].astype(bf16)
    table_ref[0] = table
    table_t = flip(table)
    counts = jnp.concatenate(
        [acc_ref[:, 128:144], jnp.zeros((hashes * buckets, 112), f32)], axis=1
    )
    count_ref[0] = jnp.transpose(counts)[0:8]

    def read(i, carry):
        start = pl.multiple_of(i * tile, tile)
        span = pl.ds(start, tile)
        q_low = qu_ref[:, span]
        norms = log_norms(q_low, bit_ref[0], bits, rows)
        logits = nn(code_ref[...], q_low)
        for r in range(hashes):
            part = slice(r * buckets, (r + 1) * buckets)
            codes_ref[part, :] = jnp.exp(logits[part] - norms[r : r + 1]).astype(bf16)
        both = nn(table_t, codes_ref[...])
        early, late = seg_rows(limit, start, tile)
        num_ref[i] = (both[0:64] * early + both[64:128] * late).astype(bf16)
        return carry

    lax.fori_loop(0, tiles, read, 0)


def backward_kernel(
    hashes, bits, rows, tile, tiles, heads, own_rows,
    spots_ref, got_ref, w_ref, sign_ref, bit_ref,
    qu_ref, ku_ref, v_ref, inv_ref, table_ref, gnum_ref, conv_ref, tap_ref,
    grad_ref, keep_ref, give_ref,
    acc_ref, codes_ref, slopes_ref, proj_ref, code_ref, code_t_ref, sum_ref,
):
    buckets = 2**bits
    limit = spots_ref[0]
    spot = spots_ref[1]
    core = spots_ref[2]
    head = pl.program_id(0)
    width = got_ref.shape[2]
    tok_rows = tile // CORES
    code_matrix(sign_ref, code_ref, hashes, bits)
    code_t_ref[...] = flip(code_ref[...])
    acc_ref[...] = jnp.zeros_like(acc_ref)

    def soften(unit, slopes):
        norms = log_norms(unit, bit_ref[0], bits, rows)
        logits = nn(code_ref[...], unit)
        for r in range(hashes):
            part = slice(r * buckets, (r + 1) * buckets)
            codes = jnp.exp(logits[part] - norms[r : r + 1])
            weighted = codes * slopes[part]
            total = jnp.sum(weighted, axis=0, keepdims=True)
            codes_ref[part, :] = codes.astype(bf16)
            slopes_ref[part, :] = (weighted - codes * total).astype(bf16)
        return nn(code_t_ref[...], slopes_ref[...])

    def unit_back(grad, unit, inverse):
        unit = unit.astype(f32)
        inner = jnp.mean(grad * unit, axis=0, keepdims=True)
        return inverse * (grad - unit * inner)

    def queries(i, carry):
        start = pl.multiple_of(i * tile, tile)
        span = pl.ds(start, tile)
        early, late = seg_rows(limit, start, tile)
        pair = masked_pair(gnum_ref[i].astype(f32), early, late)
        unit = qu_ref[:, span]
        grad = soften(unit, nn(table_ref[0], pair))
        acc_ref[...] += nt(codes_ref[...], pair)
        proj_ref[head, 0:64, span] = unit_back(grad, unit, inv_ref[0, 0:1, span]).astype(bf16)
        return carry

    lax.fori_loop(0, tiles, queries, 0)
    table_grad = acc_ref[...].astype(bf16)
    table_grad_t = flip(table_grad)

    def keys(i, carry):
        start = pl.multiple_of(i * tile, tile)
        span = pl.ds(start, tile)
        early, late = seg_rows(limit, start, tile)
        values = v_ref[:, pl.ds(pl.multiple_of(start + 128, 128), tile)]
        pair = masked_pair(values.astype(f32), early, late)
        unit = ku_ref[:, span]
        grad = soften(unit, nn(table_grad, pair))
        both = nn(table_grad_t, codes_ref[...])
        here = (spot == i).astype(f32)
        value_grad = both[0:64] * early + both[64:128] * late + conv_ref[...] * here
        proj_ref[head, 64:128, span] = unit_back(grad, unit, inv_ref[0, 1:2, span]).astype(bf16)
        proj_ref[head, 128:192, span] = value_grad.astype(bf16)
        return carry

    lax.fori_loop(0, tiles, keys, 0)

    def weights(i, carry):
        span = pl.ds(pl.multiple_of(i * tile, tile), tile)
        toks = got_ref[pl.ds(i * CORES, CORES), 0:tok_rows, :].reshape(tile, width)
        sum_ref[head] += nn(proj_ref[head, :, span], toks)
        return carry

    sum_ref[head] = jnp.zeros((192, width), f32)
    lax.fori_loop(0, tiles, weights, 0)

    @pl.when(head == heads - 1)
    def _():
        def inputs(i, carry):
            span = pl.ds(pl.multiple_of(i * tile, tile), tile)
            part = nn(w_ref[...], proj_ref[:, :, span].reshape(heads * 192, tile))
            first, second = part[:, :tok_rows].astype(bf16), part[:, tok_rows:].astype(bf16)

            @pl.when(core == 0)
            def _():
                keep_ref[i] = first
                give_ref[i] = second

            @pl.when(core != 0)
            def _():
                keep_ref[i] = second
                give_ref[i] = first

            return carry

        lax.fori_loop(0, tiles, inputs, 0)
        grad = jnp.transpose(sum_ref[...].reshape(heads * 192, width))
        grad_ref[:, :, 0 : heads * 192] = grad.reshape(
            tiles, CORES * own_rows, heads * 192
        ).astype(bf16)
        grad_ref[:, :, heads * 192 :] = jnp.zeros((tiles, CORES * own_rows, 64), bf16)
        taps = jnp.concatenate([tap_ref[h, 0:1, 0:64] for h in range(heads)], axis=0)
        for c in range(tiles):
            grad_ref[c, 0:heads, heads * 192 :] = taps.astype(bf16)


def window_same(spots_ref, tile):
    start = spots_ref[1] * tile
    width = tile + 256
    edge = lax.broadcasted_iota(jnp.int32, (width, tile), 0) + (start - 128)
    own = lax.broadcasted_iota(jnp.int32, (width, tile), 1) + start
    return (edge >= spots_ref[0]) == (own >= spots_ref[0])


def banded(base, same, tile):
    width = tile + 256
    spread = jnp.broadcast_to(base, (width, width))
    spread = pltpu.roll(spread, 0, 1, stride=1, stride_axis=0)[:, :tile]
    matrix = jnp.where(same, spread, 0.0)
    upper = matrix.astype(bf16)
    return upper, (matrix - upper.astype(f32)).astype(bf16)


def conv_kernel(tile, spots_ref, left_ref, right_ref, base_ref, out_ref):
    upper, lower = banded(base_ref[0, 0:1], window_same(spots_ref, tile), tile)
    window = jnp.concatenate([left_ref[...], right_ref[...]], axis=1)
    out_ref[...] = nn(window, upper) + nn(window, lower)


def conv_back_kernel(
    tile, taps, spots_ref, left_ref, right_ref, before_ref, low_ref, high_ref, after_ref, base_ref,
    out_ref, tap_ref,
):
    upper, lower = banded(base_ref[0, 0:1], window_same(spots_ref, tile), tile)
    grads = jnp.concatenate([before_ref[...], low_ref[...], high_ref[...], after_ref[...]], axis=1)
    out_ref[...] = nn(grads, upper) + nn(grads, lower)
    width = tile + 256
    values = jnp.concatenate([left_ref[...], right_ref[...]], axis=1).astype(f32)
    own = jnp.concatenate([low_ref[...], high_ref[...]], axis=1).astype(f32)
    start = spots_ref[1] * tile
    limit = spots_ref[0]
    pos = lax.broadcasted_iota(jnp.int32, (1, tile), 1) + start
    lane = lax.broadcasted_iota(jnp.int32, (8, 128), 1)
    rim = taps // 2

    def one(o, total):
        moved = pltpu.roll(values, width - (128 - rim) - o, 1)[:, :tile]
        row = jnp.sum(moved * own, axis=0, keepdims=True)
        same = (pos >= limit) == (pos + (o - rim) >= limit)
        tap = jnp.sum(jnp.where(same, row, 0.0), axis=1, keepdims=True)
        return total + jnp.where(lane == o, tap, 0.0)

    tap_ref[0] = lax.fori_loop(0, taps, one, jnp.zeros((8, 128), f32))


def context_kernel(heads, spots_ref, got_ref, conv_ref, keep_ref, give_ref, num_ref):
    total = jnp.sum(got_ref[...].astype(f32), axis=0)
    num_ref[...] = total
    tile = total.shape[1]
    parts = [head_units(total[64 * h : 64 * (h + 1)])[0] for h in range(heads)]
    context = (jnp.concatenate(parts, axis=0) + conv_ref[...]).astype(bf16)
    first, second = context[:, : tile // CORES], context[:, tile // CORES :]

    @pl.when(spots_ref[2] == 0)
    def _():
        keep_ref[...] = first
        give_ref[...] = second

    @pl.when(spots_ref[2] != 0)
    def _():
        keep_ref[...] = second
        give_ref[...] = first


def mixer_kernel(spots_ref, keep_ref, other_ref, out_ref, context_ref, part_ref):
    keep, other = keep_ref[...].astype(f32), other_ref[...].astype(f32)
    zero = spots_ref[2] == 0
    pair = jnp.concatenate([jnp.where(zero, keep, other), jnp.where(zero, other, keep)], axis=0)
    context = jnp.transpose(pair).astype(bf16)
    context_ref[...] = context
    part_ref[...] = nt(context, out_ref[...]).astype(bf16)


def hidden_kernel(
    tok_ref, own_ref, other_ref, norm_ref, up_ref, down_ref,
    hat_ref, inv_ref, hidden_ref, active_ref, part_ref,
):
    mixed = own_ref[...].astype(f32) + other_ref[...].astype(f32)
    hat, inverse = normalize(tok_ref[...].astype(f32) + mixed)
    hat_ref[...] = hat
    inv_ref[...] = inverse
    low = (hat * norm_ref[0:1] + norm_ref[1:2]).astype(bf16)
    hidden = nn(low, up_ref[...])
    hidden_ref[...] = hidden
    active = (0.5 * hidden * (1.0 + lax.erf(hidden * math.sqrt(0.5)))).astype(bf16)
    active_ref[...] = active
    part_ref[...] = nt(active, down_ref[...]).astype(bf16)


def feed_kernel(
    hat_ref, hidden_ref, own_ref, other_ref, cot_ref, norm_ref, up_ref, down_ref,
    out_ref, second_ref, feed_ref, slope_ref, part_ref, sums_ref,
):
    first_out = hat_ref[...] * norm_ref[0:1] + norm_ref[1:2]
    fed = own_ref[...].astype(f32) + other_ref[...].astype(f32)
    hat, inverse = normalize(first_out + fed)
    out_ref[...] = hat * norm_ref[2:3] + norm_ref[3:4]
    grad, gains, offsets = norm_back(cot_ref[...].astype(f32), hat, inverse, norm_ref[2:3])
    second_ref[...] = grad
    sums_ref[0:1] = gains
    sums_ref[1:2] = offsets
    low = grad.astype(bf16)
    feed_ref[...] = low
    active_grad = nn(low, down_ref[...])
    hidden = hidden_ref[...]
    cdf = 0.5 * (1.0 + lax.erf(hidden * math.sqrt(0.5)))
    density = jnp.exp(-0.5 * hidden * hidden) * (1.0 / math.sqrt(2.0 * math.pi))
    slope = (active_grad * (cdf + hidden * density)).astype(bf16)
    slope_ref[...] = slope
    part_ref[...] = nt(slope, up_ref[...]).astype(bf16)


def mixer_back_kernel(
    spots_ref, second_ref, own_ref, other_ref, hat_ref, inv_ref, norm_ref, out_ref, sums_ref,
    grad_ref, low_ref, keep_ref, give_ref, all_sums_ref,
):
    first = second_ref[...] + (own_ref[...].astype(f32) + other_ref[...].astype(f32))
    grad, gains, offsets = norm_back(first, hat_ref[...], inv_ref[...], norm_ref[0:1])
    grad_ref[...] = grad
    all_sums_ref[0:1] = gains
    all_sums_ref[1:2] = offsets
    all_sums_ref[2:4] = sums_ref[...]
    low = grad.astype(bf16)
    low_ref[...] = low
    context = jnp.transpose(nn(low, out_ref[...]))
    half = context.shape[0] // CORES
    zero = spots_ref[2] == 0
    keep_ref[...] = jnp.where(zero, context[:half], context[half:])
    give_ref[...] = jnp.where(zero, context[half:], context[:half])


def attention_back_kernel(
    heads, spots_ref, keep_ref, other_ref, num_ref, sums_ref, count_ref,
    send_ref, low_ref, high_ref,
):
    zero = spots_ref[2] == 0
    keep, other = keep_ref[...], other_ref[...]
    grad = jnp.concatenate([jnp.where(zero, keep, other), jnp.where(zero, other, keep)], axis=1)
    half = keep.shape[1]
    low = grad.astype(bf16)
    low_ref[...] = low[:, :half]
    high_ref[...] = low[:, half:]
    parts = []
    for h in range(heads):
        span = slice(64 * h, 64 * (h + 1))
        attention, inverse = head_units(num_ref[span])
        inner = jnp.mean(grad[span] * attention, axis=0, keepdims=True)
        parts.append(inverse * (grad[span] - attention * inner))
    gnum = jnp.concatenate(parts, axis=0).astype(bf16)
    tile = gnum.shape[1]
    feats = 64 * heads
    pieces = sums_ref.shape[1] // tile
    sums = sums_ref[...].astype(bf16).astype(f32)
    sums = jnp.concatenate(
        [sums[:, tile * i : tile * (i + 1)] for i in range(pieces)], axis=0
    )
    for c in range(send_ref.shape[0]):
        send_ref[c, 0:feats, :] = gnum
        extra = jnp.concatenate([sums, count_ref[c]], axis=0)
        send_ref[c, feats:, :] = extra.astype(bf16)


def big_grad_kernel(
    mixer_ref, context_ref, hat_ref, norm_ref, slope_ref, feed_ref, active_ref, out_ref
):
    low = hat_ref[...] * norm_ref[0:1] + norm_ref[1:2]
    out_width, ff = context_ref.shape[1], slope_ref.shape[1]
    out_ref[:, :out_width] = nn(flip(mixer_ref[...]), context_ref[...]).astype(bf16)
    first = jnp.transpose(low.astype(bf16).astype(f32)).astype(bf16)
    out_ref[:, out_width : out_width + ff] = nn(first, slope_ref[...]).astype(bf16)
    out_ref[:, out_width + ff :] = nn(flip(feed_ref[...]), active_ref[...]).astype(bf16)


def on_device(
    tokens,
    cotangent,
    doc_lengths,
    plane_bits,
    qkv_weight,
    qkv_first,
    qkv_second,
    out_weight,
    out_first,
    out_second,
    up_weight,
    up_first,
    up_second,
    down_weight,
    down_first,
    down_second,
    norm_params,
    norm_first,
    norm_second,
    conv_taps,
    conv_first,
    conv_second,
):
    tok_rows, width = tokens.shape
    hash_count, bits, group_heads, head_dim = plane_bits.shape
    buckets = 2**bits
    taps = conv_taps.shape[1]
    rim = taps // 2
    seq_count = lax.axis_size("seq")
    chips = seq_count // CORES
    place = lax.axis_index("seq")
    side = lax.axis_index("head")
    spot, core = place // CORES, place % CORES
    heads = group_heads // CORES
    feats = heads * head_dim
    group_feats = group_heads * head_dim
    hashes = hash_count // chips
    rows = -(-hashes // 8) * 8
    tile = CORES * tok_rows
    total = chips * tile
    own_rows = width // seq_count
    ff = up_weight.shape[1]
    code_rows = hashes * buckets
    planes_of = [[CORES * c + k for c in range(chips)] for k in range(CORES)]
    across = partial(
        lax.all_to_all, axis_name="seq", split_axis=0, concat_axis=0, tiled=True,
        axis_index_groups=planes_of,
    )
    core_swap = partial(
        lax.ppermute, axis_name="seq", perm=[(i, i ^ 1) for i in range(seq_count)]
    )
    head_swap = partial(lax.ppermute, axis_name="head", perm=[(0, 1), (1, 0)])
    spots = jnp.stack([doc_lengths[0], spot.astype(jnp.int32), core.astype(jnp.int32)])

    smem = pl.BlockSpec(memory_space=pltpu.SMEM)
    params = pltpu.CompilerParams(
        dimension_semantics=("arbitrary",), vmem_limit_bytes=VMEM_LIMIT
    )
    shape = jax.ShapeDtypeStruct

    def whole(*dims):
        return pl.BlockSpec(dims, lambda h: (0,) * len(dims), pipeline_mode=pl.Buffered(1))

    def by_head(*dims):
        return pl.BlockSpec((1,) + dims, lambda h: (h,) + (0,) * len(dims))

    def head_rows(*dims):
        return pl.BlockSpec((head_dim,) + dims, lambda h: (h,) + (0,) * len(dims))

    def full(value):
        return pl.BlockSpec(value.shape, lambda i: (0,) * value.ndim)

    def columns(block, which):
        return pl.BlockSpec((width, block), lambda i: (0, which))

    def once(kernel, name, outs, args, specs=None):
        if specs is None:
            specs = [None] * len(args)
        specs = [
            (smem if arg is spots else full(arg)) if spec is None else spec
            for spec, arg in zip(specs, args)
        ]
        return pl.pallas_call(
            kernel,
            grid=(1,),
            in_specs=specs,
            out_specs=[full(o) for o in outs],
            out_shape=outs,
            compiler_params=params,
            name=name,
        )(*args)

    low_qkv = qkv_weight.astype(bf16)
    first_send = jnp.concatenate(
        [
            tokens,
            jnp.concatenate([low_qkv[0], low_qkv[1]], axis=1),
            jnp.concatenate([low_qkv[2], out_weight.T.astype(bf16)], axis=1),
        ],
        axis=0,
    )
    got = lax.all_gather(first_send, "seq", axis=0, tiled=False)
    qk_all = got[:, tok_rows : tok_rows + own_rows].reshape(width, 2 * group_feats)
    vo_all = got[:, tok_rows + own_rows :].reshape(width, 2 * group_feats)
    second_send = jnp.concatenate([up_weight.astype(bf16), down_weight.T.astype(bf16)], axis=1)
    second_send, unused = lax.optimization_barrier((second_send, got[0, 0, 0:1]))
    ff_all = lax.all_gather(second_send, "seq", axis=0, tiled=True)

    own_planes = lax.dynamic_slice(
        plane_bits, (spot * hashes, 0, core * heads, 0), (hashes, bits, heads, head_dim)
    )
    scale = sharpness / math.sqrt(head_dim)
    signs = scale * (2 * own_planes - 1).astype(f32)
    sign_w = jnp.pad(
        jnp.transpose(signs, (2, 0, 1, 3)), ((0, 0), (0, 0), (0, 8 - bits), (0, 0))
    ).astype(bf16)
    bit_w = jnp.pad(
        jnp.transpose(signs, (2, 1, 0, 3)), ((0, 0), (0, 0), (0, rows - hashes), (0, 0))
    )
    bit_w = bit_w.reshape(heads, bits * rows, head_dim).astype(bf16)

    num_parts, q_unit, k_unit, values, inverses, tables, counts, w_cols = pl.pallas_call(
        partial(forward_kernel, hashes, bits, rows, tile, chips, heads, group_feats),
        grid=(heads,),
        in_specs=[
            smem,
            whole(*got.shape),
            whole(*qk_all.shape),
            whole(*vo_all.shape),
            by_head(hashes, 8, head_dim),
            by_head(bits * rows, head_dim),
        ],
        out_specs=[
            pl.BlockSpec((chips, head_dim, tile), lambda h: (0, h, 0)),
            head_rows(total),
            head_rows(total),
            head_rows(total + 256),
            by_head(8, total),
            by_head(code_rows, 2 * head_dim),
            by_head(8, code_rows),
            whole(width, 3 * feats),
        ],
        out_shape=[
            shape((chips, feats, tile), bf16),
            shape((feats, total), bf16),
            shape((feats, total), bf16),
            shape((feats, total + 256), bf16),
            shape((heads, 8, total), f32),
            shape((heads, code_rows, 2 * head_dim), bf16),
            shape((heads, 8, code_rows), f32),
            shape((width, 3 * feats), bf16),
        ],
        scratch_shapes=[
            pltpu.VMEM((code_rows, 2 * head_dim + 16), f32),
            pltpu.VMEM((code_rows, tile), bf16),
            pltpu.VMEM((code_rows, head_dim), bf16),
            pltpu.VMEM((heads, 3 * head_dim, width), bf16),
        ],
        compiler_params=params,
        name="hash_forward",
    )(spots, got, qk_all, vo_all, sign_w, bit_w)
    num_got = across(num_parts)

    own_taps = lax.dynamic_slice(conv_taps, (core * heads, 0), (heads, taps))
    lead = tile + 128 - rim
    bases = jnp.zeros((heads, 16, tile + 256), f32)
    bases = bases.at[:, 0, lead : lead + taps].set(own_taps[:, ::-1])
    bases = bases.at[:, 8, lead : lead + taps].set(own_taps)
    window = [
        pl.BlockSpec((head_dim, tile), lambda h, s: (h, s[1])),
        pl.BlockSpec((head_dim, tile), lambda h, s: (h, s[1] + 1)),
    ]
    half_rows = pl.BlockSpec((head_dim, tok_rows), lambda h, s: (h, 0))
    conv = pl.pallas_call(
        partial(conv_kernel, tile),
        grid_spec=pltpu.PrefetchScalarGridSpec(
            num_scalar_prefetch=1,
            grid=(heads,),
            in_specs=window + [pl.BlockSpec((1, 8, tile + 256), lambda h, s: (h, 0, 0))],
            out_specs=pl.BlockSpec((head_dim, tile), lambda h, s: (h, 0)),
        ),
        out_shape=shape((feats, tile), f32),
        compiler_params=params,
        name="conv_forward",
    )(spots, values, values, bases)

    chip_buckets = buckets // chips
    count_rows = -(-2 * hashes * heads * chip_buckets // tile)
    sum_rows = 4 * width // tile
    extra_rows = -(-(sum_rows + count_rows) // 16) * 16
    count_send = counts[:, 0:2].reshape(heads, 2, hashes, chips, chip_buckets)
    count_send = jnp.transpose(count_send, (3, 1, 2, 0, 4)).reshape(chips, -1)
    count_send = jnp.pad(
        count_send, ((0, 0), (0, (extra_rows - sum_rows) * tile - count_send.shape[1]))
    ).reshape(chips, extra_rows - sum_rows, tile)

    keep, give, numerator = once(
        partial(context_kernel, heads), "context",
        [shape((feats, tok_rows), bf16), shape((feats, tok_rows), bf16), shape((feats, tile), f32)],
        [spots, num_got, conv],
    )
    context, mixer_part = once(
        mixer_kernel, "mixer",
        [shape((tok_rows, group_feats), bf16), shape((tok_rows, width), bf16)],
        [spots, keep, core_swap(give), vo_all],
        [None, None, None, columns(group_feats, 1)],
    )
    first_hat, first_inverse, hidden, active, feed_part = once(
        hidden_kernel, "feed_forward",
        [
            shape((tok_rows, width), f32),
            shape((tok_rows, 1), f32),
            shape((tok_rows, ff), f32),
            shape((tok_rows, ff), bf16),
            shape((tok_rows, width), bf16),
        ],
        [tokens, mixer_part, head_swap(mixer_part), norm_params, ff_all, ff_all],
        [None, None, None, None, columns(ff, 0), columns(ff, 1)],
    )
    block_out, grad_second, feed_low, slope_low, first_part, second_sums = once(
        feed_kernel, "feed_back",
        [
            shape((tok_rows, width), f32),
            shape((tok_rows, width), f32),
            shape((tok_rows, width), bf16),
            shape((tok_rows, ff), bf16),
            shape((tok_rows, width), bf16),
            shape((2, width), f32),
        ],
        [first_hat, hidden, feed_part, head_swap(feed_part), cotangent, norm_params, ff_all, ff_all],
        [None, None, None, None, None, None, columns(ff, 0), columns(ff, 1)],
    )
    grad_mixer, mixer_low, keep, give, norm_sums = once(
        mixer_back_kernel, "mixer_back",
        [
            shape((tok_rows, width), f32),
            shape((tok_rows, width), bf16),
            shape((feats, tok_rows), f32),
            shape((feats, tok_rows), f32),
            shape((4, width), f32),
        ],
        [
            spots, grad_second, first_part, head_swap(first_part), first_hat, first_inverse,
            norm_params, vo_all, second_sums,
        ],
        [None, None, None, None, None, None, None, columns(group_feats, 1), None],
    )
    gnum_send, grad_low, grad_high = once(
        partial(attention_back_kernel, heads), "attention_back",
        [
            shape((chips, feats + extra_rows, tile), bf16),
            shape((feats, tok_rows), bf16),
            shape((feats, tok_rows), bf16),
        ],
        [spots, keep, core_swap(give), numerator, norm_sums, count_send],
    )
    gnum_got = across(gnum_send)

    (big_grad,) = once(
        big_grad_kernel, "weight_grads",
        [shape((width, group_feats + 2 * ff), bf16)],
        [mixer_low, context, first_hat, norm_params, slope_low, feed_low, active],
    )
    big_owned = lax.psum_scatter(big_grad, "seq", scatter_dimension=0, tiled=True).astype(f32)

    up_moves = [(i, i + CORES) for i in range(seq_count - CORES)]
    down_moves = [(j, i) for i, j in up_moves]
    before = lax.ppermute(grad_high, "seq", up_moves)
    after = lax.ppermute(grad_low, "seq", down_moves)
    conv_grad, tap_parts = pl.pallas_call(
        partial(conv_back_kernel, tile, taps),
        grid_spec=pltpu.PrefetchScalarGridSpec(
            num_scalar_prefetch=1,
            grid=(heads,),
            in_specs=window
            + [half_rows] * 4
            + [pl.BlockSpec((1, 8, tile + 256), lambda h, s: (h, 1, 0))],
            out_specs=[
                pl.BlockSpec((head_dim, tile), lambda h, s: (h, 0)),
                pl.BlockSpec((1, 8, 128), lambda h, s: (h, 0, 0)),
            ],
        ),
        out_shape=[shape((feats, tile), f32), shape((heads, 8, 128), f32)],
        compiler_params=params,
        name="conv_backward",
    )(spots, values, values, before, grad_low, grad_high, after, bases)

    qkv_send, back_keep, back_give = pl.pallas_call(
        partial(backward_kernel, hashes, bits, rows, tile, chips, heads, own_rows),
        grid=(heads,),
        in_specs=[
            smem,
            whole(*got.shape),
            whole(*w_cols.shape),
            by_head(hashes, 8, head_dim),
            by_head(bits * rows, head_dim),
            head_rows(total),
            head_rows(total),
            head_rows(total + 256),
            by_head(8, total),
            by_head(code_rows, 2 * head_dim),
            pl.BlockSpec((chips, head_dim, tile), lambda h: (0, h, 0)),
            head_rows(tile),
            whole(*tap_parts.shape),
        ],
        out_specs=[
            whole(chips, CORES * own_rows, 3 * feats + 64),
            whole(chips, width, tok_rows),
            whole(chips, width, tok_rows),
        ],
        out_shape=[
            shape((chips, CORES * own_rows, 3 * feats + 64), bf16),
            shape((chips, width, tok_rows), bf16),
            shape((chips, width, tok_rows), bf16),
        ],
        scratch_shapes=[
            pltpu.VMEM((code_rows, 2 * head_dim), f32),
            pltpu.VMEM((code_rows, tile), bf16),
            pltpu.VMEM((code_rows, tile), bf16),
            pltpu.VMEM((heads, 3 * head_dim, total), bf16),
            pltpu.VMEM((code_rows, head_dim), bf16),
            pltpu.VMEM((head_dim, code_rows), bf16),
            pltpu.VMEM((heads, 3 * head_dim, width), f32),
        ],
        compiler_params=params,
        name="hash_backward",
    )(
        spots, got, w_cols, sign_w, bit_w,
        q_unit, k_unit, values, inverses, tables, gnum_got, conv_grad, tap_parts,
    )

    chip_sum = back_keep.astype(f32) + core_swap(back_give).astype(f32)
    half = width // 2
    chip_sum = chip_sum.astype(bf16).reshape(chips, 2, half, tok_rows)
    keep = lax.dynamic_index_in_dim(chip_sum, side, 1, keepdims=False)
    give = lax.dynamic_index_in_dim(chip_sum, 1 - side, 1, keepdims=False)
    pair_sum = keep.astype(f32) + head_swap(give).astype(f32)

    qkv_half = jnp.sum(across(qkv_send).astype(f32), axis=0)
    back_half = jnp.sum(across(pair_sum.astype(bf16)).astype(f32), axis=0)
    by_core = qkv_half.reshape(CORES, own_rows, 3 * feats + 64)
    qkv_mine = lax.dynamic_index_in_dim(by_core, core, 0, keepdims=False)[:, : 3 * feats]
    qkv_give = lax.dynamic_index_in_dim(by_core, 1 - core, 0, keepdims=False)[:, : 3 * feats]
    qkv_other = core_swap(qkv_give)

    extras = gnum_got[:, feats:].astype(f32)
    norm_half = jnp.sum(extras[:, :sum_rows], axis=0)
    count_half = extras[:, sum_rows:].reshape(chips, -1)[:, : 2 * hashes * heads * chip_buckets]
    count_half = count_half.reshape(chips, 2, hashes, heads, CORES, chip_buckets // CORES)
    count_mine = lax.dynamic_index_in_dim(count_half, core, 4, keepdims=False)
    count_give = lax.dynamic_index_in_dim(count_half, 1 - core, 4, keepdims=False)
    tap_half = qkv_half[:heads, 3 * feats : 3 * feats + taps]
    swapped = core_swap(
        jnp.concatenate([norm_half.reshape(-1), count_give.reshape(-1), tap_half.reshape(-1)])
    )
    norm_size, count_size = norm_half.size, count_give.size

    def in_order(mine, other, axis):
        first = jnp.where(core == 0, mine, other)
        return jnp.concatenate([first, jnp.where(core == 0, other, mine)], axis=axis)

    norm_grad = norm_half + swapped[:norm_size].reshape(norm_half.shape)
    norm_grad = jnp.transpose(
        norm_grad.reshape(width // tile, 4, tile), (1, 0, 2)
    ).reshape(4, width)
    count_other = swapped[norm_size : norm_size + count_size].reshape(count_mine.shape)
    occupancy = jnp.transpose(
        in_order(count_mine, count_other, 3), (1, 0, 2, 3, 4)
    ).reshape(2, hash_count, group_heads, buckets // seq_count)
    occupancy = occupancy * (buckets / (tok_rows * seq_count))
    conv_tap_grad = in_order(tap_half, swapped[norm_size + count_size :].reshape(heads, taps), 0)

    def weight_order(part):
        return jnp.transpose(part.reshape(own_rows, heads, 3, head_dim), (2, 0, 1, 3)).reshape(
            3, own_rows, feats
        )

    qkv_owned = in_order(weight_order(qkv_mine), weight_order(qkv_other), 2)
    back_low = lax.optimization_barrier(back_half.astype(bf16))
    back_other = head_swap(back_low)
    upper = jnp.where(side == 0, back_low, back_other)
    lower = jnp.where(side == 0, back_other, back_low)
    tokens_grad = grad_mixer + jnp.concatenate([upper, lower], axis=0).T.astype(f32)

    out_owned = big_owned[:, :group_feats].T
    up_owned = big_owned[:, group_feats : group_feats + ff]
    down_owned = big_owned[:, group_feats + ff :].T
    qkv_new, qkv_first_new, qkv_second_new = adam_step(
        qkv_weight, qkv_first, qkv_second, qkv_owned, D ** (-0.5)
    )
    out_new, out_first_new, out_second_new = adam_step(
        out_weight, out_first, out_second, out_owned, D ** (-0.5)
    )
    up_new, up_first_new, up_second_new = adam_step(
        up_weight, up_first, up_second, up_owned, D ** (-0.5)
    )
    down_new, down_first_new, down_second_new = adam_step(
        down_weight, down_first, down_second, down_owned, FF ** (-0.5)
    )
    norm_new, norm_first_new, norm_second_new = adam_step(
        norm_params, norm_first, norm_second, norm_grad, 0.3
    )
    conv_new, conv_first_new, conv_second_new = adam_step(
        conv_taps, conv_first, conv_second, conv_tap_grad, CONV ** (-0.5)
    )
    return (
        block_out,
        tokens_grad,
        occupancy,
        qkv_new,
        qkv_first_new,
        qkv_second_new,
        qkv_new.astype(jnp.bfloat16),
        out_new,
        out_first_new,
        out_second_new,
        out_new.astype(jnp.bfloat16),
        up_new,
        up_first_new,
        up_second_new,
        up_new.astype(jnp.bfloat16),
        down_new,
        down_first_new,
        down_second_new,
        down_new.astype(jnp.bfloat16),
        norm_new,
        norm_first_new,
        norm_second_new,
        conv_new,
        conv_first_new,
        conv_second_new,
    )


def solution(mesh):
    in_specs = (
        P("seq", None),
        P("seq", None),
        P(),
        P(None, None, "head", None),
        P(None, "seq", "head"),
        P(None, "seq", "head"),
        P(None, "seq", "head"),
        P("head", "seq"),
        P("head", "seq"),
        P("head", "seq"),
        P("seq", "head"),
        P("seq", "head"),
        P("seq", "head"),
        P("head", "seq"),
        P("head", "seq"),
        P("head", "seq"),
        P(),
        P(),
        P(),
        P("head", None),
        P("head", None),
        P("head", None),
    )
    out_specs = (
        P("seq", None),
        P("seq", None),
        P(None, None, "head", "seq"),
        P(None, "seq", "head"),
        P(None, "seq", "head"),
        P(None, "seq", "head"),
        P(None, "seq", "head"),
        P("head", "seq"),
        P("head", "seq"),
        P("head", "seq"),
        P("head", "seq"),
        P("seq", "head"),
        P("seq", "head"),
        P("seq", "head"),
        P("seq", "head"),
        P("head", "seq"),
        P("head", "seq"),
        P("head", "seq"),
        P("head", "seq"),
        P(),
        P(),
        P(),
        P("head", None),
        P("head", None),
        P("head", None),
    )
    return jax.shard_map(
        on_device, mesh=mesh, in_specs=in_specs, out_specs=out_specs, check_vma=False
    )
```

```python
from functools import partial
import math

import jax
import jax.numpy as jnp
from jax import lax
from jax.experimental import pallas as pl
from jax.experimental.pallas import tpu as pltpu
from jax.sharding import PartitionSpec as P

D = 768
FF = 3072
CONV = 33
STEP = 7
CORES = 2

sharpness = 4.0
norm_eps = 1e-06
layer_eps = 1e-05
beta_one = 0.9
beta_two = 0.999
adam_eps = 1e-08
decay_rate = 0.01
highest = lax.Precision.HIGHEST
f32 = jnp.float32
bf16 = jnp.bfloat16
VMEM_LIMIT = 56 * 1024 * 1024
WORK = 2


def nn(a, b):
    return lax.dot_general(a, b, (((1,), (0,)), ((), ())), preferred_element_type=f32)


def nt(a, b):
    return lax.dot_general(a, b, (((1,), (1,)), ((), ())), preferred_element_type=f32)


def normalize(source):
    centered = source - jnp.mean(source, axis=-1, keepdims=True)
    inverse = lax.rsqrt(jnp.mean(centered * centered, axis=-1, keepdims=True) + layer_eps)
    return (centered * inverse, inverse)


def norm_back(grad, normed, inverse, gain):
    scaled = grad * gain
    inner = (
        scaled
        - jnp.mean(scaled, axis=-1, keepdims=True)
        - normed * jnp.mean(scaled * normed, axis=-1, keepdims=True)
    )
    gains = jnp.sum(grad * normed, axis=0, keepdims=True)
    return (inverse * inner, gains, jnp.sum(grad, axis=0, keepdims=True))


def adam_step(weight, first, second, grad, rate):
    first_new = beta_one * first + (1.0 - beta_one) * grad
    second_new = beta_two * second + (1.0 - beta_two) * grad * grad
    fix_one = 1.0 - beta_one**STEP
    fix_two = 1.0 - beta_two**STEP
    update = first_new / fix_one / (jnp.sqrt(second_new / fix_two) + adam_eps) + decay_rate * weight
    return (weight - rate * update, first_new, second_new)


def head_units(source):
    inverse = lax.rsqrt(jnp.mean(source * source, axis=0, keepdims=True) + norm_eps)
    return source * inverse, inverse


def seg_rows(limit, start, width):
    pos = start + lax.broadcasted_iota(jnp.int32, (1, width), 1)
    late = (pos >= limit).astype(f32)
    return 1.0 - late, late


def masked_pair(rows, early, late):
    return jnp.concatenate([rows * early, rows * late], axis=0).astype(bf16)


def flip(value):
    return jnp.transpose(value.astype(f32)).astype(bf16)


def bit_factors(bit_planes, unit, bits, hashes, rows):
    z = nn(bit_planes, unit)
    decay = jnp.exp(-jnp.abs(z))
    large = 1.0 / (1.0 + decay)
    small = decay * large
    ones = jnp.where(z >= 0.0, large, small)
    zeros = jnp.where(z >= 0.0, small, large)
    ones = [ones[j * rows : (j + 1) * rows] for j in range(bits)]
    zeros = [zeros[j * rows : (j + 1) * rows] for j in range(bits)]
    if rows != hashes:
        live = lax.broadcasted_iota(jnp.int32, ones[0].shape, 0) < hashes
        return ones, [jnp.where(live, ones[0], 0.0)] + ones[1:], [
            jnp.where(live, zeros[0], 0.0)
        ] + zeros[1:]
    return ones, ones, zeros


def products(ones, zeros, first, last):
    found = [zeros[first], ones[first]]
    for j in range(first + 1, last):
        found = [part * zeros[j] for part in found] + [part * ones[j] for part in found]
    return found


def code_parts(bit_planes, unit, bits, hashes, rows):
    plain, ones, zeros = bit_factors(bit_planes, unit, bits, hashes, rows)
    return plain, products(ones, zeros, 0, 3), products(ones, zeros, 3, bits)


def store_codes(codes_ref, head, lows, highs, rows):
    for g, high in enumerate(highs):
        for s in range(0, len(lows), 2):
            spot = (g * len(lows) + s) * rows
            pair = jnp.concatenate([lows[s] * high, lows[s + 1] * high], axis=0)
            codes_ref[head, spot : spot + 2 * rows, :] = pair.astype(bf16)


def forward_kernel(
    hashes, bits, rows, tile, steps, heads,
    spots_ref, got_ref, w_ref, bit_ref,
    num_ref, qu_ref, ku_ref, v_ref, inv_ref, table_ref, count_ref,
    acc_ref, codes_ref, wt_ref, table_t_ref,
):
    limit = spots_ref[0]
    phase, i = pl.program_id(0), pl.program_id(1)
    feats = heads * 64
    chips = num_ref.shape[0]
    block = tile // chips
    start = pl.multiple_of(i * tile, tile)
    span = pl.ds(start, tile)
    early, late = seg_rows(limit, start, tile)

    @pl.when((phase == 0) & (i == 0))
    def _():
        wt_ref[...] = flip(w_ref[...])
        acc_ref[...] = jnp.zeros_like(acc_ref)
        v_ref[:, 0:128] = jnp.zeros((feats, 128), bf16)
        v_ref[:, 128 + steps * tile :] = jnp.zeros((feats, 128), bf16)
        inv_ref[...] = jnp.zeros_like(inv_ref)

    @pl.when(phase == 0)
    def _():
        proj = nt(wt_ref[...], got_ref[...].reshape(tile, got_ref.shape[2]))
        values = proj[2 * feats :].astype(bf16)
        v_ref[:, pl.ds(pl.multiple_of(start + 128, 128), tile)] = values
        marks = jnp.concatenate([early, late, jnp.zeros((14, tile), f32)], axis=0).astype(bf16)
        units = []
        for h in range(heads):
            mine = slice(64 * h, 64 * (h + 1))
            q_unit, q_inv = head_units(proj[mine])
            k_unit, k_inv = head_units(proj[feats + 64 * h : feats + 64 * (h + 1)])
            units.append(k_unit.astype(bf16))
            qu_ref[mine, span] = q_unit.astype(bf16)
            ku_ref[mine, span] = units[h]
            inv_ref[h : h + 1, span] = q_inv
            inv_ref[8 + h : 9 + h, span] = k_inv
        for h in range(heads):
            plain, lows, highs = code_parts(bit_ref[h], units[h], bits, hashes, rows)
            store_codes(codes_ref, h, lows, highs, rows)
        for h in range(heads):
            pair = masked_pair(values[64 * h : 64 * (h + 1)].astype(f32), early, late)
            pair = jnp.concatenate([pair, marks], axis=0)
            acc_ref[h] += nt(codes_ref[h], pair)

    @pl.when((phase == 1) & (i == 0))
    def _():
        for h in range(heads):
            table = acc_ref[h, :, 0:128].astype(bf16)
            table_ref[h] = table
            table_t_ref[h] = flip(table)
            counts = jnp.concatenate(
                [acc_ref[h, :, 128:144], jnp.zeros((acc_ref.shape[1], 112), f32)], axis=1
            )
            count_ref[h] = jnp.transpose(counts)[0:8]

    @pl.when(phase == 1)
    def _():
        for h in range(heads):
            unit = qu_ref[64 * h : 64 * (h + 1), span]
            plain, lows, highs = code_parts(bit_ref[h], unit, bits, hashes, rows)
            store_codes(codes_ref, h, lows, highs, rows)
        for h in range(heads):
            mine = slice(64 * h, 64 * (h + 1))
            both = nn(table_t_ref[h], codes_ref[h])
            low = (both[0:64] * early + both[64:128] * late).astype(bf16)
            for c in range(chips):
                num_ref[c, mine, :] = low[:, c * block : (c + 1) * block]


def soften(bit_planes, unit, slopes, codes_ref, head, bits, hashes, rows):
    plain, lows, highs = code_parts(bit_planes, unit, bits, hashes, rows)
    by_low = [None] * len(lows)
    by_bit = [None] * (bits - 3)
    for g, high in enumerate(highs):
        row = None
        for s in range(0, len(lows), 2):
            spot = (g * len(lows) + s) * rows
            parts = [lows[s] * high, lows[s + 1] * high]
            codes_ref[head, spot : spot + 2 * rows, :] = jnp.concatenate(parts, axis=0).astype(bf16)
            for k in range(2):
                term = parts[k] * slopes[spot + k * rows : spot + (k + 1) * rows]
                by_low[s + k] = term if by_low[s + k] is None else by_low[s + k] + term
                row = term if row is None else row + term
        for j in range(bits - 3):
            if (g >> j) & 1:
                by_bit[j] = row if by_bit[j] is None else by_bit[j] + row
    pairs = [sum(part for s, part in enumerate(by_low) if (s >> j) & 1) for j in range(3)]
    whole = sum(by_low)
    slopes = [part - plain[j] * whole for j, part in enumerate(pairs + by_bit)]
    return jnp.concatenate(slopes, axis=0).astype(bf16)


def unit_back(grad, unit, inverse):
    unit = unit.astype(f32)
    inner = jnp.mean(grad * unit, axis=0, keepdims=True)
    return inverse * (grad - unit * inner)


def backward_kernel(
    hashes, bits, rows, tile, steps, heads, own_rows,
    spots_ref, got_ref, w_ref, bit_ref, bit_t_ref,
    qu_ref, ku_ref, v_ref, inv_ref, table_ref, gnum_ref, conv_ref, tap_ref,
    grad_ref, keep_ref, give_ref,
    acc_ref, codes_ref, proj_ref, sum_ref, table_t_ref, table_g_ref,
):
    limit = spots_ref[0]
    spot = spots_ref[1]
    core = spots_ref[2]
    phase, i = pl.program_id(0), pl.program_id(1)
    width = got_ref.shape[2]
    feats = heads * 64
    blocks = keep_ref.shape[0]
    block = tile // blocks
    tok_rows = block // CORES
    start = pl.multiple_of(i * tile, tile)
    span = pl.ds(start, tile)
    early, late = seg_rows(limit, start, tile)

    @pl.when((phase == 0) & (i == 0))
    def _():
        acc_ref[...] = jnp.zeros_like(acc_ref)
        sum_ref[...] = jnp.zeros_like(sum_ref)

    @pl.when(phase == 0)
    def _():
        spans = [slice(64 * h, 64 * (h + 1)) for h in range(heads)]
        pairs, grads, slopes = [], [], []
        for mine in spans:
            gnum = jnp.concatenate([gnum_ref[c, mine, :] for c in range(blocks)], axis=1)
            pairs.append(masked_pair(gnum.astype(f32), early, late))
        for h, mine in enumerate(spans):
            slopes.append(
                soften(
                    bit_ref[h], qu_ref[mine, span], nn(table_ref[h], pairs[h]), codes_ref, h,
                    bits, hashes, rows,
                )
            )
        for h in range(heads):
            acc_ref[h] += nt(codes_ref[h], pairs[h])
        for h, mine in enumerate(spans):
            grad = nn(bit_t_ref[h], slopes[h])
            grad = unit_back(grad, qu_ref[mine, span], inv_ref[h : h + 1, span])
            proj_ref[mine, span] = grad.astype(bf16)

    @pl.when((phase == 1) & (i == 0))
    def _():
        for h in range(heads):
            table_g_ref[h] = acc_ref[h].astype(bf16)
            table_t_ref[h] = flip(table_g_ref[h])

    @pl.when(phase == 1)
    def _():
        conv = []
        for c in range(blocks):
            step = i * blocks + c - spot + 1
            near = ((step >= 0) & (step <= 2)).astype(f32)
            step = jnp.clip(step, 0, 2)
            conv.append(conv_ref[:, pl.ds(pl.multiple_of(step * block, block), block)] * near)
        conv = jnp.concatenate(conv, axis=1)
        spans = [slice(64 * h, 64 * (h + 1)) for h in range(heads)]
        slopes, parts = [], []
        for h, mine in enumerate(spans):
            values = v_ref[mine, pl.ds(pl.multiple_of(start + 128, 128), tile)]
            pair = masked_pair(values.astype(f32), early, late)
            slopes.append(
                soften(
                    bit_ref[h], ku_ref[mine, span], nn(table_g_ref[h], pair), codes_ref, h,
                    bits, hashes, rows,
                )
            )
        for h, mine in enumerate(spans):
            both = nn(table_t_ref[h], codes_ref[h])
            value_grad = both[0:64] * early + both[64:128] * late + conv[mine]
            grad = nn(bit_t_ref[h], slopes[h])
            grad = unit_back(grad, ku_ref[mine, span], inv_ref[8 + h : 9 + h, span])
            parts.append((grad.astype(bf16), value_grad.astype(bf16)))
        full = jnp.concatenate(
            [proj_ref[:, span]] + [part[0] for part in parts] + [part[1] for part in parts], axis=0
        )
        sum_ref[...] += nn(full, got_ref[...].reshape(tile, width))
        part = nn(w_ref[...], full)
        for c in range(blocks):
            first = part[:, c * block : c * block + tok_rows]
            second = part[:, c * block + tok_rows : (c + 1) * block]
            keep_ref[c] = jnp.where(core == 0, first, second).astype(bf16)
            give_ref[c] = jnp.where(core == 0, second, first).astype(bf16)

    @pl.when((phase == 1) & (i == steps - 1))
    def _():
        grad = jnp.transpose(sum_ref[...])
        chips = grad_ref.shape[0]
        grad_ref[:, :, 0 : heads * 192] = grad.reshape(
            chips, CORES * own_rows, heads * 192
        ).astype(bf16)
        grad_ref[:, :, heads * 192 :] = jnp.zeros((chips, CORES * own_rows, 64), bf16)
        taps = jnp.concatenate([tap_ref[h, 0:1, 0:64] for h in range(heads)], axis=0)
        for c in range(chips):
            grad_ref[c, 0:heads, heads * 192 :] = taps.astype(bf16)


def window_same(spots_ref, tile):
    start = spots_ref[1] * tile
    width = tile + 256
    edge = lax.broadcasted_iota(jnp.int32, (width, tile), 0) + (start - 128)
    own = lax.broadcasted_iota(jnp.int32, (width, tile), 1) + start
    return (edge >= spots_ref[0]) == (own >= spots_ref[0])


def banded(base, same, tile):
    width = tile + 256
    spread = jnp.broadcast_to(base, (width, width))
    spread = pltpu.roll(spread, 0, 1, stride=1, stride_axis=0)[:, :tile]
    matrix = jnp.where(same, spread, 0.0)
    upper = matrix.astype(bf16)
    return upper, (matrix - upper.astype(f32)).astype(bf16)


def conv_kernel(tile, spots_ref, left_ref, right_ref, base_ref, out_ref):
    upper, lower = banded(base_ref[0, 0:1], window_same(spots_ref, tile), tile)
    window = jnp.concatenate([left_ref[...], right_ref[...]], axis=1)
    out_ref[...] = nn(window, upper) + nn(window, lower)


def conv_back_kernel(
    tile, taps, spots_ref, left_ref, right_ref, low_ref, high_ref, base_ref, out_ref, tap_ref
):
    upper, lower = banded(base_ref[0, 0:1], window_same(spots_ref, tile), tile)
    own = jnp.concatenate([low_ref[...], high_ref[...]], axis=1)
    out_ref[...] = jnp.zeros_like(out_ref)
    out_ref[:, 128 : 128 + tile + 256] = nt(own, upper) + nt(own, lower)
    width = tile + 256
    rim = taps // 2
    values = jnp.concatenate([left_ref[...], right_ref[...]], axis=1).astype(f32)
    own = own.astype(f32)
    sums = []
    for o in range(taps):
        moved = pltpu.roll(values, width - (128 - rim) - o, 1)[:, :tile]
        sums.append(jnp.sum(moved * own, axis=0, keepdims=True))
    sums = jnp.concatenate(sums + [jnp.zeros((128 - taps, tile), f32)], axis=0)
    pos = lax.broadcasted_iota(jnp.int32, (128, tile), 1) + spots_ref[1] * tile
    other = pos + lax.broadcasted_iota(jnp.int32, (128, tile), 0) - rim
    same = (pos >= spots_ref[0]) == (other >= spots_ref[0])
    total = jnp.sum(jnp.where(same, sums, 0.0), axis=1, keepdims=True)
    tap_ref[0] = jnp.transpose(jnp.broadcast_to(total, (128, 128)))[0:8]


def context_kernel(heads, spots_ref, got_ref, conv_ref, keep_ref, give_ref, num_ref):
    total = jnp.sum(got_ref[...].astype(f32), axis=0)
    num_ref[...] = total
    tile = total.shape[1]
    parts = [head_units(total[64 * h : 64 * (h + 1)])[0] for h in range(heads)]
    context = (jnp.concatenate(parts, axis=0) + conv_ref[...]).astype(bf16)
    first, second = context[:, : tile // CORES], context[:, tile // CORES :]

    @pl.when(spots_ref[2] == 0)
    def _():
        keep_ref[...] = first
        give_ref[...] = second

    @pl.when(spots_ref[2] != 0)
    def _():
        keep_ref[...] = second
        give_ref[...] = first


def mixer_kernel(spots_ref, keep_ref, other_ref, out_ref, context_ref, part_ref):
    keep, other = keep_ref[...].astype(f32), other_ref[...].astype(f32)
    zero = spots_ref[2] == 0
    pair = jnp.concatenate([jnp.where(zero, keep, other), jnp.where(zero, other, keep)], axis=0)
    context = jnp.transpose(pair).astype(bf16)
    context_ref[...] = context
    part_ref[...] = nt(context, out_ref[...]).astype(bf16)


def hidden_kernel(
    tok_ref, own_ref, other_ref, norm_ref, up_ref, down_ref,
    hat_ref, inv_ref, hidden_ref, active_ref, part_ref,
):
    mixed = own_ref[...].astype(f32) + other_ref[...].astype(f32)
    hat, inverse = normalize(tok_ref[...].astype(f32) + mixed)
    hat_ref[...] = hat
    inv_ref[...] = inverse
    low = (hat * norm_ref[0:1] + norm_ref[1:2]).astype(bf16)
    hidden = nn(low, up_ref[...])
    hidden_ref[...] = hidden
    active = (0.5 * hidden * (1.0 + lax.erf(hidden * math.sqrt(0.5)))).astype(bf16)
    active_ref[...] = active
    part_ref[...] = nt(active, down_ref[...]).astype(bf16)


def feed_kernel(
    hat_ref, hidden_ref, own_ref, other_ref, cot_ref, norm_ref, up_ref, down_ref,
    out_ref, second_ref, feed_ref, slope_ref, part_ref, sums_ref,
):
    first_out = hat_ref[...] * norm_ref[0:1] + norm_ref[1:2]
    fed = own_ref[...].astype(f32) + other_ref[...].astype(f32)
    hat, inverse = normalize(first_out + fed)
    out_ref[...] = hat * norm_ref[2:3] + norm_ref[3:4]
    grad, gains, offsets = norm_back(cot_ref[...].astype(f32), hat, inverse, norm_ref[2:3])
    second_ref[...] = grad
    sums_ref[0:1] = gains
    sums_ref[1:2] = offsets
    low = grad.astype(bf16)
    feed_ref[...] = low
    active_grad = nn(low, down_ref[...])
    hidden = hidden_ref[...]
    cdf = 0.5 * (1.0 + lax.erf(hidden * math.sqrt(0.5)))
    density = jnp.exp(-0.5 * hidden * hidden) * (1.0 / math.sqrt(2.0 * math.pi))
    slope = (active_grad * (cdf + hidden * density)).astype(bf16)
    slope_ref[...] = slope
    part_ref[...] = nt(slope, up_ref[...]).astype(bf16)


def mixer_back_kernel(
    spots_ref, second_ref, own_ref, other_ref, hat_ref, inv_ref, norm_ref, out_ref, sums_ref,
    grad_ref, low_ref, keep_ref, give_ref, all_sums_ref,
):
    first = second_ref[...] + (own_ref[...].astype(f32) + other_ref[...].astype(f32))
    grad, gains, offsets = norm_back(first, hat_ref[...], inv_ref[...], norm_ref[0:1])
    grad_ref[...] = grad
    all_sums_ref[0:1] = gains
    all_sums_ref[1:2] = offsets
    all_sums_ref[2:4] = sums_ref[...]
    low = grad.astype(bf16)
    low_ref[...] = low
    context = jnp.transpose(nn(low, out_ref[...]))
    half = context.shape[0] // CORES
    zero = spots_ref[2] == 0
    keep_ref[...] = jnp.where(zero, context[:half], context[half:])
    give_ref[...] = jnp.where(zero, context[half:], context[:half])


def attention_back_kernel(
    heads, spots_ref, keep_ref, other_ref, num_ref, sums_ref, count_ref,
    send_ref, low_ref, high_ref,
):
    zero = spots_ref[2] == 0
    keep, other = keep_ref[...], other_ref[...]
    grad = jnp.concatenate([jnp.where(zero, keep, other), jnp.where(zero, other, keep)], axis=1)
    half = keep.shape[1]
    low = grad.astype(bf16)
    low_ref[...] = low[:, :half]
    high_ref[...] = low[:, half:]
    parts = []
    for h in range(heads):
        span = slice(64 * h, 64 * (h + 1))
        attention, inverse = head_units(num_ref[span])
        inner = jnp.mean(grad[span] * attention, axis=0, keepdims=True)
        parts.append(inverse * (grad[span] - attention * inner))
    gnum = jnp.concatenate(parts, axis=0).astype(bf16)
    tile = gnum.shape[1]
    feats = 64 * heads
    pieces = sums_ref.shape[1] // tile
    sums = sums_ref[...].astype(bf16).astype(f32)
    sums = jnp.concatenate(
        [sums[:, tile * i : tile * (i + 1)] for i in range(pieces)], axis=0
    )
    for c in range(send_ref.shape[0]):
        send_ref[c, 0:feats, :] = gnum
        extra = jnp.concatenate([sums, count_ref[c]], axis=0)
        send_ref[c, feats:, :] = extra.astype(bf16)


def big_grad_kernel(
    mixer_ref, context_ref, hat_ref, norm_ref, slope_ref, feed_ref, active_ref, out_ref
):
    low = hat_ref[...] * norm_ref[0:1] + norm_ref[1:2]
    ff = slope_ref.shape[1]
    out_ref[:, :ff] = nn(flip(low.astype(bf16)), slope_ref[...]).astype(bf16)
    out_ref[:, ff : 2 * ff] = nn(flip(feed_ref[...]), active_ref[...]).astype(bf16)
    out_ref[:, 2 * ff :] = nn(flip(mixer_ref[...]), context_ref[...]).astype(bf16)


def on_device(
    tokens,
    cotangent,
    doc_lengths,
    plane_bits,
    qkv_weight,
    qkv_first,
    qkv_second,
    out_weight,
    out_first,
    out_second,
    up_weight,
    up_first,
    up_second,
    down_weight,
    down_first,
    down_second,
    norm_params,
    norm_first,
    norm_second,
    conv_taps,
    conv_first,
    conv_second,
):
    tok_rows, width = tokens.shape
    hash_count, bits, group_heads, head_dim = plane_bits.shape
    buckets = 2**bits
    taps = conv_taps.shape[1]
    rim = taps // 2
    seq_count = lax.axis_size("seq")
    chips = seq_count // CORES
    place = lax.axis_index("seq")
    side = lax.axis_index("head")
    spot, core = place // CORES, place % CORES
    heads = group_heads // CORES
    feats = heads * head_dim
    group_feats = group_heads * head_dim
    hashes = hash_count // chips
    rows = -(-hashes // 8) * 8
    tile = CORES * tok_rows
    total = chips * tile
    own_rows = width // seq_count
    ff = up_weight.shape[1]
    code_rows = rows * buckets
    blocks = WORK if chips % WORK == 0 else 1
    steps = chips // blocks
    work = blocks * tile
    planes_of = [[CORES * c + k for c in range(chips)] for k in range(CORES)]
    across = partial(
        lax.all_to_all, axis_name="seq", split_axis=0, concat_axis=0, tiled=True,
        axis_index_groups=planes_of,
    )
    core_swap = partial(
        lax.ppermute, axis_name="seq", perm=[(i, i ^ 1) for i in range(seq_count)]
    )
    head_swap = partial(lax.ppermute, axis_name="head", perm=[(0, 1), (1, 0)])
    spots = jnp.stack([doc_lengths[0], spot.astype(jnp.int32), core.astype(jnp.int32)])

    smem = pl.BlockSpec(memory_space=pltpu.SMEM)
    params = pltpu.CompilerParams(
        dimension_semantics=("arbitrary",), vmem_limit_bytes=VMEM_LIMIT
    )
    shape = jax.ShapeDtypeStruct

    def full(value):
        return pl.BlockSpec(value.shape, lambda i: (0,) * value.ndim)

    def columns(block, which):
        return pl.BlockSpec((width, block), lambda i: (0, which))

    def once(kernel, name, outs, args, specs=None):
        if specs is None:
            specs = [None] * len(args)
        specs = [
            (smem if arg is spots else full(arg)) if spec is None else spec
            for spec, arg in zip(specs, args)
        ]
        return pl.pallas_call(
            kernel,
            grid=(1,),
            in_specs=specs,
            out_specs=[full(o) for o in outs],
            out_shape=outs,
            compiler_params=params,
            name=name,
        )(*args)

    def in_order(mine, other, axis):
        first = jnp.where(core == 0, mine, other)
        return jnp.concatenate([first, jnp.where(core == 0, other, mine)], axis=axis)

    got = lax.all_gather(tokens, "seq", axis=0, tiled=False)

    low_qkv = qkv_weight.astype(bf16).reshape(3, own_rows, CORES, feats)
    pick = partial(lax.dynamic_index_in_dim, low_qkv, axis=2, keepdims=False)
    by_rows = lambda part: jnp.transpose(part, (1, 0, 2)).reshape(own_rows, 3 * feats)
    qkv_mine, qkv_give = by_rows(pick(core)), by_rows(pick(1 - core))
    chip_rows = in_order(qkv_mine, core_swap(qkv_give), 0)
    qkv_all = lax.all_gather(
        chip_rows, "seq", axis=0, tiled=True, axis_index_groups=planes_of
    )
    second_send = jnp.concatenate(
        [up_weight.astype(bf16), down_weight.T.astype(bf16), out_weight.T.astype(bf16)], axis=1
    )
    second_send, unused = lax.optimization_barrier((second_send, got[0, 0, 0:1]))
    ff_all = lax.all_gather(second_send, "seq", axis=0, tiled=True)

    own_planes = lax.dynamic_slice(
        plane_bits, (spot * hashes, 0, core * heads, 0), (hashes, bits, heads, head_dim)
    )
    scale = sharpness / math.sqrt(head_dim)
    signs = scale * (2 * own_planes - 1).astype(f32)
    bit_w = jnp.pad(
        jnp.transpose(signs, (2, 1, 0, 3)), ((0, 0), (0, 0), (0, rows - hashes), (0, 0))
    )
    bit_w = bit_w.reshape(heads, bits * rows, head_dim).astype(bf16)
    bit_wt = jnp.transpose(bit_w, (0, 2, 1))

    def resident(*dims):
        return pl.BlockSpec(dims, lambda p, i: (0,) * len(dims), pipeline_mode=pl.Buffered(1))

    def stepped(phase, *dims):
        def place(p, i):
            rest = steps - 1 if phase == 0 else 0
            return (jnp.where(p == phase, i, rest),) + (0,) * (len(dims) - 1)

        return pl.BlockSpec(dims, place)

    hash_params = pltpu.CompilerParams(
        dimension_semantics=("arbitrary", "arbitrary"), vmem_limit_bytes=VMEM_LIMIT
    )
    num_parts, q_unit, k_unit, values, inverses, tables, counts = pl.pallas_call(
        partial(forward_kernel, hashes, bits, rows, work, steps, heads),
        grid=(2, steps),
        in_specs=[
            smem,
            stepped(0, CORES * blocks, tok_rows, width),
            resident(*qkv_all.shape),
            resident(*bit_w.shape),
        ],
        out_specs=[
            stepped(1, blocks, feats, tile),
            resident(feats, total),
            resident(feats, total),
            resident(feats, total + 256),
            resident(16, total),
            resident(heads, code_rows, 2 * head_dim),
            resident(heads, 8, code_rows),
        ],
        out_shape=[
            shape((chips, feats, tile), bf16),
            shape((feats, total), bf16),
            shape((feats, total), bf16),
            shape((feats, total + 256), bf16),
            shape((16, total), f32),
            shape((heads, code_rows, 2 * head_dim), bf16),
            shape((heads, 8, code_rows), f32),
        ],
        scratch_shapes=[
            pltpu.VMEM((heads, code_rows, 2 * head_dim + 16), f32),
            pltpu.VMEM((heads, code_rows, work), bf16),
            pltpu.VMEM((3 * feats, width), bf16),
            pltpu.VMEM((heads, 2 * head_dim, code_rows), bf16),
        ],
        compiler_params=hash_params,
        name="hash_forward",
    )(spots, got, qkv_all, bit_w)
    num_got = across(num_parts)

    own_taps = lax.dynamic_slice(conv_taps, (core * heads, 0), (heads, taps))
    lead = tile + 128 - rim
    bases = jnp.zeros((heads, 8, tile + 256), f32)
    bases = bases.at[:, 0, lead : lead + taps].set(own_taps[:, ::-1])
    window = [
        pl.BlockSpec((head_dim, tile), lambda h, s: (h, s[1])),
        pl.BlockSpec((head_dim, tile), lambda h, s: (h, s[1] + 1)),
    ]
    half_rows = pl.BlockSpec((head_dim, tok_rows), lambda h, s: (h, 0))
    conv = pl.pallas_call(
        partial(conv_kernel, tile),
        grid_spec=pltpu.PrefetchScalarGridSpec(
            num_scalar_prefetch=1,
            grid=(heads,),
            in_specs=window + [pl.BlockSpec((1, 8, tile + 256), lambda h, s: (h, 0, 0))],
            out_specs=pl.BlockSpec((head_dim, tile), lambda h, s: (h, 0)),
        ),
        out_shape=shape((feats, tile), f32),
        compiler_params=params,
        name="conv_forward",
    )(spots, values, values, bases)

    chip_buckets = buckets // chips
    count_rows = -(-2 * hashes * heads * chip_buckets // tile)
    sum_rows = 4 * width // tile
    extra_rows = -(-(sum_rows + count_rows) // 16) * 16
    count_send = counts[:, 0:2].reshape(heads, 2, chips, chip_buckets, rows)[..., :hashes]
    count_send = jnp.transpose(count_send, (2, 1, 4, 0, 3)).reshape(chips, -1)
    count_send = jnp.pad(
        count_send, ((0, 0), (0, (extra_rows - sum_rows) * tile - count_send.shape[1]))
    ).reshape(chips, extra_rows - sum_rows, tile)

    keep, give, numerator = once(
        partial(context_kernel, heads), "context",
        [shape((feats, tok_rows), bf16), shape((feats, tok_rows), bf16), shape((feats, tile), f32)],
        [spots, num_got, conv],
    )
    context, mixer_part = once(
        mixer_kernel, "mixer",
        [shape((tok_rows, group_feats), bf16), shape((tok_rows, width), bf16)],
        [spots, keep, core_swap(give), ff_all],
        [None, None, None, columns(group_feats, 2 * ff // group_feats)],
    )
    first_hat, first_inverse, hidden, active, feed_part = once(
        hidden_kernel, "feed_forward",
        [
            shape((tok_rows, width), f32),
            shape((tok_rows, 1), f32),
            shape((tok_rows, ff), f32),
            shape((tok_rows, ff), bf16),
            shape((tok_rows, width), bf16),
        ],
        [tokens, mixer_part, head_swap(mixer_part), norm_params, ff_all, ff_all],
        [None, None, None, None, columns(ff, 0), columns(ff, 1)],
    )
    block_out, grad_second, feed_low, slope_low, first_part, second_sums = once(
        feed_kernel, "feed_back",
        [
            shape((tok_rows, width), f32),
            shape((tok_rows, width), f32),
            shape((tok_rows, width), bf16),
            shape((tok_rows, ff), bf16),
            shape((tok_rows, width), bf16),
            shape((2, width), f32),
        ],
        [first_hat, hidden, feed_part, head_swap(feed_part), cotangent, norm_params, ff_all, ff_all],
        [None, None, None, None, None, None, columns(ff, 0), columns(ff, 1)],
    )
    grad_mixer, mixer_low, keep, give, norm_sums = once(
        mixer_back_kernel, "mixer_back",
        [
            shape((tok_rows, width), f32),
            shape((tok_rows, width), bf16),
            shape((feats, tok_rows), f32),
            shape((feats, tok_rows), f32),
            shape((4, width), f32),
        ],
        [
            spots, grad_second, first_part, head_swap(first_part), first_hat, first_inverse,
            norm_params, ff_all, second_sums,
        ],
        [None, None, None, None, None, None, None, columns(group_feats, 2 * ff // group_feats), None],
    )
    gnum_send, grad_low, grad_high = once(
        partial(attention_back_kernel, heads), "attention_back",
        [
            shape((chips, feats + extra_rows, tile), bf16),
            shape((feats, tok_rows), bf16),
            shape((feats, tok_rows), bf16),
        ],
        [spots, keep, core_swap(give), numerator, norm_sums, count_send],
    )
    gnum_got = across(gnum_send)

    mixer_low, unused = lax.optimization_barrier((mixer_low, grad_low[0:1, 0:1]))
    (big_grad,) = once(
        big_grad_kernel, "weight_grads",
        [shape((width, group_feats + 2 * ff), bf16)],
        [mixer_low, context, first_hat, norm_params, slope_low, feed_low, active],
    )
    big_owned = lax.psum_scatter(big_grad, "seq", scatter_dimension=0, tiled=True).astype(f32)

    conv_grad, tap_parts = pl.pallas_call(
        partial(conv_back_kernel, tile, taps),
        grid_spec=pltpu.PrefetchScalarGridSpec(
            num_scalar_prefetch=1,
            grid=(heads,),
            in_specs=window
            + [half_rows] * 2
            + [pl.BlockSpec((1, 8, tile + 256), lambda h, s: (h, 0, 0))],
            out_specs=[
                pl.BlockSpec((head_dim, 3 * tile), lambda h, s: (h, 0)),
                pl.BlockSpec((1, 8, 128), lambda h, s: (h, 0, 0)),
            ],
        ),
        out_shape=[shape((feats, 3 * tile), f32), shape((heads, 8, 128), f32)],
        compiler_params=params,
        name="conv_backward",
    )(spots, values, values, grad_low, grad_high, bases)

    qkv_send, back_keep, back_give = pl.pallas_call(
        partial(backward_kernel, hashes, bits, rows, work, steps, heads, own_rows),
        grid=(2, steps),
        in_specs=[
            smem,
            stepped(1, CORES * blocks, tok_rows, width),
            resident(*qkv_all.shape),
            resident(*bit_w.shape),
            resident(*bit_wt.shape),
            resident(feats, total),
            resident(feats, total),
            resident(feats, total + 256),
            resident(16, total),
            resident(heads, code_rows, 2 * head_dim),
            stepped(0, blocks, feats, tile),
            resident(feats, 3 * tile),
            resident(*tap_parts.shape),
        ],
        out_specs=[
            resident(chips, CORES * own_rows, 3 * feats + 64),
            stepped(1, blocks, width, tok_rows),
            stepped(1, blocks, width, tok_rows),
        ],
        out_shape=[
            shape((chips, CORES * own_rows, 3 * feats + 64), bf16),
            shape((chips, width, tok_rows), bf16),
            shape((chips, width, tok_rows), bf16),
        ],
        scratch_shapes=[
            pltpu.VMEM((heads, code_rows, 2 * head_dim), f32),
            pltpu.VMEM((heads, code_rows, work), bf16),
            pltpu.VMEM((feats, total), bf16),
            pltpu.VMEM((3 * feats, width), f32),
            pltpu.VMEM((heads, 2 * head_dim, code_rows), bf16),
            pltpu.VMEM((heads, code_rows, 2 * head_dim), bf16),
        ],
        compiler_params=hash_params,
        name="hash_backward",
    )(
        spots, got, qkv_all, bit_w, bit_wt,
        q_unit, k_unit, values, inverses, tables, gnum_got, conv_grad, tap_parts,
    )

    chip_sum = back_keep.astype(f32) + core_swap(back_give).astype(f32)
    half = width // 2
    chip_sum = chip_sum.astype(bf16).reshape(chips, 2, half, tok_rows)
    keep = lax.dynamic_index_in_dim(chip_sum, side, 1, keepdims=False)
    give = lax.dynamic_index_in_dim(chip_sum, 1 - side, 1, keepdims=False)
    pair_sum = keep.astype(f32) + head_swap(give).astype(f32)

    qkv_half = jnp.sum(across(qkv_send).astype(f32), axis=0)
    back_half = jnp.sum(across(pair_sum.astype(bf16)).astype(f32), axis=0)
    by_core = qkv_half.reshape(CORES, own_rows, 3 * feats + 64)
    qkv_mine = lax.dynamic_index_in_dim(by_core, core, 0, keepdims=False)[:, : 3 * feats]
    qkv_give = lax.dynamic_index_in_dim(by_core, 1 - core, 0, keepdims=False)[:, : 3 * feats]
    qkv_other = core_swap(qkv_give)

    extras = gnum_got[:, feats:].astype(f32)
    norm_half = jnp.sum(extras[:, :sum_rows], axis=0)
    count_half = extras[:, sum_rows:].reshape(chips, -1)[:, : 2 * hashes * heads * chip_buckets]
    count_half = count_half.reshape(chips, 2, hashes, heads, CORES, chip_buckets // CORES)
    count_mine = lax.dynamic_index_in_dim(count_half, core, 4, keepdims=False)
    count_give = lax.dynamic_index_in_dim(count_half, 1 - core, 4, keepdims=False)
    tap_half = qkv_half[:heads, 3 * feats : 3 * feats + taps]
    swapped = core_swap(
        jnp.concatenate([norm_half.reshape(-1), count_give.reshape(-1), tap_half.reshape(-1)])
    )
    norm_size, count_size = norm_half.size, count_give.size

    norm_grad = norm_half + swapped[:norm_size].reshape(norm_half.shape)
    norm_grad = jnp.transpose(
        norm_grad.reshape(width // tile, 4, tile), (1, 0, 2)
    ).reshape(4, width)
    count_other = swapped[norm_size : norm_size + count_size].reshape(count_mine.shape)
    occupancy = jnp.transpose(
        in_order(count_mine, count_other, 3), (1, 0, 2, 3, 4)
    ).reshape(2, hash_count, group_heads, buckets // seq_count)
    occupancy = occupancy * (buckets / (tok_rows * seq_count))
    conv_tap_grad = in_order(tap_half, swapped[norm_size + count_size :].reshape(heads, taps), 0)

    def weight_order(part):
        return jnp.transpose(part.reshape(own_rows, 3, feats), (1, 0, 2))

    qkv_owned = in_order(weight_order(qkv_mine), weight_order(qkv_other), 2)
    back_low = lax.optimization_barrier(back_half.astype(bf16))
    back_other = head_swap(back_low)
    upper = jnp.where(side == 0, back_low, back_other)
    lower = jnp.where(side == 0, back_other, back_low)
    tokens_grad = grad_mixer + jnp.concatenate([upper, lower], axis=0).T.astype(f32)

    up_owned = big_owned[:, :ff]
    down_owned = big_owned[:, ff : 2 * ff].T
    out_owned = big_owned[:, 2 * ff :].T
    qkv_new, qkv_first_new, qkv_second_new = adam_step(
        qkv_weight, qkv_first, qkv_second, qkv_owned, D ** (-0.5)
    )
    out_new, out_first_new, out_second_new = adam_step(
        out_weight, out_first, out_second, out_owned, D ** (-0.5)
    )
    up_new, up_first_new, up_second_new = adam_step(
        up_weight, up_first, up_second, up_owned, D ** (-0.5)
    )
    down_new, down_first_new, down_second_new = adam_step(
        down_weight, down_first, down_second, down_owned, FF ** (-0.5)
    )
    norm_new, norm_first_new, norm_second_new = adam_step(
        norm_params, norm_first, norm_second, norm_grad, 0.3
    )
    conv_new, conv_first_new, conv_second_new = adam_step(
        conv_taps, conv_first, conv_second, conv_tap_grad, CONV ** (-0.5)
    )
    return (
        block_out,
        tokens_grad,
        occupancy,
        qkv_new,
        qkv_first_new,
        qkv_second_new,
        qkv_new.astype(jnp.bfloat16),
        out_new,
        out_first_new,
        out_second_new,
        out_new.astype(jnp.bfloat16),
        up_new,
        up_first_new,
        up_second_new,
        up_new.astype(jnp.bfloat16),
        down_new,
        down_first_new,
        down_second_new,
        down_new.astype(jnp.bfloat16),
        norm_new,
        norm_first_new,
        norm_second_new,
        conv_new,
        conv_first_new,
        conv_second_new,
    )


def solution(mesh):
    in_specs = (
        P("seq", None),
        P("seq", None),
        P(),
        P(None, None, "head", None),
        P(None, "seq", "head"),
        P(None, "seq", "head"),
        P(None, "seq", "head"),
        P("head", "seq"),
        P("head", "seq"),
        P("head", "seq"),
        P("seq", "head"),
        P("seq", "head"),
        P("seq", "head"),
        P("head", "seq"),
        P("head", "seq"),
        P("head", "seq"),
        P(),
        P(),
        P(),
        P("head", None),
        P("head", None),
        P("head", None),
    )
    out_specs = (
        P("seq", None),
        P("seq", None),
        P(None, None, "head", "seq"),
        P(None, "seq", "head"),
        P(None, "seq", "head"),
        P(None, "seq", "head"),
        P(None, "seq", "head"),
        P("head", "seq"),
        P("head", "seq"),
        P("head", "seq"),
        P("head", "seq"),
        P("seq", "head"),
        P("seq", "head"),
        P("seq", "head"),
        P("seq", "head"),
        P("head", "seq"),
        P("head", "seq"),
        P("head", "seq"),
        P("head", "seq"),
        P(),
        P(),
        P(),
        P("head", None),
        P("head", None),
        P("head", None),
    )
    return jax.shard_map(
        on_device, mesh=mesh, in_specs=in_specs, out_specs=out_specs, check_vma=False
    )
```

```python
from functools import partial
import math

import jax
import jax.numpy as jnp
import numpy as np
from jax import lax
from jax.experimental import pallas as pl
from jax.experimental.pallas import tpu as pltpu
from jax.sharding import PartitionSpec as P

D = 768
FF = 3072
CONV = 33
STEP = 7
CORES = 2

sharpness = 4.0
norm_eps = 1e-06
layer_eps = 1e-05
beta_one = 0.9
beta_two = 0.999
adam_eps = 1e-08
decay_rate = 0.01
highest = lax.Precision.HIGHEST
f32 = jnp.float32
bf16 = jnp.bfloat16
VMEM_LIMIT = 56 * 1024 * 1024
SMALL_LIMIT = 16 * 1024 * 1024
WORK = 2
SPOTS = 4
RING = (0, 2, 4, 6, 7, 5, 3, 1)


def nn(a, b):
    return lax.dot_general(a, b, (((1,), (0,)), ((), ())), preferred_element_type=f32)


def nt(a, b):
    return lax.dot_general(a, b, (((1,), (1,)), ((), ())), preferred_element_type=f32)


def normalize(source):
    centered = source - jnp.mean(source, axis=-1, keepdims=True)
    inverse = lax.rsqrt(jnp.mean(centered * centered, axis=-1, keepdims=True) + layer_eps)
    return (centered * inverse, inverse)


def norm_back(grad, normed, inverse, gain):
    scaled = grad * gain
    inner = (
        scaled
        - jnp.mean(scaled, axis=-1, keepdims=True)
        - normed * jnp.mean(scaled * normed, axis=-1, keepdims=True)
    )
    gains = jnp.sum(grad * normed, axis=0, keepdims=True)
    return (inverse * inner, gains, jnp.sum(grad, axis=0, keepdims=True))


def adam_step(weight, first, second, grad, rate):
    first_new = beta_one * first + (1.0 - beta_one) * grad
    second_new = beta_two * second + (1.0 - beta_two) * grad * grad
    fix_one = 1.0 - beta_one**STEP
    fix_two = 1.0 - beta_two**STEP
    update = first_new / fix_one / (jnp.sqrt(second_new / fix_two) + adam_eps) + decay_rate * weight
    return (weight - rate * update, first_new, second_new)


def head_units(source):
    inverse = lax.rsqrt(jnp.mean(source * source, axis=0, keepdims=True) + norm_eps)
    return source * inverse, inverse


def seg_rows(limit, start, width):
    pos = start + lax.broadcasted_iota(jnp.int32, (1, width), 1)
    late = (pos >= limit).astype(f32)
    return 1.0 - late, late


def masked_pair(rows, early, late):
    return jnp.concatenate([rows * early, rows * late], axis=0).astype(bf16)


def flip(value):
    return jnp.transpose(value.astype(f32)).astype(bf16)


def bit_factors(bit_planes, unit, bits, hashes, rows):
    z = nn(bit_planes, unit)
    decay = jnp.exp(-jnp.abs(z))
    large = 1.0 / (1.0 + decay)
    small = decay * large
    ones = jnp.where(z >= 0.0, large, small)
    zeros = jnp.where(z >= 0.0, small, large)
    ones = [ones[j * rows : (j + 1) * rows] for j in range(bits)]
    zeros = [zeros[j * rows : (j + 1) * rows] for j in range(bits)]
    if rows != hashes:
        live = lax.broadcasted_iota(jnp.int32, ones[0].shape, 0) < hashes
        return ones, [jnp.where(live, ones[0], 0.0)] + ones[1:], [
            jnp.where(live, zeros[0], 0.0)
        ] + zeros[1:]
    return ones, ones, zeros


def products(ones, zeros, first, last):
    found = [zeros[first], ones[first]]
    for j in range(first + 1, last):
        found = [part * zeros[j] for part in found] + [part * ones[j] for part in found]
    return found


def code_parts(bit_planes, unit, bits, hashes, rows):
    plain, ones, zeros = bit_factors(bit_planes, unit, bits, hashes, rows)
    return plain, products(ones, zeros, 0, 3), products(ones, zeros, 3, bits)


def store_codes(codes_ref, head, lows, highs, rows):
    for g, high in enumerate(highs):
        for s in range(0, len(lows), 2):
            spot = (g * len(lows) + s) * rows
            pair = jnp.concatenate([lows[s] * high, lows[s + 1] * high], axis=0)
            codes_ref[head, spot : spot + 2 * rows, :] = pair.astype(bf16)


def token_copies(spots_ref, part_refs, tok_ref, sem_ref):
    return [
        pltpu.make_async_copy(
            ref.at[:, pl.ds(0, tok_ref.shape[1])],
            tok_ref.at[pl.ds(spots_ref[SPOTS + i], ref.shape[0])],
            sem_ref.at[i],
        )
        for i, ref in enumerate(part_refs)
    ]


def forward_kernel(
    hashes, bits, rows, tile, steps, heads, parts, weight_parts, weight_row, spots_ref, *refs
):
    part_refs, refs = refs[:parts], refs[parts:]
    weight_refs, refs = refs[:weight_parts], refs[weight_parts:]
    bit_ref, num_ref, qu_ref, ku_ref, v_ref, inv_ref, table_ref, count_ref, w_ref = refs[:9]
    acc_ref, codes_ref, wt_ref, table_t_ref, tok_ref, got_ref, sem_ref = refs[9:]
    limit = spots_ref[0]
    phase, i = pl.program_id(0), pl.program_id(1)
    feats = heads * 64
    chips = num_ref.shape[0]
    block = tile // chips
    start = pl.multiple_of(i * tile, tile)
    span = pl.ds(start, tile)
    early, late = seg_rows(limit, start, tile)

    @pl.when((phase == 0) & (i == 0))
    def _():
        copies = token_copies(spots_ref, part_refs, tok_ref, sem_ref)
        loads = [
            pltpu.make_async_copy(
                ref.at[:, pl.ds(weight_row, got_ref.shape[1])],
                got_ref.at[pl.ds(spots_ref[SPOTS + parts + i], ref.shape[0])],
                sem_ref.at[parts + i],
            )
            for i, ref in enumerate(weight_refs)
        ]
        for copy in loads + copies:
            copy.start()
        acc_ref[...] = jnp.zeros_like(acc_ref)
        v_ref[:, 0:128] = jnp.zeros((feats, 128), bf16)
        v_ref[:, 128 + steps * tile :] = jnp.zeros((feats, 128), bf16)
        inv_ref[...] = jnp.zeros_like(inv_ref)
        for copy in loads:
            copy.wait()
        got = got_ref[...]
        got = got.reshape(got.shape[0] * got.shape[1], got.shape[2])[:, : 3 * feats]
        w_ref[...] = got
        wt_ref[...] = flip(got)
        for copy in copies:
            copy.wait()

    @pl.when(phase == 0)
    def _():
        devices, tok_rows, width = tok_ref.shape
        here = pl.ds(i * (devices // steps), devices // steps)
        proj = nt(wt_ref[...], tok_ref[here].reshape(tile, width))
        values = proj[2 * feats :].astype(bf16)
        v_ref[:, pl.ds(pl.multiple_of(start + 128, 128), tile)] = values
        marks = jnp.concatenate([early, late, jnp.zeros((14, tile), f32)], axis=0).astype(bf16)
        units = []
        for h in range(heads):
            mine = slice(64 * h, 64 * (h + 1))
            q_unit, q_inv = head_units(proj[mine])
            k_unit, k_inv = head_units(proj[feats + 64 * h : feats + 64 * (h + 1)])
            units.append(k_unit.astype(bf16))
            qu_ref[mine, span] = q_unit.astype(bf16)
            ku_ref[mine, span] = units[h]
            inv_ref[h : h + 1, span] = q_inv
            inv_ref[8 + h : 9 + h, span] = k_inv
        for h in range(heads):
            plain, lows, highs = code_parts(bit_ref[h], units[h], bits, hashes, rows)
            store_codes(codes_ref, h, lows, highs, rows)
        for h in range(heads):
            pair = masked_pair(values[64 * h : 64 * (h + 1)].astype(f32), early, late)
            pair = jnp.concatenate([pair, marks], axis=0)
            acc_ref[h] += nt(codes_ref[h], pair)

    @pl.when((phase == 1) & (i == 0))
    def _():
        for h in range(heads):
            table = acc_ref[h, :, 0:128].astype(bf16)
            table_ref[h] = table
            table_t_ref[h] = flip(table)
            counts = jnp.concatenate(
                [acc_ref[h, :, 128:144], jnp.zeros((acc_ref.shape[1], 112), f32)], axis=1
            )
            count_ref[h] = jnp.transpose(counts)[0:8]

    @pl.when(phase == 1)
    def _():
        for h in range(heads):
            unit = qu_ref[64 * h : 64 * (h + 1), span]
            plain, lows, highs = code_parts(bit_ref[h], unit, bits, hashes, rows)
            store_codes(codes_ref, h, lows, highs, rows)
        for h in range(heads):
            mine = slice(64 * h, 64 * (h + 1))
            both = nn(table_t_ref[h], codes_ref[h])
            low = (both[0:64] * early + both[64:128] * late).astype(bf16)
            for c in range(chips):
                num_ref[c, mine, :] = low[:, c * block : (c + 1) * block]


def soften(bit_planes, unit, slopes, codes_ref, head, bits, hashes, rows):
    plain, lows, highs = code_parts(bit_planes, unit, bits, hashes, rows)
    by_low = [None] * len(lows)
    by_bit = [None] * (bits - 3)
    for g, high in enumerate(highs):
        row = None
        for s in range(0, len(lows), 2):
            spot = (g * len(lows) + s) * rows
            parts = [lows[s] * high, lows[s + 1] * high]
            codes_ref[head, spot : spot + 2 * rows, :] = jnp.concatenate(parts, axis=0).astype(bf16)
            for k in range(2):
                term = parts[k] * slopes[spot + k * rows : spot + (k + 1) * rows]
                by_low[s + k] = term if by_low[s + k] is None else by_low[s + k] + term
                row = term if row is None else row + term
        for j in range(bits - 3):
            if (g >> j) & 1:
                by_bit[j] = row if by_bit[j] is None else by_bit[j] + row
    pairs = [sum(part for s, part in enumerate(by_low) if (s >> j) & 1) for j in range(3)]
    whole = sum(by_low)
    slopes = [part - plain[j] * whole for j, part in enumerate(pairs + by_bit)]
    return jnp.concatenate(slopes, axis=0).astype(bf16)


def unit_back(grad, unit, inverse):
    unit = unit.astype(f32)
    inner = jnp.mean(grad * unit, axis=0, keepdims=True)
    return inverse * (grad - unit * inner)


def backward_kernel(hashes, bits, rows, tile, steps, heads, own_rows, parts, spots_ref, *refs):
    part_refs, refs = refs[:parts], refs[parts:]
    w_ref, bit_ref, bit_t_ref, qu_ref, ku_ref, v_ref, inv_ref, table_ref = refs[:8]
    gnum_ref, conv_ref, tap_ref, grad_ref, keep_ref, give_ref = refs[8:14]
    acc_ref, codes_ref, proj_ref, sum_ref, table_t_ref, table_g_ref, tok_ref, sem_ref = refs[14:]
    limit = spots_ref[0]
    spot = spots_ref[1]
    core = spots_ref[2]
    phase, i = pl.program_id(0), pl.program_id(1)
    devices, unused, width = tok_ref.shape
    copies = token_copies(spots_ref, part_refs, tok_ref, sem_ref)
    feats = heads * 64
    blocks = keep_ref.shape[0]
    block = tile // blocks
    tok_rows = block // CORES
    start = pl.multiple_of(i * tile, tile)
    span = pl.ds(start, tile)
    early, late = seg_rows(limit, start, tile)

    @pl.when((phase == 0) & (i == 0))
    def _():
        for copy in copies:
            copy.start()
        acc_ref[...] = jnp.zeros_like(acc_ref)
        sum_ref[...] = jnp.zeros_like(sum_ref)

    @pl.when(phase == 0)
    def _():
        spans = [slice(64 * h, 64 * (h + 1)) for h in range(heads)]
        pairs, grads, slopes = [], [], []
        for mine in spans:
            gnum = jnp.concatenate([gnum_ref[c, mine, :] for c in range(blocks)], axis=1)
            pairs.append(masked_pair(gnum.astype(f32), early, late))
        for h, mine in enumerate(spans):
            slopes.append(
                soften(
                    bit_ref[h], qu_ref[mine, span], nn(table_ref[h], pairs[h]), codes_ref, h,
                    bits, hashes, rows,
                )
            )
        for h in range(heads):
            acc_ref[h] += nt(codes_ref[h], pairs[h])
        for h, mine in enumerate(spans):
            grad = nn(bit_t_ref[h], slopes[h])
            grad = unit_back(grad, qu_ref[mine, span], inv_ref[h : h + 1, span])
            proj_ref[mine, span] = grad.astype(bf16)

    @pl.when((phase == 1) & (i == 0))
    def _():
        for copy in copies:
            copy.wait()
        for h in range(heads):
            table_g_ref[h] = acc_ref[h].astype(bf16)
            table_t_ref[h] = flip(table_g_ref[h])

    @pl.when(phase == 1)
    def _():
        conv = []
        for c in range(blocks):
            step = i * blocks + c - spot + 1
            near = ((step >= 0) & (step <= 2)).astype(f32)
            step = jnp.clip(step, 0, 2)
            conv.append(conv_ref[:, pl.ds(pl.multiple_of(step * block, block), block)] * near)
        conv = jnp.concatenate(conv, axis=1)
        spans = [slice(64 * h, 64 * (h + 1)) for h in range(heads)]
        slopes, parts = [], []
        for h, mine in enumerate(spans):
            values = v_ref[mine, pl.ds(pl.multiple_of(start + 128, 128), tile)]
            pair = masked_pair(values.astype(f32), early, late)
            slopes.append(
                soften(
                    bit_ref[h], ku_ref[mine, span], nn(table_g_ref[h], pair), codes_ref, h,
                    bits, hashes, rows,
                )
            )
        for h, mine in enumerate(spans):
            both = nn(table_t_ref[h], codes_ref[h])
            value_grad = both[0:64] * early + both[64:128] * late + conv[mine]
            grad = nn(bit_t_ref[h], slopes[h])
            grad = unit_back(grad, ku_ref[mine, span], inv_ref[8 + h : 9 + h, span])
            parts.append((grad.astype(bf16), value_grad.astype(bf16)))
        full = jnp.concatenate(
            [proj_ref[:, span]] + [part[0] for part in parts] + [part[1] for part in parts], axis=0
        )
        here = pl.ds(i * (devices // steps), devices // steps)
        sum_ref[...] += nn(full, tok_ref[here].reshape(tile, width))
        part = nn(w_ref[...], full)
        for c in range(blocks):
            first = part[:, c * block : c * block + tok_rows]
            second = part[:, c * block + tok_rows : (c + 1) * block]
            keep_ref[c] = jnp.where(core == 0, first, second).astype(bf16)
            give_ref[c] = jnp.where(core == 0, second, first).astype(bf16)

    @pl.when((phase == 1) & (i == steps - 1))
    def _():
        grad = jnp.transpose(sum_ref[...])
        chips = grad_ref.shape[0]
        grad_ref[:, :, 0 : heads * 192] = grad.reshape(
            chips, CORES * own_rows, heads * 192
        ).astype(bf16)
        grad_ref[:, :, heads * 192 :] = jnp.zeros((chips, CORES * own_rows, 64), bf16)
        taps = jnp.concatenate([tap_ref[h, 0:1, 0:64] for h in range(heads)], axis=0)
        for c in range(chips):
            grad_ref[c, 0:heads, heads * 192 :] = taps.astype(bf16)


def window_same(spots_ref, tile):
    start = spots_ref[1] * tile
    width = tile + 256
    edge = lax.broadcasted_iota(jnp.int32, (width, tile), 0) + (start - 128)
    own = lax.broadcasted_iota(jnp.int32, (width, tile), 1) + start
    return (edge >= spots_ref[0]) == (own >= spots_ref[0])


def banded(base, same, tile):
    width = tile + 256
    spread = jnp.broadcast_to(base, (width, width))
    spread = pltpu.roll(spread, 0, 1, stride=1, stride_axis=0)[:, :tile]
    matrix = jnp.where(same, spread, 0.0)
    upper = matrix.astype(bf16)
    return upper, (matrix - upper.astype(f32)).astype(bf16)


def conv_kernel(tile, spots_ref, left_ref, right_ref, base_ref, out_ref):
    upper, lower = banded(base_ref[0, 0:1], window_same(spots_ref, tile), tile)
    window = jnp.concatenate([left_ref[...], right_ref[...]], axis=1)
    out_ref[...] = nn(window, upper) + nn(window, lower)


def conv_back_kernel(
    tile, taps, spots_ref, left_ref, right_ref, low_ref, high_ref, base_ref, out_ref, tap_ref
):
    upper, lower = banded(base_ref[0, 0:1], window_same(spots_ref, tile), tile)
    own = jnp.concatenate([low_ref[...], high_ref[...]], axis=1)
    out_ref[...] = jnp.zeros_like(out_ref)
    out_ref[:, 128 : 128 + tile + 256] = nt(own, upper) + nt(own, lower)
    width = tile + 256
    rim = taps // 2
    values = jnp.concatenate([left_ref[...], right_ref[...]], axis=1).astype(f32)
    own = own.astype(f32)
    sums = []
    for o in range(taps):
        moved = pltpu.roll(values, width - (128 - rim) - o, 1)[:, :tile]
        sums.append(jnp.sum(moved * own, axis=0, keepdims=True))
    sums = jnp.concatenate(sums + [jnp.zeros((128 - taps, tile), f32)], axis=0)
    pos = lax.broadcasted_iota(jnp.int32, (128, tile), 1) + spots_ref[1] * tile
    other = pos + lax.broadcasted_iota(jnp.int32, (128, tile), 0) - rim
    same = (pos >= spots_ref[0]) == (other >= spots_ref[0])
    total = jnp.sum(jnp.where(same, sums, 0.0), axis=1, keepdims=True)
    tap_ref[0] = jnp.transpose(jnp.broadcast_to(total, (128, 128)))[0:8]


def context_kernel(heads, spots_ref, got_ref, conv_ref, keep_ref, give_ref, num_ref):
    total = jnp.sum(got_ref[...].astype(f32), axis=0)
    num_ref[...] = total
    tile = total.shape[1]
    parts = [head_units(total[64 * h : 64 * (h + 1)])[0] for h in range(heads)]
    context = (jnp.concatenate(parts, axis=0) + conv_ref[...]).astype(bf16)
    first, second = context[:, : tile // CORES], context[:, tile // CORES :]

    @pl.when(spots_ref[2] == 0)
    def _():
        keep_ref[...] = first
        give_ref[...] = second

    @pl.when(spots_ref[2] != 0)
    def _():
        keep_ref[...] = second
        give_ref[...] = first


def mixer_kernel(spots_ref, keep_ref, other_ref, w_ref, context_ref, part_ref):
    keep, other = keep_ref[...].astype(f32), other_ref[...].astype(f32)
    zero = spots_ref[2] == 0
    pair = jnp.concatenate([jnp.where(zero, keep, other), jnp.where(zero, other, keep)], axis=0)
    context = jnp.transpose(pair).astype(bf16)
    context_ref[...] = context
    part_ref[...] = nt(context, w_ref[:, w_ref.shape[1] - context.shape[1] :]).astype(bf16)


def hidden_kernel(
    tok_ref, own_ref, other_ref, norm_ref, w_ref, hat_ref, inv_ref, hidden_ref, active_ref, part_ref
):
    ff = hidden_ref.shape[1]
    mixed = own_ref[...].astype(f32) + other_ref[...].astype(f32)
    hat, inverse = normalize(tok_ref[...].astype(f32) + mixed)
    hat_ref[...] = hat
    inv_ref[...] = inverse
    low = (hat * norm_ref[0:1] + norm_ref[1:2]).astype(bf16)
    hidden = nn(low, w_ref[:, :ff])
    hidden_ref[...] = hidden
    active = (0.5 * hidden * (1.0 + lax.erf(hidden * math.sqrt(0.5)))).astype(bf16)
    active_ref[...] = active
    part_ref[...] = nt(active, w_ref[:, ff : 2 * ff]).astype(bf16)


def feed_kernel(
    hat_ref, hidden_ref, own_ref, other_ref, cot_ref, norm_ref, w_ref,
    out_ref, second_ref, feed_ref, slope_ref, part_ref, sums_ref,
):
    ff = hidden_ref.shape[1]
    first_out = hat_ref[...] * norm_ref[0:1] + norm_ref[1:2]
    fed = own_ref[...].astype(f32) + other_ref[...].astype(f32)
    hat, inverse = normalize(first_out + fed)
    out_ref[...] = hat * norm_ref[2:3] + norm_ref[3:4]
    grad, gains, offsets = norm_back(cot_ref[...].astype(f32), hat, inverse, norm_ref[2:3])
    second_ref[...] = grad
    sums_ref[0:1] = gains
    sums_ref[1:2] = offsets
    low = grad.astype(bf16)
    feed_ref[...] = low
    active_grad = nn(low, w_ref[:, ff : 2 * ff])
    hidden = hidden_ref[...]
    cdf = 0.5 * (1.0 + lax.erf(hidden * math.sqrt(0.5)))
    density = jnp.exp(-0.5 * hidden * hidden) * (1.0 / math.sqrt(2.0 * math.pi))
    slope = (active_grad * (cdf + hidden * density)).astype(bf16)
    slope_ref[...] = slope
    part_ref[...] = nt(slope, w_ref[:, :ff]).astype(bf16)


def mixer_back_kernel(
    spots_ref, second_ref, own_ref, other_ref, hat_ref, inv_ref, norm_ref, w_ref, sums_ref,
    grad_ref, low_ref, keep_ref, give_ref, all_sums_ref,
):
    first = second_ref[...] + (own_ref[...].astype(f32) + other_ref[...].astype(f32))
    grad, gains, offsets = norm_back(first, hat_ref[...], inv_ref[...], norm_ref[0:1])
    grad_ref[...] = grad
    all_sums_ref[0:1] = gains
    all_sums_ref[1:2] = offsets
    all_sums_ref[2:4] = sums_ref[...]
    low = grad.astype(bf16)
    low_ref[...] = low
    half = keep_ref.shape[0]
    context = jnp.transpose(nn(low, w_ref[:, w_ref.shape[1] - CORES * half :]))
    half = context.shape[0] // CORES
    zero = spots_ref[2] == 0
    keep_ref[...] = jnp.where(zero, context[:half], context[half:])
    give_ref[...] = jnp.where(zero, context[half:], context[:half])


def attention_back_kernel(
    heads, spots_ref, keep_ref, other_ref, num_ref, sums_ref, count_ref,
    send_ref, low_ref, high_ref,
):
    zero = spots_ref[2] == 0
    keep, other = keep_ref[...], other_ref[...]
    grad = jnp.concatenate([jnp.where(zero, keep, other), jnp.where(zero, other, keep)], axis=1)
    half = keep.shape[1]
    low = grad.astype(bf16)
    low_ref[...] = low[:, :half]
    high_ref[...] = low[:, half:]
    parts = []
    for h in range(heads):
        span = slice(64 * h, 64 * (h + 1))
        attention, inverse = head_units(num_ref[span])
        inner = jnp.mean(grad[span] * attention, axis=0, keepdims=True)
        parts.append(inverse * (grad[span] - attention * inner))
    gnum = jnp.concatenate(parts, axis=0).astype(bf16)
    tile = gnum.shape[1]
    feats = 64 * heads
    pieces = sums_ref.shape[1] // tile
    chips = send_ref.shape[0]
    piece = count_ref.shape[2] // chips
    blank = jnp.zeros((1, tile // 2 - piece), f32)
    spare = jnp.zeros((send_ref.shape[1] - feats - 4 * pieces - heads, tile), f32)
    sums = sums_ref[...].astype(bf16).astype(f32)
    sums = jnp.concatenate(
        [sums[:, tile * i : tile * (i + 1)] for i in range(pieces)], axis=0
    )
    for c in range(chips):
        send_ref[c, 0:feats, :] = gnum
        counts = []
        for h in range(heads):
            row = [count_ref[h, d : d + 1, c * piece : (c + 1) * piece] for d in range(2)]
            counts.append(
                jnp.concatenate([row[0], blank, row[1], blank], axis=1)
                if blank.shape[1]
                else jnp.concatenate(row, axis=1)
            )
        extra = jnp.concatenate([sums] + counts + [spare], axis=0)
        send_ref[c, feats:, :] = extra.astype(bf16)


def feed_grad_kernel(hat_ref, norm_ref, slope_ref, feed_ref, active_ref, out_ref):
    ff = slope_ref.shape[1]
    low = hat_ref[...] * norm_ref[0:1] + norm_ref[1:2]
    out_ref[:, :ff] = nn(flip(low.astype(bf16)), slope_ref[...]).astype(bf16)
    out_ref[:, ff : 2 * ff] = nn(flip(feed_ref[...]), active_ref[...]).astype(bf16)


def out_grad_kernel(mixer_ref, context_ref, all_ref, out_ref):
    out_ref[...] = nn(flip(mixer_ref[...]), context_ref[...]).astype(bf16)


def pack_kernel(spots_ref, up_ref, down_ref, out_ref, after_ref, bit_ref, all_ref):
    ff = up_ref.shape[1]
    all_ref[:, :ff] = up_ref[...].astype(bf16)
    all_ref[:, ff : 2 * ff] = down_ref[...].astype(bf16)
    all_ref[:, 2 * ff :] = out_ref[...].astype(bf16)


def chip_sum_kernel(spots_ref, own_ref, other_ref, keep_ref, give_ref):
    total = own_ref[...].astype(f32) + other_ref[...].astype(f32)
    half = total.shape[1] // 2
    first, second = total[:, :half], total[:, half:]
    zero = spots_ref[3] == 0
    keep_ref[...] = jnp.where(zero, first, second).astype(bf16)
    give_ref[...] = jnp.where(zero, second, first).astype(bf16)


def pair_sum_kernel(own_ref, other_ref, out_ref):
    out_ref[...] = (own_ref[...].astype(f32) + other_ref[...].astype(f32)).astype(bf16)


def weight_sum_kernel(spots_ref, got_ref, after_ref, keep_ref, give_ref):
    total = jnp.sum(got_ref[...].astype(f32), axis=0)
    half = total.shape[0] // CORES
    zero = spots_ref[2] == 0
    keep_ref[...] = jnp.where(zero, total[:half], total[half:])
    give_ref[...] = jnp.where(zero, total[half:], total[:half])


def adam_refs(grad, ins, outs, rate):
    new, first, second = adam_step(ins[0], ins[1], ins[2], grad, rate)
    outs[0][...] = new
    outs[1][...] = first
    outs[2][...] = second
    outs[3][...] = new.astype(bf16)


def big_adam_kernel(grad_ref, *refs):
    ins, outs = refs[:9], refs[9:]
    ff = ins[0].shape[1]
    spans = (slice(0, ff), slice(ff, 2 * ff), slice(2 * ff, grad_ref.shape[1]))
    for k, (span, rate) in enumerate(zip(spans, (D ** (-0.5), FF ** (-0.5), D ** (-0.5)))):
        state = [ref[...] for ref in ins[3 * k : 3 * k + 3]]
        adam_refs(grad_ref[:, span].astype(f32), state, outs[4 * k : 4 * k + 4], rate)


def qkv_adam_kernel(spots_ref, mine_ref, other_ref, *refs):
    zero = spots_ref[2] == 0
    feats = refs[0].shape[2] // CORES
    for p in range(3):
        span = slice(p * feats, (p + 1) * feats)
        mine, other = mine_ref[:, span], other_ref[:, span]
        grad = jnp.concatenate([jnp.where(zero, mine, other), jnp.where(zero, other, mine)], axis=1)
        adam_refs(grad, [ref[p] for ref in refs[:3]], [ref.at[p] for ref in refs[3:]], D ** (-0.5))


def back_sum_kernel(got_ref, *refs):
    refs[-1][...] = jnp.sum(got_ref[...].astype(f32), axis=0).astype(bf16)


def on_device(
    tokens,
    cotangent,
    doc_lengths,
    plane_bits,
    qkv_weight,
    qkv_first,
    qkv_second,
    out_weight,
    out_first,
    out_second,
    up_weight,
    up_first,
    up_second,
    down_weight,
    down_first,
    down_second,
    norm_params,
    norm_first,
    norm_second,
    conv_taps,
    conv_first,
    conv_second,
):
    tok_rows, width = tokens.shape
    hash_count, bits, group_heads, head_dim = plane_bits.shape
    buckets = 2**bits
    taps = conv_taps.shape[1]
    rim = taps // 2
    seq_count = lax.axis_size("seq")
    chips = seq_count // CORES
    place = lax.axis_index("seq")
    side = lax.axis_index("head")
    spot, core = place // CORES, place % CORES
    heads = group_heads // CORES
    feats = heads * head_dim
    group_feats = group_heads * head_dim
    hashes = hash_count // chips
    rows = -(-hashes // 8) * 8
    tile = CORES * tok_rows
    total = chips * tile
    own_rows = width // seq_count
    ff = up_weight.shape[1]
    code_rows = rows * buckets
    blocks = WORK if chips % WORK == 0 else 1
    steps = chips // blocks
    work = blocks * tile
    planes_of = [[CORES * c + k for c in range(chips)] for k in range(CORES)]
    across = partial(
        lax.all_to_all, axis_name="seq", split_axis=0, concat_axis=0, tiled=True,
        axis_index_groups=planes_of,
    )
    core_swap = partial(
        lax.ppermute, axis_name="seq", perm=[(i, i ^ 1) for i in range(seq_count)]
    )
    head_swap = partial(lax.ppermute, axis_name="head", perm=[(0, 1), (1, 0)])
    def in_order(mine, other, axis):
        first = jnp.where(core == 0, mine, other)
        return jnp.concatenate([first, jnp.where(core == 0, other, mine)], axis=axis)

    low_qkv = qkv_weight.astype(bf16).reshape(3, own_rows, CORES, feats)
    pick = partial(lax.dynamic_index_in_dim, low_qkv, axis=2, keepdims=False)
    by_rows = lambda part: jnp.transpose(part, (1, 0, 2)).reshape(own_rows, 3 * feats)
    qkv_mine, qkv_give = by_rows(pick(core)), by_rows(pick(1 - core))
    chip_rows = in_order(qkv_mine, core_swap(qkv_give), 0)
    chip_rows = jnp.pad(chip_rows, ((0, 0), (0, width - 3 * feats)))

    if chips == len(RING):
        order = np.array(RING)
        seats = np.argsort(order)
        ahead = [
            (CORES * order[i] + k, CORES * order[(i + 1) % chips] + k)
            for i in range(chips)
            for k in range(CORES)
        ]
        behind = [(b, a) for a, b in ahead]
        block = jnp.concatenate([tokens, chip_rows], axis=0)
        block_parts, turns, moved = [block], [0], [block, block]
        for step in range(1, chips // 2 + 1):
            moved[0] = lax.ppermute(moved[0], "seq", ahead)
            block_parts.append(moved[0])
            turns.append(chips - step)
            if 2 * step < chips:
                moved[1] = lax.ppermute(moved[1], "seq", behind)
                moved = list(lax.optimization_barrier(tuple(moved)))
                block_parts[-1] = moved[0]
                block_parts.append(moved[1])
                turns.append(step)
                last_part = moved[1]
        token_parts = [p[None] for p in block_parts + [core_swap(part) for part in block_parts]]
        weight_parts, weight_row = token_parts[:chips], tok_rows
        spot_of = np.array([[order[(seats[c] + t) % chips] for t in turns] for c in range(chips)])
        spot_of = np.repeat(spot_of, CORES, axis=0)
        core_of = np.arange(seq_count)[:, None] % CORES
        place_of = [CORES * spot_of + core_of, CORES * spot_of + 1 - core_of, spot_of]
    else:
        token_parts = [lax.all_gather(tokens, "seq", axis=0, tiled=False)]
        weight_parts = [
            lax.all_gather(chip_rows, "seq", axis=0, tiled=False, axis_index_groups=planes_of)
        ]
        weight_row = 0
        place_of = [np.zeros((seq_count, 2))]
        last_part = token_parts[0]
    parts = len(token_parts)
    weight_count = len(weight_parts)
    device = np.arange(seq_count)[:, None]
    facts = np.concatenate([device // CORES, device % CORES, 0 * device] + place_of, axis=1)
    facts = np.stack([facts + k * (np.arange(facts.shape[1]) == 2) for k in range(2)])
    facts = lax.dynamic_slice(
        jnp.asarray(facts.astype(np.int32)), (side, place, 0), (1, 1, facts.shape[2])
    )
    spots = jnp.concatenate([doc_lengths[0:1], facts.reshape(-1)])

    smem = pl.BlockSpec(memory_space=pltpu.SMEM)
    anywhere = pl.BlockSpec(memory_space=pl.ANY)
    params = pltpu.CompilerParams(
        dimension_semantics=("arbitrary",), vmem_limit_bytes=VMEM_LIMIT
    )
    shape = jax.ShapeDtypeStruct

    def full(value):
        return pl.BlockSpec(value.shape, lambda i: (0,) * value.ndim)

    def piped(kernel, name, outs, args, specs=None):
        if specs is None:
            specs = [None] * len(args)
        specs = [
            (smem if arg is spots else full(arg)) if spec is None else spec
            for spec, arg in zip(specs, args)
        ]
        return pl.pallas_call(
            kernel,
            grid=(1,),
            in_specs=specs,
            out_specs=[full(o) for o in outs],
            out_shape=outs,
            compiler_params=params,
            name=name,
        )(*args)

    inside = pl.BlockSpec(memory_space=pltpu.VMEM)

    def once(kernel, name, outs, args, after=(), outside=(), aliases=None, limit=SMALL_LIMIT):
        specs, values = [], []
        for arg in args:
            specs.append(smem if arg is spots else inside)
            values.append(
                arg if arg is spots else pltpu.with_memory_space_constraint(arg, pltpu.VMEM)
            )
        for arg in after:
            specs.append(anywhere)
            values.append(arg)
        return pl.pallas_call(
            kernel,
            in_specs=specs,
            out_specs=[inside] * len(outs),
            out_shape=[
                o if i in outside else pltpu.VMEM(o.shape, o.dtype) for i, o in enumerate(outs)
            ],
            compiler_params=pltpu.CompilerParams(vmem_limit_bytes=limit),
            name=name,
        )(*values)

    own_planes = lax.dynamic_slice(
        plane_bits, (spot * hashes, 0, core * heads, 0), (hashes, bits, heads, head_dim)
    )
    scale = sharpness / math.sqrt(head_dim)
    signs = scale * (2 * own_planes - 1).astype(f32)
    bit_w = jnp.pad(
        jnp.transpose(signs, (2, 1, 0, 3)), ((0, 0), (0, 0), (0, rows - hashes), (0, 0))
    )
    bit_w = bit_w.reshape(heads, bits * rows, head_dim).astype(bf16)
    bit_wt = jnp.transpose(bit_w, (0, 2, 1))

    (second_send,) = piped(
        pack_kernel, "pack",
        [shape((own_rows, 2 * ff + group_feats), bf16)],
        [spots, up_weight, down_weight.T, out_weight.T, last_part, bit_w],
        [None] * 4 + [anywhere] * 2,
    )
    ff_all = lax.all_gather(second_send, "seq", axis=0, tiled=True)

    def resident(*dims):
        return pl.BlockSpec(dims, lambda p, i: (0,) * len(dims), pipeline_mode=pl.Buffered(1))

    def stepped(phase, *dims):
        def place(p, i):
            rest = steps - 1 if phase == 0 else 0
            return (jnp.where(p == phase, i, rest),) + (0,) * (len(dims) - 1)

        return pl.BlockSpec(dims, place)

    hash_params = pltpu.CompilerParams(
        dimension_semantics=("arbitrary", "arbitrary"), vmem_limit_bytes=VMEM_LIMIT
    )
    num_parts, q_unit, k_unit, values, inverses, tables, counts, qkv_all = pl.pallas_call(
        partial(forward_kernel, hashes, bits, rows, work, steps, heads, parts, weight_count, weight_row),
        grid=(2, steps),
        in_specs=[
            smem,
            *[anywhere] * (parts + weight_count),
            resident(*bit_w.shape),
        ],
        out_specs=[
            stepped(1, blocks, feats, tile),
            resident(feats, total),
            resident(feats, total),
            resident(feats, total + 256),
            resident(16, total),
            resident(heads, code_rows, 2 * head_dim),
            resident(heads, 8, code_rows),
            resident(width, 3 * feats),
        ],
        out_shape=[
            shape((chips, feats, tile), bf16),
            shape((feats, total), bf16),
            shape((feats, total), bf16),
            shape((feats, total + 256), bf16),
            shape((16, total), f32),
            shape((heads, code_rows, 2 * head_dim), bf16),
            shape((heads, 8, code_rows), f32),
            shape((width, 3 * feats), bf16),
        ],
        scratch_shapes=[
            pltpu.VMEM((heads, code_rows, 2 * head_dim + 16), f32),
            pltpu.VMEM((heads, code_rows, work), bf16),
            pltpu.VMEM((3 * feats, width), bf16),
            pltpu.VMEM((heads, 2 * head_dim, code_rows), bf16),
            pltpu.VMEM((seq_count, tok_rows, width), bf16),
            pltpu.VMEM((chips, CORES * own_rows, width), bf16),
            pltpu.SemaphoreType.DMA((parts + weight_count,)),
        ],
        compiler_params=hash_params,
        name="hash_forward",
    )(spots, *token_parts, *weight_parts, bit_w)
    num_got = across(num_parts)

    own_taps = lax.dynamic_slice(conv_taps, (core * heads, 0), (heads, taps))
    lead = tile + 128 - rim
    bases = jnp.zeros((heads, 8, tile + 256), f32)
    bases = bases.at[:, 0, lead : lead + taps].set(own_taps[:, ::-1])
    window = [
        pl.BlockSpec((head_dim, tile), lambda h, s: (h, s[1])),
        pl.BlockSpec((head_dim, tile), lambda h, s: (h, s[1] + 1)),
    ]
    half_rows = pl.BlockSpec((head_dim, tok_rows), lambda h, s: (h, 0))
    conv = pl.pallas_call(
        partial(conv_kernel, tile),
        grid_spec=pltpu.PrefetchScalarGridSpec(
            num_scalar_prefetch=1,
            grid=(heads,),
            in_specs=window + [pl.BlockSpec((1, 8, tile + 256), lambda h, s: (h, 0, 0))],
            out_specs=pl.BlockSpec((head_dim, tile), lambda h, s: (h, 0)),
        ),
        out_shape=shape((feats, tile), f32),
        compiler_params=params,
        name="conv_forward",
    )(spots, values, values, bases)

    chip_buckets = buckets // chips
    sum_rows = 4 * width // tile
    extra_rows = -(-(sum_rows + heads) // 16) * 16

    keep, give, numerator = once(
        partial(context_kernel, heads), "context",
        [shape((feats, tok_rows), bf16), shape((feats, tok_rows), bf16), shape((feats, tile), f32)],
        [spots, num_got, conv],
    )
    context, mixer_part = once(
        mixer_kernel, "mixer",
        [shape((tok_rows, group_feats), bf16), shape((tok_rows, width), bf16)],
        [spots, keep, core_swap(give), ff_all],
    )
    first_hat, first_inverse, hidden, active, feed_part = once(
        hidden_kernel, "feed_forward",
        [
            shape((tok_rows, width), f32),
            shape((tok_rows, 1), f32),
            shape((tok_rows, ff), f32),
            shape((tok_rows, ff), bf16),
            shape((tok_rows, width), bf16),
        ],
        [tokens, mixer_part, head_swap(mixer_part), norm_params, ff_all],
    )
    block_out, grad_second, feed_low, slope_low, first_part, second_sums = once(
        feed_kernel, "feed_back",
        [
            shape((tok_rows, width), f32),
            shape((tok_rows, width), f32),
            shape((tok_rows, width), bf16),
            shape((tok_rows, ff), bf16),
            shape((tok_rows, width), bf16),
            shape((2, width), f32),
        ],
        [first_hat, hidden, feed_part, head_swap(feed_part), cotangent, norm_params, ff_all],
        outside=(0,),
    )
    grad_mixer, mixer_low, keep, give, norm_sums = once(
        mixer_back_kernel, "mixer_back",
        [
            shape((tok_rows, width), f32),
            shape((tok_rows, width), bf16),
            shape((feats, tok_rows), f32),
            shape((feats, tok_rows), f32),
            shape((4, width), f32),
        ],
        [
            spots, grad_second, first_part, head_swap(first_part), first_hat, first_inverse,
            norm_params, ff_all, second_sums,
        ],
        outside=(0,),
    )
    gnum_send, grad_low, grad_high = once(
        partial(attention_back_kernel, heads), "attention_back",
        [
            shape((chips, feats + extra_rows, tile), bf16),
            shape((feats, tok_rows), bf16),
            shape((feats, tok_rows), bf16),
        ],
        [spots, keep, core_swap(give), numerator, norm_sums, counts],
        outside=(0, 1, 2),
    )
    gnum_got = across(gnum_send)

    columns = 2 * ff + group_feats
    feed_grads = pl.pallas_call(
        feed_grad_kernel,
        grid=(1,),
        in_specs=[full(v) for v in (first_hat, norm_params, slope_low, feed_low, active)],
        out_specs=pl.BlockSpec((width, 2 * ff), lambda i: (0, 0)),
        out_shape=shape((width, columns), bf16),
        compiler_params=params,
        name="feed_grads",
    )(first_hat, norm_params, slope_low, feed_low, active)
    big_grad = pl.pallas_call(
        out_grad_kernel,
        grid=(1,),
        in_specs=[full(mixer_low), full(context), anywhere],
        out_specs=pl.BlockSpec((width, group_feats), lambda i: (0, 2 * ff // group_feats)),
        out_shape=shape((width, columns), bf16),
        input_output_aliases={2: 0},
        compiler_params=params,
        name="out_grads",
    )(mixer_low, context, feed_grads)
    big_owned = lax.psum_scatter(big_grad, "seq", scatter_dimension=0, tiled=True)

    conv_grad, tap_parts = pl.pallas_call(
        partial(conv_back_kernel, tile, taps),
        grid_spec=pltpu.PrefetchScalarGridSpec(
            num_scalar_prefetch=1,
            grid=(heads,),
            in_specs=window
            + [half_rows] * 2
            + [pl.BlockSpec((1, 8, tile + 256), lambda h, s: (h, 0, 0))],
            out_specs=[
                pl.BlockSpec((head_dim, 3 * tile), lambda h, s: (h, 0)),
                pl.BlockSpec((1, 8, 128), lambda h, s: (h, 0, 0)),
            ],
        ),
        out_shape=[shape((feats, 3 * tile), f32), shape((heads, 8, 128), f32)],
        compiler_params=params,
        name="conv_backward",
    )(spots, values, values, grad_low, grad_high, bases)

    qkv_send, back_keep, back_give = pl.pallas_call(
        partial(backward_kernel, hashes, bits, rows, work, steps, heads, own_rows, parts),
        grid=(2, steps),
        in_specs=[
            smem,
            *[anywhere] * parts,
            resident(*qkv_all.shape),
            resident(*bit_w.shape),
            resident(*bit_wt.shape),
            resident(feats, total),
            resident(feats, total),
            resident(feats, total + 256),
            resident(16, total),
            resident(heads, code_rows, 2 * head_dim),
            stepped(0, blocks, feats, tile),
            resident(feats, 3 * tile),
            resident(*tap_parts.shape),
        ],
        out_specs=[
            resident(chips, CORES * own_rows, 3 * feats + 64),
            stepped(1, blocks, width, tok_rows),
            stepped(1, blocks, width, tok_rows),
        ],
        out_shape=[
            shape((chips, CORES * own_rows, 3 * feats + 64), bf16),
            shape((chips, width, tok_rows), bf16),
            shape((chips, width, tok_rows), bf16),
        ],
        scratch_shapes=[
            pltpu.VMEM((heads, code_rows, 2 * head_dim), f32),
            pltpu.VMEM((heads, code_rows, work), bf16),
            pltpu.VMEM((feats, total), bf16),
            pltpu.VMEM((3 * feats, width), f32),
            pltpu.VMEM((heads, 2 * head_dim, code_rows), bf16),
            pltpu.VMEM((heads, code_rows, 2 * head_dim), bf16),
            pltpu.VMEM((seq_count, tok_rows, width), bf16),
            pltpu.SemaphoreType.DMA((parts,)),
        ],
        compiler_params=hash_params,
        name="hash_backward",
    )(
        spots, *token_parts, qkv_all, bit_w, bit_wt,
        q_unit, k_unit, values, inverses, tables, gnum_got, conv_grad, tap_parts,
    )

    half = width // 2
    group = chips // 2
    per_chip = lambda *dims: pl.BlockSpec((group,) + dims, lambda i: (i, 0, 0))
    keep, give = pl.pallas_call(
        chip_sum_kernel,
        grid=(2,),
        in_specs=[smem, per_chip(width, tok_rows), per_chip(width, tok_rows)],
        out_specs=[per_chip(half, tok_rows), per_chip(half, tok_rows)],
        out_shape=[shape((chips, half, tok_rows), bf16)] * 2,
        compiler_params=params,
        name="chip_sum",
    )(spots, back_keep, core_swap(back_give))
    pair_sum = pl.pallas_call(
        pair_sum_kernel,
        grid=(2,),
        in_specs=[per_chip(half, tok_rows), per_chip(half, tok_rows)],
        out_specs=per_chip(half, tok_rows),
        out_shape=shape((chips, half, tok_rows), bf16),
        compiler_params=params,
        name="pair_sum",
    )(keep, head_swap(give))

    qkv_mine, qkv_give = piped(
        weight_sum_kernel, "weight_sum",
        [shape((own_rows, 3 * feats + 64), f32)] * 2,
        [spots, across(qkv_send), pair_sum],
        [None, None, anywhere],
    )
    qkv_other = core_swap(qkv_give)
    back_got = across(pair_sum)

    extras = gnum_got[:, feats:].astype(f32)
    norm_half = jnp.sum(extras[:, :sum_rows], axis=0)
    count_half = extras[:, sum_rows : sum_rows + heads].reshape(chips, heads, 2, tile // 2)
    count_half = count_half[..., : chip_buckets * rows]
    count_half = count_half.reshape(chips, heads, 2, CORES, chip_buckets // CORES, rows)
    count_half = jnp.transpose(count_half[..., :hashes], (3, 0, 2, 5, 1, 4))
    count_mine = lax.dynamic_index_in_dim(count_half, core, 0, keepdims=False)
    count_give = lax.dynamic_index_in_dim(count_half, 1 - core, 0, keepdims=False)
    tap_first = jnp.where(core == 0, qkv_mine[:heads], qkv_give[:heads])
    tap_half = tap_first[:, 3 * feats : 3 * feats + taps]
    swapped = core_swap(
        jnp.concatenate([norm_half.reshape(-1), count_give.reshape(-1), tap_half.reshape(-1)])
    )
    norm_size, count_size = norm_half.size, count_give.size

    norm_grad = norm_half + swapped[:norm_size].reshape(norm_half.shape)
    norm_grad = jnp.transpose(
        norm_grad.reshape(width // tile, 4, tile), (1, 0, 2)
    ).reshape(4, width)
    count_other = swapped[norm_size : norm_size + count_size].reshape(count_mine.shape)
    occupancy = jnp.transpose(
        in_order(count_mine, count_other, 3), (1, 0, 2, 3, 4)
    ).reshape(2, hash_count, group_heads, buckets // seq_count)
    occupancy = occupancy * (buckets / (tok_rows * seq_count))
    conv_tap_grad = in_order(tap_half, swapped[norm_size + count_size :].reshape(heads, taps), 0)

    matrix = lambda value: [shape(value.shape, f32)] * 3 + [shape(value.shape, bf16)]
    (
        up_new, up_first_new, up_second_new, up_copy,
        down_new, down_first_new, down_second_new, down_copy,
        out_new, out_first_new, out_second_new, out_copy,
    ) = piped(
        big_adam_kernel, "big_adam",
        matrix(up_weight) + matrix(down_weight.T) + matrix(out_weight.T),
        [
            big_owned, up_weight, up_first, up_second,
            down_weight.T, down_first.T, down_second.T,
            out_weight.T, out_first.T, out_second.T,
        ],
    )
    qkv_new, qkv_first_new, qkv_second_new, qkv_copy = piped(
        qkv_adam_kernel, "qkv_adam", matrix(qkv_weight),
        [spots, qkv_mine, qkv_other, qkv_weight, qkv_first, qkv_second],
    )
    norm_new, norm_first_new, norm_second_new = adam_step(
        norm_params, norm_first, norm_second, norm_grad, 0.3
    )
    conv_new, conv_first_new, conv_second_new = adam_step(
        conv_taps, conv_first, conv_second, conv_tap_grad, CONV ** (-0.5)
    )
    (back_low,) = piped(
        back_sum_kernel, "back_sum",
        [shape((half, tok_rows), bf16)],
        [back_got, up_new, down_new, out_new],
        [None] + [anywhere] * 3,
    )
    back_other = head_swap(back_low)
    upper = jnp.where(side == 0, back_low, back_other)
    lower = jnp.where(side == 0, back_other, back_low)
    tokens_grad = grad_mixer + jnp.concatenate([upper, lower], axis=0).T.astype(f32)
    return (
        block_out,
        tokens_grad,
        occupancy,
        qkv_new,
        qkv_first_new,
        qkv_second_new,
        qkv_copy,
        out_new.T,
        out_first_new.T,
        out_second_new.T,
        out_copy.T,
        up_new,
        up_first_new,
        up_second_new,
        up_copy,
        down_new.T,
        down_first_new.T,
        down_second_new.T,
        down_copy.T,
        norm_new,
        norm_first_new,
        norm_second_new,
        conv_new,
        conv_first_new,
        conv_second_new,
    )


def solution(mesh):
    in_specs = (
        P("seq", None),
        P("seq", None),
        P(),
        P(None, None, "head", None),
        P(None, "seq", "head"),
        P(None, "seq", "head"),
        P(None, "seq", "head"),
        P("head", "seq"),
        P("head", "seq"),
        P("head", "seq"),
        P("seq", "head"),
        P("seq", "head"),
        P("seq", "head"),
        P("head", "seq"),
        P("head", "seq"),
        P("head", "seq"),
        P(),
        P(),
        P(),
        P("head", None),
        P("head", None),
        P("head", None),
    )
    out_specs = (
        P("seq", None),
        P("seq", None),
        P(None, None, "head", "seq"),
        P(None, "seq", "head"),
        P(None, "seq", "head"),
        P(None, "seq", "head"),
        P(None, "seq", "head"),
        P("head", "seq"),
        P("head", "seq"),
        P("head", "seq"),
        P("head", "seq"),
        P("seq", "head"),
        P("seq", "head"),
        P("seq", "head"),
        P("seq", "head"),
        P("head", "seq"),
        P("head", "seq"),
        P("head", "seq"),
        P("head", "seq"),
        P(),
        P(),
        P(),
        P("head", None),
        P("head", None),
        P("head", None),
    )
    return jax.shard_map(
        on_device, mesh=mesh, in_specs=in_specs, out_specs=out_specs, check_vma=False
    )
```

```python
from functools import partial
import math

import jax
import jax.numpy as jnp
import numpy as np
from jax import lax
from jax.experimental import pallas as pl
from jax.experimental.pallas import tpu as pltpu
from jax.sharding import PartitionSpec as P

D = 768
FF = 3072
CONV = 33
STEP = 7
CORES = 2

sharpness = 4.0
norm_eps = 1e-06
layer_eps = 1e-05
beta_one = 0.9
beta_two = 0.999
adam_eps = 1e-08
decay_rate = 0.01
highest = lax.Precision.HIGHEST
f32 = jnp.float32
bf16 = jnp.bfloat16
VMEM_LIMIT = 56 * 1024 * 1024
SMALL_LIMIT = 16 * 1024 * 1024
WORK = 2
SPOTS = 4
RING = (0, 2, 4, 6, 7, 5, 3, 1)


def nn(a, b):
    return lax.dot_general(a, b, (((1,), (0,)), ((), ())), preferred_element_type=f32)


def nt(a, b):
    return lax.dot_general(a, b, (((1,), (1,)), ((), ())), preferred_element_type=f32)


def normalize(source):
    centered = source - jnp.mean(source, axis=-1, keepdims=True)
    inverse = lax.rsqrt(jnp.mean(centered * centered, axis=-1, keepdims=True) + layer_eps)
    return (centered * inverse, inverse)


def norm_back(grad, normed, inverse, gain):
    scaled = grad * gain
    inner = (
        scaled
        - jnp.mean(scaled, axis=-1, keepdims=True)
        - normed * jnp.mean(scaled * normed, axis=-1, keepdims=True)
    )
    gains = jnp.sum(grad * normed, axis=0, keepdims=True)
    return (inverse * inner, gains, jnp.sum(grad, axis=0, keepdims=True))


def adam_step(weight, first, second, grad, rate):
    first_new = beta_one * first + (1.0 - beta_one) * grad
    second_new = beta_two * second + (1.0 - beta_two) * grad * grad
    fix_one = 1.0 - beta_one**STEP
    fix_two = 1.0 - beta_two**STEP
    update = first_new / fix_one / (jnp.sqrt(second_new / fix_two) + adam_eps) + decay_rate * weight
    return (weight - rate * update, first_new, second_new)


def head_units(source):
    inverse = lax.rsqrt(jnp.mean(source * source, axis=0, keepdims=True) + norm_eps)
    return source * inverse, inverse


def seg_rows(limit, start, width):
    pos = start + lax.broadcasted_iota(jnp.int32, (1, width), 1)
    late = (pos >= limit).astype(f32)
    return 1.0 - late, late


def masked_pair(rows, early, late):
    return jnp.concatenate([rows * early, rows * late], axis=0).astype(bf16)


def flip(value):
    return jnp.transpose(value.astype(f32)).astype(bf16)


def bit_factors(bit_planes, unit, bits, hashes, rows):
    z = nn(bit_planes, unit)
    decay = jnp.exp(-jnp.abs(z))
    large = 1.0 / (1.0 + decay)
    small = decay * large
    ones = jnp.where(z >= 0.0, large, small)
    zeros = jnp.where(z >= 0.0, small, large)
    ones = [ones[j * rows : (j + 1) * rows] for j in range(bits)]
    zeros = [zeros[j * rows : (j + 1) * rows] for j in range(bits)]
    if rows != hashes:
        live = lax.broadcasted_iota(jnp.int32, ones[0].shape, 0) < hashes
        return ones, [jnp.where(live, ones[0], 0.0)] + ones[1:], [
            jnp.where(live, zeros[0], 0.0)
        ] + zeros[1:]
    return ones, ones, zeros


def products(ones, zeros, first, last):
    found = [zeros[first], ones[first]]
    for j in range(first + 1, last):
        found = [part * zeros[j] for part in found] + [part * ones[j] for part in found]
    return found


def code_parts(bit_planes, unit, bits, hashes, rows):
    plain, ones, zeros = bit_factors(bit_planes, unit, bits, hashes, rows)
    return plain, products(ones, zeros, 0, 3), products(ones, zeros, 3, bits)


def store_codes(codes_ref, head, lows, highs, rows):
    for g, high in enumerate(highs):
        for s in range(0, len(lows), 2):
            spot = (g * len(lows) + s) * rows
            pair = jnp.concatenate([lows[s] * high, lows[s + 1] * high], axis=0)
            codes_ref[head, spot : spot + 2 * rows, :] = pair.astype(bf16)


def token_copies(spots_ref, part_refs, tok_ref, sem_ref):
    return [
        pltpu.make_async_copy(
            ref.at[:, pl.ds(0, tok_ref.shape[1])],
            tok_ref.at[pl.ds(spots_ref[SPOTS + i], ref.shape[0])],
            sem_ref.at[i],
        )
        for i, ref in enumerate(part_refs)
    ]


def forward_kernel(
    hashes, bits, rows, tile, steps, heads, parts, weight_spots, spots_ref, *refs
):
    part_refs, refs = refs[:parts], refs[parts:]
    weight_refs, refs = refs[: len(weight_spots)], refs[len(weight_spots) :]
    bit_ref, num_ref, qu_ref, ku_ref, v_ref, inv_ref, table_ref, count_ref, w_ref = refs[:9]
    acc_ref, codes_ref, wt_ref, table_t_ref, tok_ref, got_ref, sem_ref = refs[9:]
    limit = spots_ref[0]
    phase, i = pl.program_id(0), pl.program_id(1)
    feats = heads * 64
    chips = num_ref.shape[0]
    block = tile // chips
    start = pl.multiple_of(i * tile, tile)
    span = pl.ds(start, tile)
    early, late = seg_rows(limit, start, tile)

    @pl.when((phase == 0) & (i == 0))
    def _():
        copies = token_copies(spots_ref, part_refs, tok_ref, sem_ref)
        loads = [
            pltpu.make_async_copy(
                ref.at[:, pl.ds(weight_spots[i], got_ref.shape[1])],
                got_ref.at[pl.ds(spots_ref[SPOTS + parts + i], ref.shape[0])],
                sem_ref.at[parts + i],
            )
            for i, ref in enumerate(weight_refs)
        ]
        for copy in loads + copies:
            copy.start()
        acc_ref[...] = jnp.zeros_like(acc_ref)
        v_ref[:, 0:128] = jnp.zeros((feats, 128), bf16)
        v_ref[:, 128 + steps * tile :] = jnp.zeros((feats, 128), bf16)
        inv_ref[...] = jnp.zeros_like(inv_ref)
        for copy in loads:
            copy.wait()
        got = got_ref[...].astype(f32)
        if len(weight_refs) > 1:
            quarter = got.shape[1] // 3
            rest = [got[:, quarter * j : quarter * (j + 1), 3 * feats :] for j in range(3)]
            got = jnp.concatenate([got[:, :, : 3 * feats], jnp.concatenate(rest, axis=2)], axis=1)
        got = got.reshape(got.shape[0] * got.shape[1], got.shape[2])[:, : 3 * feats].astype(bf16)
        w_ref[...] = got
        wt_ref[...] = flip(got)
        for copy in copies:
            copy.wait()

    @pl.when(phase == 0)
    def _():
        devices, tok_rows, width = tok_ref.shape
        here = pl.ds(i * (devices // steps), devices // steps)
        proj = nt(wt_ref[...], tok_ref[here].reshape(tile, width))
        values = proj[2 * feats :].astype(bf16)
        v_ref[:, pl.ds(pl.multiple_of(start + 128, 128), tile)] = values
        marks = jnp.concatenate([early, late, jnp.zeros((14, tile), f32)], axis=0).astype(bf16)
        units = []
        for h in range(heads):
            mine = slice(64 * h, 64 * (h + 1))
            q_unit, q_inv = head_units(proj[mine])
            k_unit, k_inv = head_units(proj[feats + 64 * h : feats + 64 * (h + 1)])
            units.append(k_unit.astype(bf16))
            qu_ref[mine, span] = q_unit.astype(bf16)
            ku_ref[mine, span] = units[h]
            inv_ref[h : h + 1, span] = q_inv
            inv_ref[8 + h : 9 + h, span] = k_inv
        for h in range(heads):
            plain, lows, highs = code_parts(bit_ref[h], units[h], bits, hashes, rows)
            store_codes(codes_ref, h, lows, highs, rows)
        for h in range(heads):
            pair = masked_pair(values[64 * h : 64 * (h + 1)].astype(f32), early, late)
            pair = jnp.concatenate([pair, marks], axis=0)
            acc_ref[h] += nt(codes_ref[h], pair)

    @pl.when((phase == 1) & (i == 0))
    def _():
        for h in range(heads):
            table = acc_ref[h, :, 0:128].astype(bf16)
            table_ref[h] = table
            table_t_ref[h] = flip(table)
            counts = jnp.concatenate(
                [acc_ref[h, :, 128:144], jnp.zeros((acc_ref.shape[1], 112), f32)], axis=1
            )
            count_ref[h] = jnp.transpose(counts)[0:8]

    @pl.when(phase == 1)
    def _():
        for h in range(heads):
            unit = qu_ref[64 * h : 64 * (h + 1), span]
            plain, lows, highs = code_parts(bit_ref[h], unit, bits, hashes, rows)
            store_codes(codes_ref, h, lows, highs, rows)
        for h in range(heads):
            mine = slice(64 * h, 64 * (h + 1))
            both = nn(table_t_ref[h], codes_ref[h])
            low = (both[0:64] * early + both[64:128] * late).astype(bf16)
            for c in range(chips):
                num_ref[c, mine, :] = low[:, c * block : (c + 1) * block]


def soften(bit_planes, unit, slopes, codes_ref, head, bits, hashes, rows):
    plain, lows, highs = code_parts(bit_planes, unit, bits, hashes, rows)
    by_low = [None] * len(lows)
    by_bit = [None] * (bits - 3)
    for g, high in enumerate(highs):
        row = None
        for s in range(0, len(lows), 2):
            spot = (g * len(lows) + s) * rows
            parts = [lows[s] * high, lows[s + 1] * high]
            codes_ref[head, spot : spot + 2 * rows, :] = jnp.concatenate(parts, axis=0).astype(bf16)
            for k in range(2):
                term = parts[k] * slopes[spot + k * rows : spot + (k + 1) * rows]
                by_low[s + k] = term if by_low[s + k] is None else by_low[s + k] + term
                row = term if row is None else row + term
        for j in range(bits - 3):
            if (g >> j) & 1:
                by_bit[j] = row if by_bit[j] is None else by_bit[j] + row
    pairs = [sum(part for s, part in enumerate(by_low) if (s >> j) & 1) for j in range(3)]
    whole = sum(by_low)
    slopes = [part - plain[j] * whole for j, part in enumerate(pairs + by_bit)]
    return jnp.concatenate(slopes, axis=0).astype(bf16)


def unit_back(grad, unit, inverse):
    unit = unit.astype(f32)
    inner = jnp.mean(grad * unit, axis=0, keepdims=True)
    return inverse * (grad - unit * inner)


def backward_kernel(
    hashes, bits, rows, tile, steps, heads, own_rows, parts, gnum_parts, spots_ref, *refs
):
    part_refs, refs = refs[:parts], refs[parts:]
    gnum_refs, refs = refs[:gnum_parts], refs[gnum_parts:]
    w_ref, bit_ref, bit_t_ref, qu_ref, ku_ref, v_ref, inv_ref, table_ref = refs[:8]
    conv_ref, tap_ref, grad_ref, keep_ref, give_ref, extra_ref = refs[8:14]
    acc_ref, codes_ref, proj_ref, sum_ref, table_t_ref, table_g_ref = refs[14:20]
    tok_ref, gnum_ref, sem_ref = refs[20:]
    limit = spots_ref[0]
    spot = spots_ref[1]
    core = spots_ref[2]
    phase, i = pl.program_id(0), pl.program_id(1)
    devices, unused, width = tok_ref.shape
    copies = token_copies(spots_ref, part_refs, tok_ref, sem_ref)
    loads = [
        (ref, pl.ds(spots_ref[SPOTS + parts + j], ref.shape[0]))
        for j, ref in enumerate(gnum_refs)
    ]
    feats = heads * 64
    blocks = keep_ref.shape[0]
    block = tile // blocks
    tok_rows = block // CORES
    start = pl.multiple_of(i * tile, tile)
    span = pl.ds(start, tile)
    early, late = seg_rows(limit, start, tile)

    @pl.when((phase == 0) & (i == 0))
    def _():
        for copy in copies:
            copy.start()
        acc_ref[...] = jnp.zeros_like(acc_ref)
        sum_ref[...] = jnp.zeros_like(sum_ref)
        for ref, where in loads:
            gnum_ref[where] = ref[:, :feats]
            extra_ref[where] = ref[:, feats:]

    @pl.when(phase == 0)
    def _():
        spans = [slice(64 * h, 64 * (h + 1)) for h in range(heads)]
        pairs, grads, slopes = [], [], []
        for mine in spans:
            gnum = jnp.concatenate([gnum_ref[i * blocks + c, mine, :] for c in range(blocks)], axis=1)
            pairs.append(masked_pair(gnum.astype(f32), early, late))
        for h, mine in enumerate(spans):
            slopes.append(
                soften(
                    bit_ref[h], qu_ref[mine, span], nn(table_ref[h], pairs[h]), codes_ref, h,
                    bits, hashes, rows,
                )
            )
        for h in range(heads):
            acc_ref[h] += nt(codes_ref[h], pairs[h])
        for h, mine in enumerate(spans):
            grad = nn(bit_t_ref[h], slopes[h])
            grad = unit_back(grad, qu_ref[mine, span], inv_ref[h : h + 1, span])
            proj_ref[mine, span] = grad.astype(bf16)

    @pl.when((phase == 1) & (i == 0))
    def _():
        for copy in copies:
            copy.wait()
        for h in range(heads):
            table_g_ref[h] = acc_ref[h].astype(bf16)
            table_t_ref[h] = flip(table_g_ref[h])

    @pl.when(phase == 1)
    def _():
        conv = []
        for c in range(blocks):
            step = i * blocks + c - spot + 1
            near = ((step >= 0) & (step <= 2)).astype(f32)
            step = jnp.clip(step, 0, 2)
            conv.append(conv_ref[:, pl.ds(pl.multiple_of(step * block, block), block)] * near)
        conv = jnp.concatenate(conv, axis=1)
        spans = [slice(64 * h, 64 * (h + 1)) for h in range(heads)]
        slopes, parts = [], []
        for h, mine in enumerate(spans):
            values = v_ref[mine, pl.ds(pl.multiple_of(start + 128, 128), tile)]
            pair = masked_pair(values.astype(f32), early, late)
            slopes.append(
                soften(
                    bit_ref[h], ku_ref[mine, span], nn(table_g_ref[h], pair), codes_ref, h,
                    bits, hashes, rows,
                )
            )
        for h, mine in enumerate(spans):
            both = nn(table_t_ref[h], codes_ref[h])
            value_grad = both[0:64] * early + both[64:128] * late + conv[mine]
            grad = nn(bit_t_ref[h], slopes[h])
            grad = unit_back(grad, ku_ref[mine, span], inv_ref[8 + h : 9 + h, span])
            parts.append((grad.astype(bf16), value_grad.astype(bf16)))
        full = jnp.concatenate(
            [proj_ref[:, span]] + [part[0] for part in parts] + [part[1] for part in parts], axis=0
        )
        here = pl.ds(i * (devices // steps), devices // steps)
        sum_ref[...] += nn(full, tok_ref[here].reshape(tile, width))
        part = nn(w_ref[...], full)
        for c in range(blocks):
            first = part[:, c * block : c * block + tok_rows]
            second = part[:, c * block + tok_rows : (c + 1) * block]
            keep_ref[c] = jnp.where(core == 0, first, second).astype(bf16)
            give_ref[c] = jnp.where(core == 0, second, first).astype(bf16)

    @pl.when((phase == 1) & (i == steps - 1))
    def _():
        grad = jnp.transpose(sum_ref[...])
        chips = grad_ref.shape[0]
        grad_ref[:, :, 0 : heads * 192] = grad.reshape(
            chips, CORES * own_rows, heads * 192
        ).astype(bf16)
        grad_ref[:, :, heads * 192 :] = jnp.zeros((chips, CORES * own_rows, 64), bf16)
        taps = jnp.concatenate([tap_ref[h, 0:1, 0:64] for h in range(heads)], axis=0)
        for c in range(chips):
            grad_ref[c, 0:heads, heads * 192 :] = taps.astype(bf16)


def window_same(spots_ref, tile):
    start = spots_ref[1] * tile
    width = tile + 256
    edge = lax.broadcasted_iota(jnp.int32, (width, tile), 0) + (start - 128)
    own = lax.broadcasted_iota(jnp.int32, (width, tile), 1) + start
    return (edge >= spots_ref[0]) == (own >= spots_ref[0])


def banded(base, same, tile):
    width = tile + 256
    spread = jnp.broadcast_to(base, (width, width))
    spread = pltpu.roll(spread, 0, 1, stride=1, stride_axis=0)[:, :tile]
    matrix = jnp.where(same, spread, 0.0)
    upper = matrix.astype(bf16)
    return upper, (matrix - upper.astype(f32)).astype(bf16)


def conv_kernel(tile, heads, spots_ref, values_ref, base_ref, out_ref, window_ref):
    same = window_same(spots_ref, tile)
    first = pl.multiple_of(spots_ref[1] * tile, tile)
    window = values_ref[:, pl.ds(first, tile + 256)]
    window_ref[...] = window
    for h in range(heads):
        mine = slice(64 * h, 64 * (h + 1))
        upper, lower = banded(base_ref[h, 0:1], same, tile)
        out_ref[mine] = nn(window[mine], upper) + nn(window[mine], lower)


def conv_back_kernel(
    tile, taps, heads, spots_ref, window_ref, low_ref, high_ref, base_ref, out_ref, tap_ref
):
    same = window_same(spots_ref, tile)
    width = tile + 256
    rim = taps // 2
    out_ref[...] = jnp.zeros_like(out_ref)
    pos = lax.broadcasted_iota(jnp.int32, (128, tile), 1) + spots_ref[1] * tile
    other = pos + lax.broadcasted_iota(jnp.int32, (128, tile), 0) - rim
    near = (pos >= spots_ref[0]) == (other >= spots_ref[0])
    for h in range(heads):
        mine = slice(64 * h, 64 * (h + 1))
        upper, lower = banded(base_ref[h, 0:1], same, tile)
        own = jnp.concatenate([low_ref[mine], high_ref[mine]], axis=1)
        out_ref[mine, 128 : 128 + width] = nt(own, upper) + nt(own, lower)
        values = window_ref[mine].astype(f32)
        own = own.astype(f32)
        sums = []
        for o in range(taps):
            moved = pltpu.roll(values, width - (128 - rim) - o, 1)[:, :tile]
            sums.append(jnp.sum(moved * own, axis=0, keepdims=True))
        sums = jnp.concatenate(sums + [jnp.zeros((128 - taps, tile), f32)], axis=0)
        total = jnp.sum(jnp.where(near, sums, 0.0), axis=1, keepdims=True)
        tap_ref[h] = jnp.transpose(jnp.broadcast_to(total, (128, 128)))[0:8]


def context_kernel(heads, spots_ref, got_ref, conv_ref, keep_ref, give_ref, num_ref):
    total = jnp.sum(got_ref[...].astype(f32), axis=0)
    num_ref[...] = total
    tile = total.shape[1]
    parts = [head_units(total[64 * h : 64 * (h + 1)])[0] for h in range(heads)]
    context = (jnp.concatenate(parts, axis=0) + conv_ref[...]).astype(bf16)
    first, second = context[:, : tile // CORES], context[:, tile // CORES :]

    @pl.when(spots_ref[2] == 0)
    def _():
        keep_ref[...] = first
        give_ref[...] = second

    @pl.when(spots_ref[2] != 0)
    def _():
        keep_ref[...] = second
        give_ref[...] = first


def mixer_kernel(spots_ref, keep_ref, other_ref, w_ref, context_ref, part_ref):
    keep, other = keep_ref[...].astype(f32), other_ref[...].astype(f32)
    zero = spots_ref[2] == 0
    pair = jnp.concatenate([jnp.where(zero, keep, other), jnp.where(zero, other, keep)], axis=0)
    context = jnp.transpose(pair).astype(bf16)
    context_ref[...] = context
    part_ref[...] = nt(context, w_ref[...]).astype(bf16)


def hidden_kernel(
    tok_ref, own_ref, other_ref, norm_ref, w_ref, hat_ref, inv_ref, hidden_ref, active_ref, part_ref
):
    ff = hidden_ref.shape[1]
    mixed = own_ref[...].astype(f32) + other_ref[...].astype(f32)
    hat, inverse = normalize(tok_ref[...].astype(f32) + mixed)
    hat_ref[...] = hat
    inv_ref[...] = inverse
    low = (hat * norm_ref[0:1] + norm_ref[1:2]).astype(bf16)
    hidden = nn(low, w_ref[:, :ff])
    hidden_ref[...] = hidden
    active = (0.5 * hidden * (1.0 + lax.erf(hidden * math.sqrt(0.5)))).astype(bf16)
    active_ref[...] = active
    part_ref[...] = nt(active, w_ref[:, ff : 2 * ff]).astype(bf16)


def feed_kernel(
    hat_ref, hidden_ref, own_ref, other_ref, cot_ref, norm_ref, w_ref,
    out_ref, second_ref, feed_ref, slope_ref, part_ref, sums_ref,
):
    ff = hidden_ref.shape[1]
    first_out = hat_ref[...] * norm_ref[0:1] + norm_ref[1:2]
    fed = own_ref[...].astype(f32) + other_ref[...].astype(f32)
    hat, inverse = normalize(first_out + fed)
    out_ref[...] = hat * norm_ref[2:3] + norm_ref[3:4]
    grad, gains, offsets = norm_back(cot_ref[...].astype(f32), hat, inverse, norm_ref[2:3])
    second_ref[...] = grad
    sums_ref[0:1] = gains
    sums_ref[1:2] = offsets
    low = grad.astype(bf16)
    feed_ref[...] = low
    active_grad = nn(low, w_ref[:, ff : 2 * ff])
    hidden = hidden_ref[...]
    cdf = 0.5 * (1.0 + lax.erf(hidden * math.sqrt(0.5)))
    density = jnp.exp(-0.5 * hidden * hidden) * (1.0 / math.sqrt(2.0 * math.pi))
    slope = (active_grad * (cdf + hidden * density)).astype(bf16)
    slope_ref[...] = slope
    part_ref[...] = nt(slope, w_ref[:, :ff]).astype(bf16)


def mixer_back_kernel(
    spots_ref, second_ref, own_ref, other_ref, hat_ref, inv_ref, norm_ref, w_ref, sums_ref,
    grad_ref, low_ref, keep_ref, give_ref, all_sums_ref,
):
    first = second_ref[...] + (own_ref[...].astype(f32) + other_ref[...].astype(f32))
    grad, gains, offsets = norm_back(first, hat_ref[...], inv_ref[...], norm_ref[0:1])
    grad_ref[...] = grad
    all_sums_ref[0:1] = gains
    all_sums_ref[1:2] = offsets
    all_sums_ref[2:4] = sums_ref[...]
    low = grad.astype(bf16)
    low_ref[...] = low
    half = keep_ref.shape[0]
    context = jnp.transpose(nn(low, w_ref[:, w_ref.shape[1] - CORES * half :]))
    half = context.shape[0] // CORES
    zero = spots_ref[2] == 0
    keep_ref[...] = jnp.where(zero, context[:half], context[half:])
    give_ref[...] = jnp.where(zero, context[half:], context[:half])


def attention_back_kernel(
    heads, spots_ref, keep_ref, other_ref, num_ref, sums_ref, count_ref,
    send_ref, low_ref, high_ref,
):
    zero = spots_ref[2] == 0
    keep, other = keep_ref[...], other_ref[...]
    grad = jnp.concatenate([jnp.where(zero, keep, other), jnp.where(zero, other, keep)], axis=1)
    half = keep.shape[1]
    low = grad.astype(bf16)
    low_ref[...] = low[:, :half]
    high_ref[...] = low[:, half:]
    parts = []
    for h in range(heads):
        span = slice(64 * h, 64 * (h + 1))
        attention, inverse = head_units(num_ref[span])
        inner = jnp.mean(grad[span] * attention, axis=0, keepdims=True)
        parts.append(inverse * (grad[span] - attention * inner))
    gnum = jnp.concatenate(parts, axis=0).astype(bf16)
    tile = gnum.shape[1]
    feats = 64 * heads
    pieces = sums_ref.shape[1] // tile
    counts = []
    for h in range(heads):
        for d in range(2):
            row = count_ref[h, d : d + 1, :]
            counts += [row[:, tile * i : tile * (i + 1)] for i in range(row.shape[1] // tile)]
    used = feats + 4 * pieces + len(counts)
    spare = jnp.zeros((send_ref.shape[0] - used, tile), f32)
    sums = sums_ref[...].astype(bf16).astype(f32)
    sums = [sums[:, tile * i : tile * (i + 1)] for i in range(pieces)]
    send_ref[0:feats, :] = gnum
    send_ref[feats:, :] = jnp.concatenate(sums + counts + [spare], axis=0).astype(bf16)


def feed_grad_kernel(hat_ref, norm_ref, slope_ref, feed_ref, active_ref, out_ref):
    ff = slope_ref.shape[1]
    low = hat_ref[...] * norm_ref[0:1] + norm_ref[1:2]
    out_ref[:, :ff] = nn(flip(low.astype(bf16)), slope_ref[...]).astype(bf16)
    out_ref[:, ff : 2 * ff] = nn(flip(feed_ref[...]), active_ref[...]).astype(bf16)


def out_grad_kernel(mixer_ref, context_ref, all_ref, out_ref):
    out_ref[...] = nn(flip(mixer_ref[...]), context_ref[...]).astype(bf16)


def pack_kernel(spots_ref, up_ref, down_ref, out_ref, after_ref, bit_ref, all_ref):
    ff = up_ref.shape[1]
    all_ref[:, :ff] = up_ref[...].astype(bf16)
    all_ref[:, ff : 2 * ff] = down_ref[...].astype(bf16)
    all_ref[:, 2 * ff :] = out_ref[...].astype(bf16)


def chip_sum_kernel(spots_ref, own_ref, other_ref, keep_ref, give_ref):
    total = own_ref[...].astype(f32) + other_ref[...].astype(f32)
    half = total.shape[1] // 2
    first, second = total[:, :half], total[:, half:]
    zero = spots_ref[3] == 0
    keep_ref[...] = jnp.where(zero, first, second).astype(bf16)
    give_ref[...] = jnp.where(zero, second, first).astype(bf16)


def pair_sum_kernel(own_ref, other_ref, out_ref, flag_ref):
    flag_ref[...] = jnp.zeros_like(flag_ref)
    out_ref[...] = (own_ref[...].astype(f32) + other_ref[...].astype(f32)).astype(bf16)


def weight_sum_kernel(spots_ref, got_ref, after_ref, keep_ref, give_ref):
    total = jnp.sum(got_ref[...].astype(f32), axis=0)
    half = total.shape[0] // CORES
    zero = spots_ref[2] == 0
    keep_ref[...] = jnp.where(zero, total[:half], total[half:])
    give_ref[...] = jnp.where(zero, total[half:], total[:half])


def adam_refs(grad, ins, outs, rate):
    new, first, second = adam_step(ins[0], ins[1], ins[2], grad, rate)
    outs[0][...] = new
    outs[1][...] = first
    outs[2][...] = second
    outs[3][...] = new.astype(bf16)


def big_adam_kernel(grad_ref, *refs):
    ins, outs, flag_ref = refs[:9], refs[9:-1], refs[-1]
    flag_ref[...] = jnp.zeros_like(flag_ref)
    ff = ins[0].shape[1]
    spans = (slice(0, ff), slice(ff, 2 * ff), slice(2 * ff, grad_ref.shape[1]))
    for k, (span, rate) in enumerate(zip(spans, (D ** (-0.5), FF ** (-0.5), D ** (-0.5)))):
        state = [ref[...] for ref in ins[3 * k : 3 * k + 3]]
        adam_refs(grad_ref[:, span].astype(f32), state, outs[4 * k : 4 * k + 4], rate)


def qkv_adam_kernel(spots_ref, mine_ref, other_ref, *refs):
    zero = spots_ref[2] == 0
    feats = refs[0].shape[2] // CORES
    for p in range(3):
        span = slice(p * feats, (p + 1) * feats)
        mine, other = mine_ref[:, span], other_ref[:, span]
        grad = jnp.concatenate([jnp.where(zero, mine, other), jnp.where(zero, other, mine)], axis=1)
        adam_refs(grad, [ref[p] for ref in refs[:3]], [ref.at[p] for ref in refs[3:]], D ** (-0.5))


def final_kernel(spots_ref, mine_ref, other_ref, mixer_ref, out_ref):
    mine, other = mine_ref[...].astype(f32), other_ref[...].astype(f32)
    zero = spots_ref[3] == 0
    total = jnp.concatenate([jnp.where(zero, mine, other), jnp.where(zero, other, mine)], axis=0)
    out_ref[...] = mixer_ref[...] + jnp.transpose(total)


def back_sum_kernel(got_ref, *refs):
    refs[-1][...] = jnp.sum(got_ref[...].astype(f32), axis=0).astype(bf16)


def on_device(
    tokens,
    cotangent,
    doc_lengths,
    plane_bits,
    qkv_weight,
    qkv_first,
    qkv_second,
    out_weight,
    out_first,
    out_second,
    up_weight,
    up_first,
    up_second,
    down_weight,
    down_first,
    down_second,
    norm_params,
    norm_first,
    norm_second,
    conv_taps,
    conv_first,
    conv_second,
):
    tok_rows, width = tokens.shape
    hash_count, bits, group_heads, head_dim = plane_bits.shape
    buckets = 2**bits
    taps = conv_taps.shape[1]
    rim = taps // 2
    seq_count = lax.axis_size("seq")
    chips = seq_count // CORES
    place = lax.axis_index("seq")
    side = lax.axis_index("head")
    spot, core = place // CORES, place % CORES
    heads = group_heads // CORES
    feats = heads * head_dim
    group_feats = group_heads * head_dim
    hashes = hash_count // chips
    rows = -(-hashes // 8) * 8
    tile = CORES * tok_rows
    total = chips * tile
    own_rows = width // seq_count
    ff = up_weight.shape[1]
    code_rows = rows * buckets
    blocks = WORK if chips % WORK == 0 else 1
    steps = chips // blocks
    work = blocks * tile
    planes_of = [[CORES * c + k for c in range(chips)] for k in range(CORES)]
    across = partial(
        lax.all_to_all, axis_name="seq", split_axis=0, concat_axis=0, tiled=True,
        axis_index_groups=planes_of,
    )
    core_swap = partial(
        lax.ppermute, axis_name="seq", perm=[(i, i ^ 1) for i in range(seq_count)]
    )
    head_swap = partial(lax.ppermute, axis_name="head", perm=[(0, 1), (1, 0)])
    def in_order(mine, other, axis):
        first = jnp.where(core == 0, mine, other)
        return jnp.concatenate([first, jnp.where(core == 0, other, mine)], axis=axis)

    low_qkv = qkv_weight.astype(bf16).reshape(3, own_rows, CORES, feats)
    pick = partial(lax.dynamic_index_in_dim, low_qkv, axis=2, keepdims=False)
    by_rows = lambda part: jnp.transpose(part, (1, 0, 2)).reshape(own_rows, 3 * feats)
    qkv_mine, qkv_give = by_rows(pick(core)), by_rows(pick(1 - core))
    chip_rows = in_order(qkv_mine, core_swap(qkv_give), 0)

    def ring(value, steps, hold):
        moved, found, turns = [value, value], [value], [0]
        for step in range(1, steps + 1):
            moved = [lax.ppermute(v, "seq", p) for v, p in zip(moved, (ahead, behind))]
            if hold:
                moved = list(lax.optimization_barrier(tuple(moved)))
            found += moved
            turns += [chips - step, step]
        return moved, found, turns

    ringed = chips == len(RING)
    if ringed:
        order = np.array(RING)
        seats = np.argsort(order)
        ahead = [
            (CORES * order[i] + k, CORES * order[(i + 1) % chips] + k)
            for i in range(chips)
            for k in range(CORES)
        ]
        behind = [(b, a) for a, b in ahead]
        quarter = CORES * own_rows // 4
        third = feats
        rest = chip_rows[3 * quarter :]
        rest = jnp.concatenate([rest[:, third * j : third * (j + 1)] for j in range(3)], axis=0)
        packed = jnp.concatenate([chip_rows[: 3 * quarter], rest], axis=1)
        block = jnp.concatenate([tokens, packed], axis=0)
        moved, block_parts, turns = ring(block, chips // 2 - 1, True)
        last_part = block_parts[2][0:8, 0:128]
        far_tokens, far_rows = lax.optimization_barrier(
            (moved[0][:tok_rows], moved[1][tok_rows:])
        )
        across_tokens = lax.ppermute(far_tokens, "seq", ahead)
        across_rows = lax.ppermute(far_rows, "seq", behind)
        across_tokens, across_rows = lax.optimization_barrier((across_tokens, across_rows))
        turns.append(chips // 2)
        token_parts = block_parts + [across_tokens]
        token_parts = [p[None] for p in token_parts + [core_swap(part) for part in token_parts]]
        weight_parts = [p[None] for p in block_parts + [across_rows]]
        weight_spots = [tok_rows] * (chips - 1) + [0]
        spot_of = np.array([[order[(seats[c] + t) % chips] for t in turns] for c in range(chips)])
        spot_of = np.repeat(spot_of, CORES, axis=0)
        core_of = np.arange(seq_count)[:, None] % CORES
        place_of = [CORES * spot_of + core_of, CORES * spot_of + 1 - core_of, spot_of]
    else:
        token_parts = [lax.all_gather(tokens, "seq", axis=0, tiled=False)]
        chip_rows = jnp.pad(chip_rows, ((0, 0), (0, width - 3 * feats)))
        weight_parts = [
            lax.all_gather(chip_rows, "seq", axis=0, tiled=False, axis_index_groups=planes_of)
        ]
        weight_spots = [0]
        place_of = [np.zeros((seq_count, 2))]
        last_part = token_parts[0]
    parts = len(token_parts)
    weight_count = len(weight_parts)
    device = np.arange(seq_count)[:, None]
    facts = np.concatenate([device // CORES, device % CORES, 0 * device] + place_of, axis=1)
    facts = np.stack([facts + k * (np.arange(facts.shape[1]) == 2) for k in range(2)])
    facts = lax.dynamic_slice(
        jnp.asarray(facts.astype(np.int32)), (side, place, 0), (1, 1, facts.shape[2])
    )
    spots = jnp.concatenate([doc_lengths[0:1], facts.reshape(-1)])

    smem = pl.BlockSpec(memory_space=pltpu.SMEM)
    anywhere = pl.BlockSpec(memory_space=pl.ANY)
    params = pltpu.CompilerParams(
        dimension_semantics=("arbitrary",), vmem_limit_bytes=VMEM_LIMIT
    )
    shape = jax.ShapeDtypeStruct

    def full(value):
        return pl.BlockSpec(value.shape, lambda i: (0,) * len(value.shape))

    def piped(kernel, name, outs, args, specs=None):
        if specs is None:
            specs = [None] * len(args)
        specs = [
            (smem if arg is spots else full(arg)) if spec is None else spec
            for spec, arg in zip(specs, args)
        ]
        return pl.pallas_call(
            kernel,
            grid=(1,),
            in_specs=specs,
            out_specs=[full(o) for o in outs],
            out_shape=outs,
            compiler_params=params,
            name=name,
        )(*args)

    inside = pl.BlockSpec(memory_space=pltpu.VMEM)
    in_vmem = lambda value: pltpu.with_memory_space_constraint(value, pltpu.VMEM)
    small = pltpu.CompilerParams(
        dimension_semantics=("arbitrary",), vmem_limit_bytes=SMALL_LIMIT
    )

    def once(kernel, name, outs, args, after=(), outside=(), blocks={}, limit=SMALL_LIMIT):
        specs, values = [], []
        for i, arg in enumerate(args):
            plain = arg is spots or i in blocks
            specs.append(smem if arg is spots else blocks.get(i, inside))
            values.append(arg if plain else in_vmem(arg))
        for arg in after:
            specs.append(anywhere)
            values.append(arg)
        return pl.pallas_call(
            kernel,
            grid=(1,) if blocks else (),
            in_specs=specs,
            out_specs=[inside] * len(outs),
            out_shape=[
                (pltpu.HBM if i in outside else pltpu.VMEM)(o.shape, o.dtype)
                for i, o in enumerate(outs)
            ],
            compiler_params=pltpu.CompilerParams(vmem_limit_bytes=limit),
            name=name,
        )(*values)

    own_planes = lax.dynamic_slice(
        plane_bits, (spot * hashes, 0, core * heads, 0), (hashes, bits, heads, head_dim)
    )
    scale = sharpness / math.sqrt(head_dim)
    signs = scale * (2 * own_planes - 1).astype(f32)
    bit_w = jnp.pad(
        jnp.transpose(signs, (2, 1, 0, 3)), ((0, 0), (0, 0), (0, rows - hashes), (0, 0))
    )
    bit_w = bit_w.reshape(heads, bits * rows, head_dim).astype(bf16)
    bit_wt = jnp.transpose(bit_w, (0, 2, 1))

    (second_send,) = piped(
        pack_kernel, "pack",
        [shape((own_rows, 2 * ff + group_feats), bf16)],
        [spots, up_weight, down_weight.T, out_weight.T, last_part, bit_w],
        [None] * 4 + [anywhere] * 2,
    )
    ff_all = lax.all_gather(second_send, "seq", axis=0, tiled=True)

    def resident(*dims):
        return pl.BlockSpec(dims, lambda p, i: (0,) * len(dims), pipeline_mode=pl.Buffered(1))

    def stepped(phase, *dims):
        def place(p, i):
            rest = steps - 1 if phase == 0 else 0
            return (jnp.where(p == phase, i, rest),) + (0,) * (len(dims) - 1)

        return pl.BlockSpec(dims, place)

    hash_params = pltpu.CompilerParams(
        dimension_semantics=("arbitrary", "arbitrary"), vmem_limit_bytes=VMEM_LIMIT
    )
    num_parts, q_unit, k_unit, values, inverses, tables, counts, qkv_all = pl.pallas_call(
        partial(forward_kernel, hashes, bits, rows, work, steps, heads, parts, weight_spots),
        grid=(2, steps),
        in_specs=[
            smem,
            *[anywhere] * (parts + weight_count),
            resident(*bit_w.shape),
        ],
        out_specs=[
            stepped(1, blocks, feats, tile),
            resident(feats, total),
            resident(feats, total),
            resident(feats, total + 256),
            resident(16, total),
            resident(heads, code_rows, 2 * head_dim),
            resident(heads, 8, code_rows),
            resident(width, 3 * feats),
        ],
        out_shape=[
            shape((chips, feats, tile), bf16),
            shape((feats, total), bf16),
            shape((feats, total), bf16),
            shape((feats, total + 256), bf16),
            shape((16, total), f32),
            shape((heads, code_rows, 2 * head_dim), bf16),
            shape((heads, 8, code_rows), f32),
            shape((width, 3 * feats), bf16),
        ],
        scratch_shapes=[
            pltpu.VMEM((heads, code_rows, 2 * head_dim + 16), f32),
            pltpu.VMEM((heads, code_rows, work), bf16),
            pltpu.VMEM((3 * feats, width), bf16),
            pltpu.VMEM((heads, 2 * head_dim, code_rows), bf16),
            pltpu.VMEM((seq_count, tok_rows, width), bf16),
            pltpu.VMEM((chips, weight_parts[-1].shape[1], width), bf16),
            pltpu.SemaphoreType.DMA((parts + weight_count,)),
        ],
        compiler_params=hash_params,
        name="hash_forward",
    )(spots, *token_parts, *weight_parts, bit_w)
    num_got = across(num_parts)

    own_taps = lax.dynamic_slice(conv_taps, (core * heads, 0), (heads, taps))
    lead = tile + 128 - rim
    bases = jnp.zeros((heads, 8, tile + 256), f32)
    bases = bases.at[:, 0, lead : lead + taps].set(own_taps[:, ::-1])
    conv, window_values = once(
        partial(conv_kernel, tile, heads), "conv_forward",
        [shape((feats, tile), f32), shape((feats, tile + 256), bf16)],
        [spots, values, bases],
    )

    chip_buckets = buckets // chips
    sum_rows = 4 * width // tile
    count_rows = 2 * heads * code_rows // tile
    extra_rows = -(-(sum_rows + count_rows) // 16) * 16

    keep, give, numerator = once(
        partial(context_kernel, heads), "context",
        [shape((feats, tok_rows), bf16), shape((feats, tok_rows), bf16), shape((feats, tile), f32)],
        [spots, num_got, conv],
    )
    context, mixer_part = once(
        mixer_kernel, "mixer",
        [shape((tok_rows, group_feats), bf16), shape((tok_rows, width), bf16)],
        [spots, keep, core_swap(give), ff_all],
        blocks={3: pl.BlockSpec((width, group_feats), lambda i: (0, 2 * ff // group_feats))},
    )
    ff_all, mixer_part = lax.optimization_barrier((ff_all, mixer_part))
    first_hat, first_inverse, hidden, active, feed_part = once(
        hidden_kernel, "feed_forward",
        [
            shape((tok_rows, width), f32),
            shape((tok_rows, 1), f32),
            shape((tok_rows, ff), f32),
            shape((tok_rows, ff), bf16),
            shape((tok_rows, width), bf16),
        ],
        [tokens, mixer_part, head_swap(mixer_part), norm_params, ff_all],
    )
    block_out, grad_second, feed_low, slope_low, first_part, second_sums = once(
        feed_kernel, "feed_back",
        [
            shape((tok_rows, width), f32),
            shape((tok_rows, width), f32),
            shape((tok_rows, width), bf16),
            shape((tok_rows, ff), bf16),
            shape((tok_rows, width), bf16),
            shape((2, width), f32),
        ],
        [first_hat, hidden, feed_part, head_swap(feed_part), cotangent, norm_params, ff_all],
        outside=(0,),
    )
    grad_mixer, mixer_low, keep, give, norm_sums = once(
        mixer_back_kernel, "mixer_back",
        [
            shape((tok_rows, width), f32),
            shape((tok_rows, width), bf16),
            shape((feats, tok_rows), f32),
            shape((feats, tok_rows), f32),
            shape((4, width), f32),
        ],
        [
            spots, grad_second, first_part, head_swap(first_part), first_hat, first_inverse,
            norm_params, ff_all, second_sums,
        ],
    )
    gnum_send, grad_low, grad_high = once(
        partial(attention_back_kernel, heads), "attention_back",
        [
            shape((feats + extra_rows, tile), bf16),
            shape((feats, tok_rows), bf16),
            shape((feats, tok_rows), bf16),
        ],
        [spots, keep, core_swap(give), numerator, norm_sums, counts],
    )
    conv_grad, tap_parts = once(
        partial(conv_back_kernel, tile, taps, heads), "conv_backward",
        [shape((feats, 3 * tile), f32), shape((heads, 8, 128), f32)],
        [spots, window_values, grad_low, grad_high, bases],
    )
    if ringed:
        moved, gnum_parts, unused = ring(gnum_send, 1, False)
        *moved, tap_parts = lax.optimization_barrier((*moved, tap_parts))
        gnum_parts = [gnum_send]
        for step in range(2, chips // 2 + 1):
            gnum_parts += moved
            moved = [
                lax.ppermute(v, "seq", p)
                for v, p in zip(moved, (ahead, behind))
                if p is ahead or 2 * step < chips
            ]
        gnum_parts = [p[None] for p in gnum_parts + moved]
    else:
        gnum_parts = [
            lax.all_gather(gnum_send, "seq", axis=0, tiled=False, axis_index_groups=planes_of)
        ]
    gnum_count = len(gnum_parts)

    columns = 2 * ff + group_feats
    feed_grads = pl.pallas_call(
        feed_grad_kernel,
        grid=(1,),
        in_specs=[inside] * 5,
        out_specs=pl.BlockSpec((width, 2 * ff), lambda i: (0, 0)),
        out_shape=pltpu.HBM((width, columns), bf16),
        compiler_params=small,
        name="feed_grads",
    )(*[in_vmem(v) for v in (first_hat, norm_params, slope_low, feed_low, active)])
    big_grad = pl.pallas_call(
        out_grad_kernel,
        grid=(1,),
        in_specs=[inside, inside, anywhere],
        out_specs=pl.BlockSpec((width, group_feats), lambda i: (0, 2 * ff // group_feats)),
        out_shape=pltpu.HBM((width, columns), bf16),
        input_output_aliases={2: 0},
        compiler_params=small,
        name="out_grads",
    )(in_vmem(mixer_low), in_vmem(context), feed_grads)
    big_owned = lax.psum_scatter(big_grad, "seq", scatter_dimension=0, tiled=True)

    qkv_send, back_keep, back_give, extras = pl.pallas_call(
        partial(backward_kernel, hashes, bits, rows, work, steps, heads, own_rows, parts, gnum_count),
        grid=(2, steps),
        in_specs=[
            smem,
            *[anywhere] * parts,
            *[inside] * gnum_count,
            resident(*qkv_all.shape),
            resident(*bit_w.shape),
            resident(*bit_wt.shape),
            resident(feats, total),
            resident(feats, total),
            resident(feats, total + 256),
            resident(16, total),
            resident(heads, code_rows, 2 * head_dim),
            resident(feats, 3 * tile),
            resident(*tap_parts.shape),
        ],
        out_specs=[
            resident(chips, CORES * own_rows, 3 * feats + 64),
            stepped(1, blocks, width, tok_rows),
            stepped(1, blocks, width, tok_rows),
            resident(chips, extra_rows, tile),
        ],
        out_shape=[
            shape((chips, CORES * own_rows, 3 * feats + 64), bf16),
            shape((chips, width, tok_rows), bf16),
            shape((chips, width, tok_rows), bf16),
            shape((chips, extra_rows, tile), bf16),
        ],
        scratch_shapes=[
            pltpu.VMEM((heads, code_rows, 2 * head_dim), f32),
            pltpu.VMEM((heads, code_rows, work), bf16),
            pltpu.VMEM((feats, total), bf16),
            pltpu.VMEM((3 * feats, width), f32),
            pltpu.VMEM((heads, 2 * head_dim, code_rows), bf16),
            pltpu.VMEM((heads, code_rows, 2 * head_dim), bf16),
            pltpu.VMEM((seq_count, tok_rows, width), bf16),
            pltpu.VMEM((chips, feats, tile), bf16),
            pltpu.SemaphoreType.DMA((parts,)),
        ],
        compiler_params=hash_params,
        name="hash_backward",
    )(
        spots, *token_parts, *[in_vmem(p) for p in gnum_parts], qkv_all, bit_w, bit_wt,
        q_unit, k_unit, values, inverses, tables, conv_grad, tap_parts,
    )

    half = width // 2
    group = chips // 2
    per_chip = lambda *dims: pl.BlockSpec((group,) + dims, lambda i: (i, 0, 0))
    keep, give = pl.pallas_call(
        chip_sum_kernel,
        grid=(2,),
        in_specs=[smem, per_chip(width, tok_rows), per_chip(width, tok_rows)],
        out_specs=[per_chip(half, tok_rows), per_chip(half, tok_rows)],
        out_shape=[shape((chips, half, tok_rows), bf16)] * 2,
        compiler_params=params,
        name="chip_sum",
    )(spots, back_keep, core_swap(back_give))
    pair_sum, pair_done = pl.pallas_call(
        pair_sum_kernel,
        grid=(2,),
        in_specs=[per_chip(half, tok_rows), per_chip(half, tok_rows)],
        out_specs=[per_chip(half, tok_rows), pl.BlockSpec((8, 128), lambda i: (0, 0))],
        out_shape=[shape((chips, half, tok_rows), bf16), shape((8, 128), f32)],
        compiler_params=params,
        name="pair_sum",
    )(keep, head_swap(give))

    qkv_mine, qkv_give = once(
        weight_sum_kernel, "weight_sum",
        [shape((own_rows, 3 * feats + 64), f32)] * 2,
        [spots, across(qkv_send)],
        after=[pair_done],
    )
    qkv_other = core_swap(qkv_give)
    back_got = across(pair_sum)

    extras = extras.astype(f32)
    norm_half = jnp.sum(extras[:, :sum_rows], axis=0)
    count_half = extras[:, sum_rows : sum_rows + count_rows]
    count_half = count_half.reshape(chips, heads, 2, chips, CORES, chip_buckets // CORES, rows)
    count_half = lax.dynamic_index_in_dim(count_half, spot, 3, keepdims=False)
    count_half = jnp.transpose(count_half[..., :hashes], (3, 0, 2, 5, 1, 4))
    count_mine = lax.dynamic_index_in_dim(count_half, core, 0, keepdims=False)
    count_give = lax.dynamic_index_in_dim(count_half, 1 - core, 0, keepdims=False)
    tap_first = jnp.where(core == 0, qkv_mine[:heads], qkv_give[:heads])
    tap_half = tap_first[:, 3 * feats : 3 * feats + taps]
    swapped = core_swap(
        jnp.concatenate([norm_half.reshape(-1), count_give.reshape(-1), tap_half.reshape(-1)])
    )
    norm_size, count_size = norm_half.size, count_give.size

    norm_grad = norm_half + swapped[:norm_size].reshape(norm_half.shape)
    norm_grad = jnp.transpose(
        norm_grad.reshape(width // tile, 4, tile), (1, 0, 2)
    ).reshape(4, width)
    count_other = swapped[norm_size : norm_size + count_size].reshape(count_mine.shape)
    occupancy = jnp.transpose(
        in_order(count_mine, count_other, 3), (1, 0, 2, 3, 4)
    ).reshape(2, hash_count, group_heads, buckets // seq_count)
    occupancy = occupancy * (buckets / (tok_rows * seq_count))
    conv_tap_grad = in_order(tap_half, swapped[norm_size + count_size :].reshape(heads, taps), 0)

    flag = shape((8, 128), f32)
    matrix = lambda value: [pltpu.HBM(value.shape, f32)] * 3 + [pltpu.HBM(value.shape, bf16)]
    (
        up_new, up_first_new, up_second_new, up_copy,
        down_new, down_first_new, down_second_new, down_copy,
        out_new, out_first_new, out_second_new, out_copy, big_done,
    ) = piped(
        big_adam_kernel, "big_adam",
        matrix(up_weight) + matrix(down_weight.T) + matrix(out_weight.T) + [flag],
        [
            big_owned, up_weight, up_first, up_second,
            down_weight.T, down_first.T, down_second.T,
            out_weight.T, out_first.T, out_second.T,
        ],
    )
    qkv_new, qkv_first_new, qkv_second_new, qkv_copy = piped(
        qkv_adam_kernel, "qkv_adam", matrix(qkv_weight),
        [spots, qkv_mine, qkv_other, qkv_weight, qkv_first, qkv_second],
    )
    norm_new, norm_first_new, norm_second_new = adam_step(
        norm_params, norm_first, norm_second, norm_grad, 0.3
    )
    conv_new, conv_first_new, conv_second_new = adam_step(
        conv_taps, conv_first, conv_second, conv_tap_grad, CONV ** (-0.5)
    )
    (back_low,) = once(
        back_sum_kernel, "back_sum",
        [shape((half, tok_rows), bf16)],
        [back_got],
        after=[big_done],
    )
    (tokens_grad,) = once(
        final_kernel, "tokens_grad",
        [shape((tok_rows, width), f32)],
        [spots, back_low, head_swap(back_low), grad_mixer],
        outside=(0,),
    )
    return (
        block_out,
        tokens_grad,
        occupancy,
        qkv_new,
        qkv_first_new,
        qkv_second_new,
        qkv_copy,
        out_new.T,
        out_first_new.T,
        out_second_new.T,
        out_copy.T,
        up_new,
        up_first_new,
        up_second_new,
        up_copy,
        down_new.T,
        down_first_new.T,
        down_second_new.T,
        down_copy.T,
        norm_new,
        norm_first_new,
        norm_second_new,
        conv_new,
        conv_first_new,
        conv_second_new,
    )


def solution(mesh):
    in_specs = (
        P("seq", None),
        P("seq", None),
        P(),
        P(None, None, "head", None),
        P(None, "seq", "head"),
        P(None, "seq", "head"),
        P(None, "seq", "head"),
        P("head", "seq"),
        P("head", "seq"),
        P("head", "seq"),
        P("seq", "head"),
        P("seq", "head"),
        P("seq", "head"),
        P("head", "seq"),
        P("head", "seq"),
        P("head", "seq"),
        P(),
        P(),
        P(),
        P("head", None),
        P("head", None),
        P("head", None),
    )
    out_specs = (
        P("seq", None),
        P("seq", None),
        P(None, None, "head", "seq"),
        P(None, "seq", "head"),
        P(None, "seq", "head"),
        P(None, "seq", "head"),
        P(None, "seq", "head"),
        P("head", "seq"),
        P("head", "seq"),
        P("head", "seq"),
        P("head", "seq"),
        P("seq", "head"),
        P("seq", "head"),
        P("seq", "head"),
        P("seq", "head"),
        P("head", "seq"),
        P("head", "seq"),
        P("head", "seq"),
        P("head", "seq"),
        P(),
        P(),
        P(),
        P("head", None),
        P("head", None),
        P("head", None),
    )
    return jax.shard_map(
        on_device, mesh=mesh, in_specs=in_specs, out_specs=out_specs, check_vma=False
    )
```

```python
from functools import partial
import math

import jax
import jax.numpy as jnp
import numpy as np
from jax import lax
from jax.experimental import pallas as pl
from jax.experimental.pallas import tpu as pltpu
from jax.sharding import PartitionSpec as P

D = 768
FF = 3072
CONV = 33
STEP = 7
CORES = 2

sharpness = 4.0
norm_eps = 1e-06
layer_eps = 1e-05
beta_one = 0.9
beta_two = 0.999
adam_eps = 1e-08
decay_rate = 0.01
highest = lax.Precision.HIGHEST
f32 = jnp.float32
bf16 = jnp.bfloat16
VMEM_LIMIT = 56 * 1024 * 1024
SMALL_LIMIT = 16 * 1024 * 1024
WORK = 2
SPOTS = 4
RING = (0, 2, 4, 6, 7, 5, 3, 1)


def nn(a, b):
    return lax.dot_general(a, b, (((1,), (0,)), ((), ())), preferred_element_type=f32)


def nt(a, b):
    return lax.dot_general(a, b, (((1,), (1,)), ((), ())), preferred_element_type=f32)


def normalize(source):
    centered = source - jnp.mean(source, axis=-1, keepdims=True)
    inverse = lax.rsqrt(jnp.mean(centered * centered, axis=-1, keepdims=True) + layer_eps)
    return (centered * inverse, inverse)


def norm_back(grad, normed, inverse, gain):
    scaled = grad * gain
    inner = (
        scaled
        - jnp.mean(scaled, axis=-1, keepdims=True)
        - normed * jnp.mean(scaled * normed, axis=-1, keepdims=True)
    )
    gains = jnp.sum(grad * normed, axis=0, keepdims=True)
    return (inverse * inner, gains, jnp.sum(grad, axis=0, keepdims=True))


def adam_step(weight, first, second, grad, rate):
    first_new = beta_one * first + (1.0 - beta_one) * grad
    second_new = beta_two * second + (1.0 - beta_two) * grad * grad
    fix_one = 1.0 - beta_one**STEP
    fix_two = 1.0 - beta_two**STEP
    update = first_new / fix_one / (jnp.sqrt(second_new / fix_two) + adam_eps) + decay_rate * weight
    return (weight - rate * update, first_new, second_new)


def head_units(source):
    inverse = lax.rsqrt(jnp.mean(source * source, axis=0, keepdims=True) + norm_eps)
    return source * inverse, inverse


def seg_rows(limit, start, width):
    pos = start + lax.broadcasted_iota(jnp.int32, (1, width), 1)
    late = (pos >= limit).astype(f32)
    return 1.0 - late, late


def masked_pair(rows, early, late):
    return jnp.concatenate([rows * early, rows * late], axis=0).astype(bf16)


def flip(value):
    return jnp.transpose(value.astype(f32)).astype(bf16)


def bit_factors(bit_planes, unit, bits, hashes, rows):
    z = nn(bit_planes, unit)
    decay = jnp.exp(-jnp.abs(z))
    large = 1.0 / (1.0 + decay)
    small = decay * large
    ones = jnp.where(z >= 0.0, large, small)
    zeros = jnp.where(z >= 0.0, small, large)
    ones = [ones[j * rows : (j + 1) * rows] for j in range(bits)]
    zeros = [zeros[j * rows : (j + 1) * rows] for j in range(bits)]
    if rows != hashes:
        live = lax.broadcasted_iota(jnp.int32, ones[0].shape, 0) < hashes
        return ones, [jnp.where(live, ones[0], 0.0)] + ones[1:], [
            jnp.where(live, zeros[0], 0.0)
        ] + zeros[1:]
    return ones, ones, zeros


def products(ones, zeros, first, last):
    found = [zeros[first], ones[first]]
    for j in range(first + 1, last):
        found = [part * zeros[j] for part in found] + [part * ones[j] for part in found]
    return found


def code_parts(bit_planes, unit, bits, hashes, rows):
    plain, ones, zeros = bit_factors(bit_planes, unit, bits, hashes, rows)
    return plain, products(ones, zeros, 0, 3), products(ones, zeros, 3, bits)


def store_codes(codes_ref, head, lows, highs, rows):
    for g, high in enumerate(highs):
        for s in range(0, len(lows), 2):
            spot = (g * len(lows) + s) * rows
            pair = jnp.concatenate([lows[s] * high, lows[s + 1] * high], axis=0)
            codes_ref[head, spot : spot + 2 * rows, :] = pair.astype(bf16)


def token_copies(spots_ref, part_refs, tok_ref, sem_ref):
    return [
        pltpu.make_async_copy(
            ref.at[:, pl.ds(0, tok_ref.shape[1])],
            tok_ref.at[pl.ds(spots_ref[SPOTS + i], ref.shape[0])],
            sem_ref.at[i],
        )
        for i, ref in enumerate(part_refs)
    ]


def forward_kernel(
    hashes, bits, rows, tile, steps, heads, parts, weight_spots, spots_ref, *refs
):
    part_refs, refs = refs[:parts], refs[parts:]
    weight_refs, refs = refs[: len(weight_spots)], refs[len(weight_spots) :]
    bit_ref, num_ref, qu_ref, ku_ref, v_ref, inv_ref, table_ref, count_ref, w_ref = refs[:9]
    acc_ref, codes_ref, wt_ref, table_t_ref, tok_ref, got_ref, sem_ref = refs[9:]
    limit = spots_ref[0]
    phase, i = pl.program_id(0), pl.program_id(1)
    feats = heads * 64
    chips = num_ref.shape[0]
    block = tile // chips
    start = pl.multiple_of(i * tile, tile)
    span = pl.ds(start, tile)
    early, late = seg_rows(limit, start, tile)

    @pl.when((phase == 0) & (i == 0))
    def _():
        copies = token_copies(spots_ref, part_refs, tok_ref, sem_ref)
        loads = [
            pltpu.make_async_copy(
                ref.at[:, pl.ds(weight_spots[i], got_ref.shape[1])],
                got_ref.at[pl.ds(spots_ref[SPOTS + parts + i], ref.shape[0])],
                sem_ref.at[parts + i],
            )
            for i, ref in enumerate(weight_refs)
        ]
        for copy in loads + copies:
            copy.start()
        acc_ref[...] = jnp.zeros_like(acc_ref)
        v_ref[:, 0:128] = jnp.zeros((feats, 128), bf16)
        v_ref[:, 128 + steps * tile :] = jnp.zeros((feats, 128), bf16)
        inv_ref[...] = jnp.zeros_like(inv_ref)
        for copy in loads:
            copy.wait()
        got = got_ref[...].astype(f32)
        if len(weight_refs) > 1:
            quarter = got.shape[1] // 3
            rest = [got[:, quarter * j : quarter * (j + 1), 3 * feats :] for j in range(3)]
            got = jnp.concatenate([got[:, :, : 3 * feats], jnp.concatenate(rest, axis=2)], axis=1)
        got = got.reshape(got.shape[0] * got.shape[1], got.shape[2])[:, : 3 * feats].astype(bf16)
        w_ref[...] = got
        wt_ref[...] = flip(got)
        for copy in copies:
            copy.wait()

    @pl.when(phase == 0)
    def _():
        devices, tok_rows, width = tok_ref.shape
        here = pl.ds(i * (devices // steps), devices // steps)
        proj = nt(wt_ref[...], tok_ref[here].reshape(tile, width))
        values = proj[2 * feats :].astype(bf16)
        v_ref[:, pl.ds(pl.multiple_of(start + 128, 128), tile)] = values
        marks = jnp.concatenate([early, late, jnp.zeros((14, tile), f32)], axis=0).astype(bf16)
        units = []
        for h in range(heads):
            mine = slice(64 * h, 64 * (h + 1))
            q_unit, q_inv = head_units(proj[mine])
            k_unit, k_inv = head_units(proj[feats + 64 * h : feats + 64 * (h + 1)])
            units.append(k_unit.astype(bf16))
            qu_ref[mine, span] = q_unit.astype(bf16)
            ku_ref[mine, span] = units[h]
            inv_ref[h : h + 1, span] = q_inv
            inv_ref[8 + h : 9 + h, span] = k_inv
        for h in range(heads):
            plain, lows, highs = code_parts(bit_ref[h], units[h], bits, hashes, rows)
            store_codes(codes_ref, h, lows, highs, rows)
        for h in range(heads):
            pair = masked_pair(values[64 * h : 64 * (h + 1)].astype(f32), early, late)
            pair = jnp.concatenate([pair, marks], axis=0)
            acc_ref[h] += nt(codes_ref[h], pair)

    @pl.when((phase == 1) & (i == 0))
    def _():
        for h in range(heads):
            table = acc_ref[h, :, 0:128].astype(bf16)
            table_ref[h] = table
            table_t_ref[h] = flip(table)
            counts = jnp.concatenate(
                [acc_ref[h, :, 128:144], jnp.zeros((acc_ref.shape[1], 112), f32)], axis=1
            )
            count_ref[h] = jnp.transpose(counts)[0:8]

    @pl.when(phase == 1)
    def _():
        for h in range(heads):
            unit = qu_ref[64 * h : 64 * (h + 1), span]
            plain, lows, highs = code_parts(bit_ref[h], unit, bits, hashes, rows)
            store_codes(codes_ref, h, lows, highs, rows)
        for h in range(heads):
            mine = slice(64 * h, 64 * (h + 1))
            both = nn(table_t_ref[h], codes_ref[h])
            low = (both[0:64] * early + both[64:128] * late).astype(bf16)
            for c in range(chips):
                num_ref[c, mine, :] = low[:, c * block : (c + 1) * block]


def soften(bit_planes, unit, slopes, codes_ref, head, bits, hashes, rows):
    plain, lows, highs = code_parts(bit_planes, unit, bits, hashes, rows)
    by_low = [None] * len(lows)
    by_bit = [None] * (bits - 3)
    for g, high in enumerate(highs):
        row = None
        for s in range(0, len(lows), 2):
            spot = (g * len(lows) + s) * rows
            parts = [lows[s] * high, lows[s + 1] * high]
            codes_ref[head, spot : spot + 2 * rows, :] = jnp.concatenate(parts, axis=0).astype(bf16)
            for k in range(2):
                term = parts[k] * slopes[spot + k * rows : spot + (k + 1) * rows]
                by_low[s + k] = term if by_low[s + k] is None else by_low[s + k] + term
                row = term if row is None else row + term
        for j in range(bits - 3):
            if (g >> j) & 1:
                by_bit[j] = row if by_bit[j] is None else by_bit[j] + row
    pairs = [sum(part for s, part in enumerate(by_low) if (s >> j) & 1) for j in range(3)]
    whole = sum(by_low)
    slopes = [part - plain[j] * whole for j, part in enumerate(pairs + by_bit)]
    return jnp.concatenate(slopes, axis=0).astype(bf16)


def unit_back(grad, unit, inverse):
    unit = unit.astype(f32)
    inner = jnp.mean(grad * unit, axis=0, keepdims=True)
    return inverse * (grad - unit * inner)


def backward_kernel(
    hashes, bits, rows, tile, steps, heads, own_rows, parts, gnum_parts, spots_ref, *refs
):
    part_refs, refs = refs[:parts], refs[parts:]
    gnum_refs, refs = refs[:gnum_parts], refs[gnum_parts:]
    w_ref, bit_ref, bit_t_ref, qu_ref, ku_ref, v_ref, inv_ref, table_ref = refs[:8]
    conv_ref, tap_ref, grad_ref, keep_ref, give_ref, extra_ref = refs[8:14]
    acc_ref, codes_ref, proj_ref, sum_ref, table_t_ref, table_g_ref = refs[14:20]
    tok_ref, gnum_ref, sem_ref = refs[20:]
    limit = spots_ref[0]
    spot = spots_ref[1]
    core = spots_ref[2]
    phase, i = pl.program_id(0), pl.program_id(1)
    devices, unused, width = tok_ref.shape
    copies = token_copies(spots_ref, part_refs, tok_ref, sem_ref)
    loads = [
        (ref, pl.ds(spots_ref[SPOTS + parts + j], ref.shape[0]))
        for j, ref in enumerate(gnum_refs)
    ]
    feats = heads * 64
    blocks = keep_ref.shape[0]
    block = tile // blocks
    tok_rows = block // CORES
    start = pl.multiple_of(i * tile, tile)
    span = pl.ds(start, tile)
    early, late = seg_rows(limit, start, tile)

    @pl.when((phase == 0) & (i == 0))
    def _():
        for copy in copies:
            copy.start()
        acc_ref[...] = jnp.zeros_like(acc_ref)
        sum_ref[...] = jnp.zeros_like(sum_ref)
        for ref, where in loads:
            gnum_ref[where] = ref[:, :feats]
            extra_ref[where] = ref[:, feats:]

    @pl.when(phase == 0)
    def _():
        spans = [slice(64 * h, 64 * (h + 1)) for h in range(heads)]
        pairs, grads, slopes = [], [], []
        for mine in spans:
            gnum = jnp.concatenate([gnum_ref[i * blocks + c, mine, :] for c in range(blocks)], axis=1)
            pairs.append(masked_pair(gnum.astype(f32), early, late))
        for h, mine in enumerate(spans):
            slopes.append(
                soften(
                    bit_ref[h], qu_ref[mine, span], nn(table_ref[h], pairs[h]), codes_ref, h,
                    bits, hashes, rows,
                )
            )
        for h in range(heads):
            acc_ref[h] += nt(codes_ref[h], pairs[h])
        for h, mine in enumerate(spans):
            grad = nn(bit_t_ref[h], slopes[h])
            grad = unit_back(grad, qu_ref[mine, span], inv_ref[h : h + 1, span])
            proj_ref[mine, span] = grad.astype(bf16)

    @pl.when((phase == 1) & (i == 0))
    def _():
        for copy in copies:
            copy.wait()
        for h in range(heads):
            table_g_ref[h] = acc_ref[h].astype(bf16)
            table_t_ref[h] = flip(table_g_ref[h])

    @pl.when(phase == 1)
    def _():
        conv = []
        for c in range(blocks):
            step = i * blocks + c - spot + 1
            near = ((step >= 0) & (step <= 2)).astype(f32)
            step = jnp.clip(step, 0, 2)
            conv.append(conv_ref[:, pl.ds(pl.multiple_of(step * block, block), block)] * near)
        conv = jnp.concatenate(conv, axis=1)
        spans = [slice(64 * h, 64 * (h + 1)) for h in range(heads)]
        slopes, parts = [], []
        for h, mine in enumerate(spans):
            values = v_ref[mine, pl.ds(pl.multiple_of(start + 128, 128), tile)]
            pair = masked_pair(values.astype(f32), early, late)
            slopes.append(
                soften(
                    bit_ref[h], ku_ref[mine, span], nn(table_g_ref[h], pair), codes_ref, h,
                    bits, hashes, rows,
                )
            )
        for h, mine in enumerate(spans):
            both = nn(table_t_ref[h], codes_ref[h])
            value_grad = both[0:64] * early + both[64:128] * late + conv[mine]
            grad = nn(bit_t_ref[h], slopes[h])
            grad = unit_back(grad, ku_ref[mine, span], inv_ref[8 + h : 9 + h, span])
            parts.append((grad.astype(bf16), value_grad.astype(bf16)))
        full = jnp.concatenate(
            [proj_ref[:, span]] + [part[0] for part in parts] + [part[1] for part in parts], axis=0
        )
        here = pl.ds(i * (devices // steps), devices // steps)
        sum_ref[...] += nn(full, tok_ref[here].reshape(tile, width))
        part = nn(w_ref[...], full)
        for c in range(blocks):
            first = part[:, c * block : c * block + tok_rows]
            second = part[:, c * block + tok_rows : (c + 1) * block]
            keep_ref[c] = jnp.where(core == 0, first, second).astype(bf16)
            give_ref[c] = jnp.where(core == 0, second, first).astype(bf16)

    @pl.when((phase == 1) & (i == steps - 1))
    def _():
        grad = jnp.transpose(sum_ref[...])
        chips = grad_ref.shape[0]
        grad_ref[:, :, 0 : heads * 192] = grad.reshape(
            chips, CORES * own_rows, heads * 192
        ).astype(bf16)
        grad_ref[:, :, heads * 192 :] = jnp.zeros((chips, CORES * own_rows, 64), bf16)
        taps = jnp.concatenate([tap_ref[h, 0:1, 0:64] for h in range(heads)], axis=0)
        for c in range(chips):
            grad_ref[c, 0:heads, heads * 192 :] = taps.astype(bf16)


def window_same(spots_ref, tile):
    start = spots_ref[1] * tile
    width = tile + 256
    edge = lax.broadcasted_iota(jnp.int32, (width, tile), 0) + (start - 128)
    own = lax.broadcasted_iota(jnp.int32, (width, tile), 1) + start
    return (edge >= spots_ref[0]) == (own >= spots_ref[0])


def banded(base, same, tile):
    width = tile + 256
    spread = jnp.broadcast_to(base, (width, width))
    spread = pltpu.roll(spread, 0, 1, stride=1, stride_axis=0)[:, :tile]
    matrix = jnp.where(same, spread, 0.0)
    upper = matrix.astype(bf16)
    return upper, (matrix - upper.astype(f32)).astype(bf16)


def conv_kernel(tile, heads, spots_ref, values_ref, base_ref, out_ref, window_ref):
    same = window_same(spots_ref, tile)
    first = pl.multiple_of(spots_ref[1] * tile, tile)
    window = values_ref[:, pl.ds(first, tile + 256)]
    window_ref[...] = window
    for h in range(heads):
        mine = slice(64 * h, 64 * (h + 1))
        upper, lower = banded(base_ref[h, 0:1], same, tile)
        out_ref[mine] = nn(window[mine], upper) + nn(window[mine], lower)


def conv_back_kernel(
    tile, taps, heads, spots_ref, window_ref, low_ref, high_ref, base_ref, out_ref, tap_ref
):
    same = window_same(spots_ref, tile)
    width = tile + 256
    rim = taps // 2
    out_ref[...] = jnp.zeros_like(out_ref)
    pos = lax.broadcasted_iota(jnp.int32, (128, tile), 1) + spots_ref[1] * tile
    other = pos + lax.broadcasted_iota(jnp.int32, (128, tile), 0) - rim
    near = (pos >= spots_ref[0]) == (other >= spots_ref[0])
    for h in range(heads):
        mine = slice(64 * h, 64 * (h + 1))
        upper, lower = banded(base_ref[h, 0:1], same, tile)
        own = jnp.concatenate([low_ref[mine], high_ref[mine]], axis=1)
        out_ref[mine, 128 : 128 + width] = nt(own, upper) + nt(own, lower)
        values = window_ref[mine].astype(f32)
        own = own.astype(f32)
        sums = []
        for o in range(taps):
            moved = pltpu.roll(values, width - (128 - rim) - o, 1)[:, :tile]
            sums.append(jnp.sum(moved * own, axis=0, keepdims=True))
        sums = jnp.concatenate(sums + [jnp.zeros((128 - taps, tile), f32)], axis=0)
        total = jnp.sum(jnp.where(near, sums, 0.0), axis=1, keepdims=True)
        tap_ref[h] = jnp.transpose(jnp.broadcast_to(total, (128, 128)))[0:8]


def context_kernel(heads, spots_ref, got_ref, conv_ref, keep_ref, give_ref, num_ref):
    total = jnp.sum(got_ref[...].astype(f32), axis=0)
    num_ref[...] = total
    tile = total.shape[1]
    parts = [head_units(total[64 * h : 64 * (h + 1)])[0] for h in range(heads)]
    context = (jnp.concatenate(parts, axis=0) + conv_ref[...]).astype(bf16)
    first, second = context[:, : tile // CORES], context[:, tile // CORES :]

    @pl.when(spots_ref[2] == 0)
    def _():
        keep_ref[...] = first
        give_ref[...] = second

    @pl.when(spots_ref[2] != 0)
    def _():
        keep_ref[...] = second
        give_ref[...] = first


def mixer_kernel(spots_ref, keep_ref, other_ref, w_ref, context_ref, part_ref):
    keep, other = keep_ref[...].astype(f32), other_ref[...].astype(f32)
    zero = spots_ref[2] == 0
    pair = jnp.concatenate([jnp.where(zero, keep, other), jnp.where(zero, other, keep)], axis=0)
    context = jnp.transpose(pair).astype(bf16)
    context_ref[...] = context
    part_ref[...] = nt(context, w_ref[...]).astype(bf16)


def hidden_kernel(
    tok_ref, own_ref, other_ref, norm_ref, w_ref, hat_ref, inv_ref, hidden_ref, active_ref, part_ref
):
    ff = hidden_ref.shape[1]
    mixed = own_ref[...].astype(f32) + other_ref[...].astype(f32)
    hat, inverse = normalize(tok_ref[...].astype(f32) + mixed)
    hat_ref[...] = hat
    inv_ref[...] = inverse
    low = (hat * norm_ref[0:1] + norm_ref[1:2]).astype(bf16)
    hidden = nn(low, w_ref[:, :ff])
    hidden_ref[...] = hidden
    active = (0.5 * hidden * (1.0 + lax.erf(hidden * math.sqrt(0.5)))).astype(bf16)
    active_ref[...] = active
    part_ref[...] = nt(active, w_ref[:, ff : 2 * ff]).astype(bf16)


def feed_kernel(
    hat_ref, hidden_ref, own_ref, other_ref, cot_ref, norm_ref, w_ref,
    out_ref, second_ref, feed_ref, slope_ref, part_ref, sums_ref,
):
    ff = hidden_ref.shape[1]
    first_out = hat_ref[...] * norm_ref[0:1] + norm_ref[1:2]
    fed = own_ref[...].astype(f32) + other_ref[...].astype(f32)
    hat, inverse = normalize(first_out + fed)
    out_ref[...] = hat * norm_ref[2:3] + norm_ref[3:4]
    grad, gains, offsets = norm_back(cot_ref[...].astype(f32), hat, inverse, norm_ref[2:3])
    second_ref[...] = grad
    sums_ref[0:1] = gains
    sums_ref[1:2] = offsets
    low = grad.astype(bf16)
    feed_ref[...] = low
    active_grad = nn(low, w_ref[:, ff : 2 * ff])
    hidden = hidden_ref[...]
    cdf = 0.5 * (1.0 + lax.erf(hidden * math.sqrt(0.5)))
    density = jnp.exp(-0.5 * hidden * hidden) * (1.0 / math.sqrt(2.0 * math.pi))
    slope = (active_grad * (cdf + hidden * density)).astype(bf16)
    slope_ref[...] = slope
    part_ref[...] = nt(slope, w_ref[:, :ff]).astype(bf16)


def mixer_back_kernel(
    spots_ref, second_ref, own_ref, other_ref, hat_ref, inv_ref, norm_ref, w_ref, sums_ref,
    grad_ref, low_ref, keep_ref, give_ref, all_sums_ref,
):
    first = second_ref[...] + (own_ref[...].astype(f32) + other_ref[...].astype(f32))
    grad, gains, offsets = norm_back(first, hat_ref[...], inv_ref[...], norm_ref[0:1])
    grad_ref[...] = grad
    all_sums_ref[0:1] = gains
    all_sums_ref[1:2] = offsets
    all_sums_ref[2:4] = sums_ref[...]
    low = grad.astype(bf16)
    low_ref[...] = low
    half = keep_ref.shape[0]
    context = jnp.transpose(nn(low, w_ref[:, w_ref.shape[1] - CORES * half :]))
    half = context.shape[0] // CORES
    zero = spots_ref[2] == 0
    keep_ref[...] = jnp.where(zero, context[:half], context[half:])
    give_ref[...] = jnp.where(zero, context[half:], context[:half])


def attention_back_kernel(
    heads, spots_ref, keep_ref, other_ref, num_ref, sums_ref, count_ref,
    send_ref, low_ref, high_ref,
):
    zero = spots_ref[2] == 0
    keep, other = keep_ref[...], other_ref[...]
    grad = jnp.concatenate([jnp.where(zero, keep, other), jnp.where(zero, other, keep)], axis=1)
    half = keep.shape[1]
    low = grad.astype(bf16)
    low_ref[...] = low[:, :half]
    high_ref[...] = low[:, half:]
    parts = []
    for h in range(heads):
        span = slice(64 * h, 64 * (h + 1))
        attention, inverse = head_units(num_ref[span])
        inner = jnp.mean(grad[span] * attention, axis=0, keepdims=True)
        parts.append(inverse * (grad[span] - attention * inner))
    gnum = jnp.concatenate(parts, axis=0).astype(bf16)
    tile = gnum.shape[1]
    feats = 64 * heads
    pieces = sums_ref.shape[1] // tile
    counts = []
    for h in range(heads):
        for d in range(2):
            row = count_ref[h, d : d + 1, :]
            counts += [row[:, tile * i : tile * (i + 1)] for i in range(row.shape[1] // tile)]
    used = feats + 4 * pieces + len(counts)
    spare = jnp.zeros((send_ref.shape[0] - used, tile), f32)
    sums = sums_ref[...].astype(bf16).astype(f32)
    sums = [sums[:, tile * i : tile * (i + 1)] for i in range(pieces)]
    send_ref[0:feats, :] = gnum
    send_ref[feats:, :] = jnp.concatenate(sums + counts + [spare], axis=0).astype(bf16)


def feed_grad_kernel(hat_ref, norm_ref, slope_ref, feed_ref, active_ref, out_ref):
    ff = slope_ref.shape[1]
    low = hat_ref[...] * norm_ref[0:1] + norm_ref[1:2]
    out_ref[:, :ff] = nn(flip(low.astype(bf16)), slope_ref[...]).astype(bf16)
    out_ref[:, ff : 2 * ff] = nn(flip(feed_ref[...]), active_ref[...]).astype(bf16)


def out_grad_kernel(mixer_ref, context_ref, all_ref, out_ref):
    out_ref[...] = nn(flip(mixer_ref[...]), context_ref[...]).astype(bf16)


def pack_kernel(spots_ref, up_ref, down_ref, out_ref, after_ref, bit_ref, all_ref):
    ff = up_ref.shape[1]
    all_ref[:, :ff] = up_ref[...].astype(bf16)
    all_ref[:, ff : 2 * ff] = down_ref[...].astype(bf16)
    all_ref[:, 2 * ff :] = out_ref[...].astype(bf16)


def chip_sum_kernel(spots_ref, own_ref, other_ref, keep_ref, give_ref):
    total = own_ref[...].astype(f32) + other_ref[...].astype(f32)
    half = total.shape[1] // 2
    first, second = total[:, :half], total[:, half:]
    zero = spots_ref[3] == 0
    keep_ref[...] = jnp.where(zero, first, second).astype(bf16)
    give_ref[...] = jnp.where(zero, second, first).astype(bf16)


def pair_sum_kernel(spots_ref, own_ref, other_ref, *refs):
    out_refs, flag_ref = refs[:-1], refs[-1]
    flag_ref[...] = jnp.zeros_like(flag_ref)
    for d, out_ref in enumerate(out_refs):
        if len(out_refs) == 1:
            total = own_ref[...].astype(f32) + other_ref[...].astype(f32)
        else:
            chip = spots_ref[1] ^ d
            total = own_ref[chip].astype(f32) + other_ref[chip].astype(f32)
        out_ref[...] = total.astype(bf16)


def weight_sum_kernel(spots_ref, got_ref, after_ref, keep_ref, give_ref):
    total = jnp.sum(got_ref[...].astype(f32), axis=0)
    half = total.shape[0] // CORES
    zero = spots_ref[2] == 0
    keep_ref[...] = jnp.where(zero, total[:half], total[half:])
    give_ref[...] = jnp.where(zero, total[half:], total[:half])


def adam_refs(grad, ins, outs, rate):
    new, first, second = adam_step(ins[0], ins[1], ins[2], grad, rate)
    outs[0][...] = new
    outs[1][...] = first
    outs[2][...] = second
    outs[3][...] = new.astype(bf16)


def big_adam_kernel(grad_ref, *refs):
    ins, outs, flag_ref = refs[:9], refs[9:-1], refs[-1]
    flag_ref[...] = jnp.zeros_like(flag_ref)
    ff = ins[0].shape[1]
    spans = (slice(0, ff), slice(ff, 2 * ff), slice(2 * ff, grad_ref.shape[1]))
    for k, (span, rate) in enumerate(zip(spans, (D ** (-0.5), FF ** (-0.5), D ** (-0.5)))):
        state = [ref[...] for ref in ins[3 * k : 3 * k + 3]]
        adam_refs(grad_ref[:, span].astype(f32), state, outs[4 * k : 4 * k + 4], rate)


def qkv_adam_kernel(spots_ref, mine_ref, other_ref, *refs):
    zero = spots_ref[2] == 0
    feats = refs[0].shape[2] // CORES
    for p in range(3):
        span = slice(p * feats, (p + 1) * feats)
        mine, other = mine_ref[:, span], other_ref[:, span]
        grad = jnp.concatenate([jnp.where(zero, mine, other), jnp.where(zero, other, mine)], axis=1)
        adam_refs(grad, [ref[p] for ref in refs[:3]], [ref.at[p] for ref in refs[3:]], D ** (-0.5))


def final_kernel(spots_ref, mine_ref, other_ref, mixer_ref, out_ref):
    mine, other = mine_ref[...].astype(f32), other_ref[...].astype(f32)
    zero = spots_ref[3] == 0
    total = jnp.concatenate([jnp.where(zero, mine, other), jnp.where(zero, other, mine)], axis=0)
    out_ref[...] = mixer_ref[...] + jnp.transpose(total)


def back_sum_kernel(*refs):
    total = jnp.sum(refs[0][...].astype(f32), axis=0)
    for ref in refs[1:-2]:
        total = total + jnp.sum(ref[...].astype(f32), axis=0)
    refs[-1][...] = total.astype(bf16)


def on_device(
    tokens,
    cotangent,
    doc_lengths,
    plane_bits,
    qkv_weight,
    qkv_first,
    qkv_second,
    out_weight,
    out_first,
    out_second,
    up_weight,
    up_first,
    up_second,
    down_weight,
    down_first,
    down_second,
    norm_params,
    norm_first,
    norm_second,
    conv_taps,
    conv_first,
    conv_second,
):
    tok_rows, width = tokens.shape
    hash_count, bits, group_heads, head_dim = plane_bits.shape
    buckets = 2**bits
    taps = conv_taps.shape[1]
    rim = taps // 2
    seq_count = lax.axis_size("seq")
    chips = seq_count // CORES
    place = lax.axis_index("seq")
    side = lax.axis_index("head")
    spot, core = place // CORES, place % CORES
    heads = group_heads // CORES
    feats = heads * head_dim
    group_feats = group_heads * head_dim
    hashes = hash_count // chips
    rows = -(-hashes // 8) * 8
    tile = CORES * tok_rows
    total = chips * tile
    own_rows = width // seq_count
    ff = up_weight.shape[1]
    code_rows = rows * buckets
    blocks = WORK if chips % WORK == 0 else 1
    steps = chips // blocks
    work = blocks * tile
    planes_of = [[CORES * c + k for c in range(chips)] for k in range(CORES)]
    across = partial(
        lax.all_to_all, axis_name="seq", split_axis=0, concat_axis=0, tiled=True,
        axis_index_groups=planes_of,
    )
    core_swap = partial(
        lax.ppermute, axis_name="seq", perm=[(i, i ^ 1) for i in range(seq_count)]
    )
    head_swap = partial(lax.ppermute, axis_name="head", perm=[(0, 1), (1, 0)])
    def in_order(mine, other, axis):
        first = jnp.where(core == 0, mine, other)
        return jnp.concatenate([first, jnp.where(core == 0, other, mine)], axis=axis)

    low_qkv = qkv_weight.astype(bf16).reshape(3, own_rows, CORES, feats)
    pick = partial(lax.dynamic_index_in_dim, low_qkv, axis=2, keepdims=False)
    by_rows = lambda part: jnp.transpose(part, (1, 0, 2)).reshape(own_rows, 3 * feats)
    qkv_mine, qkv_give = by_rows(pick(core)), by_rows(pick(1 - core))
    chip_rows = in_order(qkv_mine, core_swap(qkv_give), 0)

    def ring(value, steps, hold):
        moved, found, turns = [value, value], [value], [0]
        for step in range(1, steps + 1):
            moved = [lax.ppermute(v, "seq", p) for v, p in zip(moved, (ahead, behind))]
            if hold:
                moved = list(lax.optimization_barrier(tuple(moved)))
            found += moved
            turns += [chips - step, step]
        return moved, found, turns

    ringed = chips == len(RING)
    if ringed:
        order = np.array(RING)
        seats = np.argsort(order)
        ahead = [
            (CORES * order[i] + k, CORES * order[(i + 1) % chips] + k)
            for i in range(chips)
            for k in range(CORES)
        ]
        behind = [(b, a) for a, b in ahead]
        quarter = CORES * own_rows // 4
        third = feats
        rest = chip_rows[3 * quarter :]
        rest = jnp.concatenate([rest[:, third * j : third * (j + 1)] for j in range(3)], axis=0)
        packed = jnp.concatenate([chip_rows[: 3 * quarter], rest], axis=1)
        block = jnp.concatenate([tokens, packed], axis=0)
        moved, block_parts, turns = ring(block, chips // 2 - 1, True)
        last_part = block_parts[2][0:8, 0:128]
        far_tokens, far_rows = lax.optimization_barrier(
            (moved[0][:tok_rows], moved[1][tok_rows:])
        )
        across_tokens = lax.ppermute(far_tokens, "seq", ahead)
        across_rows = lax.ppermute(far_rows, "seq", behind)
        across_tokens, across_rows = lax.optimization_barrier((across_tokens, across_rows))
        turns.append(chips // 2)
        token_parts = block_parts + [across_tokens]
        token_parts = [p[None] for p in token_parts + [core_swap(part) for part in token_parts]]
        weight_parts = [p[None] for p in block_parts + [across_rows]]
        weight_spots = [tok_rows] * (chips - 1) + [0]
        spot_of = np.array([[order[(seats[c] + t) % chips] for t in turns] for c in range(chips)])
        spot_of = np.repeat(spot_of, CORES, axis=0)
        core_of = np.arange(seq_count)[:, None] % CORES
        place_of = [CORES * spot_of + core_of, CORES * spot_of + 1 - core_of, spot_of]
    else:
        token_parts = [lax.all_gather(tokens, "seq", axis=0, tiled=False)]
        chip_rows = jnp.pad(chip_rows, ((0, 0), (0, width - 3 * feats)))
        weight_parts = [
            lax.all_gather(chip_rows, "seq", axis=0, tiled=False, axis_index_groups=planes_of)
        ]
        weight_spots = [0]
        place_of = [np.zeros((seq_count, 2))]
        last_part = token_parts[0]
    parts = len(token_parts)
    weight_count = len(weight_parts)
    device = np.arange(seq_count)[:, None]
    facts = np.concatenate([device // CORES, device % CORES, 0 * device] + place_of, axis=1)
    facts = np.stack([facts + k * (np.arange(facts.shape[1]) == 2) for k in range(2)])
    facts = lax.dynamic_slice(
        jnp.asarray(facts.astype(np.int32)), (side, place, 0), (1, 1, facts.shape[2])
    )
    spots = jnp.concatenate([doc_lengths[0:1], facts.reshape(-1)])

    smem = pl.BlockSpec(memory_space=pltpu.SMEM)
    anywhere = pl.BlockSpec(memory_space=pl.ANY)
    params = pltpu.CompilerParams(
        dimension_semantics=("arbitrary",), vmem_limit_bytes=VMEM_LIMIT
    )
    shape = jax.ShapeDtypeStruct

    def full(value):
        return pl.BlockSpec(value.shape, lambda i: (0,) * len(value.shape))

    def piped(kernel, name, outs, args, specs=None):
        if specs is None:
            specs = [None] * len(args)
        specs = [
            (smem if arg is spots else full(arg)) if spec is None else spec
            for spec, arg in zip(specs, args)
        ]
        return pl.pallas_call(
            kernel,
            grid=(1,),
            in_specs=specs,
            out_specs=[full(o) for o in outs],
            out_shape=outs,
            compiler_params=params,
            name=name,
        )(*args)

    inside = pl.BlockSpec(memory_space=pltpu.VMEM)
    in_vmem = lambda value: pltpu.with_memory_space_constraint(value, pltpu.VMEM)
    small = pltpu.CompilerParams(
        dimension_semantics=("arbitrary",), vmem_limit_bytes=SMALL_LIMIT
    )

    def once(kernel, name, outs, args, after=(), outside=(), blocks={}, limit=SMALL_LIMIT):
        specs, values = [], []
        for i, arg in enumerate(args):
            plain = arg is spots or i in blocks
            specs.append(smem if arg is spots else blocks.get(i, inside))
            values.append(arg if plain else in_vmem(arg))
        for arg in after:
            specs.append(anywhere)
            values.append(arg)
        return pl.pallas_call(
            kernel,
            grid=(1,) if blocks else (),
            in_specs=specs,
            out_specs=[inside] * len(outs),
            out_shape=[
                (pltpu.HBM if i in outside else pltpu.VMEM)(o.shape, o.dtype)
                for i, o in enumerate(outs)
            ],
            compiler_params=pltpu.CompilerParams(vmem_limit_bytes=limit),
            name=name,
        )(*values)

    own_planes = lax.dynamic_slice(
        plane_bits, (spot * hashes, 0, core * heads, 0), (hashes, bits, heads, head_dim)
    )
    scale = sharpness / math.sqrt(head_dim)
    signs = scale * (2 * own_planes - 1).astype(f32)
    bit_w = jnp.pad(
        jnp.transpose(signs, (2, 1, 0, 3)), ((0, 0), (0, 0), (0, rows - hashes), (0, 0))
    )
    bit_w = bit_w.reshape(heads, bits * rows, head_dim).astype(bf16)
    bit_wt = jnp.transpose(bit_w, (0, 2, 1))

    (second_send,) = piped(
        pack_kernel, "pack",
        [shape((own_rows, 2 * ff + group_feats), bf16)],
        [spots, up_weight, down_weight.T, out_weight.T, last_part, bit_w],
        [None] * 4 + [anywhere] * 2,
    )
    ff_all = lax.all_gather(second_send, "seq", axis=0, tiled=True)

    def resident(*dims):
        return pl.BlockSpec(dims, lambda p, i: (0,) * len(dims), pipeline_mode=pl.Buffered(1))

    def stepped(phase, *dims):
        def place(p, i):
            rest = steps - 1 if phase == 0 else 0
            return (jnp.where(p == phase, i, rest),) + (0,) * (len(dims) - 1)

        return pl.BlockSpec(dims, place)

    hash_params = pltpu.CompilerParams(
        dimension_semantics=("arbitrary", "arbitrary"), vmem_limit_bytes=VMEM_LIMIT
    )
    num_parts, q_unit, k_unit, values, inverses, tables, counts, qkv_all = pl.pallas_call(
        partial(forward_kernel, hashes, bits, rows, work, steps, heads, parts, weight_spots),
        grid=(2, steps),
        in_specs=[
            smem,
            *[anywhere] * (parts + weight_count),
            resident(*bit_w.shape),
        ],
        out_specs=[
            stepped(1, blocks, feats, tile),
            resident(feats, total),
            resident(feats, total),
            resident(feats, total + 256),
            resident(16, total),
            resident(heads, code_rows, 2 * head_dim),
            resident(heads, 8, code_rows),
            resident(width, 3 * feats),
        ],
        out_shape=[
            shape((chips, feats, tile), bf16),
            shape((feats, total), bf16),
            shape((feats, total), bf16),
            shape((feats, total + 256), bf16),
            shape((16, total), f32),
            shape((heads, code_rows, 2 * head_dim), bf16),
            shape((heads, 8, code_rows), f32),
            shape((width, 3 * feats), bf16),
        ],
        scratch_shapes=[
            pltpu.VMEM((heads, code_rows, 2 * head_dim + 16), f32),
            pltpu.VMEM((heads, code_rows, work), bf16),
            pltpu.VMEM((3 * feats, width), bf16),
            pltpu.VMEM((heads, 2 * head_dim, code_rows), bf16),
            pltpu.VMEM((seq_count, tok_rows, width), bf16),
            pltpu.VMEM((chips, weight_parts[-1].shape[1], width), bf16),
            pltpu.SemaphoreType.DMA((parts + weight_count,)),
        ],
        compiler_params=hash_params,
        name="hash_forward",
    )(spots, *token_parts, *weight_parts, bit_w)
    num_got = across(num_parts)

    own_taps = lax.dynamic_slice(conv_taps, (core * heads, 0), (heads, taps))
    lead = tile + 128 - rim
    bases = jnp.zeros((heads, 8, tile + 256), f32)
    bases = bases.at[:, 0, lead : lead + taps].set(own_taps[:, ::-1])
    conv, window_values = once(
        partial(conv_kernel, tile, heads), "conv_forward",
        [shape((feats, tile), f32), shape((feats, tile + 256), bf16)],
        [spots, values, bases],
    )

    chip_buckets = buckets // chips
    sum_rows = 4 * width // tile
    count_rows = 2 * heads * code_rows // tile
    extra_rows = -(-(sum_rows + count_rows) // 16) * 16

    keep, give, numerator = once(
        partial(context_kernel, heads), "context",
        [shape((feats, tok_rows), bf16), shape((feats, tok_rows), bf16), shape((feats, tile), f32)],
        [spots, num_got, conv],
    )
    context, mixer_part = once(
        mixer_kernel, "mixer",
        [shape((tok_rows, group_feats), bf16), shape((tok_rows, width), bf16)],
        [spots, keep, core_swap(give), ff_all],
        blocks={3: pl.BlockSpec((width, group_feats), lambda i: (0, 2 * ff // group_feats))},
    )
    ff_all, mixer_part = lax.optimization_barrier((ff_all, mixer_part))
    first_hat, first_inverse, hidden, active, feed_part = once(
        hidden_kernel, "feed_forward",
        [
            shape((tok_rows, width), f32),
            shape((tok_rows, 1), f32),
            shape((tok_rows, ff), f32),
            shape((tok_rows, ff), bf16),
            shape((tok_rows, width), bf16),
        ],
        [tokens, mixer_part, head_swap(mixer_part), norm_params, ff_all],
    )
    block_out, grad_second, feed_low, slope_low, first_part, second_sums = once(
        feed_kernel, "feed_back",
        [
            shape((tok_rows, width), f32),
            shape((tok_rows, width), f32),
            shape((tok_rows, width), bf16),
            shape((tok_rows, ff), bf16),
            shape((tok_rows, width), bf16),
            shape((2, width), f32),
        ],
        [first_hat, hidden, feed_part, head_swap(feed_part), cotangent, norm_params, ff_all],
        outside=(0,),
    )
    grad_mixer, mixer_low, keep, give, norm_sums = once(
        mixer_back_kernel, "mixer_back",
        [
            shape((tok_rows, width), f32),
            shape((tok_rows, width), bf16),
            shape((feats, tok_rows), f32),
            shape((feats, tok_rows), f32),
            shape((4, width), f32),
        ],
        [
            spots, grad_second, first_part, head_swap(first_part), first_hat, first_inverse,
            norm_params, ff_all, second_sums,
        ],
    )
    gnum_send, grad_low, grad_high = once(
        partial(attention_back_kernel, heads), "attention_back",
        [
            shape((feats + extra_rows, tile), bf16),
            shape((feats, tok_rows), bf16),
            shape((feats, tok_rows), bf16),
        ],
        [spots, keep, core_swap(give), numerator, norm_sums, counts],
    )
    conv_grad, tap_parts = once(
        partial(conv_back_kernel, tile, taps, heads), "conv_backward",
        [shape((feats, 3 * tile), f32), shape((heads, 8, 128), f32)],
        [spots, window_values, grad_low, grad_high, bases],
    )
    if ringed:
        moved, gnum_parts, unused = ring(gnum_send, 1, False)
        *moved, tap_parts = lax.optimization_barrier((*moved, tap_parts))
        gnum_parts = [gnum_send]
        for step in range(2, chips // 2 + 1):
            gnum_parts += moved
            moved = [
                lax.ppermute(v, "seq", p)
                for v, p in zip(moved, (ahead, behind))
                if p is ahead or 2 * step < chips
            ]
        gnum_parts = [p[None] for p in gnum_parts + moved]
    else:
        gnum_parts = [
            lax.all_gather(gnum_send, "seq", axis=0, tiled=False, axis_index_groups=planes_of)
        ]
    gnum_count = len(gnum_parts)

    columns = 2 * ff + group_feats
    feed_grads = pl.pallas_call(
        feed_grad_kernel,
        grid=(1,),
        in_specs=[inside] * 5,
        out_specs=pl.BlockSpec((width, 2 * ff), lambda i: (0, 0)),
        out_shape=pltpu.HBM((width, columns), bf16),
        compiler_params=small,
        name="feed_grads",
    )(*[in_vmem(v) for v in (first_hat, norm_params, slope_low, feed_low, active)])
    big_grad = pl.pallas_call(
        out_grad_kernel,
        grid=(1,),
        in_specs=[inside, inside, anywhere],
        out_specs=pl.BlockSpec((width, group_feats), lambda i: (0, 2 * ff // group_feats)),
        out_shape=pltpu.HBM((width, columns), bf16),
        input_output_aliases={2: 0},
        compiler_params=small,
        name="out_grads",
    )(in_vmem(mixer_low), in_vmem(context), feed_grads)
    big_owned = lax.psum_scatter(big_grad, "seq", scatter_dimension=0, tiled=True)

    qkv_send, back_keep, back_give, extras = pl.pallas_call(
        partial(backward_kernel, hashes, bits, rows, work, steps, heads, own_rows, parts, gnum_count),
        grid=(2, steps),
        in_specs=[
            smem,
            *[anywhere] * parts,
            *[inside] * gnum_count,
            resident(*qkv_all.shape),
            resident(*bit_w.shape),
            resident(*bit_wt.shape),
            resident(feats, total),
            resident(feats, total),
            resident(feats, total + 256),
            resident(16, total),
            resident(heads, code_rows, 2 * head_dim),
            resident(feats, 3 * tile),
            resident(*tap_parts.shape),
        ],
        out_specs=[
            resident(chips, CORES * own_rows, 3 * feats + 64),
            stepped(1, blocks, width, tok_rows),
            stepped(1, blocks, width, tok_rows),
            resident(chips, extra_rows, tile),
        ],
        out_shape=[
            shape((chips, CORES * own_rows, 3 * feats + 64), bf16),
            shape((chips, width, tok_rows), bf16),
            shape((chips, width, tok_rows), bf16),
            shape((chips, extra_rows, tile), bf16),
        ],
        scratch_shapes=[
            pltpu.VMEM((heads, code_rows, 2 * head_dim), f32),
            pltpu.VMEM((heads, code_rows, work), bf16),
            pltpu.VMEM((feats, total), bf16),
            pltpu.VMEM((3 * feats, width), f32),
            pltpu.VMEM((heads, 2 * head_dim, code_rows), bf16),
            pltpu.VMEM((heads, code_rows, 2 * head_dim), bf16),
            pltpu.VMEM((seq_count, tok_rows, width), bf16),
            pltpu.VMEM((chips, feats, tile), bf16),
            pltpu.SemaphoreType.DMA((parts,)),
        ],
        compiler_params=hash_params,
        name="hash_backward",
    )(
        spots, *token_parts, *[in_vmem(p) for p in gnum_parts], qkv_all, bit_w, bit_wt,
        q_unit, k_unit, values, inverses, tables, conv_grad, tap_parts,
    )

    half = width // 2
    group = chips // 2
    per_chip = lambda *dims: pl.BlockSpec((group,) + dims, lambda i: (i, 0, 0))
    keep, give = pl.pallas_call(
        chip_sum_kernel,
        grid=(2,),
        in_specs=[smem, per_chip(width, tok_rows), per_chip(width, tok_rows)],
        out_specs=[per_chip(half, tok_rows), per_chip(half, tok_rows)],
        out_shape=[shape((chips, half, tok_rows), bf16)] * 2,
        compiler_params=params,
        name="chip_sum",
    )(spots, back_keep, core_swap(back_give))
    *pair_sums, pair_done = once(
        pair_sum_kernel, "pair_sum",
        [shape((half, tok_rows) if ringed else (chips, half, tok_rows), bf16)]
        * (chips if ringed else 1)
        + [shape((8, 128), f32)],
        [spots, keep, head_swap(give)],
        outside=tuple(range(1, chips)) if ringed else (),
    )
    qkv_got = across(qkv_send)
    if ringed:
        back_got = [pair_sums[0]]
        for d in range(1, chips):
            perm = [(CORES * c + k, CORES * (c ^ d) + k) for c in range(chips) for k in range(CORES)]
            back_got.append(lax.ppermute(pair_sums[d], "seq", perm))
        qkv_got, *tied = lax.optimization_barrier((qkv_got, *back_got[1:5]))
        back_got = [back_got[0]] + tied + back_got[1 + len(tied) :]
        back_got = [p[None] for p in back_got]
    else:
        back_got = [across(pair_sums[0])]

    qkv_mine, qkv_give = once(
        weight_sum_kernel, "weight_sum",
        [shape((own_rows, 3 * feats + 64), f32)] * 2,
        [spots, qkv_got],
        after=[pair_done],
    )
    qkv_other = core_swap(qkv_give)

    extras = extras.astype(f32)
    norm_half = jnp.sum(extras[:, :sum_rows], axis=0)
    count_half = extras[:, sum_rows : sum_rows + count_rows]
    count_half = count_half.reshape(chips, heads, 2, chips, CORES, chip_buckets // CORES, rows)
    count_half = lax.dynamic_index_in_dim(count_half, spot, 3, keepdims=False)
    count_half = jnp.transpose(count_half[..., :hashes], (3, 0, 2, 5, 1, 4))
    count_mine = lax.dynamic_index_in_dim(count_half, core, 0, keepdims=False)
    count_give = lax.dynamic_index_in_dim(count_half, 1 - core, 0, keepdims=False)
    tap_first = jnp.where(core == 0, qkv_mine[:heads], qkv_give[:heads])
    tap_half = tap_first[:, 3 * feats : 3 * feats + taps]
    swapped = core_swap(
        jnp.concatenate([norm_half.reshape(-1), count_give.reshape(-1), tap_half.reshape(-1)])
    )
    norm_size, count_size = norm_half.size, count_give.size

    norm_grad = norm_half + swapped[:norm_size].reshape(norm_half.shape)
    norm_grad = jnp.transpose(
        norm_grad.reshape(width // tile, 4, tile), (1, 0, 2)
    ).reshape(4, width)
    count_other = swapped[norm_size : norm_size + count_size].reshape(count_mine.shape)
    occupancy = jnp.transpose(
        in_order(count_mine, count_other, 3), (1, 0, 2, 3, 4)
    ).reshape(2, hash_count, group_heads, buckets // seq_count)
    occupancy = occupancy * (buckets / (tok_rows * seq_count))
    conv_tap_grad = in_order(tap_half, swapped[norm_size + count_size :].reshape(heads, taps), 0)

    flag = shape((8, 128), f32)
    matrix = lambda value: [pltpu.HBM(value.shape, f32)] * 3 + [pltpu.HBM(value.shape, bf16)]
    (
        up_new, up_first_new, up_second_new, up_copy,
        down_new, down_first_new, down_second_new, down_copy,
        out_new, out_first_new, out_second_new, out_copy, big_done,
    ) = piped(
        big_adam_kernel, "big_adam",
        matrix(up_weight) + matrix(down_weight.T) + matrix(out_weight.T) + [flag],
        [
            big_owned, up_weight, up_first, up_second,
            down_weight.T, down_first.T, down_second.T,
            out_weight.T, out_first.T, out_second.T,
        ],
    )
    qkv_new, qkv_first_new, qkv_second_new, qkv_copy = piped(
        qkv_adam_kernel, "qkv_adam", matrix(qkv_weight),
        [spots, qkv_mine, qkv_other, qkv_weight, qkv_first, qkv_second],
    )
    norm_new, norm_first_new, norm_second_new = adam_step(
        norm_params, norm_first, norm_second, norm_grad, 0.3
    )
    conv_new, conv_first_new, conv_second_new = adam_step(
        conv_taps, conv_first, conv_second, conv_tap_grad, CONV ** (-0.5)
    )
    (back_low,) = once(
        back_sum_kernel, "back_sum",
        [shape((half, tok_rows), bf16)],
        back_got,
        after=[big_done],
    )
    (tokens_grad,) = once(
        final_kernel, "tokens_grad",
        [shape((tok_rows, width), f32)],
        [spots, back_low, head_swap(back_low), grad_mixer],
        outside=(0,),
    )
    return (
        block_out,
        tokens_grad,
        occupancy,
        qkv_new,
        qkv_first_new,
        qkv_second_new,
        qkv_copy,
        out_new.T,
        out_first_new.T,
        out_second_new.T,
        out_copy.T,
        up_new,
        up_first_new,
        up_second_new,
        up_copy,
        down_new.T,
        down_first_new.T,
        down_second_new.T,
        down_copy.T,
        norm_new,
        norm_first_new,
        norm_second_new,
        conv_new,
        conv_first_new,
        conv_second_new,
    )


def solution(mesh):
    in_specs = (
        P("seq", None),
        P("seq", None),
        P(),
        P(None, None, "head", None),
        P(None, "seq", "head"),
        P(None, "seq", "head"),
        P(None, "seq", "head"),
        P("head", "seq"),
        P("head", "seq"),
        P("head", "seq"),
        P("seq", "head"),
        P("seq", "head"),
        P("seq", "head"),
        P("head", "seq"),
        P("head", "seq"),
        P("head", "seq"),
        P(),
        P(),
        P(),
        P("head", None),
        P("head", None),
        P("head", None),
    )
    out_specs = (
        P("seq", None),
        P("seq", None),
        P(None, None, "head", "seq"),
        P(None, "seq", "head"),
        P(None, "seq", "head"),
        P(None, "seq", "head"),
        P(None, "seq", "head"),
        P("head", "seq"),
        P("head", "seq"),
        P("head", "seq"),
        P("head", "seq"),
        P("seq", "head"),
        P("seq", "head"),
        P("seq", "head"),
        P("seq", "head"),
        P("head", "seq"),
        P("head", "seq"),
        P("head", "seq"),
        P("head", "seq"),
        P(),
        P(),
        P(),
        P("head", None),
        P("head", None),
        P("head", None),
    )
    return jax.shard_map(
        on_device, mesh=mesh, in_specs=in_specs, out_specs=out_specs, check_vma=False
    )
```

```python
from functools import partial
import math

import jax
import jax.numpy as jnp
import numpy as np
from jax import lax
from jax.experimental import pallas as pl
from jax.experimental.pallas import tpu as pltpu
from jax.sharding import PartitionSpec as P

D = 768
FF = 3072
CONV = 33
STEP = 7
CORES = 2

sharpness = 4.0
norm_eps = 1e-06
layer_eps = 1e-05
beta_one = 0.9
beta_two = 0.999
adam_eps = 1e-08
decay_rate = 0.01
highest = lax.Precision.HIGHEST
f32 = jnp.float32
bf16 = jnp.bfloat16
VMEM_LIMIT = 56 * 1024 * 1024
SMALL_LIMIT = 16 * 1024 * 1024
WORK = 2
SPOTS = 4
RING = (0, 2, 4, 6, 7, 5, 3, 1)


def nn(a, b):
    return lax.dot_general(a, b, (((1,), (0,)), ((), ())), preferred_element_type=f32)


def nt(a, b):
    return lax.dot_general(a, b, (((1,), (1,)), ((), ())), preferred_element_type=f32)


def normalize(source):
    centered = source - jnp.mean(source, axis=-1, keepdims=True)
    inverse = lax.rsqrt(jnp.mean(centered * centered, axis=-1, keepdims=True) + layer_eps)
    return (centered * inverse, inverse)


def norm_back(grad, normed, inverse, gain):
    scaled = grad * gain
    inner = (
        scaled
        - jnp.mean(scaled, axis=-1, keepdims=True)
        - normed * jnp.mean(scaled * normed, axis=-1, keepdims=True)
    )
    gains = jnp.sum(grad * normed, axis=0, keepdims=True)
    return (inverse * inner, gains, jnp.sum(grad, axis=0, keepdims=True))


def adam_step(weight, first, second, grad, rate):
    first_new = beta_one * first + (1.0 - beta_one) * grad
    second_new = beta_two * second + (1.0 - beta_two) * grad * grad
    fix_one = 1.0 - beta_one**STEP
    fix_two = 1.0 - beta_two**STEP
    update = first_new / fix_one / (jnp.sqrt(second_new / fix_two) + adam_eps) + decay_rate * weight
    return (weight - rate * update, first_new, second_new)


def head_units(source):
    inverse = lax.rsqrt(jnp.mean(source * source, axis=0, keepdims=True) + norm_eps)
    return source * inverse, inverse


def seg_rows(limit, start, width):
    pos = start + lax.broadcasted_iota(jnp.int32, (1, width), 1)
    late = (pos >= limit).astype(f32)
    return 1.0 - late, late


def masked_pair(rows, early, late):
    return jnp.concatenate([rows * early, rows * late], axis=0).astype(bf16)


def flip(value):
    return jnp.transpose(value.astype(f32)).astype(bf16)


def bit_factors(bit_planes, unit, bits, hashes, rows):
    z = nn(bit_planes, unit)
    decay = jnp.exp(-jnp.abs(z))
    large = 1.0 / (1.0 + decay)
    small = decay * large
    ones = jnp.where(z >= 0.0, large, small)
    zeros = jnp.where(z >= 0.0, small, large)
    ones = [ones[j * rows : (j + 1) * rows] for j in range(bits)]
    zeros = [zeros[j * rows : (j + 1) * rows] for j in range(bits)]
    if rows != hashes:
        live = lax.broadcasted_iota(jnp.int32, ones[0].shape, 0) < hashes
        return ones, [jnp.where(live, ones[0], 0.0)] + ones[1:], [
            jnp.where(live, zeros[0], 0.0)
        ] + zeros[1:]
    return ones, ones, zeros


def products(ones, zeros, first, last):
    found = [zeros[first], ones[first]]
    for j in range(first + 1, last):
        found = [part * zeros[j] for part in found] + [part * ones[j] for part in found]
    return found


def code_parts(bit_planes, unit, bits, hashes, rows):
    plain, ones, zeros = bit_factors(bit_planes, unit, bits, hashes, rows)
    return plain, products(ones, zeros, 0, 3), products(ones, zeros, 3, bits)


def store_codes(codes_ref, head, lows, highs, rows):
    for g, high in enumerate(highs):
        for s in range(0, len(lows), 2):
            spot = (g * len(lows) + s) * rows
            pair = jnp.concatenate([lows[s] * high, lows[s + 1] * high], axis=0)
            codes_ref[head, spot : spot + 2 * rows, :] = pair.astype(bf16)


def token_copies(spots_ref, part_refs, tok_ref, sem_ref):
    return [
        pltpu.make_async_copy(
            ref.at[:, pl.ds(0, tok_ref.shape[1])],
            tok_ref.at[pl.ds(spots_ref[SPOTS + i], ref.shape[0])],
            sem_ref.at[i],
        )
        for i, ref in enumerate(part_refs)
    ]


def forward_kernel(
    hashes, bits, rows, tile, steps, heads, parts, weight_spots, spots_ref, *refs
):
    part_refs, refs = refs[:parts], refs[parts:]
    weight_refs, refs = refs[: len(weight_spots)], refs[len(weight_spots) :]
    bit_ref, num_ref, qu_ref, ku_ref, v_ref, inv_ref, table_ref, count_ref, w_ref = refs[:9]
    acc_ref, codes_ref, wt_ref, table_t_ref, tok_ref, got_ref, sem_ref = refs[9:]
    limit = spots_ref[0]
    phase, i = pl.program_id(0), pl.program_id(1)
    feats = heads * 64
    chips = num_ref.shape[0]
    block = tile // chips
    start = pl.multiple_of(i * tile, tile)
    span = pl.ds(start, tile)
    early, late = seg_rows(limit, start, tile)

    @pl.when((phase == 0) & (i == 0))
    def _():
        copies = token_copies(spots_ref, part_refs, tok_ref, sem_ref)
        loads = [
            pltpu.make_async_copy(
                ref.at[:, pl.ds(weight_spots[i], got_ref.shape[1])],
                got_ref.at[pl.ds(spots_ref[SPOTS + parts + i], ref.shape[0])],
                sem_ref.at[parts + i],
            )
            for i, ref in enumerate(weight_refs)
        ]
        for copy in loads + copies:
            copy.start()
        acc_ref[...] = jnp.zeros_like(acc_ref)
        v_ref[:, 0:128] = jnp.zeros((feats, 128), bf16)
        v_ref[:, 128 + steps * tile :] = jnp.zeros((feats, 128), bf16)
        inv_ref[...] = jnp.zeros_like(inv_ref)
        for copy in loads:
            copy.wait()
        got = got_ref[...].astype(f32)
        if len(weight_refs) > 1:
            quarter = got.shape[1] // 3
            rest = [got[:, quarter * j : quarter * (j + 1), 3 * feats :] for j in range(3)]
            got = jnp.concatenate([got[:, :, : 3 * feats], jnp.concatenate(rest, axis=2)], axis=1)
        got = got.reshape(got.shape[0] * got.shape[1], got.shape[2])[:, : 3 * feats].astype(bf16)
        w_ref[...] = got
        wt_ref[...] = flip(got)
        for copy in copies:
            copy.wait()

    @pl.when(phase == 0)
    def _():
        devices, tok_rows, width = tok_ref.shape
        here = pl.ds(i * (devices // steps), devices // steps)
        proj = nt(wt_ref[...], tok_ref[here].reshape(tile, width))
        values = proj[2 * feats :].astype(bf16)
        v_ref[:, pl.ds(pl.multiple_of(start + 128, 128), tile)] = values
        marks = jnp.concatenate([early, late, jnp.zeros((14, tile), f32)], axis=0).astype(bf16)
        units = []
        for h in range(heads):
            mine = slice(64 * h, 64 * (h + 1))
            q_unit, q_inv = head_units(proj[mine])
            k_unit, k_inv = head_units(proj[feats + 64 * h : feats + 64 * (h + 1)])
            units.append(k_unit.astype(bf16))
            qu_ref[mine, span] = q_unit.astype(bf16)
            ku_ref[mine, span] = units[h]
            inv_ref[h : h + 1, span] = q_inv
            inv_ref[8 + h : 9 + h, span] = k_inv
        for h in range(heads):
            plain, lows, highs = code_parts(bit_ref[h], units[h], bits, hashes, rows)
            store_codes(codes_ref, h, lows, highs, rows)
        for h in range(heads):
            pair = masked_pair(values[64 * h : 64 * (h + 1)].astype(f32), early, late)
            pair = jnp.concatenate([pair, marks], axis=0)
            acc_ref[h] += nt(codes_ref[h], pair)

    @pl.when((phase == 1) & (i == 0))
    def _():
        for h in range(heads):
            table = acc_ref[h, :, 0:128].astype(bf16)
            table_ref[h] = table
            table_t_ref[h] = flip(table)
            counts = jnp.concatenate(
                [acc_ref[h, :, 128:144], jnp.zeros((acc_ref.shape[1], 112), f32)], axis=1
            )
            count_ref[h] = jnp.transpose(counts)[0:8]

    @pl.when(phase == 1)
    def _():
        for h in range(heads):
            unit = qu_ref[64 * h : 64 * (h + 1), span]
            plain, lows, highs = code_parts(bit_ref[h], unit, bits, hashes, rows)
            store_codes(codes_ref, h, lows, highs, rows)
        for h in range(heads):
            mine = slice(64 * h, 64 * (h + 1))
            both = nn(table_t_ref[h], codes_ref[h])
            low = (both[0:64] * early + both[64:128] * late).astype(bf16)
            for c in range(chips):
                num_ref[c, mine, :] = low[:, c * block : (c + 1) * block]


def soften(bit_planes, unit, slopes, codes_ref, head, bits, hashes, rows):
    plain, lows, highs = code_parts(bit_planes, unit, bits, hashes, rows)
    by_low = [None] * len(lows)
    by_bit = [None] * (bits - 3)
    for g, high in enumerate(highs):
        row = None
        for s in range(0, len(lows), 2):
            spot = (g * len(lows) + s) * rows
            parts = [lows[s] * high, lows[s + 1] * high]
            codes_ref[head, spot : spot + 2 * rows, :] = jnp.concatenate(parts, axis=0).astype(bf16)
            for k in range(2):
                term = parts[k] * slopes[spot + k * rows : spot + (k + 1) * rows]
                by_low[s + k] = term if by_low[s + k] is None else by_low[s + k] + term
                row = term if row is None else row + term
        for j in range(bits - 3):
            if (g >> j) & 1:
                by_bit[j] = row if by_bit[j] is None else by_bit[j] + row
    pairs = [sum(part for s, part in enumerate(by_low) if (s >> j) & 1) for j in range(3)]
    whole = sum(by_low)
    slopes = [part - plain[j] * whole for j, part in enumerate(pairs + by_bit)]
    return jnp.concatenate(slopes, axis=0).astype(bf16)


def unit_back(grad, unit, inverse):
    unit = unit.astype(f32)
    inner = jnp.mean(grad * unit, axis=0, keepdims=True)
    return inverse * (grad - unit * inner)


def backward_kernel(
    hashes, bits, rows, tile, steps, heads, own_rows, parts, gnum_parts, spots_ref, *refs
):
    part_refs, refs = refs[:parts], refs[parts:]
    gnum_refs, refs = refs[:gnum_parts], refs[gnum_parts:]
    w_ref, bit_ref, bit_t_ref, qu_ref, ku_ref, v_ref, inv_ref, table_ref = refs[:8]
    conv_ref, tap_ref, grad_ref, keep_ref, give_ref, extra_ref = refs[8:14]
    acc_ref, codes_ref, proj_ref, sum_ref, table_t_ref, table_g_ref = refs[14:20]
    tok_ref, gnum_ref, sem_ref = refs[20:]
    limit = spots_ref[0]
    spot = spots_ref[1]
    core = spots_ref[2]
    phase, i = pl.program_id(0), pl.program_id(1)
    devices, unused, width = tok_ref.shape
    copies = token_copies(spots_ref, part_refs, tok_ref, sem_ref)
    loads = [
        (ref, pl.ds(spots_ref[SPOTS + parts + j], ref.shape[0]))
        for j, ref in enumerate(gnum_refs)
    ]
    feats = heads * 64
    blocks = keep_ref.shape[0]
    block = tile // blocks
    tok_rows = block // CORES
    start = pl.multiple_of(i * tile, tile)
    span = pl.ds(start, tile)
    early, late = seg_rows(limit, start, tile)

    @pl.when((phase == 0) & (i == 0))
    def _():
        for copy in copies:
            copy.start()
        acc_ref[...] = jnp.zeros_like(acc_ref)
        sum_ref[...] = jnp.zeros_like(sum_ref)
        for ref, where in loads:
            gnum_ref[where] = ref[:, :feats]
            extra_ref[where] = ref[:, feats:]

    @pl.when(phase == 0)
    def _():
        spans = [slice(64 * h, 64 * (h + 1)) for h in range(heads)]
        pairs, grads, slopes = [], [], []
        for mine in spans:
            gnum = jnp.concatenate([gnum_ref[i * blocks + c, mine, :] for c in range(blocks)], axis=1)
            pairs.append(masked_pair(gnum.astype(f32), early, late))
        for h, mine in enumerate(spans):
            slopes.append(
                soften(
                    bit_ref[h], qu_ref[mine, span], nn(table_ref[h], pairs[h]), codes_ref, h,
                    bits, hashes, rows,
                )
            )
        for h in range(heads):
            acc_ref[h] += nt(codes_ref[h], pairs[h])
        for h, mine in enumerate(spans):
            grad = nn(bit_t_ref[h], slopes[h])
            grad = unit_back(grad, qu_ref[mine, span], inv_ref[h : h + 1, span])
            proj_ref[mine, span] = grad.astype(bf16)

    @pl.when((phase == 1) & (i == 0))
    def _():
        for copy in copies:
            copy.wait()
        for h in range(heads):
            table_g_ref[h] = acc_ref[h].astype(bf16)
            table_t_ref[h] = flip(table_g_ref[h])

    @pl.when(phase == 1)
    def _():
        conv = []
        for c in range(blocks):
            step = i * blocks + c - spot + 1
            near = ((step >= 0) & (step <= 2)).astype(f32)
            step = jnp.clip(step, 0, 2)
            conv.append(conv_ref[:, pl.ds(pl.multiple_of(step * block, block), block)] * near)
        conv = jnp.concatenate(conv, axis=1)
        spans = [slice(64 * h, 64 * (h + 1)) for h in range(heads)]
        slopes, parts = [], []
        for h, mine in enumerate(spans):
            values = v_ref[mine, pl.ds(pl.multiple_of(start + 128, 128), tile)]
            pair = masked_pair(values.astype(f32), early, late)
            slopes.append(
                soften(
                    bit_ref[h], ku_ref[mine, span], nn(table_g_ref[h], pair), codes_ref, h,
                    bits, hashes, rows,
                )
            )
        for h, mine in enumerate(spans):
            both = nn(table_t_ref[h], codes_ref[h])
            value_grad = both[0:64] * early + both[64:128] * late + conv[mine]
            grad = nn(bit_t_ref[h], slopes[h])
            grad = unit_back(grad, ku_ref[mine, span], inv_ref[8 + h : 9 + h, span])
            parts.append((grad.astype(bf16), value_grad.astype(bf16)))
        full = jnp.concatenate(
            [proj_ref[:, span]] + [part[0] for part in parts] + [part[1] for part in parts], axis=0
        )
        here = pl.ds(i * (devices // steps), devices // steps)
        sum_ref[...] += nn(full, tok_ref[here].reshape(tile, width))
        part = nn(w_ref[...], full)
        for c in range(blocks):
            first = part[:, c * block : c * block + tok_rows]
            second = part[:, c * block + tok_rows : (c + 1) * block]
            keep_ref[c] = jnp.where(core == 0, first, second).astype(bf16)
            give_ref[c] = jnp.where(core == 0, second, first).astype(bf16)

    @pl.when((phase == 1) & (i == steps - 1))
    def _():
        grad = jnp.transpose(sum_ref[...])
        chips = grad_ref.shape[0]
        grad_ref[:, :, 0 : heads * 192] = grad.reshape(
            chips, CORES * own_rows, heads * 192
        ).astype(bf16)
        grad_ref[:, :, heads * 192 :] = jnp.zeros((chips, CORES * own_rows, 64), bf16)
        taps = jnp.concatenate([tap_ref[h, 0:1, 0:64] for h in range(heads)], axis=0)
        for c in range(chips):
            grad_ref[c, 0:heads, heads * 192 :] = taps.astype(bf16)


def window_same(spots_ref, tile):
    start = spots_ref[1] * tile
    width = tile + 256
    edge = lax.broadcasted_iota(jnp.int32, (width, tile), 0) + (start - 128)
    own = lax.broadcasted_iota(jnp.int32, (width, tile), 1) + start
    return (edge >= spots_ref[0]) == (own >= spots_ref[0])


def banded(base, same, tile):
    width = tile + 256
    spread = jnp.broadcast_to(base, (width, width))
    spread = pltpu.roll(spread, 0, 1, stride=1, stride_axis=0)[:, :tile]
    matrix = jnp.where(same, spread, 0.0)
    upper = matrix.astype(bf16)
    return upper, (matrix - upper.astype(f32)).astype(bf16)


def conv_kernel(tile, heads, spots_ref, values_ref, base_ref, out_ref, window_ref):
    same = window_same(spots_ref, tile)
    first = pl.multiple_of(spots_ref[1] * tile, tile)
    window = values_ref[:, pl.ds(first, tile + 256)]
    window_ref[...] = window
    for h in range(heads):
        mine = slice(64 * h, 64 * (h + 1))
        upper, lower = banded(base_ref[h, 0:1], same, tile)
        out_ref[mine] = nn(window[mine], upper) + nn(window[mine], lower)


def conv_back_kernel(
    tile, taps, heads, spots_ref, window_ref, low_ref, high_ref, base_ref, out_ref, tap_ref
):
    same = window_same(spots_ref, tile)
    width = tile + 256
    rim = taps // 2
    out_ref[...] = jnp.zeros_like(out_ref)
    pos = lax.broadcasted_iota(jnp.int32, (128, tile), 1) + spots_ref[1] * tile
    other = pos + lax.broadcasted_iota(jnp.int32, (128, tile), 0) - rim
    near = (pos >= spots_ref[0]) == (other >= spots_ref[0])
    for h in range(heads):
        mine = slice(64 * h, 64 * (h + 1))
        upper, lower = banded(base_ref[h, 0:1], same, tile)
        own = jnp.concatenate([low_ref[mine], high_ref[mine]], axis=1)
        out_ref[mine, 128 : 128 + width] = nt(own, upper) + nt(own, lower)
        values = window_ref[mine].astype(f32)
        own = own.astype(f32)
        sums = []
        for o in range(taps):
            moved = pltpu.roll(values, width - (128 - rim) - o, 1)[:, :tile]
            sums.append(jnp.sum(moved * own, axis=0, keepdims=True))
        sums = jnp.concatenate(sums + [jnp.zeros((128 - taps, tile), f32)], axis=0)
        total = jnp.sum(jnp.where(near, sums, 0.0), axis=1, keepdims=True)
        tap_ref[h] = jnp.transpose(jnp.broadcast_to(total, (128, 128)))[0:8]


def context_kernel(heads, spots_ref, got_ref, conv_ref, keep_ref, give_ref, num_ref):
    total = jnp.sum(got_ref[...].astype(f32), axis=0)
    num_ref[...] = total
    tile = total.shape[1]
    parts = [head_units(total[64 * h : 64 * (h + 1)])[0] for h in range(heads)]
    context = (jnp.concatenate(parts, axis=0) + conv_ref[...]).astype(bf16)
    first, second = context[:, : tile // CORES], context[:, tile // CORES :]

    @pl.when(spots_ref[2] == 0)
    def _():
        keep_ref[...] = first
        give_ref[...] = second

    @pl.when(spots_ref[2] != 0)
    def _():
        keep_ref[...] = second
        give_ref[...] = first


def mixer_kernel(spots_ref, keep_ref, other_ref, w_ref, context_ref, part_ref):
    keep, other = keep_ref[...].astype(f32), other_ref[...].astype(f32)
    zero = spots_ref[2] == 0
    pair = jnp.concatenate([jnp.where(zero, keep, other), jnp.where(zero, other, keep)], axis=0)
    context = jnp.transpose(pair).astype(bf16)
    context_ref[...] = context
    part_ref[...] = nt(context, w_ref[...]).astype(bf16)


def hidden_kernel(
    tok_ref, own_ref, other_ref, norm_ref, w_ref, hat_ref, inv_ref, hidden_ref, active_ref, part_ref
):
    ff = hidden_ref.shape[1]
    mixed = own_ref[...].astype(f32) + other_ref[...].astype(f32)
    hat, inverse = normalize(tok_ref[...].astype(f32) + mixed)
    hat_ref[...] = hat
    inv_ref[...] = inverse
    low = (hat * norm_ref[0:1] + norm_ref[1:2]).astype(bf16)
    hidden = nn(low, w_ref[:, :ff])
    hidden_ref[...] = hidden
    active = (0.5 * hidden * (1.0 + lax.erf(hidden * math.sqrt(0.5)))).astype(bf16)
    active_ref[...] = active
    part_ref[...] = nt(active, w_ref[:, ff : 2 * ff]).astype(bf16)


def feed_kernel(
    hat_ref, hidden_ref, own_ref, other_ref, cot_ref, norm_ref, w_ref,
    out_ref, second_ref, feed_ref, slope_ref, part_ref, sums_ref,
):
    ff = hidden_ref.shape[1]
    first_out = hat_ref[...] * norm_ref[0:1] + norm_ref[1:2]
    fed = own_ref[...].astype(f32) + other_ref[...].astype(f32)
    hat, inverse = normalize(first_out + fed)
    out_ref[...] = hat * norm_ref[2:3] + norm_ref[3:4]
    grad, gains, offsets = norm_back(cot_ref[...].astype(f32), hat, inverse, norm_ref[2:3])
    second_ref[...] = grad
    sums_ref[0:1] = gains
    sums_ref[1:2] = offsets
    low = grad.astype(bf16)
    feed_ref[...] = low
    active_grad = nn(low, w_ref[:, ff : 2 * ff])
    hidden = hidden_ref[...]
    cdf = 0.5 * (1.0 + lax.erf(hidden * math.sqrt(0.5)))
    density = jnp.exp(-0.5 * hidden * hidden) * (1.0 / math.sqrt(2.0 * math.pi))
    slope = (active_grad * (cdf + hidden * density)).astype(bf16)
    slope_ref[...] = slope
    part_ref[...] = nt(slope, w_ref[:, :ff]).astype(bf16)


def mixer_back_kernel(
    spots_ref, second_ref, own_ref, other_ref, hat_ref, inv_ref, norm_ref, w_ref, sums_ref,
    grad_ref, low_ref, keep_ref, give_ref, all_sums_ref,
):
    first = second_ref[...] + (own_ref[...].astype(f32) + other_ref[...].astype(f32))
    grad, gains, offsets = norm_back(first, hat_ref[...], inv_ref[...], norm_ref[0:1])
    grad_ref[...] = grad
    all_sums_ref[0:1] = gains
    all_sums_ref[1:2] = offsets
    all_sums_ref[2:4] = sums_ref[...]
    low = grad.astype(bf16)
    low_ref[...] = low
    half = keep_ref.shape[0]
    context = jnp.transpose(nn(low, w_ref[:, w_ref.shape[1] - CORES * half :]))
    half = context.shape[0] // CORES
    zero = spots_ref[2] == 0
    keep_ref[...] = jnp.where(zero, context[:half], context[half:])
    give_ref[...] = jnp.where(zero, context[half:], context[:half])


def attention_back_kernel(
    heads, spots_ref, keep_ref, other_ref, num_ref, sums_ref, count_ref,
    send_ref, low_ref, high_ref,
):
    zero = spots_ref[2] == 0
    keep, other = keep_ref[...], other_ref[...]
    grad = jnp.concatenate([jnp.where(zero, keep, other), jnp.where(zero, other, keep)], axis=1)
    half = keep.shape[1]
    low = grad.astype(bf16)
    low_ref[...] = low[:, :half]
    high_ref[...] = low[:, half:]
    parts = []
    for h in range(heads):
        span = slice(64 * h, 64 * (h + 1))
        attention, inverse = head_units(num_ref[span])
        inner = jnp.mean(grad[span] * attention, axis=0, keepdims=True)
        parts.append(inverse * (grad[span] - attention * inner))
    gnum = jnp.concatenate(parts, axis=0).astype(bf16)
    tile = gnum.shape[1]
    feats = 64 * heads
    pieces = sums_ref.shape[1] // tile
    counts = []
    for h in range(heads):
        for d in range(2):
            row = count_ref[h, d : d + 1, :]
            counts += [row[:, tile * i : tile * (i + 1)] for i in range(row.shape[1] // tile)]
    used = feats + 4 * pieces + len(counts)
    spare = jnp.zeros((send_ref.shape[0] - used, tile), f32)
    sums = sums_ref[...].astype(bf16).astype(f32)
    sums = [sums[:, tile * i : tile * (i + 1)] for i in range(pieces)]
    send_ref[0:feats, :] = gnum
    send_ref[feats:, :] = jnp.concatenate(sums + counts + [spare], axis=0).astype(bf16)


def feed_grad_kernel(hat_ref, norm_ref, slope_ref, feed_ref, active_ref, out_ref):
    ff = slope_ref.shape[1]
    low = hat_ref[...] * norm_ref[0:1] + norm_ref[1:2]
    out_ref[:, :ff] = nn(flip(low.astype(bf16)), slope_ref[...]).astype(bf16)
    out_ref[:, ff : 2 * ff] = nn(flip(feed_ref[...]), active_ref[...]).astype(bf16)


def out_grad_kernel(mixer_ref, context_ref, all_ref, out_ref):
    out_ref[...] = nn(flip(mixer_ref[...]), context_ref[...]).astype(bf16)


def pack_kernel(spots_ref, up_ref, down_ref, out_ref, after_ref, bit_ref, all_ref):
    ff = up_ref.shape[1]
    all_ref[:, :ff] = up_ref[...].astype(bf16)
    all_ref[:, ff : 2 * ff] = down_ref[...].astype(bf16)
    all_ref[:, 2 * ff :] = out_ref[...].astype(bf16)


def chip_sum_kernel(spots_ref, own_ref, other_ref, keep_ref, give_ref):
    total = own_ref[...].astype(f32) + other_ref[...].astype(f32)
    half = total.shape[1] // 2
    first, second = total[:, :half], total[:, half:]
    zero = spots_ref[3] == 0
    keep_ref[...] = jnp.where(zero, first, second).astype(bf16)
    give_ref[...] = jnp.where(zero, second, first).astype(bf16)


def pair_sum_kernel(spots_ref, own_ref, other_ref, *refs):
    out_refs, flag_ref = refs[:-1], refs[-1]
    flag_ref[...] = jnp.zeros_like(flag_ref)
    for d, out_ref in enumerate(out_refs):
        if len(out_refs) == 1:
            total = own_ref[...].astype(f32) + other_ref[...].astype(f32)
        else:
            chip = spots_ref[1] ^ d
            total = own_ref[chip].astype(f32) + other_ref[chip].astype(f32)
        out_ref[...] = total.astype(bf16)


def weight_sum_kernel(spots_ref, got_ref, after_ref, keep_ref, give_ref):
    total = jnp.sum(got_ref[...].astype(f32), axis=0)
    half = total.shape[0] // CORES
    zero = spots_ref[2] == 0
    keep_ref[...] = jnp.where(zero, total[:half], total[half:])
    give_ref[...] = jnp.where(zero, total[half:], total[:half])


def adam_refs(grad, ins, outs, rate):
    new, first, second = adam_step(ins[0], ins[1], ins[2], grad, rate)
    outs[0][...] = new
    outs[1][...] = first
    outs[2][...] = second
    outs[3][...] = new.astype(bf16)


def big_adam_kernel(grad_ref, *refs):
    ins, outs, flag_ref = refs[:9], refs[9:-1], refs[-1]
    flag_ref[...] = jnp.zeros_like(flag_ref)
    ff = ins[0].shape[1]
    spans = (slice(0, ff), slice(ff, 2 * ff), slice(2 * ff, grad_ref.shape[1]))
    for k, (span, rate) in enumerate(zip(spans, (D ** (-0.5), FF ** (-0.5), D ** (-0.5)))):
        state = [ref[...] for ref in ins[3 * k : 3 * k + 3]]
        adam_refs(grad_ref[:, span].astype(f32), state, outs[4 * k : 4 * k + 4], rate)


def qkv_adam_kernel(spots_ref, mine_ref, other_ref, *refs):
    zero = spots_ref[2] == 0
    feats = refs[0].shape[2] // CORES
    for p in range(3):
        span = slice(p * feats, (p + 1) * feats)
        mine, other = mine_ref[:, span], other_ref[:, span]
        grad = jnp.concatenate([jnp.where(zero, mine, other), jnp.where(zero, other, mine)], axis=1)
        adam_refs(grad, [ref[p] for ref in refs[:3]], [ref.at[p] for ref in refs[3:]], D ** (-0.5))


def final_kernel(spots_ref, mine_ref, other_ref, mixer_ref, out_ref):
    mine, other = mine_ref[...].astype(f32), other_ref[...].astype(f32)
    zero = spots_ref[3] == 0
    total = jnp.concatenate([jnp.where(zero, mine, other), jnp.where(zero, other, mine)], axis=0)
    out_ref[...] = mixer_ref[...] + jnp.transpose(total)


def back_sum_kernel(*refs):
    total = jnp.sum(refs[0][...].astype(f32), axis=0)
    for ref in refs[1:-2]:
        total = total + jnp.sum(ref[...].astype(f32), axis=0)
    refs[-1][...] = total.astype(bf16)


def on_device(
    tokens,
    cotangent,
    doc_lengths,
    plane_bits,
    qkv_weight,
    qkv_first,
    qkv_second,
    out_weight,
    out_first,
    out_second,
    up_weight,
    up_first,
    up_second,
    down_weight,
    down_first,
    down_second,
    norm_params,
    norm_first,
    norm_second,
    conv_taps,
    conv_first,
    conv_second,
):
    tok_rows, width = tokens.shape
    hash_count, bits, group_heads, head_dim = plane_bits.shape
    buckets = 2**bits
    taps = conv_taps.shape[1]
    rim = taps // 2
    seq_count = lax.axis_size("seq")
    chips = seq_count // CORES
    place = lax.axis_index("seq")
    side = lax.axis_index("head")
    spot, core = place // CORES, place % CORES
    heads = group_heads // CORES
    feats = heads * head_dim
    group_feats = group_heads * head_dim
    hashes = hash_count // chips
    rows = -(-hashes // 8) * 8
    tile = CORES * tok_rows
    total = chips * tile
    own_rows = width // seq_count
    ff = up_weight.shape[1]
    code_rows = rows * buckets
    blocks = WORK if chips % WORK == 0 else 1
    steps = chips // blocks
    work = blocks * tile
    planes_of = [[CORES * c + k for c in range(chips)] for k in range(CORES)]
    across = partial(
        lax.all_to_all, axis_name="seq", split_axis=0, concat_axis=0, tiled=True,
        axis_index_groups=planes_of,
    )
    core_swap = partial(
        lax.ppermute, axis_name="seq", perm=[(i, i ^ 1) for i in range(seq_count)]
    )
    head_swap = partial(lax.ppermute, axis_name="head", perm=[(0, 1), (1, 0)])
    def in_order(mine, other, axis):
        first = jnp.where(core == 0, mine, other)
        return jnp.concatenate([first, jnp.where(core == 0, other, mine)], axis=axis)

    low_qkv = qkv_weight.astype(bf16).reshape(3, own_rows, CORES, feats)
    pick = partial(lax.dynamic_index_in_dim, low_qkv, axis=2, keepdims=False)
    by_rows = lambda part: jnp.transpose(part, (1, 0, 2)).reshape(own_rows, 3 * feats)
    qkv_mine, qkv_give = by_rows(pick(core)), by_rows(pick(1 - core))
    chip_rows = in_order(qkv_mine, core_swap(qkv_give), 0)

    def ring(value, steps, hold):
        moved, found, turns = [value, value], [value], [0]
        for step in range(1, steps + 1):
            moved = [lax.ppermute(v, "seq", p) for v, p in zip(moved, (ahead, behind))]
            if hold:
                moved = list(lax.optimization_barrier(tuple(moved)))
            found += moved
            turns += [chips - step, step]
        return moved, found, turns

    ringed = chips == len(RING)
    if ringed:
        order = np.array(RING)
        seats = np.argsort(order)
        ahead = [
            (CORES * order[i] + k, CORES * order[(i + 1) % chips] + k)
            for i in range(chips)
            for k in range(CORES)
        ]
        behind = [(b, a) for a, b in ahead]
        quarter = CORES * own_rows // 4
        third = feats
        rest = chip_rows[3 * quarter :]
        rest = jnp.concatenate([rest[:, third * j : third * (j + 1)] for j in range(3)], axis=0)
        packed = jnp.concatenate([chip_rows[: 3 * quarter], rest], axis=1)
        block = jnp.concatenate([tokens, packed], axis=0)
        moved, block_parts, turns = ring(block, chips // 2 - 1, True)
        last_part = block_parts[2][0:8, 0:128]
        far_tokens, far_rows = lax.optimization_barrier(
            (moved[0][:tok_rows], moved[1][tok_rows:])
        )
        across_tokens = lax.ppermute(far_tokens, "seq", ahead)
        across_rows = lax.ppermute(far_rows, "seq", behind)
        across_tokens, across_rows = lax.optimization_barrier((across_tokens, across_rows))
        turns.append(chips // 2)
        token_parts = block_parts + [across_tokens]
        token_parts = [p[None] for p in token_parts + [core_swap(part) for part in token_parts]]
        weight_parts = [p[None] for p in block_parts + [across_rows]]
        weight_spots = [tok_rows] * (chips - 1) + [0]
        spot_of = np.array([[order[(seats[c] + t) % chips] for t in turns] for c in range(chips)])
        spot_of = np.repeat(spot_of, CORES, axis=0)
        core_of = np.arange(seq_count)[:, None] % CORES
        place_of = [CORES * spot_of + core_of, CORES * spot_of + 1 - core_of, spot_of]
    else:
        token_parts = [lax.all_gather(tokens, "seq", axis=0, tiled=False)]
        chip_rows = jnp.pad(chip_rows, ((0, 0), (0, width - 3 * feats)))
        weight_parts = [
            lax.all_gather(chip_rows, "seq", axis=0, tiled=False, axis_index_groups=planes_of)
        ]
        weight_spots = [0]
        place_of = [np.zeros((seq_count, 2))]
        last_part = token_parts[0]
    parts = len(token_parts)
    weight_count = len(weight_parts)
    device = np.arange(seq_count)[:, None]
    facts = np.concatenate([device // CORES, device % CORES, 0 * device] + place_of, axis=1)
    facts = np.stack([facts + k * (np.arange(facts.shape[1]) == 2) for k in range(2)])
    facts = lax.dynamic_slice(
        jnp.asarray(facts.astype(np.int32)), (side, place, 0), (1, 1, facts.shape[2])
    )
    spots = jnp.concatenate([doc_lengths[0:1], facts.reshape(-1)])

    smem = pl.BlockSpec(memory_space=pltpu.SMEM)
    anywhere = pl.BlockSpec(memory_space=pl.ANY)
    params = pltpu.CompilerParams(
        dimension_semantics=("arbitrary",), vmem_limit_bytes=VMEM_LIMIT
    )
    shape = jax.ShapeDtypeStruct

    def full(value):
        return pl.BlockSpec(value.shape, lambda i: (0,) * len(value.shape))

    def piped(kernel, name, outs, args, specs=None):
        if specs is None:
            specs = [None] * len(args)
        specs = [
            (smem if arg is spots else full(arg)) if spec is None else spec
            for spec, arg in zip(specs, args)
        ]
        return pl.pallas_call(
            kernel,
            grid=(1,),
            in_specs=specs,
            out_specs=[full(o) for o in outs],
            out_shape=outs,
            compiler_params=params,
            name=name,
        )(*args)

    inside = pl.BlockSpec(memory_space=pltpu.VMEM)
    in_vmem = lambda value: pltpu.with_memory_space_constraint(value, pltpu.VMEM)
    small = pltpu.CompilerParams(
        dimension_semantics=("arbitrary",), vmem_limit_bytes=SMALL_LIMIT
    )

    def once(kernel, name, outs, args, after=(), outside=(), blocks={}, limit=SMALL_LIMIT):
        specs, values = [], []
        for i, arg in enumerate(args):
            plain = arg is spots or i in blocks
            specs.append(smem if arg is spots else blocks.get(i, inside))
            if i in blocks:
                arg = pltpu.with_memory_space_constraint(arg, pltpu.HBM)
            values.append(arg if plain else in_vmem(arg))
        for arg in after:
            specs.append(anywhere)
            values.append(arg)
        return pl.pallas_call(
            kernel,
            grid=(1,) if blocks else (),
            in_specs=specs,
            out_specs=[inside] * len(outs),
            out_shape=[
                (pltpu.HBM if i in outside else pltpu.VMEM)(o.shape, o.dtype)
                for i, o in enumerate(outs)
            ],
            compiler_params=pltpu.CompilerParams(vmem_limit_bytes=limit),
            name=name,
        )(*values)

    own_planes = lax.dynamic_slice(
        plane_bits, (spot * hashes, 0, core * heads, 0), (hashes, bits, heads, head_dim)
    )
    scale = sharpness / math.sqrt(head_dim)
    signs = scale * (2 * own_planes - 1).astype(f32)
    bit_w = jnp.pad(
        jnp.transpose(signs, (2, 1, 0, 3)), ((0, 0), (0, 0), (0, rows - hashes), (0, 0))
    )
    bit_w = bit_w.reshape(heads, bits * rows, head_dim).astype(bf16)
    bit_wt = jnp.transpose(bit_w, (0, 2, 1))

    (second_send,) = piped(
        pack_kernel, "pack",
        [shape((own_rows, 2 * ff + group_feats), bf16)],
        [spots, up_weight, down_weight.T, out_weight.T, last_part, bit_w],
        [None] * 4 + [anywhere] * 2,
    )
    ff_all = lax.all_gather(second_send, "seq", axis=0, tiled=True)

    def resident(*dims):
        return pl.BlockSpec(dims, lambda p, i: (0,) * len(dims), pipeline_mode=pl.Buffered(1))

    def stepped(phase, *dims):
        def place(p, i):
            rest = steps - 1 if phase == 0 else 0
            return (jnp.where(p == phase, i, rest),) + (0,) * (len(dims) - 1)

        return pl.BlockSpec(dims, place)

    hash_params = pltpu.CompilerParams(
        dimension_semantics=("arbitrary", "arbitrary"), vmem_limit_bytes=VMEM_LIMIT
    )
    num_parts, q_unit, k_unit, values, inverses, tables, counts, qkv_all = pl.pallas_call(
        partial(forward_kernel, hashes, bits, rows, work, steps, heads, parts, weight_spots),
        grid=(2, steps),
        in_specs=[
            smem,
            *[anywhere] * (parts + weight_count),
            resident(*bit_w.shape),
        ],
        out_specs=[
            stepped(1, blocks, feats, tile),
            resident(feats, total),
            resident(feats, total),
            resident(feats, total + 256),
            resident(16, total),
            resident(heads, code_rows, 2 * head_dim),
            resident(heads, 8, code_rows),
            resident(width, 3 * feats),
        ],
        out_shape=[
            shape((chips, feats, tile), bf16),
            shape((feats, total), bf16),
            shape((feats, total), bf16),
            shape((feats, total + 256), bf16),
            shape((16, total), f32),
            shape((heads, code_rows, 2 * head_dim), bf16),
            shape((heads, 8, code_rows), f32),
            shape((width, 3 * feats), bf16),
        ],
        scratch_shapes=[
            pltpu.VMEM((heads, code_rows, 2 * head_dim + 16), f32),
            pltpu.VMEM((heads, code_rows, work), bf16),
            pltpu.VMEM((3 * feats, width), bf16),
            pltpu.VMEM((heads, 2 * head_dim, code_rows), bf16),
            pltpu.VMEM((seq_count, tok_rows, width), bf16),
            pltpu.VMEM((chips, weight_parts[-1].shape[1], width), bf16),
            pltpu.SemaphoreType.DMA((parts + weight_count,)),
        ],
        compiler_params=hash_params,
        name="hash_forward",
    )(spots, *token_parts, *weight_parts, bit_w)
    num_got = across(num_parts)

    own_taps = lax.dynamic_slice(conv_taps, (core * heads, 0), (heads, taps))
    lead = tile + 128 - rim
    bases = jnp.zeros((heads, 8, tile + 256), f32)
    bases = bases.at[:, 0, lead : lead + taps].set(own_taps[:, ::-1])
    conv, window_values = once(
        partial(conv_kernel, tile, heads), "conv_forward",
        [shape((feats, tile), f32), shape((feats, tile + 256), bf16)],
        [spots, values, bases],
    )

    chip_buckets = buckets // chips
    sum_rows = 4 * width // tile
    count_rows = 2 * heads * code_rows // tile
    extra_rows = -(-(sum_rows + count_rows) // 16) * 16

    keep, give, numerator = once(
        partial(context_kernel, heads), "context",
        [shape((feats, tok_rows), bf16), shape((feats, tok_rows), bf16), shape((feats, tile), f32)],
        [spots, num_got, conv],
    )
    context, mixer_part = once(
        mixer_kernel, "mixer",
        [shape((tok_rows, group_feats), bf16), shape((tok_rows, width), bf16)],
        [spots, keep, core_swap(give), ff_all],
        blocks={3: pl.BlockSpec((width, group_feats), lambda i: (0, 2 * ff // group_feats))},
    )
    ff_all, mixer_part = lax.optimization_barrier((ff_all, mixer_part))
    first_hat, first_inverse, hidden, active, feed_part = once(
        hidden_kernel, "feed_forward",
        [
            shape((tok_rows, width), f32),
            shape((tok_rows, 1), f32),
            shape((tok_rows, ff), f32),
            shape((tok_rows, ff), bf16),
            shape((tok_rows, width), bf16),
        ],
        [tokens, mixer_part, head_swap(mixer_part), norm_params, ff_all],
    )
    block_out, grad_second, feed_low, slope_low, first_part, second_sums = once(
        feed_kernel, "feed_back",
        [
            shape((tok_rows, width), f32),
            shape((tok_rows, width), f32),
            shape((tok_rows, width), bf16),
            shape((tok_rows, ff), bf16),
            shape((tok_rows, width), bf16),
            shape((2, width), f32),
        ],
        [first_hat, hidden, feed_part, head_swap(feed_part), cotangent, norm_params, ff_all],
        outside=(0,),
    )
    grad_mixer, mixer_low, keep, give, norm_sums = once(
        mixer_back_kernel, "mixer_back",
        [
            shape((tok_rows, width), f32),
            shape((tok_rows, width), bf16),
            shape((feats, tok_rows), f32),
            shape((feats, tok_rows), f32),
            shape((4, width), f32),
        ],
        [
            spots, grad_second, first_part, head_swap(first_part), first_hat, first_inverse,
            norm_params, ff_all, second_sums,
        ],
    )
    gnum_send, grad_low, grad_high = once(
        partial(attention_back_kernel, heads), "attention_back",
        [
            shape((feats + extra_rows, tile), bf16),
            shape((feats, tok_rows), bf16),
            shape((feats, tok_rows), bf16),
        ],
        [spots, keep, core_swap(give), numerator, norm_sums, counts],
    )
    conv_grad, tap_parts = once(
        partial(conv_back_kernel, tile, taps, heads), "conv_backward",
        [shape((feats, 3 * tile), f32), shape((heads, 8, 128), f32)],
        [spots, window_values, grad_low, grad_high, bases],
    )
    if ringed:
        moved, gnum_parts, unused = ring(gnum_send, 1, False)
        *moved, tap_parts = lax.optimization_barrier((*moved, tap_parts))
        gnum_parts = [gnum_send]
        for step in range(2, chips // 2 + 1):
            gnum_parts += moved
            moved = [
                lax.ppermute(v, "seq", p)
                for v, p in zip(moved, (ahead, behind))
                if p is ahead or 2 * step < chips
            ]
        gnum_parts = [p[None] for p in gnum_parts + moved]
    else:
        gnum_parts = [
            lax.all_gather(gnum_send, "seq", axis=0, tiled=False, axis_index_groups=planes_of)
        ]
    gnum_count = len(gnum_parts)

    columns = 2 * ff + group_feats
    feed_grads = pl.pallas_call(
        feed_grad_kernel,
        grid=(1,),
        in_specs=[inside] * 5,
        out_specs=pl.BlockSpec((width, 2 * ff), lambda i: (0, 0)),
        out_shape=pltpu.HBM((width, columns), bf16),
        compiler_params=small,
        name="feed_grads",
    )(*[in_vmem(v) for v in (first_hat, norm_params, slope_low, feed_low, active)])
    big_grad = pl.pallas_call(
        out_grad_kernel,
        grid=(1,),
        in_specs=[inside, inside, anywhere],
        out_specs=pl.BlockSpec((width, group_feats), lambda i: (0, 2 * ff // group_feats)),
        out_shape=pltpu.HBM((width, columns), bf16),
        input_output_aliases={2: 0},
        compiler_params=small,
        name="out_grads",
    )(in_vmem(mixer_low), in_vmem(context), feed_grads)
    big_owned = lax.psum_scatter(big_grad, "seq", scatter_dimension=0, tiled=True)

    qkv_send, back_keep, back_give, extras = pl.pallas_call(
        partial(backward_kernel, hashes, bits, rows, work, steps, heads, own_rows, parts, gnum_count),
        grid=(2, steps),
        in_specs=[
            smem,
            *[anywhere] * parts,
            *[inside] * gnum_count,
            resident(*qkv_all.shape),
            resident(*bit_w.shape),
            resident(*bit_wt.shape),
            resident(feats, total),
            resident(feats, total),
            resident(feats, total + 256),
            resident(16, total),
            resident(heads, code_rows, 2 * head_dim),
            resident(feats, 3 * tile),
            resident(*tap_parts.shape),
        ],
        out_specs=[
            resident(chips, CORES * own_rows, 3 * feats + 64),
            stepped(1, blocks, width, tok_rows),
            stepped(1, blocks, width, tok_rows),
            resident(chips, extra_rows, tile),
        ],
        out_shape=[
            shape((chips, CORES * own_rows, 3 * feats + 64), bf16),
            shape((chips, width, tok_rows), bf16),
            shape((chips, width, tok_rows), bf16),
            shape((chips, extra_rows, tile), bf16),
        ],
        scratch_shapes=[
            pltpu.VMEM((heads, code_rows, 2 * head_dim), f32),
            pltpu.VMEM((heads, code_rows, work), bf16),
            pltpu.VMEM((feats, total), bf16),
            pltpu.VMEM((3 * feats, width), f32),
            pltpu.VMEM((heads, 2 * head_dim, code_rows), bf16),
            pltpu.VMEM((heads, code_rows, 2 * head_dim), bf16),
            pltpu.VMEM((seq_count, tok_rows, width), bf16),
            pltpu.VMEM((chips, feats, tile), bf16),
            pltpu.SemaphoreType.DMA((parts,)),
        ],
        compiler_params=hash_params,
        name="hash_backward",
    )(
        spots, *token_parts, *[in_vmem(p) for p in gnum_parts], qkv_all, bit_w, bit_wt,
        q_unit, k_unit, values, inverses, tables, conv_grad, tap_parts,
    )

    half = width // 2
    group = chips // 2
    per_chip = lambda *dims: pl.BlockSpec((group,) + dims, lambda i: (i, 0, 0))
    keep, give = pl.pallas_call(
        chip_sum_kernel,
        grid=(2,),
        in_specs=[smem, per_chip(width, tok_rows), per_chip(width, tok_rows)],
        out_specs=[per_chip(half, tok_rows), per_chip(half, tok_rows)],
        out_shape=[shape((chips, half, tok_rows), bf16)] * 2,
        compiler_params=params,
        name="chip_sum",
    )(spots, back_keep, core_swap(back_give))
    *pair_sums, pair_done = once(
        pair_sum_kernel, "pair_sum",
        [shape((half, tok_rows) if ringed else (chips, half, tok_rows), bf16)]
        * (chips if ringed else 1)
        + [shape((8, 128), f32)],
        [spots, keep, head_swap(give)],
        outside=tuple(range(1, chips)) if ringed else (),
    )
    qkv_got = across(qkv_send)
    if ringed:
        back_got = [pair_sums[0]]
        for d in range(1, chips):
            perm = [(CORES * c + k, CORES * (c ^ d) + k) for c in range(chips) for k in range(CORES)]
            back_got.append(lax.ppermute(pair_sums[d], "seq", perm))
        qkv_got, *tied = lax.optimization_barrier((qkv_got, *back_got[1:5]))
        back_got = [back_got[0]] + tied + back_got[1 + len(tied) :]
        back_got = [p[None] for p in back_got]
    else:
        back_got = [across(pair_sums[0])]

    qkv_mine, qkv_give = once(
        weight_sum_kernel, "weight_sum",
        [shape((own_rows, 3 * feats + 64), f32)] * 2,
        [spots, qkv_got],
        after=[pair_done],
    )
    qkv_other = core_swap(qkv_give)

    extras = extras.astype(f32)
    norm_half = jnp.sum(extras[:, :sum_rows], axis=0)
    count_half = extras[:, sum_rows : sum_rows + count_rows]
    count_half = count_half.reshape(chips, heads, 2, chips, CORES, chip_buckets // CORES, rows)
    count_half = lax.dynamic_index_in_dim(count_half, spot, 3, keepdims=False)
    count_half = jnp.transpose(count_half[..., :hashes], (3, 0, 2, 5, 1, 4))
    count_mine = lax.dynamic_index_in_dim(count_half, core, 0, keepdims=False)
    count_give = lax.dynamic_index_in_dim(count_half, 1 - core, 0, keepdims=False)
    tap_first = jnp.where(core == 0, qkv_mine[:heads], qkv_give[:heads])
    tap_half = tap_first[:, 3 * feats : 3 * feats + taps]
    swapped = core_swap(
        jnp.concatenate([norm_half.reshape(-1), count_give.reshape(-1), tap_half.reshape(-1)])
    )
    norm_size, count_size = norm_half.size, count_give.size

    norm_grad = norm_half + swapped[:norm_size].reshape(norm_half.shape)
    norm_grad = jnp.transpose(
        norm_grad.reshape(width // tile, 4, tile), (1, 0, 2)
    ).reshape(4, width)
    count_other = swapped[norm_size : norm_size + count_size].reshape(count_mine.shape)
    occupancy = jnp.transpose(
        in_order(count_mine, count_other, 3), (1, 0, 2, 3, 4)
    ).reshape(2, hash_count, group_heads, buckets // seq_count)
    occupancy = occupancy * (buckets / (tok_rows * seq_count))
    conv_tap_grad = in_order(tap_half, swapped[norm_size + count_size :].reshape(heads, taps), 0)

    flag = shape((8, 128), f32)
    matrix = lambda value: [pltpu.HBM(value.shape, f32)] * 3 + [pltpu.HBM(value.shape, bf16)]
    (
        up_new, up_first_new, up_second_new, up_copy,
        down_new, down_first_new, down_second_new, down_copy,
        out_new, out_first_new, out_second_new, out_copy, big_done,
    ) = piped(
        big_adam_kernel, "big_adam",
        matrix(up_weight) + matrix(down_weight.T) + matrix(out_weight.T) + [flag],
        [
            big_owned, up_weight, up_first, up_second,
            down_weight.T, down_first.T, down_second.T,
            out_weight.T, out_first.T, out_second.T,
        ],
    )
    qkv_new, qkv_first_new, qkv_second_new, qkv_copy = piped(
        qkv_adam_kernel, "qkv_adam", matrix(qkv_weight),
        [spots, qkv_mine, qkv_other, qkv_weight, qkv_first, qkv_second],
    )
    norm_new, norm_first_new, norm_second_new = adam_step(
        norm_params, norm_first, norm_second, norm_grad, 0.3
    )
    conv_new, conv_first_new, conv_second_new = adam_step(
        conv_taps, conv_first, conv_second, conv_tap_grad, CONV ** (-0.5)
    )
    (back_low,) = once(
        back_sum_kernel, "back_sum",
        [shape((half, tok_rows), bf16)],
        back_got,
        after=[big_done],
    )
    (tokens_grad,) = once(
        final_kernel, "tokens_grad",
        [shape((tok_rows, width), f32)],
        [spots, back_low, head_swap(back_low), grad_mixer],
        outside=(0,),
    )
    return (
        block_out,
        tokens_grad,
        occupancy,
        qkv_new,
        qkv_first_new,
        qkv_second_new,
        qkv_copy,
        out_new.T,
        out_first_new.T,
        out_second_new.T,
        out_copy.T,
        up_new,
        up_first_new,
        up_second_new,
        up_copy,
        down_new.T,
        down_first_new.T,
        down_second_new.T,
        down_copy.T,
        norm_new,
        norm_first_new,
        norm_second_new,
        conv_new,
        conv_first_new,
        conv_second_new,
    )


def solution(mesh):
    in_specs = (
        P("seq", None),
        P("seq", None),
        P(),
        P(None, None, "head", None),
        P(None, "seq", "head"),
        P(None, "seq", "head"),
        P(None, "seq", "head"),
        P("head", "seq"),
        P("head", "seq"),
        P("head", "seq"),
        P("seq", "head"),
        P("seq", "head"),
        P("seq", "head"),
        P("head", "seq"),
        P("head", "seq"),
        P("head", "seq"),
        P(),
        P(),
        P(),
        P("head", None),
        P("head", None),
        P("head", None),
    )
    out_specs = (
        P("seq", None),
        P("seq", None),
        P(None, None, "head", "seq"),
        P(None, "seq", "head"),
        P(None, "seq", "head"),
        P(None, "seq", "head"),
        P(None, "seq", "head"),
        P("head", "seq"),
        P("head", "seq"),
        P("head", "seq"),
        P("head", "seq"),
        P("seq", "head"),
        P("seq", "head"),
        P("seq", "head"),
        P("seq", "head"),
        P("head", "seq"),
        P("head", "seq"),
        P("head", "seq"),
        P("head", "seq"),
        P(),
        P(),
        P(),
        P("head", None),
        P("head", None),
        P("head", None),
    )
    return jax.shard_map(
        on_device, mesh=mesh, in_specs=in_specs, out_specs=out_specs, check_vma=False
    )
```

```python
from functools import partial
import math

import jax
import jax.numpy as jnp
import numpy as np
from jax import lax
from jax.experimental import pallas as pl
from jax.experimental.pallas import tpu as pltpu
from jax.sharding import PartitionSpec as P

D = 768
FF = 3072
CONV = 33
STEP = 7
CORES = 2

sharpness = 4.0
norm_eps = 1e-06
layer_eps = 1e-05
beta_one = 0.9
beta_two = 0.999
adam_eps = 1e-08
decay_rate = 0.01
highest = lax.Precision.HIGHEST
f32 = jnp.float32
bf16 = jnp.bfloat16
VMEM_LIMIT = 56 * 1024 * 1024
SMALL_LIMIT = 16 * 1024 * 1024
WORK = 2
SPOTS = 4
RING = (0, 2, 4, 6, 7, 5, 3, 1)


def nn(a, b):
    return lax.dot_general(a, b, (((1,), (0,)), ((), ())), preferred_element_type=f32)


def nt(a, b):
    return lax.dot_general(a, b, (((1,), (1,)), ((), ())), preferred_element_type=f32)


def normalize(source):
    centered = source - jnp.mean(source, axis=-1, keepdims=True)
    inverse = lax.rsqrt(jnp.mean(centered * centered, axis=-1, keepdims=True) + layer_eps)
    return (centered * inverse, inverse)


def norm_back(grad, normed, inverse, gain):
    scaled = grad * gain
    inner = (
        scaled
        - jnp.mean(scaled, axis=-1, keepdims=True)
        - normed * jnp.mean(scaled * normed, axis=-1, keepdims=True)
    )
    gains = jnp.sum(grad * normed, axis=0, keepdims=True)
    return (inverse * inner, gains, jnp.sum(grad, axis=0, keepdims=True))


def adam_step(weight, first, second, grad, rate):
    first_new = beta_one * first + (1.0 - beta_one) * grad
    second_new = beta_two * second + (1.0 - beta_two) * grad * grad
    fix_one = 1.0 - beta_one**STEP
    fix_two = 1.0 - beta_two**STEP
    update = first_new / fix_one / (jnp.sqrt(second_new / fix_two) + adam_eps) + decay_rate * weight
    return (weight - rate * update, first_new, second_new)


def head_units(source):
    inverse = lax.rsqrt(jnp.mean(source * source, axis=0, keepdims=True) + norm_eps)
    return source * inverse, inverse


def seg_rows(limit, start, width):
    pos = start + lax.broadcasted_iota(jnp.int32, (1, width), 1)
    late = (pos >= limit).astype(f32)
    return 1.0 - late, late


def masked_pair(rows, early, late):
    return jnp.concatenate([rows * early, rows * late], axis=0).astype(bf16)


def flip(value):
    return jnp.transpose(value.astype(f32)).astype(bf16)


def bit_factors(bit_planes, unit, bits, hashes, rows):
    z = nn(bit_planes, unit)
    decay = jnp.exp(-jnp.abs(z))
    large = 1.0 / (1.0 + decay)
    small = decay * large
    ones = jnp.where(z >= 0.0, large, small)
    zeros = jnp.where(z >= 0.0, small, large)
    ones = [ones[j * rows : (j + 1) * rows] for j in range(bits)]
    zeros = [zeros[j * rows : (j + 1) * rows] for j in range(bits)]
    if rows != hashes:
        live = lax.broadcasted_iota(jnp.int32, ones[0].shape, 0) < hashes
        return ones, [jnp.where(live, ones[0], 0.0)] + ones[1:], [
            jnp.where(live, zeros[0], 0.0)
        ] + zeros[1:]
    return ones, ones, zeros


def products(ones, zeros, first, last):
    found = [zeros[first], ones[first]]
    for j in range(first + 1, last):
        found = [part * zeros[j] for part in found] + [part * ones[j] for part in found]
    return found


def code_parts(bit_planes, unit, bits, hashes, rows):
    plain, ones, zeros = bit_factors(bit_planes, unit, bits, hashes, rows)
    return plain, products(ones, zeros, 0, 3), products(ones, zeros, 3, bits)


def store_codes(codes_ref, head, lows, highs, rows):
    for g, high in enumerate(highs):
        for s in range(0, len(lows), 2):
            spot = (g * len(lows) + s) * rows
            pair = jnp.concatenate([lows[s] * high, lows[s + 1] * high], axis=0)
            codes_ref[head, spot : spot + 2 * rows, :] = pair.astype(bf16)


def token_copies(spots_ref, part_refs, tok_ref, sem_ref):
    return [
        pltpu.make_async_copy(
            ref.at[:, pl.ds(0, tok_ref.shape[1])],
            tok_ref.at[pl.ds(spots_ref[SPOTS + i], ref.shape[0])],
            sem_ref.at[i],
        )
        for i, ref in enumerate(part_refs)
    ]


def forward_kernel(
    hashes, bits, rows, tile, steps, heads, parts, weight_spots, spots_ref, *refs
):
    part_refs, refs = refs[:parts], refs[parts:]
    weight_refs, refs = refs[: len(weight_spots)], refs[len(weight_spots) :]
    bit_ref, num_ref, qu_ref, ku_ref, v_ref, inv_ref, table_ref, count_ref, w_ref = refs[:9]
    acc_ref, codes_ref, wt_ref, table_t_ref, tok_ref, got_ref, sem_ref = refs[9:]
    limit = spots_ref[0]
    phase, i = pl.program_id(0), pl.program_id(1)
    feats = heads * 64
    chips = num_ref.shape[0]
    block = tile // chips
    start = pl.multiple_of(i * tile, tile)
    span = pl.ds(start, tile)
    early, late = seg_rows(limit, start, tile)

    @pl.when((phase == 0) & (i == 0))
    def _():
        copies = token_copies(spots_ref, part_refs, tok_ref, sem_ref)
        loads = [
            pltpu.make_async_copy(
                ref.at[:, pl.ds(weight_spots[i], got_ref.shape[1])],
                got_ref.at[pl.ds(spots_ref[SPOTS + parts + i], ref.shape[0])],
                sem_ref.at[parts + i],
            )
            for i, ref in enumerate(weight_refs)
        ]
        for copy in loads + copies:
            copy.start()
        acc_ref[...] = jnp.zeros_like(acc_ref)
        v_ref[:, 0:128] = jnp.zeros((feats, 128), bf16)
        v_ref[:, 128 + steps * tile :] = jnp.zeros((feats, 128), bf16)
        inv_ref[...] = jnp.zeros_like(inv_ref)
        for copy in loads:
            copy.wait()
        got = got_ref[...].astype(f32)
        if len(weight_refs) > 1:
            quarter = got.shape[1] // 3
            rest = [got[:, quarter * j : quarter * (j + 1), 3 * feats :] for j in range(3)]
            got = jnp.concatenate([got[:, :, : 3 * feats], jnp.concatenate(rest, axis=2)], axis=1)
        got = got.reshape(got.shape[0] * got.shape[1], got.shape[2])[:, : 3 * feats].astype(bf16)
        w_ref[...] = got
        wt_ref[...] = flip(got)
        for copy in copies:
            copy.wait()

    @pl.when(phase == 0)
    def _():
        devices, tok_rows, width = tok_ref.shape
        here = pl.ds(i * (devices // steps), devices // steps)
        proj = nt(wt_ref[...], tok_ref[here].reshape(tile, width))
        values = proj[2 * feats :].astype(bf16)
        v_ref[:, pl.ds(pl.multiple_of(start + 128, 128), tile)] = values
        marks = jnp.concatenate([early, late, jnp.zeros((14, tile), f32)], axis=0).astype(bf16)
        units = []
        for h in range(heads):
            mine = slice(64 * h, 64 * (h + 1))
            q_unit, q_inv = head_units(proj[mine])
            k_unit, k_inv = head_units(proj[feats + 64 * h : feats + 64 * (h + 1)])
            units.append(k_unit.astype(bf16))
            qu_ref[mine, span] = q_unit.astype(bf16)
            ku_ref[mine, span] = units[h]
            inv_ref[h : h + 1, span] = q_inv
            inv_ref[8 + h : 9 + h, span] = k_inv
        for h in range(heads):
            plain, lows, highs = code_parts(bit_ref[h], units[h], bits, hashes, rows)
            store_codes(codes_ref, h, lows, highs, rows)
        for h in range(heads):
            pair = masked_pair(values[64 * h : 64 * (h + 1)].astype(f32), early, late)
            pair = jnp.concatenate([pair, marks], axis=0)
            acc_ref[h] += nt(codes_ref[h], pair)

    @pl.when((phase == 1) & (i == 0))
    def _():
        for h in range(heads):
            table = acc_ref[h, :, 0:128].astype(bf16)
            table_ref[h] = table
            table_t_ref[h] = flip(table)
            counts = jnp.concatenate(
                [acc_ref[h, :, 128:144], jnp.zeros((acc_ref.shape[1], 112), f32)], axis=1
            )
            count_ref[h] = jnp.transpose(counts)[0:8]

    @pl.when(phase == 1)
    def _():
        for h in range(heads):
            unit = qu_ref[64 * h : 64 * (h + 1), span]
            plain, lows, highs = code_parts(bit_ref[h], unit, bits, hashes, rows)
            store_codes(codes_ref, h, lows, highs, rows)
        for h in range(heads):
            mine = slice(64 * h, 64 * (h + 1))
            both = nn(table_t_ref[h], codes_ref[h])
            low = (both[0:64] * early + both[64:128] * late).astype(bf16)
            for c in range(chips):
                num_ref[c, mine, :] = low[:, c * block : (c + 1) * block]


def soften(bit_planes, unit, slopes, codes_ref, head, bits, hashes, rows):
    plain, lows, highs = code_parts(bit_planes, unit, bits, hashes, rows)
    by_low = [None] * len(lows)
    by_bit = [None] * (bits - 3)
    for g, high in enumerate(highs):
        row = None
        for s in range(0, len(lows), 2):
            spot = (g * len(lows) + s) * rows
            parts = [lows[s] * high, lows[s + 1] * high]
            codes_ref[head, spot : spot + 2 * rows, :] = jnp.concatenate(parts, axis=0).astype(bf16)
            for k in range(2):
                term = parts[k] * slopes[spot + k * rows : spot + (k + 1) * rows]
                by_low[s + k] = term if by_low[s + k] is None else by_low[s + k] + term
                row = term if row is None else row + term
        for j in range(bits - 3):
            if (g >> j) & 1:
                by_bit[j] = row if by_bit[j] is None else by_bit[j] + row
    pairs = [sum(part for s, part in enumerate(by_low) if (s >> j) & 1) for j in range(3)]
    whole = sum(by_low)
    slopes = [part - plain[j] * whole for j, part in enumerate(pairs + by_bit)]
    return jnp.concatenate(slopes, axis=0).astype(bf16)


def unit_back(grad, unit, inverse):
    unit = unit.astype(f32)
    inner = jnp.mean(grad * unit, axis=0, keepdims=True)
    return inverse * (grad - unit * inner)


def backward_kernel(
    hashes, bits, rows, tile, steps, heads, own_rows, parts, gnum_parts, spots_ref, *refs
):
    part_refs, refs = refs[:parts], refs[parts:]
    gnum_refs, refs = refs[:gnum_parts], refs[gnum_parts:]
    w_ref, bit_ref, bit_t_ref, qu_ref, ku_ref, v_ref, inv_ref, table_ref = refs[:8]
    conv_ref, tap_ref, grad_ref, keep_ref, give_ref, extra_ref = refs[8:14]
    acc_ref, codes_ref, proj_ref, sum_ref, table_t_ref, table_g_ref = refs[14:20]
    tok_ref, gnum_ref, sem_ref = refs[20:]
    limit = spots_ref[0]
    spot = spots_ref[1]
    core = spots_ref[2]
    phase, i = pl.program_id(0), pl.program_id(1)
    devices, unused, width = tok_ref.shape
    copies = token_copies(spots_ref, part_refs, tok_ref, sem_ref)
    loads = [
        (ref, pl.ds(spots_ref[SPOTS + parts + j], ref.shape[0]))
        for j, ref in enumerate(gnum_refs)
    ]
    feats = heads * 64
    blocks = keep_ref.shape[0]
    block = tile // blocks
    tok_rows = block // CORES
    start = pl.multiple_of(i * tile, tile)
    span = pl.ds(start, tile)
    early, late = seg_rows(limit, start, tile)

    @pl.when((phase == 0) & (i == 0))
    def _():
        for copy in copies:
            copy.start()
        acc_ref[...] = jnp.zeros_like(acc_ref)
        sum_ref[...] = jnp.zeros_like(sum_ref)
        for ref, where in loads:
            gnum_ref[where] = ref[:, :feats]
            extra_ref[where] = ref[:, feats:]

    @pl.when(phase == 0)
    def _():
        spans = [slice(64 * h, 64 * (h + 1)) for h in range(heads)]
        pairs, grads, slopes = [], [], []
        for mine in spans:
            gnum = jnp.concatenate([gnum_ref[i * blocks + c, mine, :] for c in range(blocks)], axis=1)
            pairs.append(masked_pair(gnum.astype(f32), early, late))
        for h, mine in enumerate(spans):
            slopes.append(
                soften(
                    bit_ref[h], qu_ref[mine, span], nn(table_ref[h], pairs[h]), codes_ref, h,
                    bits, hashes, rows,
                )
            )
        for h in range(heads):
            acc_ref[h] += nt(codes_ref[h], pairs[h])
        for h, mine in enumerate(spans):
            grad = nn(bit_t_ref[h], slopes[h])
            grad = unit_back(grad, qu_ref[mine, span], inv_ref[h : h + 1, span])
            proj_ref[mine, span] = grad.astype(bf16)

    @pl.when((phase == 1) & (i == 0))
    def _():
        for copy in copies:
            copy.wait()
        for h in range(heads):
            table_g_ref[h] = acc_ref[h].astype(bf16)
            table_t_ref[h] = flip(table_g_ref[h])

    @pl.when(phase == 1)
    def _():
        conv = []
        for c in range(blocks):
            step = i * blocks + c - spot + 1
            near = ((step >= 0) & (step <= 2)).astype(f32)
            step = jnp.clip(step, 0, 2)
            conv.append(conv_ref[:, pl.ds(pl.multiple_of(step * block, block), block)] * near)
        conv = jnp.concatenate(conv, axis=1)
        spans = [slice(64 * h, 64 * (h + 1)) for h in range(heads)]
        slopes, parts = [], []
        for h, mine in enumerate(spans):
            values = v_ref[mine, pl.ds(pl.multiple_of(start + 128, 128), tile)]
            pair = masked_pair(values.astype(f32), early, late)
            slopes.append(
                soften(
                    bit_ref[h], ku_ref[mine, span], nn(table_g_ref[h], pair), codes_ref, h,
                    bits, hashes, rows,
                )
            )
        for h, mine in enumerate(spans):
            both = nn(table_t_ref[h], codes_ref[h])
            value_grad = both[0:64] * early + both[64:128] * late + conv[mine]
            grad = nn(bit_t_ref[h], slopes[h])
            grad = unit_back(grad, ku_ref[mine, span], inv_ref[8 + h : 9 + h, span])
            parts.append((grad.astype(bf16), value_grad.astype(bf16)))
        full = jnp.concatenate(
            [proj_ref[:, span]] + [part[0] for part in parts] + [part[1] for part in parts], axis=0
        )
        here = pl.ds(i * (devices // steps), devices // steps)
        sum_ref[...] += nn(full, tok_ref[here].reshape(tile, width))
        part = nn(w_ref[...], full)
        for c in range(blocks):
            first = part[:, c * block : c * block + tok_rows]
            second = part[:, c * block + tok_rows : (c + 1) * block]
            keep_ref[c] = jnp.where(core == 0, first, second).astype(bf16)
            give_ref[c] = jnp.where(core == 0, second, first).astype(bf16)

    @pl.when((phase == 1) & (i == steps - 1))
    def _():
        grad = jnp.transpose(sum_ref[...])
        chips = grad_ref.shape[0]
        grad_ref[:, :, 0 : heads * 192] = grad.reshape(
            chips, CORES * own_rows, heads * 192
        ).astype(bf16)
        grad_ref[:, :, heads * 192 :] = jnp.zeros((chips, CORES * own_rows, 64), bf16)
        taps = jnp.concatenate([tap_ref[h, 0:1, 0:64] for h in range(heads)], axis=0)
        for c in range(chips):
            grad_ref[c, 0:heads, heads * 192 :] = taps.astype(bf16)


def window_same(spots_ref, tile):
    start = spots_ref[1] * tile
    width = tile + 256
    edge = lax.broadcasted_iota(jnp.int32, (width, tile), 0) + (start - 128)
    own = lax.broadcasted_iota(jnp.int32, (width, tile), 1) + start
    return (edge >= spots_ref[0]) == (own >= spots_ref[0])


def banded(base, same, tile):
    width = tile + 256
    spread = jnp.broadcast_to(base, (width, width))
    spread = pltpu.roll(spread, 0, 1, stride=1, stride_axis=0)[:, :tile]
    matrix = jnp.where(same, spread, 0.0)
    upper = matrix.astype(bf16)
    return upper, (matrix - upper.astype(f32)).astype(bf16)


def conv_kernel(tile, heads, spots_ref, values_ref, base_ref, out_ref, window_ref):
    same = window_same(spots_ref, tile)
    first = pl.multiple_of(spots_ref[1] * tile, tile)
    window = values_ref[:, pl.ds(first, tile + 256)]
    window_ref[...] = window
    for h in range(heads):
        mine = slice(64 * h, 64 * (h + 1))
        upper, lower = banded(base_ref[h, 0:1], same, tile)
        out_ref[mine] = nn(window[mine], upper) + nn(window[mine], lower)


def conv_back_kernel(
    tile, taps, heads, spots_ref, window_ref, low_ref, high_ref, base_ref, out_ref, tap_ref
):
    same = window_same(spots_ref, tile)
    width = tile + 256
    rim = taps // 2
    out_ref[...] = jnp.zeros_like(out_ref)
    pos = lax.broadcasted_iota(jnp.int32, (128, tile), 1) + spots_ref[1] * tile
    other = pos + lax.broadcasted_iota(jnp.int32, (128, tile), 0) - rim
    near = (pos >= spots_ref[0]) == (other >= spots_ref[0])

    def one(h, carry):
        mine = pl.ds(pl.multiple_of(h * 64, 64), 64)
        upper, lower = banded(base_ref[h, 0:1], same, tile)
        own = jnp.concatenate([low_ref[mine, :], high_ref[mine, :]], axis=1)
        out_ref[mine, 128 : 128 + width] = nt(own, upper) + nt(own, lower)
        values = window_ref[mine, :].astype(f32)
        own = own.astype(f32)
        sums = []
        for o in range(taps):
            moved = pltpu.roll(values, width - (128 - rim) - o, 1)[:, :tile]
            sums.append(jnp.sum(moved * own, axis=0, keepdims=True))
        sums = jnp.concatenate(sums + [jnp.zeros((128 - taps, tile), f32)], axis=0)
        total = jnp.sum(jnp.where(near, sums, 0.0), axis=1, keepdims=True)
        tap_ref[h] = jnp.transpose(jnp.broadcast_to(total, (128, 128)))[0:8]
        return carry

    lax.fori_loop(0, heads, one, 0)


def context_kernel(heads, spots_ref, got_ref, conv_ref, keep_ref, give_ref, num_ref):
    total = jnp.sum(got_ref[...].astype(f32), axis=0)
    num_ref[...] = total
    tile = total.shape[1]
    parts = [head_units(total[64 * h : 64 * (h + 1)])[0] for h in range(heads)]
    context = (jnp.concatenate(parts, axis=0) + conv_ref[...]).astype(bf16)
    first, second = context[:, : tile // CORES], context[:, tile // CORES :]

    @pl.when(spots_ref[2] == 0)
    def _():
        keep_ref[...] = first
        give_ref[...] = second

    @pl.when(spots_ref[2] != 0)
    def _():
        keep_ref[...] = second
        give_ref[...] = first


def mixer_kernel(spots_ref, keep_ref, other_ref, w_ref, context_ref, part_ref):
    keep, other = keep_ref[...].astype(f32), other_ref[...].astype(f32)
    zero = spots_ref[2] == 0
    pair = jnp.concatenate([jnp.where(zero, keep, other), jnp.where(zero, other, keep)], axis=0)
    context = jnp.transpose(pair).astype(bf16)
    context_ref[...] = context
    part_ref[...] = nt(context, w_ref[...]).astype(bf16)


def hidden_kernel(
    tok_ref, own_ref, other_ref, norm_ref, w_ref, hat_ref, inv_ref, hidden_ref, active_ref, part_ref
):
    ff = hidden_ref.shape[1]
    mixed = own_ref[...].astype(f32) + other_ref[...].astype(f32)
    hat, inverse = normalize(tok_ref[...].astype(f32) + mixed)
    hat_ref[...] = hat
    inv_ref[...] = inverse
    low = (hat * norm_ref[0:1] + norm_ref[1:2]).astype(bf16)
    hidden = nn(low, w_ref[:, :ff])
    hidden_ref[...] = hidden
    active = (0.5 * hidden * (1.0 + lax.erf(hidden * math.sqrt(0.5)))).astype(bf16)
    active_ref[...] = active
    part_ref[...] = nt(active, w_ref[:, ff : 2 * ff]).astype(bf16)


def feed_kernel(
    hat_ref, hidden_ref, own_ref, other_ref, cot_ref, norm_ref, w_ref,
    out_ref, second_ref, feed_ref, slope_ref, part_ref, sums_ref,
):
    ff = hidden_ref.shape[1]
    first_out = hat_ref[...] * norm_ref[0:1] + norm_ref[1:2]
    fed = own_ref[...].astype(f32) + other_ref[...].astype(f32)
    hat, inverse = normalize(first_out + fed)
    out_ref[...] = hat * norm_ref[2:3] + norm_ref[3:4]
    grad, gains, offsets = norm_back(cot_ref[...].astype(f32), hat, inverse, norm_ref[2:3])
    second_ref[...] = grad
    sums_ref[0:1] = gains
    sums_ref[1:2] = offsets
    low = grad.astype(bf16)
    feed_ref[...] = low
    active_grad = nn(low, w_ref[:, ff : 2 * ff])
    hidden = hidden_ref[...]
    cdf = 0.5 * (1.0 + lax.erf(hidden * math.sqrt(0.5)))
    density = jnp.exp(-0.5 * hidden * hidden) * (1.0 / math.sqrt(2.0 * math.pi))
    slope = (active_grad * (cdf + hidden * density)).astype(bf16)
    slope_ref[...] = slope
    part_ref[...] = nt(slope, w_ref[:, :ff]).astype(bf16)


def mixer_back_kernel(
    spots_ref, second_ref, own_ref, other_ref, hat_ref, inv_ref, norm_ref, w_ref, sums_ref,
    grad_ref, low_ref, keep_ref, give_ref, all_sums_ref,
):
    first = second_ref[...] + (own_ref[...].astype(f32) + other_ref[...].astype(f32))
    grad, gains, offsets = norm_back(first, hat_ref[...], inv_ref[...], norm_ref[0:1])
    grad_ref[...] = grad
    all_sums_ref[0:1] = gains
    all_sums_ref[1:2] = offsets
    all_sums_ref[2:4] = sums_ref[...]
    low = grad.astype(bf16)
    low_ref[...] = low
    half = keep_ref.shape[0]
    context = jnp.transpose(nn(low, w_ref[:, w_ref.shape[1] - CORES * half :]))
    half = context.shape[0] // CORES
    zero = spots_ref[2] == 0
    keep_ref[...] = jnp.where(zero, context[:half], context[half:])
    give_ref[...] = jnp.where(zero, context[half:], context[:half])


def attention_back_kernel(
    heads, spots_ref, keep_ref, other_ref, num_ref, sums_ref, count_ref,
    send_ref, low_ref, high_ref,
):
    zero = spots_ref[2] == 0
    keep, other = keep_ref[...], other_ref[...]
    grad = jnp.concatenate([jnp.where(zero, keep, other), jnp.where(zero, other, keep)], axis=1)
    half = keep.shape[1]
    low = grad.astype(bf16)
    low_ref[...] = low[:, :half]
    high_ref[...] = low[:, half:]
    parts = []
    for h in range(heads):
        span = slice(64 * h, 64 * (h + 1))
        attention, inverse = head_units(num_ref[span])
        inner = jnp.mean(grad[span] * attention, axis=0, keepdims=True)
        parts.append(inverse * (grad[span] - attention * inner))
    gnum = jnp.concatenate(parts, axis=0).astype(bf16)
    tile = gnum.shape[1]
    feats = 64 * heads
    pieces = sums_ref.shape[1] // tile
    counts = []
    for h in range(heads):
        for d in range(2):
            row = count_ref[h, d : d + 1, :]
            counts += [row[:, tile * i : tile * (i + 1)] for i in range(row.shape[1] // tile)]
    used = feats + 4 * pieces + len(counts)
    spare = jnp.zeros((send_ref.shape[0] - used, tile), f32)
    sums = sums_ref[...].astype(bf16).astype(f32)
    sums = [sums[:, tile * i : tile * (i + 1)] for i in range(pieces)]
    send_ref[0:feats, :] = gnum
    send_ref[feats:, :] = jnp.concatenate(sums + counts + [spare], axis=0).astype(bf16)


def feed_grad_kernel(hat_ref, norm_ref, slope_ref, feed_ref, active_ref, out_ref):
    ff = slope_ref.shape[1]
    low = hat_ref[...] * norm_ref[0:1] + norm_ref[1:2]
    out_ref[:, :ff] = nn(flip(low.astype(bf16)), slope_ref[...]).astype(bf16)
    out_ref[:, ff : 2 * ff] = nn(flip(feed_ref[...]), active_ref[...]).astype(bf16)


def out_grad_kernel(mixer_ref, context_ref, all_ref, out_ref):
    out_ref[...] = nn(flip(mixer_ref[...]), context_ref[...]).astype(bf16)


def pack_kernel(spots_ref, up_ref, down_ref, out_ref, after_ref, bit_ref, all_ref):
    ff = up_ref.shape[1]
    all_ref[:, :ff] = up_ref[...].astype(bf16)
    all_ref[:, ff : 2 * ff] = down_ref[...].astype(bf16)
    all_ref[:, 2 * ff :] = out_ref[...].astype(bf16)


def chip_sum_kernel(spots_ref, own_ref, other_ref, keep_ref, give_ref):
    total = own_ref[...].astype(f32) + other_ref[...].astype(f32)
    half = total.shape[1] // 2
    first, second = total[:, :half], total[:, half:]
    zero = spots_ref[3] == 0
    keep_ref[...] = jnp.where(zero, first, second).astype(bf16)
    give_ref[...] = jnp.where(zero, second, first).astype(bf16)


def pair_sum_kernel(spots_ref, own_ref, other_ref, *refs):
    out_refs, flag_ref = refs[:-1], refs[-1]
    flag_ref[...] = jnp.zeros_like(flag_ref)
    for d, out_ref in enumerate(out_refs):
        if len(out_refs) == 1:
            total = own_ref[...].astype(f32) + other_ref[...].astype(f32)
        else:
            chip = spots_ref[1] ^ d
            total = own_ref[chip].astype(f32) + other_ref[chip].astype(f32)
        out_ref[...] = total.astype(bf16)


def weight_sum_kernel(spots_ref, got_ref, after_ref, keep_ref, give_ref):
    total = jnp.sum(got_ref[...].astype(f32), axis=0)
    half = total.shape[0] // CORES
    zero = spots_ref[2] == 0
    keep_ref[...] = jnp.where(zero, total[:half], total[half:])
    give_ref[...] = jnp.where(zero, total[half:], total[:half])


def adam_refs(grad, ins, outs, rate):
    new, first, second = adam_step(ins[0], ins[1], ins[2], grad, rate)
    outs[0][...] = new
    outs[1][...] = first
    outs[2][...] = second
    outs[3][...] = new.astype(bf16)


def big_adam_kernel(grad_ref, *refs):
    ins, outs, flag_ref = refs[:9], refs[9:-1], refs[-1]
    flag_ref[...] = jnp.zeros_like(flag_ref)
    ff = ins[0].shape[1]
    spans = (slice(0, ff), slice(ff, 2 * ff), slice(2 * ff, grad_ref.shape[1]))
    for k, (span, rate) in enumerate(zip(spans, (D ** (-0.5), FF ** (-0.5), D ** (-0.5)))):
        state = [ref[...] for ref in ins[3 * k : 3 * k + 3]]
        adam_refs(grad_ref[:, span].astype(f32), state, outs[4 * k : 4 * k + 4], rate)


def qkv_adam_kernel(spots_ref, mine_ref, other_ref, *refs):
    zero = spots_ref[2] == 0
    feats = refs[0].shape[2] // CORES
    for p in range(3):
        span = slice(p * feats, (p + 1) * feats)
        mine, other = mine_ref[:, span], other_ref[:, span]
        grad = jnp.concatenate([jnp.where(zero, mine, other), jnp.where(zero, other, mine)], axis=1)
        adam_refs(grad, [ref[p] for ref in refs[:3]], [ref.at[p] for ref in refs[3:]], D ** (-0.5))


def final_kernel(spots_ref, mine_ref, other_ref, mixer_ref, out_ref):
    mine, other = mine_ref[...].astype(f32), other_ref[...].astype(f32)
    zero = spots_ref[3] == 0
    total = jnp.concatenate([jnp.where(zero, mine, other), jnp.where(zero, other, mine)], axis=0)
    out_ref[...] = mixer_ref[...] + jnp.transpose(total)


def back_sum_kernel(*refs):
    total = jnp.sum(refs[0][...].astype(f32), axis=0)
    for ref in refs[1:-2]:
        total = total + jnp.sum(ref[...].astype(f32), axis=0)
    refs[-1][...] = total.astype(bf16)


def on_device(
    tokens,
    cotangent,
    doc_lengths,
    plane_bits,
    qkv_weight,
    qkv_first,
    qkv_second,
    out_weight,
    out_first,
    out_second,
    up_weight,
    up_first,
    up_second,
    down_weight,
    down_first,
    down_second,
    norm_params,
    norm_first,
    norm_second,
    conv_taps,
    conv_first,
    conv_second,
):
    tok_rows, width = tokens.shape
    hash_count, bits, group_heads, head_dim = plane_bits.shape
    buckets = 2**bits
    taps = conv_taps.shape[1]
    rim = taps // 2
    seq_count = lax.axis_size("seq")
    chips = seq_count // CORES
    place = lax.axis_index("seq")
    side = lax.axis_index("head")
    spot, core = place // CORES, place % CORES
    heads = group_heads // CORES
    feats = heads * head_dim
    group_feats = group_heads * head_dim
    hashes = hash_count // chips
    rows = -(-hashes // 8) * 8
    tile = CORES * tok_rows
    total = chips * tile
    own_rows = width // seq_count
    ff = up_weight.shape[1]
    code_rows = rows * buckets
    blocks = WORK if chips % WORK == 0 else 1
    steps = chips // blocks
    work = blocks * tile
    wide = 2 * blocks if chips % (2 * blocks) == 0 else blocks
    planes_of = [[CORES * c + k for c in range(chips)] for k in range(CORES)]
    across = partial(
        lax.all_to_all, axis_name="seq", split_axis=0, concat_axis=0, tiled=True,
        axis_index_groups=planes_of,
    )
    core_swap = partial(
        lax.ppermute, axis_name="seq", perm=[(i, i ^ 1) for i in range(seq_count)]
    )
    head_swap = partial(lax.ppermute, axis_name="head", perm=[(0, 1), (1, 0)])
    def in_order(mine, other, axis):
        first = jnp.where(core == 0, mine, other)
        return jnp.concatenate([first, jnp.where(core == 0, other, mine)], axis=axis)

    low_qkv = qkv_weight.astype(bf16).reshape(3, own_rows, CORES, feats)
    pick = partial(lax.dynamic_index_in_dim, low_qkv, axis=2, keepdims=False)
    by_rows = lambda part: jnp.transpose(part, (1, 0, 2)).reshape(own_rows, 3 * feats)
    qkv_mine, qkv_give = by_rows(pick(core)), by_rows(pick(1 - core))
    chip_rows = in_order(qkv_mine, core_swap(qkv_give), 0)

    def ring(value, steps, hold):
        moved, found, turns = [value, value], [value], [0]
        for step in range(1, steps + 1):
            moved = [lax.ppermute(v, "seq", p) for v, p in zip(moved, (ahead, behind))]
            if hold:
                moved = list(lax.optimization_barrier(tuple(moved)))
            found += moved
            turns += [chips - step, step]
        return moved, found, turns

    ringed = chips == len(RING)
    if ringed:
        order = np.array(RING)
        seats = np.argsort(order)
        ahead = [
            (CORES * order[i] + k, CORES * order[(i + 1) % chips] + k)
            for i in range(chips)
            for k in range(CORES)
        ]
        behind = [(b, a) for a, b in ahead]
        quarter = CORES * own_rows // 4
        third = feats
        rest = chip_rows[3 * quarter :]
        rest = jnp.concatenate([rest[:, third * j : third * (j + 1)] for j in range(3)], axis=0)
        packed = jnp.concatenate([chip_rows[: 3 * quarter], rest], axis=1)
        block = jnp.concatenate([tokens, packed], axis=0)
        moved, block_parts, turns = ring(block, chips // 2 - 1, True)
        last_part = block_parts[2][0:8, 0:128]
        far_tokens, far_rows = lax.optimization_barrier(
            (moved[0][:tok_rows], moved[1][tok_rows:])
        )
        across_tokens = lax.ppermute(far_tokens, "seq", ahead)
        across_rows = lax.ppermute(far_rows, "seq", behind)
        across_tokens, across_rows = lax.optimization_barrier((across_tokens, across_rows))
        turns.append(chips // 2)
        token_parts = block_parts + [across_tokens]
        token_parts = [p[None] for p in token_parts + [core_swap(part) for part in token_parts]]
        weight_parts = [p[None] for p in block_parts + [across_rows]]
        weight_spots = [tok_rows] * (chips - 1) + [0]
        spot_of = np.array([[order[(seats[c] + t) % chips] for t in turns] for c in range(chips)])
        spot_of = np.repeat(spot_of, CORES, axis=0)
        core_of = np.arange(seq_count)[:, None] % CORES
        place_of = [CORES * spot_of + core_of, CORES * spot_of + 1 - core_of, spot_of]
    else:
        token_parts = [lax.all_gather(tokens, "seq", axis=0, tiled=False)]
        chip_rows = jnp.pad(chip_rows, ((0, 0), (0, width - 3 * feats)))
        weight_parts = [
            lax.all_gather(chip_rows, "seq", axis=0, tiled=False, axis_index_groups=planes_of)
        ]
        weight_spots = [0]
        place_of = [np.zeros((seq_count, 2))]
        last_part = token_parts[0]
    parts = len(token_parts)
    weight_count = len(weight_parts)
    device = np.arange(seq_count)[:, None]
    facts = np.concatenate([device // CORES, device % CORES, 0 * device] + place_of, axis=1)
    facts = np.stack([facts + k * (np.arange(facts.shape[1]) == 2) for k in range(2)])
    facts = lax.dynamic_slice(
        jnp.asarray(facts.astype(np.int32)), (side, place, 0), (1, 1, facts.shape[2])
    )
    spots = jnp.concatenate([doc_lengths[0:1], facts.reshape(-1)])

    smem = pl.BlockSpec(memory_space=pltpu.SMEM)
    anywhere = pl.BlockSpec(memory_space=pl.ANY)
    params = pltpu.CompilerParams(
        dimension_semantics=("arbitrary",), vmem_limit_bytes=VMEM_LIMIT
    )
    shape = jax.ShapeDtypeStruct

    def full(value):
        return pl.BlockSpec(value.shape, lambda i: (0,) * len(value.shape))

    def piped(kernel, name, outs, args, specs=None):
        if specs is None:
            specs = [None] * len(args)
        specs = [
            (smem if arg is spots else full(arg)) if spec is None else spec
            for spec, arg in zip(specs, args)
        ]
        return pl.pallas_call(
            kernel,
            grid=(1,),
            in_specs=specs,
            out_specs=[full(o) for o in outs],
            out_shape=outs,
            compiler_params=params,
            name=name,
        )(*args)

    inside = pl.BlockSpec(memory_space=pltpu.VMEM)
    in_vmem = lambda value: pltpu.with_memory_space_constraint(value, pltpu.VMEM)
    small = pltpu.CompilerParams(
        dimension_semantics=("arbitrary",), vmem_limit_bytes=SMALL_LIMIT
    )

    def once(kernel, name, outs, args, after=(), outside=(), blocks={}, limit=SMALL_LIMIT):
        specs, values = [], []
        for i, arg in enumerate(args):
            plain = arg is spots or i in blocks
            specs.append(smem if arg is spots else blocks.get(i, inside))
            if i in blocks:
                arg = pltpu.with_memory_space_constraint(arg, pltpu.HBM)
            values.append(arg if plain else in_vmem(arg))
        for arg in after:
            specs.append(anywhere)
            values.append(arg)
        return pl.pallas_call(
            kernel,
            grid=(1,) if blocks else (),
            in_specs=specs,
            out_specs=[inside] * len(outs),
            out_shape=[
                (pltpu.HBM if i in outside else pltpu.VMEM)(o.shape, o.dtype)
                for i, o in enumerate(outs)
            ],
            compiler_params=pltpu.CompilerParams(vmem_limit_bytes=limit),
            name=name,
        )(*values)

    own_planes = lax.dynamic_slice(
        plane_bits, (spot * hashes, 0, core * heads, 0), (hashes, bits, heads, head_dim)
    )
    scale = sharpness / math.sqrt(head_dim)
    signs = scale * (2 * own_planes - 1).astype(f32)
    bit_w = jnp.pad(
        jnp.transpose(signs, (2, 1, 0, 3)), ((0, 0), (0, 0), (0, rows - hashes), (0, 0))
    )
    bit_w = bit_w.reshape(heads, bits * rows, head_dim).astype(bf16)
    bit_wt = jnp.transpose(bit_w, (0, 2, 1))

    (second_send,) = piped(
        pack_kernel, "pack",
        [shape((own_rows, 2 * ff + group_feats), bf16)],
        [spots, up_weight, down_weight.T, out_weight.T, last_part, bit_w],
        [None] * 4 + [anywhere] * 2,
    )
    ff_all = lax.all_gather(second_send, "seq", axis=0, tiled=True)

    def resident(*dims):
        return pl.BlockSpec(dims, lambda p, i: (0,) * len(dims), pipeline_mode=pl.Buffered(1))

    def stepped(phase, *dims):
        def place(p, i):
            rest = steps - 1 if phase == 0 else 0
            return (jnp.where(p == phase, i, rest),) + (0,) * (len(dims) - 1)

        return pl.BlockSpec(dims, place)

    hash_params = pltpu.CompilerParams(
        dimension_semantics=("arbitrary", "arbitrary"), vmem_limit_bytes=VMEM_LIMIT
    )
    num_parts, q_unit, k_unit, values, inverses, tables, counts, qkv_all = pl.pallas_call(
        partial(forward_kernel, hashes, bits, rows, wide * tile, chips // wide, heads, parts, weight_spots),
        grid=(2, chips // wide),
        in_specs=[
            smem,
            *[anywhere] * (parts + weight_count),
            resident(*bit_w.shape),
        ],
        out_specs=[
            stepped(1, wide, feats, tile),
            resident(feats, total),
            resident(feats, total),
            resident(feats, total + 256),
            resident(16, total),
            resident(heads, code_rows, 2 * head_dim),
            resident(heads, 8, code_rows),
            resident(width, 3 * feats),
        ],
        out_shape=[
            shape((chips, feats, tile), bf16),
            shape((feats, total), bf16),
            shape((feats, total), bf16),
            shape((feats, total + 256), bf16),
            shape((16, total), f32),
            shape((heads, code_rows, 2 * head_dim), bf16),
            shape((heads, 8, code_rows), f32),
            shape((width, 3 * feats), bf16),
        ],
        scratch_shapes=[
            pltpu.VMEM((heads, code_rows, 2 * head_dim + 16), f32),
            pltpu.VMEM((heads, code_rows, wide * tile), bf16),
            pltpu.VMEM((3 * feats, width), bf16),
            pltpu.VMEM((heads, 2 * head_dim, code_rows), bf16),
            pltpu.VMEM((seq_count, tok_rows, width), bf16),
            pltpu.VMEM((chips, weight_parts[-1].shape[1], width), bf16),
            pltpu.SemaphoreType.DMA((parts + weight_count,)),
        ],
        compiler_params=hash_params,
        name="hash_forward",
    )(spots, *token_parts, *weight_parts, bit_w)
    num_got = across(num_parts)

    own_taps = lax.dynamic_slice(conv_taps, (core * heads, 0), (heads, taps))
    lead = tile + 128 - rim
    bases = jnp.zeros((heads, 8, tile + 256), f32)
    bases = bases.at[:, 0, lead : lead + taps].set(own_taps[:, ::-1])
    conv, window_values = once(
        partial(conv_kernel, tile, heads), "conv_forward",
        [shape((feats, tile), f32), shape((feats, tile + 256), bf16)],
        [spots, values, bases],
    )

    chip_buckets = buckets // chips
    sum_rows = 4 * width // tile
    count_rows = 2 * heads * code_rows // tile
    extra_rows = -(-(sum_rows + count_rows) // 16) * 16

    keep, give, numerator = once(
        partial(context_kernel, heads), "context",
        [shape((feats, tok_rows), bf16), shape((feats, tok_rows), bf16), shape((feats, tile), f32)],
        [spots, num_got, conv],
    )
    context, mixer_part = once(
        mixer_kernel, "mixer",
        [shape((tok_rows, group_feats), bf16), shape((tok_rows, width), bf16)],
        [spots, keep, core_swap(give), ff_all],
        blocks={3: pl.BlockSpec((width, group_feats), lambda i: (0, 2 * ff // group_feats))},
    )
    ff_all, mixer_part = lax.optimization_barrier((ff_all, mixer_part))
    first_hat, first_inverse, hidden, active, feed_part = once(
        hidden_kernel, "feed_forward",
        [
            shape((tok_rows, width), f32),
            shape((tok_rows, 1), f32),
            shape((tok_rows, ff), f32),
            shape((tok_rows, ff), bf16),
            shape((tok_rows, width), bf16),
        ],
        [tokens, mixer_part, head_swap(mixer_part), norm_params, ff_all],
    )
    block_out, grad_second, feed_low, slope_low, first_part, second_sums = once(
        feed_kernel, "feed_back",
        [
            shape((tok_rows, width), f32),
            shape((tok_rows, width), f32),
            shape((tok_rows, width), bf16),
            shape((tok_rows, ff), bf16),
            shape((tok_rows, width), bf16),
            shape((2, width), f32),
        ],
        [first_hat, hidden, feed_part, head_swap(feed_part), cotangent, norm_params, ff_all],
        outside=(0,),
    )
    grad_mixer, mixer_low, keep, give, norm_sums = once(
        mixer_back_kernel, "mixer_back",
        [
            shape((tok_rows, width), f32),
            shape((tok_rows, width), bf16),
            shape((feats, tok_rows), f32),
            shape((feats, tok_rows), f32),
            shape((4, width), f32),
        ],
        [
            spots, grad_second, first_part, head_swap(first_part), first_hat, first_inverse,
            norm_params, ff_all, second_sums,
        ],
    )
    gnum_send, grad_low, grad_high = once(
        partial(attention_back_kernel, heads), "attention_back",
        [
            shape((feats + extra_rows, tile), bf16),
            shape((feats, tok_rows), bf16),
            shape((feats, tok_rows), bf16),
        ],
        [spots, keep, core_swap(give), numerator, norm_sums, counts],
    )
    conv_grad, tap_parts = once(
        partial(conv_back_kernel, tile, taps, heads), "conv_backward",
        [shape((feats, 3 * tile), f32), shape((heads, 8, 128), f32)],
        [spots, window_values, grad_low, grad_high, bases],
    )
    if ringed:
        moved, gnum_parts, unused = ring(gnum_send, 1, False)
        *moved, tap_parts = lax.optimization_barrier((*moved, tap_parts))
        gnum_parts = [gnum_send]
        for step in range(2, chips // 2 + 1):
            gnum_parts += moved
            moved = [
                lax.ppermute(v, "seq", p)
                for v, p in zip(moved, (ahead, behind))
                if p is ahead or 2 * step < chips
            ]
        gnum_parts = [p[None] for p in gnum_parts + moved]
    else:
        gnum_parts = [
            lax.all_gather(gnum_send, "seq", axis=0, tiled=False, axis_index_groups=planes_of)
        ]
    gnum_count = len(gnum_parts)

    columns = 2 * ff + group_feats
    feed_grads = pl.pallas_call(
        feed_grad_kernel,
        grid=(1,),
        in_specs=[inside] * 5,
        out_specs=pl.BlockSpec((width, 2 * ff), lambda i: (0, 0)),
        out_shape=pltpu.HBM((width, columns), bf16),
        compiler_params=small,
        name="feed_grads",
    )(*[in_vmem(v) for v in (first_hat, norm_params, slope_low, feed_low, active)])
    big_grad = pl.pallas_call(
        out_grad_kernel,
        grid=(1,),
        in_specs=[inside, inside, anywhere],
        out_specs=pl.BlockSpec((width, group_feats), lambda i: (0, 2 * ff // group_feats)),
        out_shape=pltpu.HBM((width, columns), bf16),
        input_output_aliases={2: 0},
        compiler_params=small,
        name="out_grads",
    )(in_vmem(mixer_low), in_vmem(context), feed_grads)
    big_owned = lax.psum_scatter(big_grad, "seq", scatter_dimension=0, tiled=True)

    qkv_send, back_keep, back_give, extras = pl.pallas_call(
        partial(backward_kernel, hashes, bits, rows, work, steps, heads, own_rows, parts, gnum_count),
        grid=(2, steps),
        in_specs=[
            smem,
            *[anywhere] * parts,
            *[inside] * gnum_count,
            resident(*qkv_all.shape),
            resident(*bit_w.shape),
            resident(*bit_wt.shape),
            resident(feats, total),
            resident(feats, total),
            resident(feats, total + 256),
            resident(16, total),
            resident(heads, code_rows, 2 * head_dim),
            resident(feats, 3 * tile),
            resident(*tap_parts.shape),
        ],
        out_specs=[
            resident(chips, CORES * own_rows, 3 * feats + 64),
            stepped(1, blocks, width, tok_rows),
            stepped(1, blocks, width, tok_rows),
            resident(chips, extra_rows, tile),
        ],
        out_shape=[
            shape((chips, CORES * own_rows, 3 * feats + 64), bf16),
            shape((chips, width, tok_rows), bf16),
            shape((chips, width, tok_rows), bf16),
            shape((chips, extra_rows, tile), bf16),
        ],
        scratch_shapes=[
            pltpu.VMEM((heads, code_rows, 2 * head_dim), f32),
            pltpu.VMEM((heads, code_rows, work), bf16),
            pltpu.VMEM((feats, total), bf16),
            pltpu.VMEM((3 * feats, width), f32),
            pltpu.VMEM((heads, 2 * head_dim, code_rows), bf16),
            pltpu.VMEM((heads, code_rows, 2 * head_dim), bf16),
            pltpu.VMEM((seq_count, tok_rows, width), bf16),
            pltpu.VMEM((chips, feats, tile), bf16),
            pltpu.SemaphoreType.DMA((parts,)),
        ],
        compiler_params=hash_params,
        name="hash_backward",
    )(
        spots, *token_parts, *[in_vmem(p) for p in gnum_parts], qkv_all, bit_w, bit_wt,
        q_unit, k_unit, values, inverses, tables, conv_grad, tap_parts,
    )

    half = width // 2
    group = chips // 2
    per_chip = lambda *dims: pl.BlockSpec((group,) + dims, lambda i: (i, 0, 0))
    keep, give = pl.pallas_call(
        chip_sum_kernel,
        grid=(2,),
        in_specs=[smem, per_chip(width, tok_rows), per_chip(width, tok_rows)],
        out_specs=[per_chip(half, tok_rows), per_chip(half, tok_rows)],
        out_shape=[shape((chips, half, tok_rows), bf16)] * 2,
        compiler_params=params,
        name="chip_sum",
    )(spots, back_keep, core_swap(back_give))
    *pair_sums, pair_done = once(
        pair_sum_kernel, "pair_sum",
        [shape((half, tok_rows) if ringed else (chips, half, tok_rows), bf16)]
        * (chips if ringed else 1)
        + [shape((8, 128), f32)],
        [spots, keep, head_swap(give)],
        outside=tuple(range(1, chips)) if ringed else (),
    )
    qkv_got = across(qkv_send)
    if ringed:
        back_got = [pair_sums[0]]
        for d in range(1, chips):
            perm = [(CORES * c + k, CORES * (c ^ d) + k) for c in range(chips) for k in range(CORES)]
            back_got.append(lax.ppermute(pair_sums[d], "seq", perm))
        qkv_got, *tied = lax.optimization_barrier((qkv_got, *back_got[1:5]))
        back_got = [back_got[0]] + tied + back_got[1 + len(tied) :]
        back_got = [p[None] for p in back_got]
    else:
        back_got = [across(pair_sums[0])]

    qkv_mine, qkv_give = once(
        weight_sum_kernel, "weight_sum",
        [shape((own_rows, 3 * feats + 64), f32)] * 2,
        [spots, qkv_got],
        after=[pair_done],
    )
    qkv_other = core_swap(qkv_give)

    extras = extras.astype(f32)
    norm_half = jnp.sum(extras[:, :sum_rows], axis=0)
    count_half = extras[:, sum_rows : sum_rows + count_rows]
    count_half = count_half.reshape(chips, heads, 2, chips, CORES, chip_buckets // CORES, rows)
    count_half = lax.dynamic_index_in_dim(count_half, spot, 3, keepdims=False)
    count_half = jnp.transpose(count_half[..., :hashes], (3, 0, 2, 5, 1, 4))
    count_mine = lax.dynamic_index_in_dim(count_half, core, 0, keepdims=False)
    count_give = lax.dynamic_index_in_dim(count_half, 1 - core, 0, keepdims=False)
    tap_first = jnp.where(core == 0, qkv_mine[:heads], qkv_give[:heads])
    tap_half = tap_first[:, 3 * feats : 3 * feats + taps]
    swapped = core_swap(
        jnp.concatenate([norm_half.reshape(-1), count_give.reshape(-1), tap_half.reshape(-1)])
    )
    norm_size, count_size = norm_half.size, count_give.size

    norm_grad = norm_half + swapped[:norm_size].reshape(norm_half.shape)
    norm_grad = jnp.transpose(
        norm_grad.reshape(width // tile, 4, tile), (1, 0, 2)
    ).reshape(4, width)
    count_other = swapped[norm_size : norm_size + count_size].reshape(count_mine.shape)
    occupancy = jnp.transpose(
        in_order(count_mine, count_other, 3), (1, 0, 2, 3, 4)
    ).reshape(2, hash_count, group_heads, buckets // seq_count)
    occupancy = occupancy * (buckets / (tok_rows * seq_count))
    conv_tap_grad = in_order(tap_half, swapped[norm_size + count_size :].reshape(heads, taps), 0)

    flag = shape((8, 128), f32)
    matrix = lambda value: [pltpu.HBM(value.shape, f32)] * 3 + [pltpu.HBM(value.shape, bf16)]
    (
        up_new, up_first_new, up_second_new, up_copy,
        down_new, down_first_new, down_second_new, down_copy,
        out_new, out_first_new, out_second_new, out_copy, big_done,
    ) = piped(
        big_adam_kernel, "big_adam",
        matrix(up_weight) + matrix(down_weight.T) + matrix(out_weight.T) + [flag],
        [
            big_owned, up_weight, up_first, up_second,
            down_weight.T, down_first.T, down_second.T,
            out_weight.T, out_first.T, out_second.T,
        ],
    )
    qkv_new, qkv_first_new, qkv_second_new, qkv_copy = piped(
        qkv_adam_kernel, "qkv_adam", matrix(qkv_weight),
        [spots, qkv_mine, qkv_other, qkv_weight, qkv_first, qkv_second],
    )
    norm_new, norm_first_new, norm_second_new = adam_step(
        norm_params, norm_first, norm_second, norm_grad, 0.3
    )
    conv_new, conv_first_new, conv_second_new = adam_step(
        conv_taps, conv_first, conv_second, conv_tap_grad, CONV ** (-0.5)
    )
    (back_low,) = once(
        back_sum_kernel, "back_sum",
        [shape((half, tok_rows), bf16)],
        back_got,
        after=[big_done],
    )
    (tokens_grad,) = once(
        final_kernel, "tokens_grad",
        [shape((tok_rows, width), f32)],
        [spots, back_low, head_swap(back_low), grad_mixer],
        outside=(0,),
    )
    return (
        block_out,
        tokens_grad,
        occupancy,
        qkv_new,
        qkv_first_new,
        qkv_second_new,
        qkv_copy,
        out_new.T,
        out_first_new.T,
        out_second_new.T,
        out_copy.T,
        up_new,
        up_first_new,
        up_second_new,
        up_copy,
        down_new.T,
        down_first_new.T,
        down_second_new.T,
        down_copy.T,
        norm_new,
        norm_first_new,
        norm_second_new,
        conv_new,
        conv_first_new,
        conv_second_new,
    )


def solution(mesh):
    in_specs = (
        P("seq", None),
        P("seq", None),
        P(),
        P(None, None, "head", None),
        P(None, "seq", "head"),
        P(None, "seq", "head"),
        P(None, "seq", "head"),
        P("head", "seq"),
        P("head", "seq"),
        P("head", "seq"),
        P("seq", "head"),
        P("seq", "head"),
        P("seq", "head"),
        P("head", "seq"),
        P("head", "seq"),
        P("head", "seq"),
        P(),
        P(),
        P(),
        P("head", None),
        P("head", None),
        P("head", None),
    )
    out_specs = (
        P("seq", None),
        P("seq", None),
        P(None, None, "head", "seq"),
        P(None, "seq", "head"),
        P(None, "seq", "head"),
        P(None, "seq", "head"),
        P(None, "seq", "head"),
        P("head", "seq"),
        P("head", "seq"),
        P("head", "seq"),
        P("head", "seq"),
        P("seq", "head"),
        P("seq", "head"),
        P("seq", "head"),
        P("seq", "head"),
        P("head", "seq"),
        P("head", "seq"),
        P("head", "seq"),
        P("head", "seq"),
        P(),
        P(),
        P(),
        P("head", None),
        P("head", None),
        P("head", None),
    )
    return jax.shard_map(
        on_device, mesh=mesh, in_specs=in_specs, out_specs=out_specs, check_vma=False
    )
```

```python
from functools import partial
import math

import jax
import jax.numpy as jnp
import numpy as np
from jax import lax
from jax.experimental import pallas as pl
from jax.experimental.pallas import tpu as pltpu
from jax.sharding import PartitionSpec as P

D = 768
FF = 3072
CONV = 33
STEP = 7
CORES = 2

sharpness = 4.0
norm_eps = 1e-06
layer_eps = 1e-05
beta_one = 0.9
beta_two = 0.999
adam_eps = 1e-08
decay_rate = 0.01
highest = lax.Precision.HIGHEST
f32 = jnp.float32
bf16 = jnp.bfloat16
VMEM_LIMIT = 56 * 1024 * 1024
SMALL_LIMIT = 16 * 1024 * 1024
WORK = 2
SPOTS = 4
RING = (0, 2, 4, 6, 7, 5, 3, 1)


def nn(a, b):
    return lax.dot_general(a, b, (((1,), (0,)), ((), ())), preferred_element_type=f32)


def nt(a, b):
    return lax.dot_general(a, b, (((1,), (1,)), ((), ())), preferred_element_type=f32)


def normalize(source):
    centered = source - jnp.mean(source, axis=-1, keepdims=True)
    inverse = lax.rsqrt(jnp.mean(centered * centered, axis=-1, keepdims=True) + layer_eps)
    return (centered * inverse, inverse)


def norm_back(grad, normed, inverse, gain):
    scaled = grad * gain
    inner = (
        scaled
        - jnp.mean(scaled, axis=-1, keepdims=True)
        - normed * jnp.mean(scaled * normed, axis=-1, keepdims=True)
    )
    gains = jnp.sum(grad * normed, axis=0, keepdims=True)
    return (inverse * inner, gains, jnp.sum(grad, axis=0, keepdims=True))


def adam_step(weight, first, second, grad, rate):
    first_new = beta_one * first + (1.0 - beta_one) * grad
    second_new = beta_two * second + (1.0 - beta_two) * grad * grad
    fix_one = 1.0 - beta_one**STEP
    fix_two = 1.0 - beta_two**STEP
    update = first_new / fix_one / (jnp.sqrt(second_new / fix_two) + adam_eps) + decay_rate * weight
    return (weight - rate * update, first_new, second_new)


def head_units(source):
    inverse = lax.rsqrt(jnp.mean(source * source, axis=0, keepdims=True) + norm_eps)
    return source * inverse, inverse


def seg_rows(limit, start, width):
    pos = start + lax.broadcasted_iota(jnp.int32, (1, width), 1)
    late = (pos >= limit).astype(f32)
    return 1.0 - late, late


def masked_pair(rows, early, late):
    return jnp.concatenate([rows * early, rows * late], axis=0).astype(bf16)


def flip(value):
    return jnp.transpose(value.astype(f32)).astype(bf16)


def bit_factors(bit_planes, unit, bits, hashes, rows):
    z = nn(bit_planes, unit)
    decay = jnp.exp(-jnp.abs(z))
    large = 1.0 / (1.0 + decay)
    small = decay * large
    ones = jnp.where(z >= 0.0, large, small)
    zeros = jnp.where(z >= 0.0, small, large)
    ones = [ones[j * rows : (j + 1) * rows] for j in range(bits)]
    zeros = [zeros[j * rows : (j + 1) * rows] for j in range(bits)]
    if rows != hashes:
        live = lax.broadcasted_iota(jnp.int32, ones[0].shape, 0) < hashes
        return ones, [jnp.where(live, ones[0], 0.0)] + ones[1:], [
            jnp.where(live, zeros[0], 0.0)
        ] + zeros[1:]
    return ones, ones, zeros


def products(ones, zeros, first, last):
    found = [zeros[first], ones[first]]
    for j in range(first + 1, last):
        found = [part * zeros[j] for part in found] + [part * ones[j] for part in found]
    return found


def code_parts(bit_planes, unit, bits, hashes, rows):
    plain, ones, zeros = bit_factors(bit_planes, unit, bits, hashes, rows)
    return plain, products(ones, zeros, 0, 3), products(ones, zeros, 3, bits)


def store_codes(codes_ref, head, lows, highs, rows):
    for g, high in enumerate(highs):
        for s in range(0, len(lows), 2):
            spot = (g * len(lows) + s) * rows
            pair = jnp.concatenate([lows[s] * high, lows[s + 1] * high], axis=0)
            codes_ref[head, spot : spot + 2 * rows, :] = pair.astype(bf16)


def token_copies(spots_ref, part_refs, tok_ref, sem_ref):
    return [
        pltpu.make_async_copy(
            ref.at[:, pl.ds(0, tok_ref.shape[1])],
            tok_ref.at[pl.ds(spots_ref[SPOTS + i], ref.shape[0])],
            sem_ref.at[i],
        )
        for i, ref in enumerate(part_refs)
    ]


def forward_kernel(
    hashes, bits, rows, tile, steps, heads, parts, weight_spots, spots_ref, *refs
):
    part_refs, refs = refs[:parts], refs[parts:]
    weight_refs, refs = refs[: len(weight_spots)], refs[len(weight_spots) :]
    bit_ref, num_ref, qu_ref, ku_ref, v_ref, inv_ref, table_ref, count_ref, w_ref = refs[:9]
    acc_ref, codes_ref, wt_ref, table_t_ref, tok_ref, got_ref, sem_ref = refs[9:]
    limit = spots_ref[0]
    phase, i = pl.program_id(0), pl.program_id(1)
    feats = heads * 64
    chips = num_ref.shape[0]
    block = tile // chips
    start = pl.multiple_of(i * tile, tile)
    span = pl.ds(start, tile)
    early, late = seg_rows(limit, start, tile)

    @pl.when((phase == 0) & (i == 0))
    def _():
        copies = token_copies(spots_ref, part_refs, tok_ref, sem_ref)
        loads = [
            pltpu.make_async_copy(
                ref.at[:, pl.ds(weight_spots[i], got_ref.shape[1])],
                got_ref.at[pl.ds(spots_ref[SPOTS + parts + i], ref.shape[0])],
                sem_ref.at[parts + i],
            )
            for i, ref in enumerate(weight_refs)
        ]
        for copy in loads + copies:
            copy.start()
        acc_ref[...] = jnp.zeros_like(acc_ref)
        v_ref[:, 0:128] = jnp.zeros((feats, 128), bf16)
        v_ref[:, 128 + steps * tile :] = jnp.zeros((feats, 128), bf16)
        inv_ref[...] = jnp.zeros_like(inv_ref)
        for copy in loads:
            copy.wait()
        got = got_ref[...].astype(f32)
        if len(weight_refs) > 1:
            quarter = got.shape[1] // 3
            rest = [got[:, quarter * j : quarter * (j + 1), 3 * feats :] for j in range(3)]
            got = jnp.concatenate([got[:, :, : 3 * feats], jnp.concatenate(rest, axis=2)], axis=1)
        got = got.reshape(got.shape[0] * got.shape[1], got.shape[2])[:, : 3 * feats].astype(bf16)
        w_ref[...] = got
        wt_ref[...] = flip(got)
        for copy in copies:
            copy.wait()

    @pl.when(phase == 0)
    def _():
        devices, tok_rows, width = tok_ref.shape
        here = pl.ds(i * (devices // steps), devices // steps)
        proj = nt(wt_ref[...], tok_ref[here].reshape(tile, width))
        values = proj[2 * feats :].astype(bf16)
        v_ref[:, pl.ds(pl.multiple_of(start + 128, 128), tile)] = values
        marks = jnp.concatenate([early, late, jnp.zeros((14, tile), f32)], axis=0).astype(bf16)
        units = []
        for h in range(heads):
            mine = slice(64 * h, 64 * (h + 1))
            q_unit, q_inv = head_units(proj[mine])
            k_unit, k_inv = head_units(proj[feats + 64 * h : feats + 64 * (h + 1)])
            units.append(k_unit.astype(bf16))
            qu_ref[mine, span] = q_unit.astype(bf16)
            ku_ref[mine, span] = units[h]
            inv_ref[h : h + 1, span] = q_inv
            inv_ref[8 + h : 9 + h, span] = k_inv
        for h in range(heads):
            plain, lows, highs = code_parts(bit_ref[h], units[h], bits, hashes, rows)
            store_codes(codes_ref, h, lows, highs, rows)
        for h in range(heads):
            pair = masked_pair(values[64 * h : 64 * (h + 1)].astype(f32), early, late)
            pair = jnp.concatenate([pair, marks], axis=0)
            acc_ref[h] += nt(codes_ref[h], pair)

    @pl.when((phase == 1) & (i == 0))
    def _():
        for h in range(heads):
            table = acc_ref[h, :, 0:128].astype(bf16)
            table_ref[h] = table
            table_t_ref[h] = flip(table)
            counts = jnp.concatenate(
                [acc_ref[h, :, 128:144], jnp.zeros((acc_ref.shape[1], 112), f32)], axis=1
            )
            count_ref[h] = jnp.transpose(counts)[0:8]

    @pl.when(phase == 1)
    def _():
        for h in range(heads):
            unit = qu_ref[64 * h : 64 * (h + 1), span]
            plain, lows, highs = code_parts(bit_ref[h], unit, bits, hashes, rows)
            store_codes(codes_ref, h, lows, highs, rows)
        for h in range(heads):
            mine = slice(64 * h, 64 * (h + 1))
            both = nn(table_t_ref[h], codes_ref[h])
            low = (both[0:64] * early + both[64:128] * late).astype(bf16)
            for c in range(chips):
                num_ref[c, mine, :] = low[:, c * block : (c + 1) * block]


def soften(bit_planes, unit, slopes, codes_ref, head, bits, hashes, rows):
    plain, lows, highs = code_parts(bit_planes, unit, bits, hashes, rows)
    by_low = [None] * len(lows)
    by_bit = [None] * (bits - 3)
    for g, high in enumerate(highs):
        row = None
        for s in range(0, len(lows), 2):
            spot = (g * len(lows) + s) * rows
            parts = [lows[s] * high, lows[s + 1] * high]
            codes_ref[head, spot : spot + 2 * rows, :] = jnp.concatenate(parts, axis=0).astype(bf16)
            for k in range(2):
                term = parts[k] * slopes[spot + k * rows : spot + (k + 1) * rows]
                by_low[s + k] = term if by_low[s + k] is None else by_low[s + k] + term
                row = term if row is None else row + term
        for j in range(bits - 3):
            if (g >> j) & 1:
                by_bit[j] = row if by_bit[j] is None else by_bit[j] + row
    pairs = [sum(part for s, part in enumerate(by_low) if (s >> j) & 1) for j in range(3)]
    whole = sum(by_low)
    slopes = [part - plain[j] * whole for j, part in enumerate(pairs + by_bit)]
    return jnp.concatenate(slopes, axis=0).astype(bf16)


def unit_back(grad, unit, inverse):
    unit = unit.astype(f32)
    inner = jnp.mean(grad * unit, axis=0, keepdims=True)
    return inverse * (grad - unit * inner)


def backward_kernel(
    hashes, bits, rows, tile, steps, heads, own_rows, parts, gnum_parts, spots_ref, *refs
):
    part_refs, refs = refs[:parts], refs[parts:]
    gnum_refs, refs = refs[:gnum_parts], refs[gnum_parts:]
    w_ref, bit_ref, bit_t_ref, qu_ref, ku_ref, v_ref, inv_ref, table_ref = refs[:8]
    conv_ref, tap_ref, grad_ref, keep_ref, give_ref, extra_ref = refs[8:14]
    acc_ref, codes_ref, proj_ref, sum_ref, table_t_ref, table_g_ref = refs[14:20]
    tok_ref, gnum_ref, sem_ref = refs[20:]
    limit = spots_ref[0]
    spot = spots_ref[1]
    core = spots_ref[2]
    phase, i = pl.program_id(0), pl.program_id(1)
    devices, unused, width = tok_ref.shape
    copies = token_copies(spots_ref, part_refs, tok_ref, sem_ref)
    loads = [
        (ref, pl.ds(spots_ref[SPOTS + parts + j], ref.shape[0]))
        for j, ref in enumerate(gnum_refs)
    ]
    feats = heads * 64
    blocks = keep_ref.shape[0]
    block = tile // blocks
    tok_rows = block // CORES
    start = pl.multiple_of(i * tile, tile)
    span = pl.ds(start, tile)
    early, late = seg_rows(limit, start, tile)

    @pl.when((phase == 0) & (i == 0))
    def _():
        for copy in copies:
            copy.start()
        acc_ref[...] = jnp.zeros_like(acc_ref)
        sum_ref[...] = jnp.zeros_like(sum_ref)
        for ref, where in loads:
            gnum_ref[where] = ref[:, :feats]
            extra_ref[where] = ref[:, feats:]

    @pl.when(phase == 0)
    def _():
        spans = [slice(64 * h, 64 * (h + 1)) for h in range(heads)]
        pairs, grads, slopes = [], [], []
        for mine in spans:
            gnum = jnp.concatenate([gnum_ref[i * blocks + c, mine, :] for c in range(blocks)], axis=1)
            pairs.append(masked_pair(gnum.astype(f32), early, late))
        for h, mine in enumerate(spans):
            slopes.append(
                soften(
                    bit_ref[h], qu_ref[mine, span], nn(table_ref[h], pairs[h]), codes_ref, h,
                    bits, hashes, rows,
                )
            )
        for h in range(heads):
            acc_ref[h] += nt(codes_ref[h], pairs[h])
        for h, mine in enumerate(spans):
            grad = nn(bit_t_ref[h], slopes[h])
            grad = unit_back(grad, qu_ref[mine, span], inv_ref[h : h + 1, span])
            proj_ref[mine, span] = grad.astype(bf16)

    @pl.when((phase == 1) & (i == 0))
    def _():
        for copy in copies:
            copy.wait()
        for h in range(heads):
            table_g_ref[h] = acc_ref[h].astype(bf16)
            table_t_ref[h] = flip(table_g_ref[h])

    @pl.when(phase == 1)
    def _():
        conv = []
        for c in range(blocks):
            step = i * blocks + c - spot + 1
            near = ((step >= 0) & (step <= 2)).astype(f32)
            step = jnp.clip(step, 0, 2)
            conv.append(conv_ref[:, pl.ds(pl.multiple_of(step * block, block), block)] * near)
        conv = jnp.concatenate(conv, axis=1)
        spans = [slice(64 * h, 64 * (h + 1)) for h in range(heads)]
        slopes, parts = [], []
        for h, mine in enumerate(spans):
            values = v_ref[mine, pl.ds(pl.multiple_of(start + 128, 128), tile)]
            pair = masked_pair(values.astype(f32), early, late)
            slopes.append(
                soften(
                    bit_ref[h], ku_ref[mine, span], nn(table_g_ref[h], pair), codes_ref, h,
                    bits, hashes, rows,
                )
            )
        for h, mine in enumerate(spans):
            both = nn(table_t_ref[h], codes_ref[h])
            value_grad = both[0:64] * early + both[64:128] * late + conv[mine]
            grad = nn(bit_t_ref[h], slopes[h])
            grad = unit_back(grad, ku_ref[mine, span], inv_ref[8 + h : 9 + h, span])
            parts.append((grad.astype(bf16), value_grad.astype(bf16)))
        full = jnp.concatenate(
            [proj_ref[:, span]] + [part[0] for part in parts] + [part[1] for part in parts], axis=0
        )
        here = pl.ds(i * (devices // steps), devices // steps)
        sum_ref[...] += nn(full, tok_ref[here].reshape(tile, width))
        part = nn(w_ref[...], full)
        for c in range(blocks):
            first = part[:, c * block : c * block + tok_rows]
            second = part[:, c * block + tok_rows : (c + 1) * block]
            keep_ref[c] = jnp.where(core == 0, first, second).astype(bf16)
            give_ref[c] = jnp.where(core == 0, second, first).astype(bf16)

    @pl.when((phase == 1) & (i == steps - 1))
    def _():
        grad = jnp.transpose(sum_ref[...])
        chips = grad_ref.shape[0]
        grad_ref[:, :, 0 : heads * 192] = grad.reshape(
            chips, CORES * own_rows, heads * 192
        ).astype(bf16)
        grad_ref[:, :, heads * 192 :] = jnp.zeros((chips, CORES * own_rows, 64), bf16)
        taps = jnp.concatenate([tap_ref[h, 0:1, 0:64] for h in range(heads)], axis=0)
        for c in range(chips):
            grad_ref[c, 0:heads, heads * 192 :] = taps.astype(bf16)


def window_same(spots_ref, tile):
    start = spots_ref[1] * tile
    width = tile + 256
    edge = lax.broadcasted_iota(jnp.int32, (width, tile), 0) + (start - 128)
    own = lax.broadcasted_iota(jnp.int32, (width, tile), 1) + start
    return (edge >= spots_ref[0]) == (own >= spots_ref[0])


def banded(base, same, tile):
    width = tile + 256
    spread = jnp.broadcast_to(base, (width, width))
    spread = pltpu.roll(spread, 0, 1, stride=1, stride_axis=0)[:, :tile]
    matrix = jnp.where(same, spread, 0.0)
    upper = matrix.astype(bf16)
    return upper, (matrix - upper.astype(f32)).astype(bf16)


def conv_kernel(tile, heads, spots_ref, values_ref, base_ref, out_ref, window_ref):
    same = window_same(spots_ref, tile)
    first = pl.multiple_of(spots_ref[1] * tile, tile)
    window = values_ref[:, pl.ds(first, tile + 256)]
    window_ref[...] = window
    for h in range(heads):
        mine = slice(64 * h, 64 * (h + 1))
        upper, lower = banded(base_ref[h, 0:1], same, tile)
        out_ref[mine] = nn(window[mine], upper) + nn(window[mine], lower)


def conv_back_kernel(
    tile, taps, heads, spots_ref, window_ref, low_ref, high_ref, base_ref, out_ref, tap_ref
):
    same = window_same(spots_ref, tile)
    width = tile + 256
    rim = taps // 2
    out_ref[...] = jnp.zeros_like(out_ref)
    pos = lax.broadcasted_iota(jnp.int32, (128, tile), 1) + spots_ref[1] * tile
    other = pos + lax.broadcasted_iota(jnp.int32, (128, tile), 0) - rim
    near = (pos >= spots_ref[0]) == (other >= spots_ref[0])

    def one(h, carry):
        mine = pl.ds(pl.multiple_of(h * 64, 64), 64)
        upper, lower = banded(base_ref[h, 0:1], same, tile)
        own = jnp.concatenate([low_ref[mine, :], high_ref[mine, :]], axis=1)
        out_ref[mine, 128 : 128 + width] = nt(own, upper) + nt(own, lower)
        values = window_ref[mine, :].astype(f32)
        own = own.astype(f32)
        sums = []
        for o in range(taps):
            moved = pltpu.roll(values, width - (128 - rim) - o, 1)[:, :tile]
            sums.append(jnp.sum(moved * own, axis=0, keepdims=True))
        sums = jnp.concatenate(sums + [jnp.zeros((128 - taps, tile), f32)], axis=0)
        total = jnp.sum(jnp.where(near, sums, 0.0), axis=1, keepdims=True)
        tap_ref[h] = jnp.transpose(jnp.broadcast_to(total, (128, 128)))[0:8]
        return carry

    lax.fori_loop(0, heads, one, 0)


def context_kernel(heads, spots_ref, got_ref, conv_ref, keep_ref, give_ref, num_ref):
    total = jnp.sum(got_ref[...].astype(f32), axis=0)
    num_ref[...] = total
    tile = total.shape[1]
    parts = [head_units(total[64 * h : 64 * (h + 1)])[0] for h in range(heads)]
    context = (jnp.concatenate(parts, axis=0) + conv_ref[...]).astype(bf16)
    first, second = context[:, : tile // CORES], context[:, tile // CORES :]

    @pl.when(spots_ref[2] == 0)
    def _():
        keep_ref[...] = first
        give_ref[...] = second

    @pl.when(spots_ref[2] != 0)
    def _():
        keep_ref[...] = second
        give_ref[...] = first


def mixer_kernel(spots_ref, keep_ref, other_ref, w_ref, context_ref, part_ref):
    keep, other = keep_ref[...].astype(f32), other_ref[...].astype(f32)
    zero = spots_ref[2] == 0
    pair = jnp.concatenate([jnp.where(zero, keep, other), jnp.where(zero, other, keep)], axis=0)
    context = jnp.transpose(pair).astype(bf16)
    context_ref[...] = context
    part_ref[...] = nt(context, w_ref[...]).astype(bf16)


def hidden_kernel(
    tok_ref, own_ref, other_ref, norm_ref, w_ref, hat_ref, inv_ref, hidden_ref, active_ref, part_ref
):
    ff = hidden_ref.shape[1]
    mixed = own_ref[...].astype(f32) + other_ref[...].astype(f32)
    hat, inverse = normalize(tok_ref[...].astype(f32) + mixed)
    hat_ref[...] = hat
    inv_ref[...] = inverse
    low = (hat * norm_ref[0:1] + norm_ref[1:2]).astype(bf16)
    hidden = nn(low, w_ref[:, :ff])
    hidden_ref[...] = hidden
    active = (0.5 * hidden * (1.0 + lax.erf(hidden * math.sqrt(0.5)))).astype(bf16)
    active_ref[...] = active
    part_ref[...] = nt(active, w_ref[:, ff : 2 * ff]).astype(bf16)


def feed_kernel(
    hat_ref, hidden_ref, own_ref, other_ref, cot_ref, norm_ref, w_ref,
    out_ref, second_ref, feed_ref, slope_ref, part_ref, sums_ref,
):
    ff = hidden_ref.shape[1]
    first_out = hat_ref[...] * norm_ref[0:1] + norm_ref[1:2]
    fed = own_ref[...].astype(f32) + other_ref[...].astype(f32)
    hat, inverse = normalize(first_out + fed)
    out_ref[...] = hat * norm_ref[2:3] + norm_ref[3:4]
    grad, gains, offsets = norm_back(cot_ref[...].astype(f32), hat, inverse, norm_ref[2:3])
    second_ref[...] = grad
    sums_ref[0:1] = gains
    sums_ref[1:2] = offsets
    low = grad.astype(bf16)
    feed_ref[...] = low
    active_grad = nn(low, w_ref[:, ff : 2 * ff])
    hidden = hidden_ref[...]
    cdf = 0.5 * (1.0 + lax.erf(hidden * math.sqrt(0.5)))
    density = jnp.exp(-0.5 * hidden * hidden) * (1.0 / math.sqrt(2.0 * math.pi))
    slope = (active_grad * (cdf + hidden * density)).astype(bf16)
    slope_ref[...] = slope
    part_ref[...] = nt(slope, w_ref[:, :ff]).astype(bf16)


def mixer_back_kernel(
    spots_ref, second_ref, own_ref, other_ref, hat_ref, inv_ref, norm_ref, w_ref, sums_ref,
    grad_ref, low_ref, keep_ref, give_ref, all_sums_ref,
):
    first = second_ref[...] + (own_ref[...].astype(f32) + other_ref[...].astype(f32))
    grad, gains, offsets = norm_back(first, hat_ref[...], inv_ref[...], norm_ref[0:1])
    grad_ref[...] = grad
    all_sums_ref[0:1] = gains
    all_sums_ref[1:2] = offsets
    all_sums_ref[2:4] = sums_ref[...]
    low = grad.astype(bf16)
    low_ref[...] = low
    half = keep_ref.shape[0]
    context = jnp.transpose(nn(low, w_ref[:, w_ref.shape[1] - CORES * half :]))
    half = context.shape[0] // CORES
    zero = spots_ref[2] == 0
    keep_ref[...] = jnp.where(zero, context[:half], context[half:])
    give_ref[...] = jnp.where(zero, context[half:], context[:half])


def attention_back_kernel(
    heads, spots_ref, keep_ref, other_ref, num_ref, sums_ref, count_ref,
    send_ref, low_ref, high_ref,
):
    zero = spots_ref[2] == 0
    keep, other = keep_ref[...], other_ref[...]
    grad = jnp.concatenate([jnp.where(zero, keep, other), jnp.where(zero, other, keep)], axis=1)
    half = keep.shape[1]
    low = grad.astype(bf16)
    low_ref[...] = low[:, :half]
    high_ref[...] = low[:, half:]
    parts = []
    for h in range(heads):
        span = slice(64 * h, 64 * (h + 1))
        attention, inverse = head_units(num_ref[span])
        inner = jnp.mean(grad[span] * attention, axis=0, keepdims=True)
        parts.append(inverse * (grad[span] - attention * inner))
    gnum = jnp.concatenate(parts, axis=0).astype(bf16)
    tile = gnum.shape[1]
    feats = 64 * heads
    pieces = sums_ref.shape[1] // tile
    counts = []
    for h in range(heads):
        for d in range(2):
            row = count_ref[h, d : d + 1, :]
            counts += [row[:, tile * i : tile * (i + 1)] for i in range(row.shape[1] // tile)]
    used = feats + 4 * pieces + len(counts)
    spare = jnp.zeros((send_ref.shape[0] - used, tile), f32)
    sums = sums_ref[...].astype(bf16).astype(f32)
    sums = [sums[:, tile * i : tile * (i + 1)] for i in range(pieces)]
    send_ref[0:feats, :] = gnum
    send_ref[feats:, :] = jnp.concatenate(sums + counts + [spare], axis=0).astype(bf16)


def feed_grad_kernel(hat_ref, norm_ref, slope_ref, feed_ref, active_ref, out_ref):
    ff = slope_ref.shape[1]
    low = hat_ref[...] * norm_ref[0:1] + norm_ref[1:2]
    out_ref[:, :ff] = nn(flip(low.astype(bf16)), slope_ref[...]).astype(bf16)
    out_ref[:, ff : 2 * ff] = nn(flip(feed_ref[...]), active_ref[...]).astype(bf16)


def out_grad_kernel(mixer_ref, context_ref, all_ref, out_ref):
    out_ref[...] = nn(flip(mixer_ref[...]), context_ref[...]).astype(bf16)


def pack_kernel(spots_ref, up_ref, down_ref, out_ref, after_ref, bit_ref, all_ref):
    ff = up_ref.shape[1]
    all_ref[:, :ff] = up_ref[...].astype(bf16)
    all_ref[:, ff : 2 * ff] = down_ref[...].astype(bf16)
    all_ref[:, 2 * ff :] = out_ref[...].astype(bf16)


def chip_sum_kernel(spots_ref, own_ref, other_ref, keep_ref, give_ref):
    total = own_ref[...].astype(f32) + other_ref[...].astype(f32)
    half = total.shape[1] // 2
    first, second = total[:, :half], total[:, half:]
    zero = spots_ref[3] == 0
    keep_ref[...] = jnp.where(zero, first, second).astype(bf16)
    give_ref[...] = jnp.where(zero, second, first).astype(bf16)


def pair_sum_kernel(spots_ref, own_ref, other_ref, *refs):
    out_refs, flag_ref = refs[:-1], refs[-1]
    flag_ref[...] = jnp.zeros_like(flag_ref)
    for d, out_ref in enumerate(out_refs):
        if len(out_refs) == 1:
            total = own_ref[...].astype(f32) + other_ref[...].astype(f32)
        else:
            chip = spots_ref[1] ^ d
            total = own_ref[chip].astype(f32) + other_ref[chip].astype(f32)
        out_ref[...] = total.astype(bf16)


def weight_sum_kernel(spots_ref, got_ref, after_ref, keep_ref, give_ref):
    total = jnp.sum(got_ref[...].astype(f32), axis=0)
    half = total.shape[0] // CORES
    zero = spots_ref[2] == 0
    keep_ref[...] = jnp.where(zero, total[:half], total[half:])
    give_ref[...] = jnp.where(zero, total[half:], total[:half])


def adam_refs(grad, ins, outs, rate):
    new, first, second = adam_step(ins[0], ins[1], ins[2], grad, rate)
    outs[0][...] = new
    outs[1][...] = first
    outs[2][...] = second
    outs[3][...] = new.astype(bf16)


def big_adam_kernel(grad_ref, *refs):
    ins, outs, flag_ref = refs[:9], refs[9:-1], refs[-1]
    flag_ref[...] = jnp.zeros_like(flag_ref)
    ff = ins[0].shape[1]
    spans = (slice(0, ff), slice(ff, 2 * ff), slice(2 * ff, grad_ref.shape[1]))
    for k, (span, rate) in enumerate(zip(spans, (D ** (-0.5), FF ** (-0.5), D ** (-0.5)))):
        state = [ref[...] for ref in ins[3 * k : 3 * k + 3]]
        adam_refs(grad_ref[:, span].astype(f32), state, outs[4 * k : 4 * k + 4], rate)


def qkv_adam_kernel(spots_ref, mine_ref, other_ref, *refs):
    zero = spots_ref[2] == 0
    feats = refs[0].shape[2] // CORES
    for p in range(3):
        span = slice(p * feats, (p + 1) * feats)
        mine, other = mine_ref[:, span], other_ref[:, span]
        grad = jnp.concatenate([jnp.where(zero, mine, other), jnp.where(zero, other, mine)], axis=1)
        adam_refs(grad, [ref[p] for ref in refs[:3]], [ref.at[p] for ref in refs[3:]], D ** (-0.5))


def final_kernel(spots_ref, mine_ref, other_ref, mixer_ref, out_ref):
    mine, other = mine_ref[...].astype(f32), other_ref[...].astype(f32)
    zero = spots_ref[3] == 0
    total = jnp.concatenate([jnp.where(zero, mine, other), jnp.where(zero, other, mine)], axis=0)
    out_ref[...] = mixer_ref[...] + jnp.transpose(total)


def back_sum_kernel(*refs):
    total = jnp.sum(refs[0][...].astype(f32), axis=0)
    for ref in refs[1:-2]:
        total = total + jnp.sum(ref[...].astype(f32), axis=0)
    refs[-1][...] = total.astype(bf16)


def on_device(
    tokens,
    cotangent,
    doc_lengths,
    plane_bits,
    qkv_weight,
    qkv_first,
    qkv_second,
    out_weight,
    out_first,
    out_second,
    up_weight,
    up_first,
    up_second,
    down_weight,
    down_first,
    down_second,
    norm_params,
    norm_first,
    norm_second,
    conv_taps,
    conv_first,
    conv_second,
):
    tok_rows, width = tokens.shape
    hash_count, bits, group_heads, head_dim = plane_bits.shape
    buckets = 2**bits
    taps = conv_taps.shape[1]
    rim = taps // 2
    seq_count = lax.axis_size("seq")
    chips = seq_count // CORES
    place = lax.axis_index("seq")
    side = lax.axis_index("head")
    spot, core = place // CORES, place % CORES
    heads = group_heads // CORES
    feats = heads * head_dim
    group_feats = group_heads * head_dim
    hashes = hash_count // chips
    rows = -(-hashes // 8) * 8
    tile = CORES * tok_rows
    total = chips * tile
    own_rows = width // seq_count
    ff = up_weight.shape[1]
    code_rows = rows * buckets
    blocks = WORK if chips % WORK == 0 else 1
    steps = chips // blocks
    work = blocks * tile
    wide = 2 * blocks if chips % (2 * blocks) == 0 else blocks
    planes_of = [[CORES * c + k for c in range(chips)] for k in range(CORES)]
    across = partial(
        lax.all_to_all, axis_name="seq", split_axis=0, concat_axis=0, tiled=True,
        axis_index_groups=planes_of,
    )
    core_swap = partial(
        lax.ppermute, axis_name="seq", perm=[(i, i ^ 1) for i in range(seq_count)]
    )
    head_swap = partial(lax.ppermute, axis_name="head", perm=[(0, 1), (1, 0)])
    def in_order(mine, other, axis):
        first = jnp.where(core == 0, mine, other)
        return jnp.concatenate([first, jnp.where(core == 0, other, mine)], axis=axis)

    low_qkv = qkv_weight.astype(bf16).reshape(3, own_rows, CORES, feats)
    pick = partial(lax.dynamic_index_in_dim, low_qkv, axis=2, keepdims=False)
    by_rows = lambda part: jnp.transpose(part, (1, 0, 2)).reshape(own_rows, 3 * feats)
    qkv_mine, qkv_give = by_rows(pick(core)), by_rows(pick(1 - core))
    chip_rows = in_order(qkv_mine, core_swap(qkv_give), 0)

    def ring(value, steps, hold):
        moved, found, turns = [value, value], [value], [0]
        for step in range(1, steps + 1):
            moved = [lax.ppermute(v, "seq", p) for v, p in zip(moved, (ahead, behind))]
            if hold:
                moved = list(lax.optimization_barrier(tuple(moved)))
            found += moved
            turns += [chips - step, step]
        return moved, found, turns

    ringed = chips == len(RING)
    if ringed:
        order = np.array(RING)
        seats = np.argsort(order)
        ahead = [
            (CORES * order[i] + k, CORES * order[(i + 1) % chips] + k)
            for i in range(chips)
            for k in range(CORES)
        ]
        behind = [(b, a) for a, b in ahead]
        quarter = CORES * own_rows // 4
        third = feats
        rest = chip_rows[3 * quarter :]
        rest = jnp.concatenate([rest[:, third * j : third * (j + 1)] for j in range(3)], axis=0)
        packed = jnp.concatenate([chip_rows[: 3 * quarter], rest], axis=1)
        block = jnp.concatenate([tokens, packed], axis=0)
        moved, block_parts, turns = ring(block, chips // 2 - 1, True)
        last_part = block_parts[2][0:8, 0:128]
        far_tokens, far_rows = lax.optimization_barrier(
            (moved[0][:tok_rows], moved[1][tok_rows:])
        )
        across_tokens = lax.ppermute(far_tokens, "seq", ahead)
        across_rows = lax.ppermute(far_rows, "seq", behind)
        across_tokens, across_rows = lax.optimization_barrier((across_tokens, across_rows))
        turns.append(chips // 2)
        token_parts = block_parts + [across_tokens]
        token_parts = [p[None] for p in token_parts + [core_swap(part) for part in token_parts]]
        weight_parts = [p[None] for p in block_parts + [across_rows]]
        weight_spots = [tok_rows] * (chips - 1) + [0]
        spot_of = np.array([[order[(seats[c] + t) % chips] for t in turns] for c in range(chips)])
        spot_of = np.repeat(spot_of, CORES, axis=0)
        core_of = np.arange(seq_count)[:, None] % CORES
        place_of = [CORES * spot_of + core_of, CORES * spot_of + 1 - core_of, spot_of]
    else:
        token_parts = [lax.all_gather(tokens, "seq", axis=0, tiled=False)]
        chip_rows = jnp.pad(chip_rows, ((0, 0), (0, width - 3 * feats)))
        weight_parts = [
            lax.all_gather(chip_rows, "seq", axis=0, tiled=False, axis_index_groups=planes_of)
        ]
        weight_spots = [0]
        place_of = [np.zeros((seq_count, 2))]
        last_part = token_parts[0]
    parts = len(token_parts)
    weight_count = len(weight_parts)
    device = np.arange(seq_count)[:, None]
    facts = np.concatenate([device // CORES, device % CORES, 0 * device] + place_of, axis=1)
    facts = np.stack([facts + k * (np.arange(facts.shape[1]) == 2) for k in range(2)])
    facts = lax.dynamic_slice(
        jnp.asarray(facts.astype(np.int32)), (side, place, 0), (1, 1, facts.shape[2])
    )
    spots = jnp.concatenate([doc_lengths[0:1], facts.reshape(-1)])

    smem = pl.BlockSpec(memory_space=pltpu.SMEM)
    anywhere = pl.BlockSpec(memory_space=pl.ANY)
    params = pltpu.CompilerParams(
        dimension_semantics=("arbitrary",), vmem_limit_bytes=VMEM_LIMIT
    )
    shape = jax.ShapeDtypeStruct

    def full(value):
        return pl.BlockSpec(value.shape, lambda i: (0,) * len(value.shape))

    def piped(kernel, name, outs, args, specs=None):
        if specs is None:
            specs = [None] * len(args)
        specs = [
            (smem if arg is spots else full(arg)) if spec is None else spec
            for spec, arg in zip(specs, args)
        ]
        return pl.pallas_call(
            kernel,
            grid=(1,),
            in_specs=specs,
            out_specs=[full(o) for o in outs],
            out_shape=outs,
            compiler_params=params,
            name=name,
        )(*args)

    inside = pl.BlockSpec(memory_space=pltpu.VMEM)
    in_vmem = lambda value: pltpu.with_memory_space_constraint(value, pltpu.VMEM)
    small = pltpu.CompilerParams(
        dimension_semantics=("arbitrary",), vmem_limit_bytes=SMALL_LIMIT
    )

    def once(kernel, name, outs, args, after=(), outside=(), blocks={}, limit=SMALL_LIMIT):
        specs, values = [], []
        for i, arg in enumerate(args):
            plain = arg is spots or i in blocks
            specs.append(smem if arg is spots else blocks.get(i, inside))
            if i in blocks:
                arg = pltpu.with_memory_space_constraint(arg, pltpu.HBM)
            values.append(arg if plain else in_vmem(arg))
        for arg in after:
            specs.append(anywhere)
            values.append(arg)
        return pl.pallas_call(
            kernel,
            grid=(1,) if blocks else (),
            in_specs=specs,
            out_specs=[inside] * len(outs),
            out_shape=[
                (pltpu.HBM if i in outside else pltpu.VMEM)(o.shape, o.dtype)
                for i, o in enumerate(outs)
            ],
            compiler_params=pltpu.CompilerParams(vmem_limit_bytes=limit),
            name=name,
        )(*values)

    own_planes = lax.dynamic_slice(
        plane_bits, (spot * hashes, 0, core * heads, 0), (hashes, bits, heads, head_dim)
    )
    scale = sharpness / math.sqrt(head_dim)
    signs = scale * (2 * own_planes - 1).astype(f32)
    bit_w = jnp.pad(
        jnp.transpose(signs, (2, 1, 0, 3)), ((0, 0), (0, 0), (0, rows - hashes), (0, 0))
    )
    bit_w = bit_w.reshape(heads, bits * rows, head_dim).astype(bf16)
    bit_wt = jnp.transpose(bit_w, (0, 2, 1))

    (second_send,) = piped(
        pack_kernel, "pack",
        [shape((own_rows, 2 * ff + group_feats), bf16)],
        [spots, up_weight, down_weight.T, out_weight.T, last_part, bit_w],
        [None] * 4 + [anywhere] * 2,
    )
    ff_all = lax.all_gather(second_send, "seq", axis=0, tiled=True)

    def resident(*dims):
        return pl.BlockSpec(dims, lambda p, i: (0,) * len(dims), pipeline_mode=pl.Buffered(1))

    def stepped(phase, *dims):
        def place(p, i):
            rest = steps - 1 if phase == 0 else 0
            return (jnp.where(p == phase, i, rest),) + (0,) * (len(dims) - 1)

        return pl.BlockSpec(dims, place)

    hash_params = pltpu.CompilerParams(
        dimension_semantics=("arbitrary", "arbitrary"), vmem_limit_bytes=VMEM_LIMIT
    )
    num_parts, q_unit, k_unit, values, inverses, tables, counts, qkv_all = pl.pallas_call(
        partial(forward_kernel, hashes, bits, rows, wide * tile, chips // wide, heads, parts, weight_spots),
        grid=(2, chips // wide),
        in_specs=[
            smem,
            *[anywhere] * (parts + weight_count),
            resident(*bit_w.shape),
        ],
        out_specs=[
            stepped(1, wide, feats, tile),
            resident(feats, total),
            resident(feats, total),
            resident(feats, total + 256),
            resident(16, total),
            resident(heads, code_rows, 2 * head_dim),
            resident(heads, 8, code_rows),
            resident(width, 3 * feats),
        ],
        out_shape=[
            shape((chips, feats, tile), bf16),
            shape((feats, total), bf16),
            shape((feats, total), bf16),
            shape((feats, total + 256), bf16),
            shape((16, total), f32),
            shape((heads, code_rows, 2 * head_dim), bf16),
            shape((heads, 8, code_rows), f32),
            shape((width, 3 * feats), bf16),
        ],
        scratch_shapes=[
            pltpu.VMEM((heads, code_rows, 2 * head_dim + 16), f32),
            pltpu.VMEM((heads, code_rows, wide * tile), bf16),
            pltpu.VMEM((3 * feats, width), bf16),
            pltpu.VMEM((heads, 2 * head_dim, code_rows), bf16),
            pltpu.VMEM((seq_count, tok_rows, width), bf16),
            pltpu.VMEM((chips, weight_parts[-1].shape[1], width), bf16),
            pltpu.SemaphoreType.DMA((parts + weight_count,)),
        ],
        compiler_params=hash_params,
        name="hash_forward",
    )(spots, *token_parts, *weight_parts, bit_w)
    num_got = across(num_parts)

    own_taps = lax.dynamic_slice(conv_taps, (core * heads, 0), (heads, taps))
    lead = tile + 128 - rim
    bases = jnp.zeros((heads, 8, tile + 256), f32)
    bases = bases.at[:, 0, lead : lead + taps].set(own_taps[:, ::-1])
    conv, window_values = once(
        partial(conv_kernel, tile, heads), "conv_forward",
        [shape((feats, tile), f32), shape((feats, tile + 256), bf16)],
        [spots, values, bases],
    )

    chip_buckets = buckets // chips
    sum_rows = 4 * width // tile
    count_rows = 2 * heads * code_rows // tile
    extra_rows = -(-(sum_rows + count_rows) // 16) * 16

    keep, give, numerator = once(
        partial(context_kernel, heads), "context",
        [shape((feats, tok_rows), bf16), shape((feats, tok_rows), bf16), shape((feats, tile), f32)],
        [spots, num_got, conv],
    )
    context, mixer_part = once(
        mixer_kernel, "mixer",
        [shape((tok_rows, group_feats), bf16), shape((tok_rows, width), bf16)],
        [spots, keep, core_swap(give), ff_all],
        blocks={3: pl.BlockSpec((width, group_feats), lambda i: (0, 2 * ff // group_feats))},
    )
    ff_all, mixer_part = lax.optimization_barrier((ff_all, mixer_part))
    first_hat, first_inverse, hidden, active, feed_part = once(
        hidden_kernel, "feed_forward",
        [
            shape((tok_rows, width), f32),
            shape((tok_rows, 1), f32),
            shape((tok_rows, ff), f32),
            shape((tok_rows, ff), bf16),
            shape((tok_rows, width), bf16),
        ],
        [tokens, mixer_part, head_swap(mixer_part), norm_params, ff_all],
    )
    block_out, grad_second, feed_low, slope_low, first_part, second_sums = once(
        feed_kernel, "feed_back",
        [
            shape((tok_rows, width), f32),
            shape((tok_rows, width), f32),
            shape((tok_rows, width), bf16),
            shape((tok_rows, ff), bf16),
            shape((tok_rows, width), bf16),
            shape((2, width), f32),
        ],
        [first_hat, hidden, feed_part, head_swap(feed_part), cotangent, norm_params, ff_all],
        outside=(0,),
    )
    grad_mixer, mixer_low, keep, give, norm_sums = once(
        mixer_back_kernel, "mixer_back",
        [
            shape((tok_rows, width), f32),
            shape((tok_rows, width), bf16),
            shape((feats, tok_rows), f32),
            shape((feats, tok_rows), f32),
            shape((4, width), f32),
        ],
        [
            spots, grad_second, first_part, head_swap(first_part), first_hat, first_inverse,
            norm_params, ff_all, second_sums,
        ],
    )
    gnum_send, grad_low, grad_high = once(
        partial(attention_back_kernel, heads), "attention_back",
        [
            shape((feats + extra_rows, tile), bf16),
            shape((feats, tok_rows), bf16),
            shape((feats, tok_rows), bf16),
        ],
        [spots, keep, core_swap(give), numerator, norm_sums, counts],
    )
    conv_grad, tap_parts = once(
        partial(conv_back_kernel, tile, taps, heads), "conv_backward",
        [shape((feats, 3 * tile), f32), shape((heads, 8, 128), f32)],
        [spots, window_values, grad_low, grad_high, bases],
    )
    if ringed:
        moved, gnum_parts, unused = ring(gnum_send, 1, False)
        *moved, tap_parts = lax.optimization_barrier((*moved, tap_parts))
        gnum_parts = [gnum_send]
        for step in range(2, chips // 2 + 1):
            gnum_parts += moved
            moved = [
                lax.ppermute(v, "seq", p)
                for v, p in zip(moved, (ahead, behind))
                if p is ahead or 2 * step < chips
            ]
        gnum_parts = [p[None] for p in gnum_parts + moved]
    else:
        gnum_parts = [
            lax.all_gather(gnum_send, "seq", axis=0, tiled=False, axis_index_groups=planes_of)
        ]
    gnum_count = len(gnum_parts)

    columns = 2 * ff + group_feats
    feed_grads = pl.pallas_call(
        feed_grad_kernel,
        grid=(1,),
        in_specs=[inside] * 5,
        out_specs=pl.BlockSpec((width, 2 * ff), lambda i: (0, 0)),
        out_shape=pltpu.HBM((width, columns), bf16),
        compiler_params=small,
        name="feed_grads",
    )(*[in_vmem(v) for v in (first_hat, norm_params, slope_low, feed_low, active)])
    big_grad = pl.pallas_call(
        out_grad_kernel,
        grid=(1,),
        in_specs=[inside, inside, anywhere],
        out_specs=pl.BlockSpec((width, group_feats), lambda i: (0, 2 * ff // group_feats)),
        out_shape=pltpu.HBM((width, columns), bf16),
        input_output_aliases={2: 0},
        compiler_params=small,
        name="out_grads",
    )(in_vmem(mixer_low), in_vmem(context), feed_grads)
    big_owned = lax.psum_scatter(big_grad, "seq", scatter_dimension=0, tiled=True)

    qkv_send, back_keep, back_give, extras = pl.pallas_call(
        partial(backward_kernel, hashes, bits, rows, work, steps, heads, own_rows, parts, gnum_count),
        grid=(2, steps),
        in_specs=[
            smem,
            *[anywhere] * parts,
            *[inside] * gnum_count,
            resident(*qkv_all.shape),
            resident(*bit_w.shape),
            resident(*bit_wt.shape),
            resident(feats, total),
            resident(feats, total),
            resident(feats, total + 256),
            resident(16, total),
            resident(heads, code_rows, 2 * head_dim),
            resident(feats, 3 * tile),
            resident(*tap_parts.shape),
        ],
        out_specs=[
            resident(chips, CORES * own_rows, 3 * feats + 64),
            stepped(1, blocks, width, tok_rows),
            stepped(1, blocks, width, tok_rows),
            resident(chips, extra_rows, tile),
        ],
        out_shape=[
            shape((chips, CORES * own_rows, 3 * feats + 64), bf16),
            shape((chips, width, tok_rows), bf16),
            shape((chips, width, tok_rows), bf16),
            shape((chips, extra_rows, tile), bf16),
        ],
        scratch_shapes=[
            pltpu.VMEM((heads, code_rows, 2 * head_dim), f32),
            pltpu.VMEM((heads, code_rows, work), bf16),
            pltpu.VMEM((feats, total), bf16),
            pltpu.VMEM((3 * feats, width), f32),
            pltpu.VMEM((heads, 2 * head_dim, code_rows), bf16),
            pltpu.VMEM((heads, code_rows, 2 * head_dim), bf16),
            pltpu.VMEM((seq_count, tok_rows, width), bf16),
            pltpu.VMEM((chips, feats, tile), bf16),
            pltpu.SemaphoreType.DMA((parts,)),
        ],
        compiler_params=hash_params,
        name="hash_backward",
    )(
        spots, *token_parts, *[in_vmem(p) for p in gnum_parts], qkv_all, bit_w, bit_wt,
        q_unit, k_unit, values, inverses, tables, conv_grad, tap_parts,
    )

    half = width // 2
    group = chips // 4
    per_chip = lambda *dims: pl.BlockSpec((group,) + dims, lambda i: (i, 0, 0))
    keep, give = pl.pallas_call(
        chip_sum_kernel,
        grid=(4,),
        in_specs=[smem, per_chip(width, tok_rows), per_chip(width, tok_rows)],
        out_specs=[per_chip(half, tok_rows), per_chip(half, tok_rows)],
        out_shape=[shape((chips, half, tok_rows), bf16)] * 2,
        compiler_params=params,
        name="chip_sum",
    )(spots, back_keep, core_swap(back_give))
    *pair_sums, pair_done = once(
        pair_sum_kernel, "pair_sum",
        [shape((half, tok_rows) if ringed else (chips, half, tok_rows), bf16)]
        * (chips if ringed else 1)
        + [shape((8, 128), f32)],
        [spots, keep, head_swap(give)],
        outside=tuple(range(1, chips)) if ringed else (),
    )
    qkv_got = across(qkv_send)
    if ringed:
        back_got = [pair_sums[0]]
        for d in range(1, chips):
            perm = [(CORES * c + k, CORES * (c ^ d) + k) for c in range(chips) for k in range(CORES)]
            back_got.append(lax.ppermute(pair_sums[d], "seq", perm))
        qkv_got, *tied = lax.optimization_barrier((qkv_got, *back_got[1:5]))
        back_got = [back_got[0]] + tied + back_got[1 + len(tied) :]
        back_got = [p[None] for p in back_got]
    else:
        back_got = [across(pair_sums[0])]

    qkv_mine, qkv_give = once(
        weight_sum_kernel, "weight_sum",
        [shape((own_rows, 3 * feats + 64), f32)] * 2,
        [spots, qkv_got],
        after=[pair_done],
    )
    qkv_other = core_swap(qkv_give)

    extras = extras.astype(f32)
    norm_half = jnp.sum(extras[:, :sum_rows], axis=0)
    count_half = extras[:, sum_rows : sum_rows + count_rows]
    count_half = count_half.reshape(chips, heads, 2, chips, CORES, chip_buckets // CORES, rows)
    count_half = lax.dynamic_index_in_dim(count_half, spot, 3, keepdims=False)
    count_half = jnp.transpose(count_half[..., :hashes], (3, 0, 2, 5, 1, 4))
    count_mine = lax.dynamic_index_in_dim(count_half, core, 0, keepdims=False)
    count_give = lax.dynamic_index_in_dim(count_half, 1 - core, 0, keepdims=False)
    tap_first = jnp.where(core == 0, qkv_mine[:heads], qkv_give[:heads])
    tap_half = tap_first[:, 3 * feats : 3 * feats + taps]
    swapped = core_swap(
        jnp.concatenate([norm_half.reshape(-1), count_give.reshape(-1), tap_half.reshape(-1)])
    )
    norm_size, count_size = norm_half.size, count_give.size

    norm_grad = norm_half + swapped[:norm_size].reshape(norm_half.shape)
    norm_grad = jnp.transpose(
        norm_grad.reshape(width // tile, 4, tile), (1, 0, 2)
    ).reshape(4, width)
    count_other = swapped[norm_size : norm_size + count_size].reshape(count_mine.shape)
    occupancy = jnp.transpose(
        in_order(count_mine, count_other, 3), (1, 0, 2, 3, 4)
    ).reshape(2, hash_count, group_heads, buckets // seq_count)
    occupancy = occupancy * (buckets / (tok_rows * seq_count))
    conv_tap_grad = in_order(tap_half, swapped[norm_size + count_size :].reshape(heads, taps), 0)

    flag = shape((8, 128), f32)
    matrix = lambda value: [pltpu.HBM(value.shape, f32)] * 3 + [pltpu.HBM(value.shape, bf16)]
    (
        up_new, up_first_new, up_second_new, up_copy,
        down_new, down_first_new, down_second_new, down_copy,
        out_new, out_first_new, out_second_new, out_copy, big_done,
    ) = piped(
        big_adam_kernel, "big_adam",
        matrix(up_weight) + matrix(down_weight.T) + matrix(out_weight.T) + [flag],
        [
            big_owned, up_weight, up_first, up_second,
            down_weight.T, down_first.T, down_second.T,
            out_weight.T, out_first.T, out_second.T,
        ],
    )
    qkv_new, qkv_first_new, qkv_second_new, qkv_copy = piped(
        qkv_adam_kernel, "qkv_adam", matrix(qkv_weight),
        [spots, qkv_mine, qkv_other, qkv_weight, qkv_first, qkv_second],
    )
    norm_new, norm_first_new, norm_second_new = adam_step(
        norm_params, norm_first, norm_second, norm_grad, 0.3
    )
    conv_new, conv_first_new, conv_second_new = adam_step(
        conv_taps, conv_first, conv_second, conv_tap_grad, CONV ** (-0.5)
    )
    (back_low,) = once(
        back_sum_kernel, "back_sum",
        [shape((half, tok_rows), bf16)],
        back_got,
        after=[big_done],
    )
    (tokens_grad,) = once(
        final_kernel, "tokens_grad",
        [shape((tok_rows, width), f32)],
        [spots, back_low, head_swap(back_low), grad_mixer],
        outside=(0,),
    )
    return (
        block_out,
        tokens_grad,
        occupancy,
        qkv_new,
        qkv_first_new,
        qkv_second_new,
        qkv_copy,
        out_new.T,
        out_first_new.T,
        out_second_new.T,
        out_copy.T,
        up_new,
        up_first_new,
        up_second_new,
        up_copy,
        down_new.T,
        down_first_new.T,
        down_second_new.T,
        down_copy.T,
        norm_new,
        norm_first_new,
        norm_second_new,
        conv_new,
        conv_first_new,
        conv_second_new,
    )


def solution(mesh):
    in_specs = (
        P("seq", None),
        P("seq", None),
        P(),
        P(None, None, "head", None),
        P(None, "seq", "head"),
        P(None, "seq", "head"),
        P(None, "seq", "head"),
        P("head", "seq"),
        P("head", "seq"),
        P("head", "seq"),
        P("seq", "head"),
        P("seq", "head"),
        P("seq", "head"),
        P("head", "seq"),
        P("head", "seq"),
        P("head", "seq"),
        P(),
        P(),
        P(),
        P("head", None),
        P("head", None),
        P("head", None),
    )
    out_specs = (
        P("seq", None),
        P("seq", None),
        P(None, None, "head", "seq"),
        P(None, "seq", "head"),
        P(None, "seq", "head"),
        P(None, "seq", "head"),
        P(None, "seq", "head"),
        P("head", "seq"),
        P("head", "seq"),
        P("head", "seq"),
        P("head", "seq"),
        P("seq", "head"),
        P("seq", "head"),
        P("seq", "head"),
        P("seq", "head"),
        P("head", "seq"),
        P("head", "seq"),
        P("head", "seq"),
        P("head", "seq"),
        P(),
        P(),
        P(),
        P("head", None),
        P("head", None),
        P("head", None),
    )
    return jax.shard_map(
        on_device, mesh=mesh, in_specs=in_specs, out_specs=out_specs, check_vma=False
    )
```
